128 devices in a mesh: lon: 8 (over y, core), lat: 16 (over x, z).
Axes of the slice: x: 4, y: 4, z: 4, core: 2. Of those that a mesh axis runs over, the one named last changes fastest.
Arguments:
- theta: float32 [16, 2048, 2048], P(None, 'lat', 'lon'), may hold values from -6 to 6
- kappa: float32 [2048, 2048], P('lat', 'lon'), may hold values from 0.03 to 0.24
- layer_weight: float32 [16], replicated, may hold values from 0.25 to 1.5
- diag: float32 [2048, 2048], P(('lon', 'lat')), may hold values from 0.2 to 2
- land_blocks: int32 [64, 64], replicated, may hold values 0 or 1
Outputs:
- new_theta: float32 [16, 2048, 2048], P(None, 'lat', 'lon')
- psi: float32 [2048, 2048], P(('lon', 'lat'))
The draws below stay inside these ranges and needn't reach their ends.
All inputs are finite; a program needn't handle non-finite values.
Results may differ from the reference program's by a relative error of at most 0.0001.
Values sent between devices are 32-bit elements; how exact they have to be, the bound alone decides.
A program may use at most 64 MiB of HBM per device.

```python
import math
import jax
import jax.numpy as jnp
from jax import lax

K = 16
BS = 32
ITERS = 4
NX = 2048
NY = 2048
MBX = 64
MBY = 64


def set_ends(result, rng, low, high):
    extent = result.shape
    spot = [jax.random.randint(jax.random.fold_in(rng, axis), (), 0, extent[axis]) for axis in range(len(extent))]
    result = result.at[tuple(spot)].set(low)
    longest = extent.index(max(extent))
    spot[longest] = (spot[longest] + 1) % extent[longest]
    return result.at[tuple(spot)].set(high)


def shard_levels(rng, dims, pieces, smallest, high):
    def one(dim, shards_of):
        steps = jax.random.uniform(jax.random.fold_in(jax.random.fold_in(rng, 6), dim), (shards_of,), jnp.float32, smallest / len(pieces), high / len(pieces))
        return jnp.repeat(jnp.exp(steps), dims[dim] // shards_of).reshape((-1,) + (1,) * (len(dims) - dim - 1))

    factor_of = one(*pieces[0])
    for cut in pieces[1:]:
        factor_of = factor_of * one(*cut)
    return factor_of


def gaussian(own_key, shape, spread, limit, split=(), held_as=jnp.bfloat16):
    drawn = jax.random.normal(own_key, shape, jnp.float32) * spread
    if len(split) > 0:
        drawn = shard_levels(own_key, shape, split, -0.22, 0.18) * drawn
    return jnp.clip(drawn, min=-limit, max=limit).astype(held_as)


def setup_inputs(seed: int = 0) -> dict:
    key_list = jax.random.split(jax.random.key(seed), 6)
    theta = gaussian(key_list[0], (K, NY, NX), 1.0, 6.0, ((1, 16), (2, 8)), jnp.float32)
    kappa = jnp.clip(jnp.exp(math.log(0.24) - 2.0794415 * jax.random.uniform(key_list[1], (NY, NX), jnp.float32) ** shard_levels(key_list[1], (NY, NX), ((0, 16), (1, 8)), -0.2, 0.2)), 0.03, 0.24)
    layer_weight = jnp.clip(jax.random.uniform(key_list[2], (K,), jnp.float32, 0.25, 1.5), 0.25, 1.5)
    diag = jnp.clip(0.2 + 1.8 * jax.random.uniform(key_list[3], (NX, NY), jnp.float32) ** shard_levels(key_list[3], (NX, NY), ((0, 128),), -0.2, 0.2), 0.2, 2.0)
    land_blocks = set_ends((jax.random.randint(key_list[4], (MBY, MBX), 0, 4) < 3).astype(jnp.int32), jax.random.fold_in(key_list[4], 1), 0, 1)
    return dict(theta=theta, kappa=kappa, layer_weight=layer_weight, diag=diag, land_blocks=land_blocks)


def spread_mask(land_blocks):
    cells = jnp.repeat(land_blocks.astype(jnp.float32), BS, axis=0)
    return jnp.repeat(cells, BS, axis=1)


def around_levels(field):
    eastward = jnp.roll(field, -1, axis=2)
    westward = jnp.roll(field, 1, axis=2)
    southern = jnp.concatenate([jnp.zeros_like(field[:, :1, :]), field[:, :-1, :]], axis=1)
    northern = jnp.concatenate([field[:, 1:, :], field[:, -1:, ::-1]], axis=1)
    return eastward + westward + southern + northern


def around_plane(field):
    eastward = jnp.roll(field, -1, axis=0)
    westward = jnp.roll(field, 1, axis=0)
    southern = jnp.concatenate([jnp.zeros_like(field[:, :1]), field[:, :-1]], axis=1)
    northern = jnp.concatenate([field[:, 1:], field[::-1, -1:]], axis=1)
    return eastward + westward + southern + northern


def reference(theta, kappa, layer_weight, diag, land_blocks):
    ocean = spread_mask(land_blocks)
    masked = ocean[None] * theta
    new_theta = theta + ocean[None] * kappa[None] * (around_levels(masked) - 4.0 * masked)
    column_sum = jnp.einsum("k,kyx->yx", layer_weight, new_theta, precision=lax.Precision.HIGHEST)
    forcing = (ocean * column_sum).T
    ocean_plane = ocean.T

    def operate(field):
        return ocean_plane * ((4.0 + diag) * field - around_plane(field))

    solution = jnp.zeros_like(forcing)
    residual = forcing
    direction = forcing
    norm_now = jnp.sum(residual * residual)
    for iteration in range(ITERS):
        applied = operate(direction)
        step_size = norm_now / jnp.sum(direction * applied)
        solution = solution + step_size * direction
        residual = residual - step_size * applied
        norm_next = jnp.sum(residual * residual)
        direction = residual + (norm_next / norm_now) * direction
        norm_now = norm_next
    return new_theta, solution
```

```python
import functools

import jax
import jax.numpy as jnp
from jax import lax
from jax.experimental import pallas as pl
from jax.experimental.pallas import tpu as pltpu
from jax.sharding import PartitionSpec as P

MESH = pl.DeviceIdType.MESH
BS = 32
HALO = 8
LANES = 128
F32 = jnp.float32
BF16 = jnp.bfloat16
BASIS = 5
PAIRS = [(a, b) for a in range(BASIS) for b in range(a, BASIS) if a < BASIS - 1]
SLOTS = 16


def iota(shape, axis):
    return lax.broadcasted_iota(jnp.int32, shape, axis)


def hot(condition):
    return jnp.where(condition, 1.0, 0.0).astype(BF16)


def bdot(left, right):
    return jnp.dot(left, right, preferred_element_type=F32)


def ndot(left, right):
    return lax.dot_general(left, right, (((1,), (1,)), ((), ())), preferred_element_type=F32)


def pieces(value):
    first = value.astype(BF16)
    rest = value - first.astype(F32)
    second = rest.astype(BF16)
    third = (rest - second.astype(F32)).astype(BF16)
    return [first, second, third]


def flip_lanes(value):
    width = value.shape[1]
    turn = hot(iota((width, width), 0) + iota((width, width), 1) == width - 1)
    parts = [bdot(piece, turn) for piece in pieces(value)]
    return (parts[0] + parts[1]) + parts[2]


def flip_rows(value, groups):
    count = value.shape[0]
    row = iota((count, count), 0)
    ends, start = jnp.zeros((count, count), jnp.int32), 0
    for size in groups:
        ends = jnp.where(row >= start, 2 * start + size - 1, ends)
        start += size
    turn = hot(row + iota((count, count), 1) == ends)
    parts = [bdot(turn, piece) for piece in pieces(value)]
    return (parts[0] + parts[1]) + parts[2]


def two_sum(a, b):
    s = a + b
    t = s - a
    return s, (a - (s - t)) + (b - t)


def halves(a):
    t = a * 4097.0
    high = t - (t - a)
    return high, a - high


def two_prod(a, b):
    p = a * b
    ah, al = halves(a)
    bh, bl = halves(b)
    return p, ((ah * bh - p) + ah * bl + al * bh) + al * bl


def quick(a, b):
    s = a + b
    return s, b - (s - a)


def df_mul(x, y):
    p, e = two_prod(x[0], y[0])
    return quick(p, e + (x[0] * y[1] + x[1] * y[0]))


def df_add(x, y):
    s, e = two_sum(x[0], y[0])
    return quick(s, e + (x[1] + y[1]))


def df_sub(x, y):
    return df_add(x, (-y[0], -y[1]))


def df_div(x, y):
    first = x[0] / y[0]
    rest = df_sub(x, df_mul(y, (first, jnp.zeros_like(first))))
    second = rest[0] / y[0]
    return quick(first, second)


def neighbours(value):
    rows, width = value.shape
    return (
        pltpu.roll(value, 1, 0)
        + pltpu.roll(value, rows - 1, 0)
        + pltpu.roll(value, 1, 1)
        + pltpu.roll(value, width - 1, 1)
    )


def kernel(
    nlon, nlat,
    weight, land, theta, kappa, diag,
    out_theta, out_psi,
    th, fresh, kp, skt, ext, edge, dg, ocs, basis, rows_out, north, south, cols_out, east, west,
    part1, part2,
    in_sem, out_sem, send_sem, recv_sem, edge_send, edge_recv, mir_send, mir_edge_send,
    diag_send, diag_recv, halo_send, halo_recv, red_send1, red_recv1, red_send2, red_recv2,
):
    levels, cy, cx = th.shape
    ny, nx = cy * nlat, cx * nlon
    strip = cx // nlat
    wide = strip + 2 * HALO
    by, bx = land.shape
    total = nlon * nlat
    i = lax.axis_index("lon")
    j = lax.axis_index("lat")
    t = i * nlat + j
    top = j == nlat - 1
    ends = jnp.logical_or(j == 0, top)

    def remote(src, dst, send, recv, lon, lat):
        return pltpu.make_async_remote_copy(
            src_ref=src, dst_ref=dst, send_sem=send, recv_sem=recv,
            device_id=(lon, lat), device_id_type=MESH,
        )

    def lon_of(value):
        return lax.rem(value + 2 * nlon, nlon)

    def lat_of(value):
        return lax.rem(value + 2 * nlat, nlat)

    chunk = levels // 4
    loads = [
        pltpu.make_async_copy(theta.at[pl.ds(q * chunk, chunk)], th.at[pl.ds(q * chunk, chunk)], in_sem.at[q])
        for q in range(4)
    ]
    load_kappa = pltpu.make_async_copy(kappa, kp, in_sem.at[4])
    load_diag = pltpu.make_async_copy(diag, dg.at[HALO:HALO + strip, 0:ny], in_sem.at[5])
    for copy in loads:
        copy.start()
    load_kappa.start()
    load_diag.start()

    barrier = pltpu.get_barrier_semaphore()

    def greet(d, _):
        other = lax.rem(t + d, total)
        pl.semaphore_signal(
            barrier, inc=1, device_id=(other // nlat, lax.rem(other, nlat)), device_id_type=MESH
        )
        return 0

    lax.fori_loop(1, total, greet, 0)

    table = land[...].astype(F32).astype(BF16)
    row_block = (j * cy + iota((cy, by), 0)) >> 5
    on_rows = bdot(hot(row_block == iota((cy, by), 1)), table).astype(BF16)
    col_block = (i * cx + iota((bx, cx), 1)) >> 5
    cols_hot = hot(col_block == iota((bx, cx), 0))
    ocean = bdot(on_rows, cols_hot)
    west_block = lax.rem(i * (cx // BS) + bx - 1, bx)
    east_block = lax.rem((i + 1) * (cx // BS), bx)
    ocean_west = bdot(on_rows, hot(iota((bx, LANES), 0) == west_block))
    ocean_east = bdot(on_rows, hot(iota((bx, LANES), 0) == east_block))
    edge_row = iota((8, by), 0)
    edge_col = iota((8, by), 1)
    south_hot = hot(jnp.logical_and(edge_row == 0, edge_col == j * (cy // BS) - 1))
    north_block = jnp.where(top, by - 1, (j + 1) * (cy // BS))
    north_hot = hot(jnp.logical_and(edge_row == 0, edge_col == north_block))
    north_cols = jnp.where(top, bx - 1 - col_block, col_block)
    ocean_south = bdot(bdot(south_hot, table).astype(BF16), cols_hot)[0:1]
    ocean_north = bdot(
        bdot(north_hot, table).astype(BF16), hot(north_cols == iota((bx, cx), 0))
    )[0:1]

    strip_x = (strip * t - HALO + nx + iota((wide, bx), 0)) % nx >> 5
    strip_hot = hot(strip_x == iota((wide, bx), 1))
    on_cols = ndot(strip_hot, table).astype(BF16)
    ocs[:, 0:ny] = bdot(on_cols, hot((iota((by, ny), 1) >> 5) == iota((by, ny), 0)))
    mirror_hot = hot((bx - 1 - strip_x) == iota((wide, bx), 1))
    on_mirror = ndot(mirror_hot, table).astype(BF16)
    keep = jnp.logical_and(iota((by, LANES), 0) == by - 1, iota((by, LANES), 1) < 8)
    ocs[:, ny:ny + LANES] = bdot(on_mirror, hot(keep))

    skt[:, 0:HALO, :] = jnp.zeros((2, HALO, cy), F32)
    skt[:, HALO + cx:, :] = jnp.zeros((2, HALO, cy), F32)
    load_kappa.wait()
    skt[1, HALO:HALO + cx, :] = kp[...].T
    column = jnp.zeros((cy, cx), F32)
    for q in range(4):
        loads[q].wait()
        for k in range(q * chunk, (q + 1) * chunk):
            column = column + weight[k] * th[k]
    skt[0, HALO:HALO + cx, :] = column.T

    pl.semaphore_wait(barrier, total - 1)

    own_lanes = pl.ds(pl.multiple_of(j * cy, LANES), cy)
    mirror_lanes = pl.ds(ny, LANES)

    def block_rows(m):
        return skt.at[:, pl.ds(pl.multiple_of(m * strip, 8), wide), :]

    first_rows = skt.at[:, HALO:2 * HALO, :]
    last_rows = skt.at[:, cx:cx + HALO, :]

    def main_copy(d):
        m = lax.rem(j + d, nlat)
        return remote(block_rows(m), ext.at[:, :, own_lanes], send_sem.at[d], recv_sem.at[j], i, m)

    def mirror_copy(m):
        return remote(
            block_rows(nlat - 1 - m), ext.at[:, :, mirror_lanes], mir_send.at[m], recv_sem.at[nlat],
            nlon - 1 - i, m,
        )

    def run_start(make):
        def step(d, _):
            make(d).start()
            return 0
        return step

    lax.fori_loop(1, nlat, run_start(main_copy), 0)
    own_copy = pltpu.make_async_copy(block_rows(j), ext.at[:, :, own_lanes], recv_sem.at[j])
    own_copy.start()
    left_edge = remote(first_rows, edge.at[:, :, own_lanes], edge_send.at[0], edge_recv.at[j], lon_of(i - 1), nlat - 1)
    right_edge = remote(last_rows, edge.at[:, :, own_lanes], edge_send.at[1], edge_recv.at[j], lon_of(i + 1), 0)
    left_edge.start()
    right_edge.start()
    folded_lon = lon_of(nlon - 2 - i)
    folded_self = folded_lon == i
    fold_edge = remote(
        last_rows, edge.at[:, :, mirror_lanes], mir_edge_send.at[0], edge_recv.at[nlat], folded_lon, nlat - 1
    )
    fold_edge_own = pltpu.make_async_copy(last_rows, edge.at[:, :, mirror_lanes], edge_recv.at[nlat])
    fold_edge_low = remote(
        first_rows, edge.at[:, :, mirror_lanes], mir_edge_send.at[1], edge_recv.at[nlat], lon_of(nlon - i), 0
    )

    @pl.when(top)
    def _():
        lax.fori_loop(0, nlat, run_start(mirror_copy), 0)
        fold_edge_low.start()

        @pl.when(folded_self)
        def _():
            fold_edge_own.start()

        @pl.when(jnp.logical_not(folded_self))
        def _():
            fold_edge.start()

    load_diag.wait()
    after, before = lax.rem(t + 1, total), lax.rem(t + total - 1, total)
    diag_up = remote(
        dg.at[strip:strip + HALO, 0:ny], dg.at[0:HALO, 0:ny], diag_send.at[0], diag_recv.at[0],
        after // nlat, lax.rem(after, nlat),
    )
    diag_down = remote(
        dg.at[HALO:2 * HALO, 0:ny], dg.at[HALO + strip:wide, 0:ny], diag_send.at[1], diag_recv.at[1],
        before // nlat, lax.rem(before, nlat),
    )
    diag_up.start()
    diag_down.start()

    rows_out[0] = th[:, 0, :]
    rows_out[1] = th[:, cy - 1, :]
    to_south = remote(rows_out.at[0], north, halo_send.at[0], halo_recv.at[0], i, lat_of(j - 1))
    to_north = remote(rows_out.at[1], south, halo_send.at[1], halo_recv.at[1], i, lat_of(j + 1))
    to_fold = remote(rows_out.at[1], north, halo_send.at[1], halo_recv.at[0], nlon - 1 - i, j)

    @pl.when(j > 0)
    def _():
        to_south.start()

    @pl.when(jnp.logical_not(top))
    def _():
        to_north.start()

    @pl.when(top)
    def _():
        to_fold.start()

    lane = iota((cy, LANES), 1)
    packed = jnp.zeros((cy, LANES), F32)
    for k in range(levels):
        packed = jnp.where(lane == k, pltpu.roll(th[k, :, 0:LANES], k, 1), packed)
        packed = jnp.where(
            lane == levels + k, pltpu.roll(th[k, :, cx - LANES:cx], levels + k + 1, 1), packed
        )
    cols_out[...] = packed
    to_west = remote(cols_out, east, halo_send.at[2], halo_recv.at[2], lon_of(i - 1), j)
    to_east = remote(cols_out, west, halo_send.at[3], halo_recv.at[3], lon_of(i + 1), j)
    to_west.start()
    to_east.start()

    diag_up.wait_recv()
    diag_down.wait_recv()
    diag_fold = remote(
        dg.at[:, ny - LANES:ny], dg.at[:, ny:ny + LANES], diag_send.at[2], diag_recv.at[2],
        nlon - 1 - i, nlat - 1 - j,
    )
    diag_fold.start()

    to_south.wait_recv()
    to_west.wait_recv()
    to_east.wait_recv()

    @pl.when(j > 0)
    def _():
        to_north.wait_recv()

    @pl.when(j == 0)
    def _():
        south[...] = jnp.zeros_like(south)

    @pl.when(top)
    def _():
        north[...] = flip_lanes(north[...])

    west[...] = west[...] * ocean_west
    east[...] = east[...] * ocean_east
    scale = ocean * kp[...]
    first_row = iota((cy, cx), 0) == 0
    last_row = iota((cy, cx), 0) == cy - 1
    first_lane = iota((cy, cx), 1) == 0
    last_lane = iota((cy, cx), 1) == cx - 1

    def update(k, _):
        level = th[k]
        held = ocean * level
        from_west = pltpu.roll(west[...], LANES - levels - k, 1)
        from_east = pltpu.roll(east[...], LANES - 1 - k, 1)
        if cx > LANES:
            pad = jnp.zeros((cy, cx - LANES), F32)
            from_west = jnp.concatenate([from_west, pad], axis=1)
            from_east = jnp.concatenate([pad, from_east], axis=1)
        beside = jnp.where(first_lane, from_west, pltpu.roll(held, 1, 1))
        beside = beside + jnp.where(last_lane, from_east, pltpu.roll(held, cx - 1, 1))
        beside = beside + jnp.where(first_row, ocean_south * south[pl.ds(k, 1), :], pltpu.roll(held, 1, 0))
        beside = beside + jnp.where(last_row, ocean_north * north[pl.ds(k, 1), :], pltpu.roll(held, cy - 1, 0))
        fresh[k] = level + scale * (beside - 4.0 * held)
        return 0

    lax.fori_loop(0, levels, update, 0)
    store_theta = pltpu.make_async_copy(fresh, out_theta, out_sem.at[0])
    store_theta.start()

    for lat in range(nlat + 1):
        lanes = pl.ds(lat * cy, cy) if lat < nlat else mirror_lanes
        pltpu.make_async_copy(block_rows(0), ext.at[:, :, lanes], recv_sem.at[lat]).wait()

    @pl.when(ends)
    def _():
        for lat in range(nlat + 1):
            lanes = pl.ds(lat * cy, cy) if lat < nlat else mirror_lanes
            pltpu.make_async_copy(first_rows, edge.at[:, :, lanes], edge_recv.at[lat]).wait()

    @pl.when(jnp.logical_not(ends))
    def _():
        edge[...] = jnp.zeros_like(edge)

    diag_fold.wait_recv()
    tall = jnp.concatenate(
        [ext[0, :, ny:], ext[1, :, ny:], dg[:, ny:], edge[0, :, ny:], edge[1, :, ny:]], axis=0
    )
    tall = flip_rows(flip_lanes(tall), (wide, wide, wide, HALO, HALO))
    ext[0, :, ny:] = tall[0:wide]
    ext[1, :, ny:] = tall[wide:2 * wide]
    dg[:, ny:] = tall[2 * wide:3 * wide]
    edge[0, :, ny:] = tall[3 * wide:3 * wide + HALO]
    edge[1, :, ny:] = tall[3 * wide + HALO:]

    @pl.when(j == 0)
    def _():
        ext[:, 0:HALO, :] = edge[...]

    @pl.when(top)
    def _():
        ext[:, HALO + strip:, :] = edge[...]

    mask = ocs[...]
    held = mask * ext[0]
    basis[0] = mask * ext[0] + mask * ext[1] * (neighbours(held) - 4.0 * held)
    diag_up.wait_send()
    diag_down.wait_send()
    diag_fold.wait_send()
    dg[...] = (dg[...] - 1.0) * 0.25
    for step in range(BASIS - 1):
        value = basis[step]
        basis[step + 1] = ocs[...] * (dg[...] * value - 0.25 * neighbours(value))

    zero = jnp.zeros((8, LANES), F32)

    def accumulate(c, carry):
        sums = list(carry)
        lanes = pl.ds(pl.multiple_of(c * LANES, LANES), LANES)
        for h in range(strip // 8):
            values = [basis[b, HALO + 8 * h:HALO + 8 * h + 8, lanes] for b in range(BASIS)]
            split = [halves(value) for value in values]
            for n, (a, b) in enumerate(PAIRS):
                p = values[a] * values[b]
                (ah, al), (bh, bl) = split[a], split[b]
                e = ((ah * bh - p) + (ah * bl + al * bh)) + al * bl
                s, f = two_sum(sums[2 * n], p)
                sums[2 * n], sums[2 * n + 1] = s, sums[2 * n + 1] + (e + f)
        return tuple(sums)

    sums = lax.fori_loop(0, ny // LANES, accumulate, (zero,) * (2 * len(PAIRS)))
    place = iota((SLOTS, LANES), 0)
    high = jnp.zeros((SLOTS, LANES), F32)
    low = jnp.zeros((SLOTS, LANES), F32)
    for n in range(len(PAIRS)):
        h, l = sums[2 * n], sums[2 * n + 1]
        for shift in (4, 2, 1):
            h, e = two_sum(h, pltpu.roll(h, shift, 0))
            l = l + pltpu.roll(l, shift, 0) + e
        high = jnp.where(place == n, h[0:1], high)
        low = jnp.where(place == n, l[0:1], low)

    def fold_in(ref, count, index):
        def add(d, carry):
            h, l = carry
            other = ref[d]
            s, e = two_sum(h, other[0:SLOTS])
            return s, l + (e + other[SLOTS:])
        start = ref[0]
        return lax.fori_loop(1, count, add, (start[0:SLOTS], start[SLOTS:]))

    own1 = part1.at[i]
    part1[pl.ds(i, 1)] = jnp.concatenate([high, low], axis=0)[None]

    def lon_copy(d):
        return remote(own1, own1, red_send1.at[d], red_recv1.at[i], lax.rem(i + d, nlon), j)

    lax.fori_loop(1, nlon, run_start(lon_copy), 0)

    def lon_wait(d, _):
        other = lax.rem(i + d, nlon)
        pltpu.make_async_copy(part1.at[other], part1.at[other], red_recv1.at[other]).wait()
        return 0

    lax.fori_loop(1, nlon, lon_wait, 0)
    high, low = fold_in(part1, nlon, i)
    own2 = part2.at[j]
    part2[pl.ds(j, 1)] = jnp.concatenate([high, low], axis=0)[None]

    def lat_copy(d):
        return remote(own2, own2, red_send2.at[d], red_recv2.at[j], i, lax.rem(j + d, nlat))

    lax.fori_loop(1, nlat, run_start(lat_copy), 0)

    def lat_wait(d, _):
        other = lax.rem(j + d, nlat)
        pltpu.make_async_copy(part2.at[other], part2.at[other], red_recv2.at[other]).wait()
        return 0

    lax.fori_loop(1, nlat, lat_wait, 0)
    high, low = fold_in(part2, nlat, j)
    shift = LANES // 2
    while shift:
        high, e = two_sum(high, pltpu.roll(high, shift, 1))
        low = low + pltpu.roll(low, shift, 1) + e
        shift //= 2
    high, low = quick(high, low)

    gram = {}
    for n, (a, b) in enumerate(PAIRS):
        gram[a, b] = gram[b, a] = (high[n:n + 1], low[n:n + 1])
    size = BASIS - 1

    def scaled(x, factor):
        return x[0] * factor, x[1] * factor

    matrix = [
        [
            df_add(
                scaled(gram[a, b + 1], 4.0),
                df_add(scaled(gram[a, b], 4.0), gram[a, b]),
            )
            for b in range(size)
        ]
        for a in range(size)
    ]
    right = [gram[0, a] for a in range(size)]
    for p in range(size):
        for a in range(p + 1, size):
            factor = df_div(matrix[a][p], matrix[p][p])
            for b in range(p + 1, size):
                matrix[a][b] = df_sub(matrix[a][b], df_mul(factor, matrix[p][b]))
            right[a] = df_sub(right[a], df_mul(factor, right[p]))
    answer = [None] * size
    for p in reversed(range(size)):
        value = right[p]
        for b in range(p + 1, size):
            value = df_sub(value, df_mul(matrix[p][b], answer[b]))
        answer[p] = df_div(value, matrix[p][p])
    spread = [jnp.broadcast_to(x[0], (strip, LANES)) for x in answer]

    def combine(c, _):
        lanes = pl.ds(pl.multiple_of(c * LANES, LANES), LANES)
        value = spread[size - 1] * basis[size - 1, HALO:HALO + strip, lanes]
        for b in reversed(range(size - 1)):
            value = value + spread[b] * basis[b, HALO:HALO + strip, lanes]
        out_psi[:, lanes] = value
        return 0

    lax.fori_loop(0, ny // LANES, combine, 0)

    def run_wait(make):
        def step(d, _):
            make(d).wait_send()
            return 0
        return step

    lax.fori_loop(1, nlat, run_wait(main_copy), 0)
    left_edge.wait_send()
    right_edge.wait_send()

    @pl.when(top)
    def _():
        lax.fori_loop(0, nlat, run_wait(mirror_copy), 0)
        fold_edge_low.wait_send()

        @pl.when(jnp.logical_not(folded_self))
        def _():
            fold_edge.wait_send()

    @pl.when(j > 0)
    def _():
        to_south.wait_send()

    to_north.wait_send()
    to_west.wait_send()
    to_east.wait_send()
    lax.fori_loop(1, nlon, run_wait(lon_copy), 0)
    lax.fori_loop(1, nlat, run_wait(lat_copy), 0)
    store_theta.wait()


def per_device(nlon, nlat, theta, kappa, layer_weight, diag, land_blocks):
    levels, cy, cx = theta.shape
    strip, ny = diag.shape
    wide = strip + 2 * HALO
    vmem = pl.BlockSpec(memory_space=pltpu.VMEM)
    anywhere = pl.BlockSpec(memory_space=pl.ANY)
    dma = pltpu.SemaphoreType.DMA
    return pl.pallas_call(
        functools.partial(kernel, nlon, nlat),
        out_shape=(
            jax.ShapeDtypeStruct(theta.shape, F32),
            jax.ShapeDtypeStruct(diag.shape, F32),
        ),
        in_specs=[pl.BlockSpec(memory_space=pltpu.SMEM), vmem, anywhere, anywhere, anywhere],
        out_specs=(anywhere, vmem),
        scratch_shapes=[
            pltpu.VMEM((levels, cy, cx), F32),
            pltpu.VMEM((levels, cy, cx), F32),
            pltpu.VMEM((cy, cx), F32),
            pltpu.VMEM((2, cx + 2 * HALO, cy), F32),
            pltpu.VMEM((2, wide, ny + LANES), F32),
            pltpu.VMEM((2, HALO, ny + LANES), F32),
            pltpu.VMEM((wide, ny + LANES), F32),
            pltpu.VMEM((wide, ny + LANES), F32),
            pltpu.VMEM((BASIS, wide, ny + LANES), F32),
            pltpu.VMEM((2, levels, cx), F32),
            pltpu.VMEM((levels, cx), F32),
            pltpu.VMEM((levels, cx), F32),
            pltpu.VMEM((cy, LANES), F32),
            pltpu.VMEM((cy, LANES), F32),
            pltpu.VMEM((cy, LANES), F32),
            pltpu.VMEM((nlon, 2 * SLOTS, LANES), F32),
            pltpu.VMEM((nlat, 2 * SLOTS, LANES), F32),
            dma((6,)),
            dma((1,)),
            dma((nlat,)),
            dma((nlat + 1,)),
            dma((2,)),
            dma((nlat + 1,)),
            dma((nlat,)),
            dma((2,)),
            dma((3,)),
            dma((3,)),
            dma((4,)),
            dma((4,)),
            dma((nlon,)),
            dma((nlon,)),
            dma((nlat,)),
            dma((nlat,)),
        ],
        compiler_params=pltpu.CompilerParams(
            collective_id=0, has_side_effects=True, vmem_limit_bytes=48 << 20
        ),
        name="ocean_step",
    )(layer_weight, land_blocks, theta, kappa, diag)


def solution(mesh):
    placed = (P(None, "lat", "lon"), P("lat", "lon"), P(), P(("lon", "lat"), None), P())
    return jax.shard_map(
        functools.partial(per_device, mesh.shape["lon"], mesh.shape["lat"]),
        mesh=mesh,
        in_specs=placed,
        out_specs=(P(None, "lat", "lon"), P(("lon", "lat"), None)),
        check_vma=False,
    )
```

```python
import functools

import jax
import jax.numpy as jnp
from jax import lax
from jax.experimental import pallas as pl
from jax.experimental.pallas import tpu as pltpu
from jax.sharding import PartitionSpec as P

MESH = pl.DeviceIdType.MESH
BS = 32
HALO = 8
LANES = 128
F32 = jnp.float32
BF16 = jnp.bfloat16
BASIS = 5
PAIRS = [(a, b) for a in range(BASIS) for b in range(a, BASIS) if a < BASIS - 1]
SLOTS = 16


def iota(shape, axis):
    return lax.broadcasted_iota(jnp.int32, shape, axis)


def hot(condition):
    return jnp.where(condition, 1.0, 0.0).astype(BF16)


def bdot(left, right):
    return jnp.dot(left, right, preferred_element_type=F32)


def ndot(left, right):
    return lax.dot_general(left, right, (((1,), (1,)), ((), ())), preferred_element_type=F32)


def pieces(value):
    first = value.astype(BF16)
    rest = value - first.astype(F32)
    second = rest.astype(BF16)
    third = (rest - second.astype(F32)).astype(BF16)
    return [first, second, third]


def flip_lanes(value):
    width = value.shape[1]
    turn = hot(iota((width, width), 0) + iota((width, width), 1) == width - 1)
    parts = [bdot(piece, turn) for piece in pieces(value)]
    return (parts[0] + parts[1]) + parts[2]


def flip_rows(value, groups):
    count = value.shape[0]
    row = iota((count, count), 0)
    ends, start = jnp.zeros((count, count), jnp.int32), 0
    for size in groups:
        ends = jnp.where(row >= start, 2 * start + size - 1, ends)
        start += size
    turn = hot(row + iota((count, count), 1) == ends)
    parts = [bdot(turn, piece) for piece in pieces(value)]
    return (parts[0] + parts[1]) + parts[2]


def two_sum(a, b):
    s = a + b
    t = s - a
    return s, (a - (s - t)) + (b - t)


def halves(a):
    t = a * 4097.0
    high = t - (t - a)
    return high, a - high


def two_prod(a, b):
    p = a * b
    ah, al = halves(a)
    bh, bl = halves(b)
    return p, ((ah * bh - p) + ah * bl + al * bh) + al * bl


def quick(a, b):
    s = a + b
    return s, b - (s - a)


def df_mul(x, y):
    p, e = two_prod(x[0], y[0])
    return quick(p, e + (x[0] * y[1] + x[1] * y[0]))


def df_add(x, y):
    s, e = two_sum(x[0], y[0])
    return quick(s, e + (x[1] + y[1]))


def df_sub(x, y):
    return df_add(x, (-y[0], -y[1]))


def df_div(x, y):
    first = x[0] / y[0]
    rest = df_sub(x, df_mul(y, (first, jnp.zeros_like(first))))
    second = rest[0] / y[0]
    return quick(first, second)


def neighbours(value):
    rows, width = value.shape
    return (
        pltpu.roll(value, 1, 0)
        + pltpu.roll(value, rows - 1, 0)
        + pltpu.roll(value, 1, 1)
        + pltpu.roll(value, width - 1, 1)
    )


def kernel(
    nlon, nlat,
    weight, land, theta, kappa, diag,
    out_theta, out_psi,
    th, fresh, kp, skt, ext, edge, dg, ocs, basis, rows_out, north, south, cols_out, east, west,
    part1, part2,
    in_sem, out_sem, send_sem, recv_sem, edge_send, edge_recv, mir_send, mir_edge_send,
    diag_send, diag_recv, halo_send, halo_recv, red_send1, red_recv1, red_send2, red_recv2,
):
    levels, cy, cx = th.shape
    ny, nx = cy * nlat, cx * nlon
    strip = cx // nlat
    wide = strip + 2 * HALO
    by, bx = land.shape
    total = nlon * nlat
    i = lax.axis_index("lon")
    j = lax.axis_index("lat")
    t = i * nlat + j
    top = j == nlat - 1
    ends = jnp.logical_or(j == 0, top)

    def remote(src, dst, send, recv, lon, lat):
        return pltpu.make_async_remote_copy(
            src_ref=src, dst_ref=dst, send_sem=send, recv_sem=recv,
            device_id=(lon, lat), device_id_type=MESH,
        )

    def lon_of(value):
        return lax.rem(value + 2 * nlon, nlon)

    def lat_of(value):
        return lax.rem(value + 2 * nlat, nlat)

    chunk = levels // 4
    loads = [
        pltpu.make_async_copy(theta.at[pl.ds(q * chunk, chunk)], th.at[pl.ds(q * chunk, chunk)], in_sem.at[q])
        for q in range(4)
    ]
    load_kappa = pltpu.make_async_copy(kappa, kp, in_sem.at[4])
    load_diag = pltpu.make_async_copy(diag, dg.at[HALO:HALO + strip, 0:ny], in_sem.at[5])
    for copy in loads:
        copy.start()
    load_kappa.start()
    load_diag.start()

    barrier = pltpu.get_barrier_semaphore()

    def greet(d, _):
        other = lax.rem(t + d, total)
        pl.semaphore_signal(
            barrier, inc=1, device_id=(other // nlat, lax.rem(other, nlat)), device_id_type=MESH
        )
        return 0

    lax.fori_loop(1, total, greet, 0)

    table = land[...].astype(F32).astype(BF16)
    row_block = (j * cy + iota((cy, by), 0)) >> 5
    on_rows = bdot(hot(row_block == iota((cy, by), 1)), table).astype(BF16)
    col_block = (i * cx + iota((bx, cx), 1)) >> 5
    cols_hot = hot(col_block == iota((bx, cx), 0))
    ocean = bdot(on_rows, cols_hot)
    west_block = lax.rem(i * (cx // BS) + bx - 1, bx)
    east_block = lax.rem((i + 1) * (cx // BS), bx)
    ocean_west = bdot(on_rows, hot(iota((bx, LANES), 0) == west_block))
    ocean_east = bdot(on_rows, hot(iota((bx, LANES), 0) == east_block))
    edge_row = iota((8, by), 0)
    edge_col = iota((8, by), 1)
    south_hot = hot(jnp.logical_and(edge_row == 0, edge_col == j * (cy // BS) - 1))
    north_block = jnp.where(top, by - 1, (j + 1) * (cy // BS))
    north_hot = hot(jnp.logical_and(edge_row == 0, edge_col == north_block))
    north_cols = jnp.where(top, bx - 1 - col_block, col_block)
    ocean_south = bdot(bdot(south_hot, table).astype(BF16), cols_hot)[0:1]
    ocean_north = bdot(
        bdot(north_hot, table).astype(BF16), hot(north_cols == iota((bx, cx), 0))
    )[0:1]

    strip_x = (strip * t - HALO + nx + iota((wide, bx), 0)) % nx >> 5
    strip_hot = hot(strip_x == iota((wide, bx), 1))
    on_cols = ndot(strip_hot, table).astype(BF16)
    ocs[:, 0:ny] = bdot(on_cols, hot((iota((by, ny), 1) >> 5) == iota((by, ny), 0)))
    mirror_hot = hot((bx - 1 - strip_x) == iota((wide, bx), 1))
    on_mirror = ndot(mirror_hot, table).astype(BF16)
    keep = jnp.logical_and(iota((by, LANES), 0) == by - 1, iota((by, LANES), 1) < 8)
    ocs[:, ny:ny + LANES] = bdot(on_mirror, hot(keep))

    skt[:, 0:HALO, :] = jnp.zeros((2, HALO, cy), F32)
    skt[:, HALO + cx:, :] = jnp.zeros((2, HALO, cy), F32)
    load_kappa.wait()
    skt[1, HALO:HALO + cx, :] = kp[...].T
    column = jnp.zeros((cy, cx), F32)
    for q in range(4):
        loads[q].wait()
        for k in range(q * chunk, (q + 1) * chunk):
            column = column + weight[k] * th[k]
    skt[0, HALO:HALO + cx, :] = column.T

    pl.semaphore_wait(barrier, total - 1)

    own_lanes = pl.ds(pl.multiple_of(j * cy, LANES), cy)
    mirror_lanes = pl.ds(ny, LANES)

    def block_rows(m):
        return skt.at[:, pl.ds(pl.multiple_of(m * strip, 8), wide), :]

    first_rows = skt.at[:, HALO:2 * HALO, :]
    last_rows = skt.at[:, cx:cx + HALO, :]

    def main_copy(d):
        m = lax.rem(j + d, nlat)
        return remote(block_rows(m), ext.at[:, :, own_lanes], send_sem.at[d], recv_sem.at[j], i, m)

    def mirror_copy(m):
        return remote(
            block_rows(nlat - 1 - m), ext.at[:, :, mirror_lanes], mir_send.at[m], recv_sem.at[nlat],
            nlon - 1 - i, m,
        )

    def run_start(make):
        def step(d, _):
            make(d).start()
            return 0
        return step

    lax.fori_loop(1, nlat, run_start(main_copy), 0)
    own_copy = pltpu.make_async_copy(block_rows(j), ext.at[:, :, own_lanes], recv_sem.at[j])
    own_copy.start()
    left_edge = remote(first_rows, edge.at[:, :, own_lanes], edge_send.at[0], edge_recv.at[j], lon_of(i - 1), nlat - 1)
    right_edge = remote(last_rows, edge.at[:, :, own_lanes], edge_send.at[1], edge_recv.at[j], lon_of(i + 1), 0)
    left_edge.start()
    right_edge.start()
    folded_lon = lon_of(nlon - 2 - i)
    folded_self = folded_lon == i
    fold_edge = remote(
        last_rows, edge.at[:, :, mirror_lanes], mir_edge_send.at[0], edge_recv.at[nlat], folded_lon, nlat - 1
    )
    fold_edge_own = pltpu.make_async_copy(last_rows, edge.at[:, :, mirror_lanes], edge_recv.at[nlat])
    fold_edge_low = remote(
        first_rows, edge.at[:, :, mirror_lanes], mir_edge_send.at[1], edge_recv.at[nlat], lon_of(nlon - i), 0
    )

    @pl.when(top)
    def _():
        lax.fori_loop(0, nlat, run_start(mirror_copy), 0)
        fold_edge_low.start()

        @pl.when(folded_self)
        def _():
            fold_edge_own.start()

        @pl.when(jnp.logical_not(folded_self))
        def _():
            fold_edge.start()

    load_diag.wait()
    after, before = lax.rem(t + 1, total), lax.rem(t + total - 1, total)
    diag_up = remote(
        dg.at[strip:strip + HALO, 0:ny], dg.at[0:HALO, 0:ny], diag_send.at[0], diag_recv.at[0],
        after // nlat, lax.rem(after, nlat),
    )
    diag_down = remote(
        dg.at[HALO:2 * HALO, 0:ny], dg.at[HALO + strip:wide, 0:ny], diag_send.at[1], diag_recv.at[1],
        before // nlat, lax.rem(before, nlat),
    )
    diag_up.start()
    diag_down.start()

    rows_out[0] = th[:, 0, :]
    rows_out[1] = th[:, cy - 1, :]
    to_south = remote(rows_out.at[0], north, halo_send.at[0], halo_recv.at[0], i, lat_of(j - 1))
    to_north = remote(rows_out.at[1], south, halo_send.at[1], halo_recv.at[1], i, lat_of(j + 1))
    to_fold = remote(rows_out.at[1], north, halo_send.at[1], halo_recv.at[0], nlon - 1 - i, j)

    @pl.when(j > 0)
    def _():
        to_south.start()

    @pl.when(jnp.logical_not(top))
    def _():
        to_north.start()

    @pl.when(top)
    def _():
        to_fold.start()

    lane = iota((cy, LANES), 1)
    packed = jnp.zeros((cy, LANES), F32)
    for k in range(levels):
        packed = jnp.where(lane == k, pltpu.roll(th[k, :, 0:LANES], k, 1), packed)
        packed = jnp.where(
            lane == levels + k, pltpu.roll(th[k, :, cx - LANES:cx], levels + k + 1, 1), packed
        )
    cols_out[...] = packed
    to_west = remote(cols_out, east, halo_send.at[2], halo_recv.at[2], lon_of(i - 1), j)
    to_east = remote(cols_out, west, halo_send.at[3], halo_recv.at[3], lon_of(i + 1), j)
    to_west.start()
    to_east.start()

    diag_up.wait_recv()
    diag_down.wait_recv()
    diag_fold = remote(
        dg.at[:, ny - LANES:ny], dg.at[:, ny:ny + LANES], diag_send.at[2], diag_recv.at[2],
        nlon - 1 - i, nlat - 1 - j,
    )
    diag_fold.start()

    to_south.wait_recv()
    to_west.wait_recv()
    to_east.wait_recv()

    @pl.when(j > 0)
    def _():
        to_north.wait_recv()

    @pl.when(j == 0)
    def _():
        south[...] = jnp.zeros_like(south)

    @pl.when(top)
    def _():
        north[...] = flip_lanes(north[...])

    west[...] = west[...] * ocean_west
    east[...] = east[...] * ocean_east
    scale = ocean * kp[...]
    first_row = iota((cy, cx), 0) == 0
    last_row = iota((cy, cx), 0) == cy - 1
    first_lane = iota((cy, cx), 1) == 0
    last_lane = iota((cy, cx), 1) == cx - 1

    def update(k, _):
        level = th[k]
        held = ocean * level
        from_west = pltpu.roll(west[...], LANES - levels - k, 1)
        from_east = pltpu.roll(east[...], LANES - 1 - k, 1)
        if cx > LANES:
            pad = jnp.zeros((cy, cx - LANES), F32)
            from_west = jnp.concatenate([from_west, pad], axis=1)
            from_east = jnp.concatenate([pad, from_east], axis=1)
        beside = jnp.where(first_lane, from_west, pltpu.roll(held, 1, 1))
        beside = beside + jnp.where(last_lane, from_east, pltpu.roll(held, cx - 1, 1))
        beside = beside + jnp.where(first_row, ocean_south * south[pl.ds(k, 1), :], pltpu.roll(held, 1, 0))
        beside = beside + jnp.where(last_row, ocean_north * north[pl.ds(k, 1), :], pltpu.roll(held, cy - 1, 0))
        fresh[k] = level + scale * (beside - 4.0 * held)
        return 0

    lax.fori_loop(0, levels, update, 0)
    store_theta = pltpu.make_async_copy(fresh, out_theta, out_sem.at[0])
    store_theta.start()

    for lat in range(nlat + 1):
        lanes = pl.ds(lat * cy, cy) if lat < nlat else mirror_lanes
        pltpu.make_async_copy(block_rows(0), ext.at[:, :, lanes], recv_sem.at[lat]).wait()

    @pl.when(ends)
    def _():
        for lat in range(nlat + 1):
            lanes = pl.ds(lat * cy, cy) if lat < nlat else mirror_lanes
            pltpu.make_async_copy(first_rows, edge.at[:, :, lanes], edge_recv.at[lat]).wait()

    @pl.when(jnp.logical_not(ends))
    def _():
        edge[...] = jnp.zeros_like(edge)

    diag_fold.wait_recv()
    tall = jnp.concatenate(
        [ext[0, :, ny:], ext[1, :, ny:], dg[:, ny:], edge[0, :, ny:], edge[1, :, ny:]], axis=0
    )
    tall = flip_rows(flip_lanes(tall), (wide, wide, wide, HALO, HALO))
    ext[0, :, ny:] = tall[0:wide]
    ext[1, :, ny:] = tall[wide:2 * wide]
    dg[:, ny:] = tall[2 * wide:3 * wide]
    edge[0, :, ny:] = tall[3 * wide:3 * wide + HALO]
    edge[1, :, ny:] = tall[3 * wide + HALO:]

    @pl.when(j == 0)
    def _():
        ext[:, 0:HALO, :] = edge[...]

    @pl.when(top)
    def _():
        ext[:, HALO + strip:, :] = edge[...]

    mask = ocs[...]
    held = mask * ext[0]
    basis[0] = mask * ext[0] + mask * ext[1] * (neighbours(held) - 4.0 * held)
    diag_up.wait_send()
    diag_down.wait_send()
    diag_fold.wait_send()
    dg[...] = (dg[...] - 1.0) * 0.25
    for step in range(BASIS - 1):
        value = basis[step]
        basis[step + 1] = ocs[...] * (dg[...] * value - 0.25 * neighbours(value))

    zero = jnp.zeros((8, LANES), F32)

    def accumulate(c, carry):
        sums = list(carry)
        lanes = pl.ds(pl.multiple_of(c * LANES, LANES), LANES)
        for h in range(strip // 8):
            values = [basis[b, HALO + 8 * h:HALO + 8 * h + 8, lanes] for b in range(BASIS)]
            split = [halves(value) for value in values]
            for n, (a, b) in enumerate(PAIRS):
                p = values[a] * values[b]
                (ah, al), (bh, bl) = split[a], split[b]
                e = ((ah * bh - p) + (ah * bl + al * bh)) + al * bl
                s, f = two_sum(sums[2 * n], p)
                sums[2 * n], sums[2 * n + 1] = s, sums[2 * n + 1] + (e + f)
        return tuple(sums)

    sums = lax.fori_loop(0, ny // LANES, accumulate, (zero,) * (2 * len(PAIRS)))
    place = iota((SLOTS, LANES), 0)
    high = jnp.zeros((SLOTS, LANES), F32)
    low = jnp.zeros((SLOTS, LANES), F32)
    for n in range(len(PAIRS)):
        h, l = sums[2 * n], sums[2 * n + 1]
        for shift in (4, 2, 1):
            h, e = two_sum(h, pltpu.roll(h, shift, 0))
            l = l + pltpu.roll(l, shift, 0) + e
        high = jnp.where(place == n, h[0:1], high)
        low = jnp.where(place == n, l[0:1], low)

    def fold_in(ref, count, index):
        def add(d, carry):
            h, l = carry
            other = ref[d]
            s, e = two_sum(h, other[0:SLOTS])
            return s, l + (e + other[SLOTS:])
        start = ref[0]
        return lax.fori_loop(1, count, add, (start[0:SLOTS], start[SLOTS:]))

    own1 = part1.at[i]
    part1[pl.ds(i, 1)] = jnp.concatenate([high, low], axis=0)[None]

    def lon_copy(d):
        return remote(own1, own1, red_send1.at[d], red_recv1.at[i], lax.rem(i + d, nlon), j)

    lax.fori_loop(1, nlon, run_start(lon_copy), 0)

    def lon_wait(d, _):
        other = lax.rem(i + d, nlon)
        pltpu.make_async_copy(part1.at[other], part1.at[other], red_recv1.at[other]).wait()
        return 0

    lax.fori_loop(1, nlon, lon_wait, 0)
    high, low = fold_in(part1, nlon, i)
    own2 = part2.at[j]
    part2[pl.ds(j, 1)] = jnp.concatenate([high, low], axis=0)[None]

    def lat_copy(d):
        return remote(own2, own2, red_send2.at[d], red_recv2.at[j], i, lax.rem(j + d, nlat))

    lax.fori_loop(1, nlat, run_start(lat_copy), 0)

    def lat_wait(d, _):
        other = lax.rem(j + d, nlat)
        pltpu.make_async_copy(part2.at[other], part2.at[other], red_recv2.at[other]).wait()
        return 0

    lax.fori_loop(1, nlat, lat_wait, 0)
    high, low = fold_in(part2, nlat, j)
    shift = LANES // 2
    while shift:
        high, e = two_sum(high, pltpu.roll(high, shift, 1))
        low = low + pltpu.roll(low, shift, 1) + e
        shift //= 2
    high, low = quick(high, low)

    gram = {}
    for n, (a, b) in enumerate(PAIRS):
        gram[a, b] = gram[b, a] = (high[n:n + 1], low[n:n + 1])
    size = BASIS - 1

    def scaled(x, factor):
        return x[0] * factor, x[1] * factor

    matrix = [
        [
            df_add(
                scaled(gram[a, b + 1], 4.0),
                df_add(scaled(gram[a, b], 4.0), gram[a, b]),
            )
            for b in range(size)
        ]
        for a in range(size)
    ]
    right = [gram[0, a] for a in range(size)]
    for p in range(size):
        for a in range(p + 1, size):
            factor = df_div(matrix[a][p], matrix[p][p])
            for b in range(p + 1, size):
                matrix[a][b] = df_sub(matrix[a][b], df_mul(factor, matrix[p][b]))
            right[a] = df_sub(right[a], df_mul(factor, right[p]))
    answer = [None] * size
    for p in reversed(range(size)):
        value = right[p]
        for b in range(p + 1, size):
            value = df_sub(value, df_mul(matrix[p][b], answer[b]))
        answer[p] = df_div(value, matrix[p][p])
    spread = [jnp.broadcast_to(x[0], (strip, LANES)) for x in answer]

    def combine(c, _):
        lanes = pl.ds(pl.multiple_of(c * LANES, LANES), LANES)
        value = spread[size - 1] * basis[size - 1, HALO:HALO + strip, lanes]
        for b in reversed(range(size - 1)):
            value = value + spread[b] * basis[b, HALO:HALO + strip, lanes]
        out_psi[:, lanes] = value
        return 0

    lax.fori_loop(0, ny // LANES, combine, 0)

    def run_wait(make):
        def step(d, _):
            make(d).wait_send()
            return 0
        return step

    lax.fori_loop(1, nlat, run_wait(main_copy), 0)
    left_edge.wait_send()
    right_edge.wait_send()

    @pl.when(top)
    def _():
        lax.fori_loop(0, nlat, run_wait(mirror_copy), 0)
        fold_edge_low.wait_send()

        @pl.when(jnp.logical_not(folded_self))
        def _():
            fold_edge.wait_send()

    @pl.when(j > 0)
    def _():
        to_south.wait_send()

    to_north.wait_send()
    to_west.wait_send()
    to_east.wait_send()
    lax.fori_loop(1, nlon, run_wait(lon_copy), 0)
    lax.fori_loop(1, nlat, run_wait(lat_copy), 0)
    store_theta.wait()


def per_device(nlon, nlat, theta, kappa, layer_weight, diag, land_blocks):
    levels, cy, cx = theta.shape
    strip, ny = diag.shape
    wide = strip + 2 * HALO
    vmem = pl.BlockSpec(memory_space=pltpu.VMEM)
    anywhere = pl.BlockSpec(memory_space=pl.ANY)
    dma = pltpu.SemaphoreType.DMA
    return pl.pallas_call(
        functools.partial(kernel, nlon, nlat),
        out_shape=(
            jax.ShapeDtypeStruct(theta.shape, F32),
            jax.ShapeDtypeStruct(diag.shape, F32),
        ),
        in_specs=[pl.BlockSpec(memory_space=pltpu.SMEM), vmem, anywhere, anywhere, anywhere],
        out_specs=(anywhere, vmem),
        scratch_shapes=[
            pltpu.VMEM((levels, cy, cx), F32),
            pltpu.VMEM((levels, cy, cx), F32),
            pltpu.VMEM((cy, cx), F32),
            pltpu.VMEM((2, cx + 2 * HALO, cy), F32),
            pltpu.VMEM((2, wide, ny + LANES), F32),
            pltpu.VMEM((2, HALO, ny + LANES), F32),
            pltpu.VMEM((wide, ny + LANES), F32),
            pltpu.VMEM((wide, ny + LANES), F32),
            pltpu.VMEM((BASIS, wide, ny + LANES), F32),
            pltpu.VMEM((2, levels, cx), F32),
            pltpu.VMEM((levels, cx), F32),
            pltpu.VMEM((levels, cx), F32),
            pltpu.VMEM((cy, LANES), F32),
            pltpu.VMEM((cy, LANES), F32),
            pltpu.VMEM((cy, LANES), F32),
            pltpu.VMEM((nlon, 2 * SLOTS, LANES), F32),
            pltpu.VMEM((nlat, 2 * SLOTS, LANES), F32),
            dma((6,)),
            dma((1,)),
            dma((nlat,)),
            dma((nlat + 1,)),
            dma((2,)),
            dma((nlat + 1,)),
            dma((nlat,)),
            dma((2,)),
            dma((3,)),
            dma((3,)),
            dma((4,)),
            dma((4,)),
            dma((nlon,)),
            dma((nlon,)),
            dma((nlat,)),
            dma((nlat,)),
        ],
        compiler_params=pltpu.CompilerParams(
            collective_id=0, has_side_effects=True, vmem_limit_bytes=67043328
        ),
        name="ocean_step",
    )(layer_weight, land_blocks, theta, kappa, diag)


def solution(mesh):
    placed = (P(None, "lat", "lon"), P("lat", "lon"), P(), P(("lon", "lat"), None), P())
    return jax.shard_map(
        functools.partial(per_device, mesh.shape["lon"], mesh.shape["lat"]),
        mesh=mesh,
        in_specs=placed,
        out_specs=(P(None, "lat", "lon"), P(("lon", "lat"), None)),
        check_vma=False,
    )
```

```python
import functools

import jax
import jax.numpy as jnp
from jax import lax
from jax.experimental import pallas as pl
from jax.experimental.pallas import tpu as pltpu
from jax.sharding import PartitionSpec as P

MESH = pl.DeviceIdType.MESH
BS = 32
HALO = 8
REACH = 5
LANES = 128
F32 = jnp.float32
BF16 = jnp.bfloat16
BASIS = 5
PAIRS = [(a, b) for a in range(BASIS) for b in range(a, BASIS) if a < BASIS - 1]
SLOTS = 16


def iota(shape, axis):
    return lax.broadcasted_iota(jnp.int32, shape, axis)


def hot(condition):
    return jnp.where(condition, 1.0, 0.0).astype(BF16)


def bdot(left, right):
    return jnp.dot(left, right, preferred_element_type=F32)


def ndot(left, right):
    return lax.dot_general(left, right, (((1,), (1,)), ((), ())), preferred_element_type=F32)


def pieces(value):
    first = value.astype(BF16)
    rest = value - first.astype(F32)
    second = rest.astype(BF16)
    third = (rest - second.astype(F32)).astype(BF16)
    return [first, second, third]


def flip_lanes(value):
    width = value.shape[1]
    turn = hot(iota((width, width), 0) + iota((width, width), 1) == width - 1)
    parts = [bdot(piece, turn) for piece in pieces(value)]
    return (parts[0] + parts[1]) + parts[2]


def flip_rows(value, groups):
    count = value.shape[0]
    row = iota((count, count), 0)
    ends, start = jnp.zeros((count, count), jnp.int32), 0
    for size in groups:
        ends = jnp.where(row >= start, 2 * start + size - 1, ends)
        start += size
    turn = hot(row + iota((count, count), 1) == ends)
    parts = [bdot(turn, piece) for piece in pieces(value)]
    return (parts[0] + parts[1]) + parts[2]


def two_sum(a, b):
    s = a + b
    t = s - a
    return s, (a - (s - t)) + (b - t)


def halves(a):
    t = a * 4097.0
    high = t - (t - a)
    return high, a - high


def two_prod(a, b):
    p = a * b
    ah, al = halves(a)
    bh, bl = halves(b)
    return p, ((ah * bh - p) + ah * bl + al * bh) + al * bl


def quick(a, b):
    s = a + b
    return s, b - (s - a)


def df_mul(x, y):
    p, e = two_prod(x[0], y[0])
    return quick(p, e + (x[0] * y[1] + x[1] * y[0]))


def df_add(x, y):
    s, e = two_sum(x[0], y[0])
    return quick(s, e + (x[1] + y[1]))


def df_sub(x, y):
    return df_add(x, (-y[0], -y[1]))


def df_div(x, y):
    first = x[0] / y[0]
    rest = df_sub(x, df_mul(y, (first, jnp.zeros_like(first))))
    second = rest[0] / y[0]
    return quick(first, second)


def neighbours(value):
    rows, width = value.shape
    return (
        pltpu.roll(value, 1, 0)
        + pltpu.roll(value, rows - 1, 0)
        + pltpu.roll(value, 1, 1)
        + pltpu.roll(value, width - 1, 1)
    )


def kernel(
    nlon, nlat,
    weight_in, land_in, theta, kappa, diag,
    out_theta, out_psi,
    weight, land, th, kp, skt, ext, edge, dg, ocs, basis, rows_out, north, south, cols_out, east, west,
    tiles, fold, fold_edge, part1, part2,
    in_sem, main_send, main_recv, edge_send, edge_recv, fold_send, fold_low_send, fold_far_send, fold_recv,
    diag_send, diag_recv, halo_send, halo_recv, red_send, red_recv,
):
    levels, cy, cx = th.shape
    ny, nx = cy * nlat, cx * nlon
    strip = cx // nlat
    wide = strip + 2 * HALO
    by, bx = land.shape
    total = nlon * nlat
    i = lax.axis_index("lon")
    j = lax.axis_index("lat")
    t = i * nlat + j
    top = j == nlat - 1
    ends = jnp.logical_or(j == 0, top)

    def remote(src, dst, send, recv, lon, lat):
        return pltpu.make_async_remote_copy(
            src_ref=src, dst_ref=dst, send_sem=send, recv_sem=recv,
            device_id=(lon, lat), device_id_type=MESH,
        )

    def lon_of(value):
        return lax.rem(value + 2 * nlon, nlon)

    def lat_of(value):
        return lax.rem(value + 2 * nlat, nlat)

    def whole(ref, sem):
        return pltpu.make_async_copy(ref, ref, sem)

    def greet(lon, lat):
        pl.semaphore_signal(barrier, inc=1, device_id=(lon, lat), device_id_type=MESH)

    chunk = levels // 4
    loads = [
        pltpu.make_async_copy(theta.at[pl.ds(q * chunk, chunk)], th.at[pl.ds(q * chunk, chunk)], in_sem.at[q])
        for q in range(4)
    ]
    load_kappa = pltpu.make_async_copy(kappa, kp, in_sem.at[4])
    load_diag = pltpu.make_async_copy(diag, dg.at[HALO:HALO + strip, 0:ny], in_sem.at[5])
    load_weight = pltpu.make_async_copy(weight_in, weight, in_sem.at[6])
    load_land = pltpu.make_async_copy(land_in, land, in_sem.at[7])
    load_kappa.start()
    load_weight.start()
    for copy in loads:
        copy.start()
    load_diag.start()
    load_land.start()
    ext[:, :, 0:HALO, :] = jnp.zeros((nlat + 1, 2, HALO, cy), F32)
    ext[:, :, HALO + strip:, :] = jnp.zeros((nlat + 1, 2, HALO, cy), F32)
    edge[...] = jnp.zeros_like(edge)

    barrier = pltpu.get_barrier_semaphore()
    for d in range(1, nlat):
        greet(i, lax.rem(j + d, nlat))
    for d in range(1, nlon):
        greet(lax.rem(i + d, nlon), j)
    greet(nlon - 1 - i, nlat - 1)
    greet(nlon - 1 - i, nlat - 1 - j)

    @pl.when(j == 0)
    def _():
        for lat in range(nlat):
            greet(lon_of(i - 1), lat)
        greet(lon_of(nlon - i), nlat - 1)

    @pl.when(top)
    def _():
        for lat in range(nlat):
            greet(lon_of(i + 1), lat)

    skt[:, 0:HALO, :] = jnp.zeros((2, HALO, cy), F32)
    skt[:, HALO + cx:, :] = jnp.zeros((2, HALO, cy), F32)
    load_kappa.wait()
    skt[1, HALO:HALO + cx, :] = kp[...].T
    load_weight.wait()
    column = jnp.zeros((cy, cx), F32)
    for q in range(4):
        loads[q].wait()
        for k in range(q * chunk, (q + 1) * chunk):
            column = column + weight[k] * th[k]
    skt[0, HALO:HALO + cx, :] = column.T

    @pl.when(top)
    def _():
        last_sums = column[cy - 8:, :]
        last_kappa = kp[cy - 8:, :]
        lanes8 = iota((8, LANES), 1)
        for m in range(nlat):
            start = strip * (nlat - 1 - m) - HALO
            tiles[m] = jnp.where(
                lanes8 < wide,
                pltpu.roll(last_sums, (-start) % cx, 1)[:, 0:LANES],
                pltpu.roll(last_kappa, (wide - start) % cx, 1)[:, 0:LANES],
            )

    pl.semaphore_wait(barrier, nlat + nlon + 1 + jnp.where(top, nlat + 1, 0))

    low_row = HALO - REACH
    span = strip + 2 * REACH

    def block_rows(m):
        return skt.at[:, pl.ds(m * strip + low_row, span), :]

    own_slot = ext.at[j, :, low_row:low_row + span, :]

    def main_copy(d):
        m = lax.rem(j + d, nlat)
        return remote(block_rows(m), own_slot, main_send, main_recv, i, m)

    for d in range(1, nlat):
        main_copy(d).start()
    pltpu.make_async_copy(block_rows(j), own_slot, main_recv).start()
    first_rows = skt.at[:, HALO:HALO + REACH, :]
    last_rows = skt.at[:, HALO + cx - REACH:HALO + cx, :]
    left_edge = remote(
        first_rows, edge.at[j, :, 0:REACH, :], edge_send.at[0], edge_recv, lon_of(i - 1), nlat - 1
    )
    right_edge = remote(
        last_rows, edge.at[j, :, low_row:HALO, :], edge_send.at[1], edge_recv, lon_of(i + 1), 0
    )
    left_edge.start()
    right_edge.start()

    def fold_copy(m):
        return remote(tiles.at[m], fold, fold_send, fold_recv.at[0], nlon - 1 - i, m)

    far_lon = lon_of(nlon - 2 - i)
    far_self = far_lon == i
    fold_far = remote(
        tiles.at[nlat - 1], fold_edge, fold_far_send, fold_recv.at[1], far_lon, nlat - 1
    )
    fold_far_own = pltpu.make_async_copy(tiles.at[nlat - 1], fold_edge, fold_recv.at[1])
    fold_low = remote(tiles.at[0], fold_edge, fold_low_send, fold_recv.at[1], lon_of(nlon - i), 0)

    @pl.when(top)
    def _():
        for m in range(nlat):
            fold_copy(m).start()
        fold_low.start()

        @pl.when(far_self)
        def _():
            fold_far_own.start()

        @pl.when(jnp.logical_not(far_self))
        def _():
            fold_far.start()

    load_diag.wait()
    after, before = lax.rem(t + 1, total), lax.rem(t + total - 1, total)
    diag_up = remote(
        dg.at[strip:strip + HALO, 0:ny], dg.at[0:HALO, 0:ny], diag_send.at[0], diag_recv.at[0],
        after // nlat, lax.rem(after, nlat),
    )
    diag_down = remote(
        dg.at[HALO:2 * HALO, 0:ny], dg.at[HALO + strip:wide, 0:ny], diag_send.at[1], diag_recv.at[1],
        before // nlat, lax.rem(before, nlat),
    )
    diag_up.start()
    diag_down.start()

    rows_out[0] = th[:, 0, :]
    rows_out[1] = th[:, cy - 1, :]
    to_south = remote(rows_out.at[0], north, halo_send.at[0], halo_recv.at[0], i, lat_of(j - 1))
    to_north = remote(rows_out.at[1], south, halo_send.at[1], halo_recv.at[1], i, lat_of(j + 1))
    to_fold = remote(rows_out.at[1], north, halo_send.at[1], halo_recv.at[0], nlon - 1 - i, j)

    @pl.when(j > 0)
    def _():
        to_south.start()

    @pl.when(jnp.logical_not(top))
    def _():
        to_north.start()

    @pl.when(top)
    def _():
        to_fold.start()

    lane = iota((cy, LANES), 1)
    packed = jnp.zeros((cy, LANES), F32)
    for k in range(levels):
        packed = jnp.where(lane == k, pltpu.roll(th[k, :, 0:LANES], k, 1), packed)
        packed = jnp.where(
            lane == levels + k, pltpu.roll(th[k, :, cx - LANES:cx], levels + k + 1, 1), packed
        )
    cols_out[...] = packed
    to_west = remote(cols_out, east, halo_send.at[2], halo_recv.at[2], lon_of(i - 1), j)
    to_east = remote(cols_out, west, halo_send.at[3], halo_recv.at[3], lon_of(i + 1), j)
    to_west.start()
    to_east.start()

    load_land.wait()
    table = land[...].astype(F32).astype(BF16)
    row_block = (j * cy + iota((cy, by), 0)) >> 5
    on_rows = bdot(hot(row_block == iota((cy, by), 1)), table).astype(BF16)
    col_block = (i * cx + iota((bx, cx), 1)) >> 5
    cols_hot = hot(col_block == iota((bx, cx), 0))
    ocean = bdot(on_rows, cols_hot)
    west_block = lax.rem(i * (cx // BS) + bx - 1, bx)
    east_block = lax.rem((i + 1) * (cx // BS), bx)
    ocean_west = bdot(on_rows, hot(iota((bx, LANES), 0) == west_block))
    ocean_east = bdot(on_rows, hot(iota((bx, LANES), 0) == east_block))
    edge_row = iota((8, by), 0)
    edge_col = iota((8, by), 1)
    south_hot = hot(jnp.logical_and(edge_row == 0, edge_col == j * (cy // BS) - 1))
    north_block = jnp.where(top, by - 1, (j + 1) * (cy // BS))
    north_hot = hot(jnp.logical_and(edge_row == 0, edge_col == north_block))
    north_cols = jnp.where(top, bx - 1 - col_block, col_block)
    ocean_south = bdot(bdot(south_hot, table).astype(BF16), cols_hot)[0:1]
    ocean_north = bdot(
        bdot(north_hot, table).astype(BF16), hot(north_cols == iota((bx, cx), 0))
    )[0:1]

    strip_x = (strip * t - HALO + nx + iota((wide, bx), 0)) % nx >> 5
    strip_hot = hot(strip_x == iota((wide, bx), 1))
    on_cols = ndot(strip_hot, table).astype(BF16)
    ocs[:, 0:ny] = bdot(on_cols, hot((iota((by, ny), 1) >> 5) == iota((by, ny), 0)))
    mirror_hot = hot((bx - 1 - strip_x) == iota((wide, bx), 1))
    on_mirror = ndot(mirror_hot, table).astype(BF16)
    keep = jnp.logical_and(iota((by, LANES), 0) == by - 1, iota((by, LANES), 1) < 8)
    ocs[:, ny:ny + LANES] = bdot(on_mirror, hot(keep))

    diag_up.wait_recv()
    diag_down.wait_recv()
    diag_fold = remote(
        dg.at[:, ny - LANES:ny], dg.at[:, ny:ny + LANES], diag_send.at[2], diag_recv.at[2],
        nlon - 1 - i, nlat - 1 - j,
    )
    diag_fold.start()

    diag_fold.wait()
    dg[:, ny:] = flip_rows(flip_lanes(dg[:, ny:]), (wide,))
    diag_up.wait_send()
    diag_down.wait_send()
    dg[...] = (dg[...] - 1.0) * 0.25

    whole(ext.at[0:nlat, :, low_row:low_row + span, :], main_recv).wait()
    whole(fold, fold_recv.at[0]).wait()

    @pl.when(ends)
    def _():
        whole(edge.at[:, :, 0:REACH, :], edge_recv).wait()
        whole(fold_edge, fold_recv.at[1]).wait()
        spot = iota((8, LANES), 1) % wide
        outer = jnp.logical_or(
            jnp.logical_and(top, spot < HALO), jnp.logical_and(j == 0, spot >= wide - HALO)
        )
        fold[...] = jnp.where(outer, fold_edge[...], fold[...])

    row = iota((2 * wide, LANES), 0)
    source = jnp.where(row < wide, wide - 1 - row, 3 * wide - 1 - row)
    pick = hot(source == iota((2 * wide, LANES), 1))
    turn = hot(iota((LANES, 8), 0) == 7 - iota((LANES, 8), 1))
    folded = [ndot(pick, bdot(turn, piece).astype(BF16)) for piece in pieces(fold[...])]
    folded = (folded[0] + folded[1]) + folded[2]
    ext[nlat, 0] = folded[0:wide]
    ext[nlat, 1] = folded[wide:]

    @pl.when(j == 0)
    def _():
        ext[0:nlat, :, 0:HALO, :] = edge[...]

    @pl.when(top)
    def _():
        ext[0:nlat, :, HALO + strip:, :] = edge[...]

    mask = ocs[...]
    column_sum, kappa_strip = [
        jnp.concatenate([ext[c, n] for c in range(nlat + 1)], axis=1) for n in range(2)
    ]
    held = mask * column_sum
    basis[0] = held + mask * kappa_strip * (neighbours(held) - 4.0 * held)
    for step in range(BASIS - 1):
        value = basis[step]
        basis[step + 1] = ocs[...] * (dg[...] * value - 0.25 * neighbours(value))

    zero = jnp.zeros((8, LANES), F32)

    def accumulate(c, carry):
        sums = list(carry)
        lanes = pl.ds(pl.multiple_of(c * LANES, LANES), LANES)
        for h in range(strip // 8):
            values = [basis[b, HALO + 8 * h:HALO + 8 * h + 8, lanes] for b in range(BASIS)]
            split = [halves(value) for value in values]
            for n, (a, b) in enumerate(PAIRS):
                p = values[a] * values[b]
                (ah, al), (bh, bl) = split[a], split[b]
                e = ((ah * bh - p) + (ah * bl + al * bh)) + al * bl
                s, f = two_sum(sums[2 * n], p)
                sums[2 * n], sums[2 * n + 1] = s, sums[2 * n + 1] + (e + f)
        return tuple(sums)

    sums = lax.fori_loop(0, ny // LANES, accumulate, (zero,) * (2 * len(PAIRS)))
    place = iota((SLOTS, LANES), 0)
    high = jnp.zeros((SLOTS, LANES), F32)
    low = jnp.zeros((SLOTS, LANES), F32)
    for n in range(len(PAIRS)):
        h, l = sums[2 * n], sums[2 * n + 1]
        for shift in (4, 2, 1):
            h, e = two_sum(h, pltpu.roll(h, shift, 0))
            l = l + pltpu.roll(l, shift, 0) + e
        high = jnp.where(place == n, h[0:1], high)
        low = jnp.where(place == n, l[0:1], low)
    shift = LANES // 2
    while shift:
        high, e = two_sum(high, pltpu.roll(high, shift, 1))
        low = low + pltpu.roll(low, shift, 1) + e
        shift //= 2
    spot = iota((SLOTS, LANES), 1)
    packed = jnp.where(spot == place, high, jnp.where(spot == place + SLOTS, low, 0.0))
    message = jnp.sum(packed, axis=0, keepdims=True)

    def fold_in(ref, count):
        value = ref[...].reshape(count, LANES)
        error = jnp.zeros_like(value)
        shift = count // 2
        while shift:
            other = pltpu.roll(error, shift, 0)
            value, e = two_sum(value, pltpu.roll(value, shift, 0))
            error = error + other + e
            shift //= 2
        value, error = value[0:1], error[0:1]
        moved = pltpu.roll(error, SLOTS, 1)
        lane = iota((1, LANES), 1)
        return value + jnp.where(jnp.logical_and(lane >= SLOTS, lane < 2 * SLOTS), moved, 0.0)

    part1[pl.ds(i, 1)] = message[None]

    def lon_copy(d):
        return remote(part1.at[i], part1.at[i], red_send.at[0], red_recv.at[0], lax.rem(i + d, nlon), j)

    for d in range(1, nlon):
        lon_copy(d).start()

    to_south.wait_recv()
    to_west.wait_recv()
    to_east.wait_recv()

    @pl.when(j > 0)
    def _():
        to_north.wait_recv()

    @pl.when(j == 0)
    def _():
        south[...] = jnp.zeros_like(south)

    @pl.when(top)
    def _():
        north[...] = flip_lanes(north[...])

    west[...] = west[...] * ocean_west
    east[...] = east[...] * ocean_east
    scale = ocean * kp[...]
    first_row = iota((cy, cx), 0) == 0
    last_row = iota((cy, cx), 0) == cy - 1
    first_lane = iota((cy, cx), 1) == 0
    last_lane = iota((cy, cx), 1) == cx - 1

    def update(k, _):
        level = th[k]
        held = ocean * level
        from_west = pltpu.roll(west[...], LANES - levels - k, 1)
        from_east = pltpu.roll(east[...], LANES - 1 - k, 1)
        if cx > LANES:
            pad = jnp.zeros((cy, cx - LANES), F32)
            from_west = jnp.concatenate([from_west, pad], axis=1)
            from_east = jnp.concatenate([pad, from_east], axis=1)
        beside = jnp.where(first_lane, from_west, pltpu.roll(held, 1, 1))
        beside = beside + jnp.where(last_lane, from_east, pltpu.roll(held, cx - 1, 1))
        beside = beside + jnp.where(first_row, ocean_south * south[pl.ds(k, 1), :], pltpu.roll(held, 1, 0))
        beside = beside + jnp.where(last_row, ocean_north * north[pl.ds(k, 1), :], pltpu.roll(held, cy - 1, 0))
        out_theta[k] = level + scale * (beside - 4.0 * held)
        return 0

    lax.fori_loop(0, levels // 2, update, 0)
    whole(part1.at[pl.ds(0, nlon - 1)], red_recv.at[0]).wait()
    message = fold_in(part1, nlon)
    part2[pl.ds(j, 1)] = message[None]

    def lat_copy(d):
        return remote(part2.at[j], part2.at[j], red_send.at[1], red_recv.at[1], i, lax.rem(j + d, nlat))

    for d in range(1, nlat):
        lat_copy(d).start()
    lax.fori_loop(levels // 2, levels, update, 0)
    whole(part2.at[pl.ds(0, nlat - 1)], red_recv.at[1]).wait()
    message = fold_in(part2, nlat)
    high, low = quick(message, pltpu.roll(message, LANES - SLOTS, 1))

    gram = {}
    for n, (a, b) in enumerate(PAIRS):
        gram[a, b] = gram[b, a] = tuple(
            jnp.broadcast_to(x[:, n:n + 1], (1, LANES)) for x in (high, low)
        )
    size = BASIS - 1

    def scaled(x, factor):
        return x[0] * factor, x[1] * factor

    matrix = [
        [
            df_add(
                scaled(gram[a, b + 1], 4.0),
                df_add(scaled(gram[a, b], 4.0), gram[a, b]),
            )
            for b in range(size)
        ]
        for a in range(size)
    ]
    right = [gram[0, a] for a in range(size)]
    for p in range(size):
        for a in range(p + 1, size):
            factor = df_div(matrix[a][p], matrix[p][p])
            for b in range(p + 1, size):
                matrix[a][b] = df_sub(matrix[a][b], df_mul(factor, matrix[p][b]))
            right[a] = df_sub(right[a], df_mul(factor, right[p]))
    answer = [None] * size
    for p in reversed(range(size)):
        value = right[p]
        for b in range(p + 1, size):
            value = df_sub(value, df_mul(matrix[p][b], answer[b]))
        answer[p] = df_div(value, matrix[p][p])
    spread = [jnp.broadcast_to(x[0], (strip, LANES)) for x in answer]

    def combine(c, _):
        lanes = pl.ds(pl.multiple_of(c * LANES, LANES), LANES)
        value = spread[size - 1] * basis[size - 1, HALO:HALO + strip, lanes]
        for b in reversed(range(size - 1)):
            value = value + spread[b] * basis[b, HALO:HALO + strip, lanes]
        out_psi[:, lanes] = value
        return 0

    lax.fori_loop(0, ny // LANES, combine, 0)

    whole(ext.at[0:nlat - 1, :, low_row:low_row + span, :], main_send).wait()
    left_edge.wait_send()
    right_edge.wait_send()

    @pl.when(top)
    def _():
        whole(tiles, fold_send).wait()
        fold_low.wait_send()

        @pl.when(jnp.logical_not(far_self))
        def _():
            fold_far.wait_send()

    @pl.when(j > 0)
    def _():
        to_south.wait_send()

    to_north.wait_send()
    to_west.wait_send()
    to_east.wait_send()
    whole(part1.at[pl.ds(0, nlon - 1)], red_send.at[0]).wait()
    whole(part2.at[pl.ds(0, nlat - 1)], red_send.at[1]).wait()


def per_device(nlon, nlat, theta, kappa, layer_weight, diag, land_blocks):
    levels, cy, cx = theta.shape
    strip, ny = diag.shape
    wide = strip + 2 * HALO
    vmem = pl.BlockSpec(memory_space=pltpu.VMEM)
    hbm = pl.BlockSpec(memory_space=pltpu.HBM)
    dma = pltpu.SemaphoreType.DMA
    operands = (layer_weight, land_blocks, theta, kappa, diag)
    return pl.pallas_call(
        functools.partial(kernel, nlon, nlat),
        out_shape=(
            jax.ShapeDtypeStruct(theta.shape, F32),
            jax.ShapeDtypeStruct(diag.shape, F32),
        ),
        in_specs=[hbm] * 5,
        out_specs=(vmem, vmem),
        scratch_shapes=[
            pltpu.SMEM(layer_weight.shape, F32),
            pltpu.VMEM(land_blocks.shape, jnp.int32),
            pltpu.VMEM((levels, cy, cx), F32),
            pltpu.VMEM((cy, cx), F32),
            pltpu.VMEM((2, cx + 2 * HALO, cy), F32),
            pltpu.VMEM((nlat + 1, 2, wide, cy), F32),
            pltpu.VMEM((nlat, 2, HALO, cy), F32),
            pltpu.VMEM((wide, ny + LANES), F32),
            pltpu.VMEM((wide, ny + LANES), F32),
            pltpu.VMEM((BASIS, wide, ny + LANES), F32),
            pltpu.VMEM((2, levels, cx), F32),
            pltpu.VMEM((levels, cx), F32),
            pltpu.VMEM((levels, cx), F32),
            pltpu.VMEM((cy, LANES), F32),
            pltpu.VMEM((cy, LANES), F32),
            pltpu.VMEM((cy, LANES), F32),
            pltpu.VMEM((nlat, 8, LANES), F32),
            pltpu.VMEM((8, LANES), F32),
            pltpu.VMEM((8, LANES), F32),
            pltpu.VMEM((nlon, 1, LANES), F32),
            pltpu.VMEM((nlat, 1, LANES), F32),
            dma((8,)),
            dma,
            dma,
            dma((2,)),
            dma,
            dma,
            dma,
            dma,
            dma((2,)),
            dma((3,)),
            dma((3,)),
            dma((4,)),
            dma((4,)),
            dma((2,)),
            dma((2,)),
        ],
        compiler_params=pltpu.CompilerParams(
            collective_id=0, has_side_effects=True, vmem_limit_bytes=32 << 20
        ),
        name="ocean_step",
    )(*[pltpu.with_memory_space_constraint(x, pltpu.HBM) for x in operands])


def solution(mesh):
    placed = (P(None, "lat", "lon"), P("lat", "lon"), P(), P(("lon", "lat"), None), P())
    return jax.shard_map(
        functools.partial(per_device, mesh.shape["lon"], mesh.shape["lat"]),
        mesh=mesh,
        in_specs=placed,
        out_specs=(P(None, "lat", "lon"), P(("lon", "lat"), None)),
        check_vma=False,
    )
```

```python
import functools

import jax
import jax.numpy as jnp
from jax import lax
from jax.experimental import pallas as pl
from jax.experimental.pallas import tpu as pltpu
from jax.sharding import PartitionSpec as P

MESH = pl.DeviceIdType.MESH
BS = 32
HALO = 8
REACH = 5
LANES = 128
F32 = jnp.float32
BF16 = jnp.bfloat16
BASIS = 5
PAIRS = [(a, b) for a in range(BASIS) for b in range(a, BASIS) if a < BASIS - 1]
SLOTS = 16


def iota(shape, axis):
    return lax.broadcasted_iota(jnp.int32, shape, axis)


def hot(condition):
    return jnp.where(condition, 1.0, 0.0).astype(BF16)


def bdot(left, right):
    return jnp.dot(left, right, preferred_element_type=F32)


def ndot(left, right):
    return lax.dot_general(left, right, (((1,), (1,)), ((), ())), preferred_element_type=F32)


def pieces(value):
    first = value.astype(BF16)
    rest = value - first.astype(F32)
    second = rest.astype(BF16)
    third = (rest - second.astype(F32)).astype(BF16)
    return [first, second, third]


def flip_lanes(value):
    width = value.shape[1]
    turn = hot(iota((width, width), 0) + iota((width, width), 1) == width - 1)
    parts = [bdot(piece, turn) for piece in pieces(value)]
    return (parts[0] + parts[1]) + parts[2]


def flip_rows(value, groups):
    count = value.shape[0]
    row = iota((count, count), 0)
    ends, start = jnp.zeros((count, count), jnp.int32), 0
    for size in groups:
        ends = jnp.where(row >= start, 2 * start + size - 1, ends)
        start += size
    turn = hot(row + iota((count, count), 1) == ends)
    parts = [bdot(turn, piece) for piece in pieces(value)]
    return (parts[0] + parts[1]) + parts[2]


def two_sum(a, b):
    s = a + b
    t = s - a
    return s, (a - (s - t)) + (b - t)


def halves(a):
    t = a * 4097.0
    high = t - (t - a)
    return high, a - high


def two_prod(a, b):
    p = a * b
    ah, al = halves(a)
    bh, bl = halves(b)
    return p, ((ah * bh - p) + ah * bl + al * bh) + al * bl


def quick(a, b):
    s = a + b
    return s, b - (s - a)


def df_mul(x, y):
    p, e = two_prod(x[0], y[0])
    return quick(p, e + (x[0] * y[1] + x[1] * y[0]))


def df_add(x, y):
    s, e = two_sum(x[0], y[0])
    return quick(s, e + (x[1] + y[1]))


def df_sub(x, y):
    return df_add(x, (-y[0], -y[1]))


def df_div(x, y):
    first = x[0] / y[0]
    rest = df_sub(x, df_mul(y, (first, jnp.zeros_like(first))))
    second = rest[0] / y[0]
    return quick(first, second)


def neighbours(value):
    rows, width = value.shape
    return (
        pltpu.roll(value, 1, 0)
        + pltpu.roll(value, rows - 1, 0)
        + pltpu.roll(value, 1, 1)
        + pltpu.roll(value, width - 1, 1)
    )


def kernel(
    nlon, nlat,
    weight_in, land_in, theta, kappa, diag,
    out_theta, out_psi,
    weight, land, th, kp, skt, ext, edge, flat, dgx, dg, ocs, quarter, basis, rows_out, north, south, cols_out, east, west,
    tiles, fold, fold_edge, part1, part2,
    in_sem, main_send, main_recv, edge_send, edge_recv, fold_send, fold_low_send, fold_far_send, fold_recv,
    diag_send, diag_recv, halo_send, halo_recv, red_send, red_recv,
):
    levels, cy, cx = th.shape
    ny, nx = cy * nlat, cx * nlon
    strip = cx // nlat
    wide = strip + 2 * HALO
    by, bx = land.shape
    total = nlon * nlat
    i = lax.axis_index("lon")
    j = lax.axis_index("lat")
    t = i * nlat + j
    top = j == nlat - 1
    ends = jnp.logical_or(j == 0, top)

    def remote(src, dst, send, recv, lon, lat):
        return pltpu.make_async_remote_copy(
            src_ref=src, dst_ref=dst, send_sem=send, recv_sem=recv,
            device_id=(lon, lat), device_id_type=MESH,
        )

    def lon_of(value):
        return lax.rem(value + 2 * nlon, nlon)

    def lat_of(value):
        return lax.rem(value + 2 * nlat, nlat)

    def whole(ref, sem):
        return pltpu.make_async_copy(ref, ref, sem)

    def greet(lon, lat):
        pl.semaphore_signal(barrier, inc=1, device_id=(lon, lat), device_id_type=MESH)

    chunk = levels // 4
    loads = [
        pltpu.make_async_copy(theta.at[pl.ds(q * chunk, chunk)], th.at[pl.ds(q * chunk, chunk)], in_sem.at[q])
        for q in range(4)
    ]
    load_kappa = pltpu.make_async_copy(kappa, kp, in_sem.at[4])
    load_diag = pltpu.make_async_copy(diag, flat, in_sem.at[5])
    load_weight = pltpu.make_async_copy(weight_in, weight, in_sem.at[6])
    load_land = pltpu.make_async_copy(land_in, land, in_sem.at[7])
    load_kappa.start()
    load_weight.start()
    for copy in loads:
        copy.start()
    load_diag.start()
    load_land.start()
    ext[:, :, 0:HALO, :] = jnp.zeros((nlat + 1, 2, HALO, cy), F32)
    ext[:, :, HALO + strip:, :] = jnp.zeros((nlat + 1, 2, HALO, cy), F32)
    edge[...] = jnp.zeros_like(edge)
    dgx[:, 0:HALO, :] = jnp.zeros((nlat + 1, HALO, cy), F32)
    dgx[:, HALO + strip:, :] = jnp.zeros((nlat + 1, HALO, cy), F32)

    barrier = pltpu.get_barrier_semaphore()
    for d in range(1, nlat):
        greet(i, lax.rem(j + d, nlat))
    for d in range(1, nlon):
        greet(lax.rem(i + d, nlon), j)
    greet(nlon - 1 - i, nlat - 1)
    for shift in (1, 0, -1):
        other = lax.rem(total - 1 - t + shift + total, total)

        @pl.when(other != t)
        def _():
            greet(other // nlat, lax.rem(other, nlat))

    @pl.when(j == 0)
    def _():
        for lat in range(nlat):
            greet(lon_of(i - 1), lat)
        greet(lon_of(nlon - i), nlat - 1)

    @pl.when(top)
    def _():
        for lat in range(nlat):
            greet(lon_of(i + 1), lat)

    skt[:, 0:HALO, :] = jnp.zeros((2, HALO, cy), F32)
    skt[:, HALO + cx:, :] = jnp.zeros((2, HALO, cy), F32)
    load_kappa.wait()
    skt[1, HALO:HALO + cx, :] = kp[...].T
    load_weight.wait()
    column = jnp.zeros((cy, cx), F32)
    for q in range(4):
        loads[q].wait()
        for k in range(q * chunk, (q + 1) * chunk):
            column = column + weight[k] * th[k]
    skt[0, HALO:HALO + cx, :] = column.T

    @pl.when(top)
    def _():
        last_sums = column[cy - 8:, :]
        last_kappa = kp[cy - 8:, :]
        lanes8 = iota((8, LANES), 1)
        for m in range(nlat):
            start = strip * (nlat - 1 - m) - HALO
            tiles[m] = jnp.where(
                lanes8 < wide,
                pltpu.roll(last_sums, (-start) % cx, 1)[:, 0:LANES],
                pltpu.roll(last_kappa, (wide - start) % cx, 1)[:, 0:LANES],
            )

    load_diag.wait()
    for c in range(nlat):
        dgx[c, HALO:HALO + strip, :] = flat[:, c * cy:(c + 1) * cy]

    own_folds = [lax.rem(total - 1 - t + shift + total, total) == t for shift in (1, -1)]
    awaited = nlat + nlon + 3 + jnp.where(top, nlat + 1, 0)
    for own in own_folds:
        awaited = awaited - jnp.where(own, 1, 0)
    pl.semaphore_wait(barrier, awaited)

    low_row = HALO - REACH
    span = strip + 2 * REACH

    def block_rows(m):
        return skt.at[:, pl.ds(m * strip + low_row, span), :]

    own_slot = ext.at[j, :, low_row:low_row + span, :]

    def main_copy(d):
        m = lax.rem(j + d, nlat)
        return remote(block_rows(m), own_slot, main_send, main_recv, i, m)

    for d in range(1, nlat):
        main_copy(d).start()
    pltpu.make_async_copy(block_rows(j), own_slot, main_recv).start()
    first_rows = skt.at[:, HALO:HALO + REACH, :]
    last_rows = skt.at[:, HALO + cx - REACH:HALO + cx, :]
    left_edge = remote(
        first_rows, edge.at[j, :, 0:REACH, :], edge_send.at[0], edge_recv, lon_of(i - 1), nlat - 1
    )
    right_edge = remote(
        last_rows, edge.at[j, :, low_row:HALO, :], edge_send.at[1], edge_recv, lon_of(i + 1), 0
    )
    left_edge.start()
    right_edge.start()

    def fold_copy(m):
        return remote(tiles.at[m], fold, fold_send, fold_recv.at[0], nlon - 1 - i, m)

    far_lon = lon_of(nlon - 2 - i)
    far_self = far_lon == i
    fold_far = remote(
        tiles.at[nlat - 1], fold_edge, fold_far_send, fold_recv.at[1], far_lon, nlat - 1
    )
    fold_far_own = pltpu.make_async_copy(tiles.at[nlat - 1], fold_edge, fold_recv.at[1])
    fold_low = remote(tiles.at[0], fold_edge, fold_low_send, fold_recv.at[1], lon_of(nlon - i), 0)

    @pl.when(top)
    def _():
        for m in range(nlat):
            fold_copy(m).start()
        fold_low.start()

        @pl.when(far_self)
        def _():
            fold_far_own.start()

        @pl.when(jnp.logical_not(far_self))
        def _():
            fold_far.start()

    after, before = lax.rem(t + 1, total), lax.rem(t + total - 1, total)
    depth = BASIS - 2
    own_low = slice(HALO, HALO + depth)
    own_high = slice(HALO + strip - depth, HALO + strip)
    halo_low = slice(HALO - depth, HALO)
    halo_high = slice(HALO + strip, HALO + strip + depth)
    diag_up = remote(
        dgx.at[0:nlat, own_high, :], dgx.at[0:nlat, halo_low, :], diag_send.at[0], diag_recv.at[0],
        after // nlat, lax.rem(after, nlat),
    )
    diag_down = remote(
        dgx.at[0:nlat, own_low, :], dgx.at[0:nlat, halo_high, :], diag_send.at[1], diag_recv.at[1],
        before // nlat, lax.rem(before, nlat),
    )
    diag_up.start()
    diag_down.start()
    middle = slice(HALO, HALO + strip)
    diag_fold = remote(
        dgx.at[nlat - 1, middle, :], dgx.at[nlat, middle, :], diag_send.at[2], diag_recv.at[2],
        nlon - 1 - i, nlat - 1 - j,
    )
    diag_fold.start()
    sides = []
    for n, (shift, src, dst) in enumerate(((1, own_low, halo_high), (-1, own_high, halo_low))):
        other = lax.rem(total - 1 - t + shift + total, total)
        src_ref, dst_ref = dgx.at[nlat - 1, src, :], dgx.at[nlat, dst, :]
        sides.append((
            remote(
                src_ref, dst_ref, diag_send.at[3 + n], diag_recv.at[3 + n], other // nlat, lax.rem(other, nlat)
            ),
            pltpu.make_async_copy(src_ref, dst_ref, diag_recv.at[3 + n]),
            own_folds[n],
        ))
    for far, near, own in sides:
        @pl.when(own)
        def _():
            near.start()

        @pl.when(jnp.logical_not(own))
        def _():
            far.start()

    rows_out[0] = th[:, 0, :]
    rows_out[1] = th[:, cy - 1, :]
    to_south = remote(rows_out.at[0], north, halo_send.at[0], halo_recv.at[0], i, lat_of(j - 1))
    to_north = remote(rows_out.at[1], south, halo_send.at[1], halo_recv.at[1], i, lat_of(j + 1))
    to_fold = remote(rows_out.at[1], north, halo_send.at[1], halo_recv.at[0], nlon - 1 - i, j)

    @pl.when(j > 0)
    def _():
        to_south.start()

    @pl.when(jnp.logical_not(top))
    def _():
        to_north.start()

    @pl.when(top)
    def _():
        to_fold.start()

    lane = iota((cy, LANES), 1)
    packed = jnp.zeros((cy, LANES), F32)
    for k in range(levels):
        packed = jnp.where(lane == k, pltpu.roll(th[k, :, 0:LANES], k, 1), packed)
        packed = jnp.where(
            lane == levels + k, pltpu.roll(th[k, :, cx - LANES:cx], levels + k + 1, 1), packed
        )
    cols_out[...] = packed
    to_west = remote(cols_out, east, halo_send.at[2], halo_recv.at[2], lon_of(i - 1), j)
    to_east = remote(cols_out, west, halo_send.at[3], halo_recv.at[3], lon_of(i + 1), j)
    to_west.start()
    to_east.start()

    load_land.wait()
    table = land[...].astype(F32).astype(BF16)
    row_block = (j * cy + iota((cy, by), 0)) >> 5
    on_rows = bdot(hot(row_block == iota((cy, by), 1)), table).astype(BF16)
    col_block = (i * cx + iota((bx, cx), 1)) >> 5
    cols_hot = hot(col_block == iota((bx, cx), 0))
    ocean = bdot(on_rows, cols_hot)
    west_block = lax.rem(i * (cx // BS) + bx - 1, bx)
    east_block = lax.rem((i + 1) * (cx // BS), bx)
    ocean_west = bdot(on_rows, hot(iota((bx, LANES), 0) == west_block))
    ocean_east = bdot(on_rows, hot(iota((bx, LANES), 0) == east_block))
    edge_row = iota((8, by), 0)
    edge_col = iota((8, by), 1)
    south_hot = hot(jnp.logical_and(edge_row == 0, edge_col == j * (cy // BS) - 1))
    north_block = jnp.where(top, by - 1, (j + 1) * (cy // BS))
    north_hot = hot(jnp.logical_and(edge_row == 0, edge_col == north_block))
    north_cols = jnp.where(top, bx - 1 - col_block, col_block)
    ocean_south = bdot(bdot(south_hot, table).astype(BF16), cols_hot)[0:1]
    ocean_north = bdot(
        bdot(north_hot, table).astype(BF16), hot(north_cols == iota((bx, cx), 0))
    )[0:1]

    strip_x = (strip * t - HALO + nx + iota((wide, bx), 0)) % nx >> 5
    strip_hot = hot(strip_x == iota((wide, bx), 1))
    on_cols = ndot(strip_hot, table).astype(BF16)
    ocs[:, 0:ny] = bdot(on_cols, hot((iota((by, ny), 1) >> 5) == iota((by, ny), 0)))
    mirror_hot = hot((bx - 1 - strip_x) == iota((wide, bx), 1))
    on_mirror = ndot(mirror_hot, table).astype(BF16)
    keep = jnp.logical_and(iota((by, LANES), 0) == by - 1, iota((by, LANES), 1) < 8)
    ocs[:, ny:ny + LANES] = bdot(on_mirror, hot(keep))

    diag_up.wait_recv()
    diag_down.wait_recv()
    diag_fold.wait_recv()
    for far, near, own in sides:
        far.wait_recv()
    for c in range(nlat):
        dg[:, c * cy:(c + 1) * cy] = dgx[c]
    dg[:, ny:] = flip_rows(flip_lanes(dgx[nlat]), (wide,))
    dg[...] = ocs[...] * ((dg[...] - 1.0) * 0.25)
    quarter[...] = ocs[...] * 0.25

    whole(ext.at[0:nlat, :, low_row:low_row + span, :], main_recv).wait()
    whole(fold, fold_recv.at[0]).wait()

    @pl.when(ends)
    def _():
        whole(edge.at[:, :, 0:REACH, :], edge_recv).wait()
        whole(fold_edge, fold_recv.at[1]).wait()
        spot = iota((8, LANES), 1) % wide
        outer = jnp.logical_or(
            jnp.logical_and(top, spot < HALO), jnp.logical_and(j == 0, spot >= wide - HALO)
        )
        fold[...] = jnp.where(outer, fold_edge[...], fold[...])

    row = iota((2 * wide, LANES), 0)
    source = jnp.where(row < wide, wide - 1 - row, 3 * wide - 1 - row)
    pick = hot(source == iota((2 * wide, LANES), 1))
    turn = hot(iota((LANES, 8), 0) == 7 - iota((LANES, 8), 1))
    folded = [ndot(pick, bdot(turn, piece).astype(BF16)) for piece in pieces(fold[...])]
    folded = (folded[0] + folded[1]) + folded[2]
    ext[nlat, 0] = folded[0:wide]
    ext[nlat, 1] = folded[wide:]

    @pl.when(j == 0)
    def _():
        ext[0:nlat, :, 0:HALO, :] = edge[...]

    @pl.when(top)
    def _():
        ext[0:nlat, :, HALO + strip:, :] = edge[...]

    mask = ocs[...]
    column_sum, kappa_strip = [
        jnp.concatenate([ext[c, n] for c in range(nlat + 1)], axis=1) for n in range(2)
    ]
    held = mask * column_sum
    basis[0] = held + mask * kappa_strip * (neighbours(held) - 4.0 * held)
    for step in range(BASIS - 1):
        value = basis[step]
        basis[step + 1] = dg[...] * value - quarter[...] * neighbours(value)

    zero = jnp.zeros((8, LANES), F32)

    def accumulate(c, carry):
        sums = list(carry)
        lanes = pl.ds(pl.multiple_of(c * LANES, LANES), LANES)
        for h in range(strip // 8):
            values = [basis[b, HALO + 8 * h:HALO + 8 * h + 8, lanes] for b in range(BASIS)]
            split = [halves(value) for value in values]
            for n, (a, b) in enumerate(PAIRS):
                (ah, al), (bh, bl) = split[a], split[b]
                e = ah * bl + al * values[b]
                s, f = two_sum(sums[2 * n], ah * bh)
                sums[2 * n], sums[2 * n + 1] = s, sums[2 * n + 1] + (e + f)
        return tuple(sums)

    sums = lax.fori_loop(0, ny // LANES, accumulate, (zero,) * (2 * len(PAIRS)))
    place = iota((SLOTS, LANES), 0)
    high = jnp.zeros((SLOTS, LANES), F32)
    low = jnp.zeros((SLOTS, LANES), F32)
    for n in range(len(PAIRS)):
        h, l = sums[2 * n], sums[2 * n + 1]
        for shift in (4, 2, 1):
            h, e = two_sum(h, pltpu.roll(h, shift, 0))
            l = l + pltpu.roll(l, shift, 0) + e
        high = jnp.where(place == n, h[0:1], high)
        low = jnp.where(place == n, l[0:1], low)
    shift = LANES // 2
    while shift:
        high, e = two_sum(high, pltpu.roll(high, shift, 1))
        low = low + pltpu.roll(low, shift, 1) + e
        shift //= 2
    spot = iota((SLOTS, LANES), 1)
    packed = jnp.where(spot == place, high, jnp.where(spot == place + SLOTS, low, 0.0))
    message = jnp.sum(packed, axis=0, keepdims=True)

    def fold_in(ref, count):
        value = ref[...].reshape(count, LANES)
        error = jnp.zeros_like(value)
        shift = count // 2
        while shift:
            other = pltpu.roll(error, shift, 0)
            value, e = two_sum(value, pltpu.roll(value, shift, 0))
            error = error + other + e
            shift //= 2
        value, error = value[0:1], error[0:1]
        moved = pltpu.roll(error, SLOTS, 1)
        lane = iota((1, LANES), 1)
        return value + jnp.where(jnp.logical_and(lane >= SLOTS, lane < 2 * SLOTS), moved, 0.0)

    part1[pl.ds(i, 1)] = message[None]

    def lon_copy(d):
        return remote(part1.at[i], part1.at[i], red_send.at[0], red_recv.at[0], lax.rem(i + d, nlon), j)

    for d in range(1, nlon):
        lon_copy(d).start()

    to_south.wait_recv()
    to_west.wait_recv()
    to_east.wait_recv()

    @pl.when(j > 0)
    def _():
        to_north.wait_recv()

    @pl.when(j == 0)
    def _():
        south[...] = jnp.zeros_like(south)

    @pl.when(top)
    def _():
        north[...] = flip_lanes(north[...])

    west[...] = west[...] * ocean_west
    east[...] = east[...] * ocean_east
    scale = ocean * kp[...]
    first_row = iota((cy, cx), 0) == 0
    last_row = iota((cy, cx), 0) == cy - 1
    first_lane = iota((cy, cx), 1) == 0
    last_lane = iota((cy, cx), 1) == cx - 1

    def update(k, _):
        level = th[k]
        held = ocean * level
        from_west = pltpu.roll(west[...], LANES - levels - k, 1)
        from_east = pltpu.roll(east[...], LANES - 1 - k, 1)
        if cx > LANES:
            pad = jnp.zeros((cy, cx - LANES), F32)
            from_west = jnp.concatenate([from_west, pad], axis=1)
            from_east = jnp.concatenate([pad, from_east], axis=1)
        beside = jnp.where(first_lane, from_west, pltpu.roll(held, 1, 1))
        beside = beside + jnp.where(last_lane, from_east, pltpu.roll(held, cx - 1, 1))
        beside = beside + jnp.where(first_row, ocean_south * south[pl.ds(k, 1), :], pltpu.roll(held, 1, 0))
        beside = beside + jnp.where(last_row, ocean_north * north[pl.ds(k, 1), :], pltpu.roll(held, cy - 1, 0))
        out_theta[k] = level + scale * (beside - 4.0 * held)
        return 0

    lax.fori_loop(0, levels // 2, update, 0)
    whole(part1.at[pl.ds(0, nlon - 1)], red_recv.at[0]).wait()
    message = fold_in(part1, nlon)
    part2[pl.ds(j, 1)] = message[None]

    def lat_copy(d):
        return remote(part2.at[j], part2.at[j], red_send.at[1], red_recv.at[1], i, lax.rem(j + d, nlat))

    for d in range(1, nlat):
        lat_copy(d).start()
    lax.fori_loop(levels // 2, levels, update, 0)
    whole(part2.at[pl.ds(0, nlat - 1)], red_recv.at[1]).wait()
    message = fold_in(part2, nlat)
    high, low = quick(message, pltpu.roll(message, LANES - SLOTS, 1))

    gram = {}
    for n, (a, b) in enumerate(PAIRS):
        gram[a, b] = gram[b, a] = tuple(
            jnp.broadcast_to(x[:, n:n + 1], (1, LANES)) for x in (high, low)
        )
    size = BASIS - 1

    def scaled(x, factor):
        return x[0] * factor, x[1] * factor

    matrix = [
        [
            df_add(
                scaled(gram[a, b + 1], 4.0),
                df_add(scaled(gram[a, b], 4.0), gram[a, b]),
            )
            for b in range(size)
        ]
        for a in range(size)
    ]
    right = [gram[0, a] for a in range(size)]
    for p in range(size):
        for a in range(p + 1, size):
            factor = df_div(matrix[a][p], matrix[p][p])
            for b in range(p + 1, size):
                matrix[a][b] = df_sub(matrix[a][b], df_mul(factor, matrix[p][b]))
            right[a] = df_sub(right[a], df_mul(factor, right[p]))
    answer = [None] * size
    for p in reversed(range(size)):
        value = right[p]
        for b in range(p + 1, size):
            value = df_sub(value, df_mul(matrix[p][b], answer[b]))
        answer[p] = df_div(value, matrix[p][p])
    spread = [jnp.broadcast_to(x[0], (strip, LANES)) for x in answer]

    def combine(c, _):
        lanes = pl.ds(pl.multiple_of(c * LANES, LANES), LANES)
        value = spread[size - 1] * basis[size - 1, HALO:HALO + strip, lanes]
        for b in reversed(range(size - 1)):
            value = value + spread[b] * basis[b, HALO:HALO + strip, lanes]
        out_psi[:, lanes] = value
        return 0

    lax.fori_loop(0, ny // LANES, combine, 0)

    whole(ext.at[0:nlat - 1, :, low_row:low_row + span, :], main_send).wait()
    left_edge.wait_send()
    right_edge.wait_send()
    diag_up.wait_send()
    diag_down.wait_send()
    diag_fold.wait_send()
    for far, near, own in sides:
        @pl.when(jnp.logical_not(own))
        def _():
            far.wait_send()

    @pl.when(top)
    def _():
        whole(tiles, fold_send).wait()
        fold_low.wait_send()

        @pl.when(jnp.logical_not(far_self))
        def _():
            fold_far.wait_send()

    @pl.when(j > 0)
    def _():
        to_south.wait_send()

    to_north.wait_send()
    to_west.wait_send()
    to_east.wait_send()
    whole(part1.at[pl.ds(0, nlon - 1)], red_send.at[0]).wait()
    whole(part2.at[pl.ds(0, nlat - 1)], red_send.at[1]).wait()


def per_device(nlon, nlat, theta, kappa, layer_weight, diag, land_blocks):
    levels, cy, cx = theta.shape
    strip, ny = diag.shape
    wide = strip + 2 * HALO
    vmem = pl.BlockSpec(memory_space=pltpu.VMEM)
    hbm = pl.BlockSpec(memory_space=pltpu.HBM)
    dma = pltpu.SemaphoreType.DMA
    operands = (layer_weight, land_blocks, theta, kappa, diag)
    return pl.pallas_call(
        functools.partial(kernel, nlon, nlat),
        out_shape=(
            jax.ShapeDtypeStruct(theta.shape, F32),
            jax.ShapeDtypeStruct(diag.shape, F32),
        ),
        in_specs=[hbm] * 5,
        out_specs=(vmem, vmem),
        scratch_shapes=[
            pltpu.SMEM(layer_weight.shape, F32),
            pltpu.VMEM(land_blocks.shape, jnp.int32),
            pltpu.VMEM((levels, cy, cx), F32),
            pltpu.VMEM((cy, cx), F32),
            pltpu.VMEM((2, cx + 2 * HALO, cy), F32),
            pltpu.VMEM((nlat + 1, 2, wide, cy), F32),
            pltpu.VMEM((nlat, 2, HALO, cy), F32),
            pltpu.VMEM((strip, ny), F32),
            pltpu.VMEM((nlat + 1, wide, cy), F32),
            pltpu.VMEM((wide, ny + LANES), F32),
            pltpu.VMEM((wide, ny + LANES), F32),
            pltpu.VMEM((wide, ny + LANES), F32),
            pltpu.VMEM((BASIS, wide, ny + LANES), F32),
            pltpu.VMEM((2, levels, cx), F32),
            pltpu.VMEM((levels, cx), F32),
            pltpu.VMEM((levels, cx), F32),
            pltpu.VMEM((cy, LANES), F32),
            pltpu.VMEM((cy, LANES), F32),
            pltpu.VMEM((cy, LANES), F32),
            pltpu.VMEM((nlat, 8, LANES), F32),
            pltpu.VMEM((8, LANES), F32),
            pltpu.VMEM((8, LANES), F32),
            pltpu.VMEM((nlon, 1, LANES), F32),
            pltpu.VMEM((nlat, 1, LANES), F32),
            dma((8,)),
            dma,
            dma,
            dma((2,)),
            dma,
            dma,
            dma,
            dma,
            dma((2,)),
            dma((5,)),
            dma((5,)),
            dma((4,)),
            dma((4,)),
            dma((2,)),
            dma((2,)),
        ],
        compiler_params=pltpu.CompilerParams(
            collective_id=0, has_side_effects=True, vmem_limit_bytes=32 << 20
        ),
        name="ocean_step",
    )(*[pltpu.with_memory_space_constraint(x, pltpu.HBM) for x in operands])


def solution(mesh):
    placed = (P(None, "lat", "lon"), P("lat", "lon"), P(), P(("lon", "lat"), None), P())
    return jax.shard_map(
        functools.partial(per_device, mesh.shape["lon"], mesh.shape["lat"]),
        mesh=mesh,
        in_specs=placed,
        out_specs=(P(None, "lat", "lon"), P(("lon", "lat"), None)),
        check_vma=False,
    )
```

```python
import functools

import jax
import jax.numpy as jnp
from jax import lax
from jax.experimental import pallas as pl
from jax.experimental.pallas import tpu as pltpu
from jax.sharding import PartitionSpec as P

MESH = pl.DeviceIdType.MESH
BS = 32
HALO = 8
REACH = 5
LANES = 128
F32 = jnp.float32
BF16 = jnp.bfloat16
BASIS = 5
PAIRS = [(a, b) for a in range(BASIS) for b in range(a, BASIS) if a < BASIS - 1]
SLOTS = 16


def iota(shape, axis):
    return lax.broadcasted_iota(jnp.int32, shape, axis)


def hot(condition):
    return jnp.where(condition, 1.0, 0.0).astype(BF16)


def bdot(left, right):
    return jnp.dot(left, right, preferred_element_type=F32)


def ndot(left, right):
    return lax.dot_general(left, right, (((1,), (1,)), ((), ())), preferred_element_type=F32)


def pieces(value):
    first = value.astype(BF16)
    rest = value - first.astype(F32)
    second = rest.astype(BF16)
    third = (rest - second.astype(F32)).astype(BF16)
    return [first, second, third]


def flip_lanes(value):
    width = value.shape[1]
    turn = hot(iota((width, width), 0) + iota((width, width), 1) == width - 1)
    parts = [bdot(piece, turn) for piece in pieces(value)]
    return (parts[0] + parts[1]) + parts[2]


def flip_rows(value, groups):
    count = value.shape[0]
    row = iota((count, count), 0)
    ends, start = jnp.zeros((count, count), jnp.int32), 0
    for size in groups:
        ends = jnp.where(row >= start, 2 * start + size - 1, ends)
        start += size
    turn = hot(row + iota((count, count), 1) == ends)
    parts = [bdot(turn, piece) for piece in pieces(value)]
    return (parts[0] + parts[1]) + parts[2]


def two_sum(a, b):
    s = a + b
    t = s - a
    return s, (a - (s - t)) + (b - t)


def halves(a):
    t = a * 4097.0
    high = t - (t - a)
    return high, a - high


def two_prod(a, b):
    p = a * b
    ah, al = halves(a)
    bh, bl = halves(b)
    return p, ((ah * bh - p) + ah * bl + al * bh) + al * bl


def quick(a, b):
    s = a + b
    return s, b - (s - a)


def df_mul(x, y):
    p, e = two_prod(x[0], y[0])
    return quick(p, e + (x[0] * y[1] + x[1] * y[0]))


def df_add(x, y):
    s, e = two_sum(x[0], y[0])
    return quick(s, e + (x[1] + y[1]))


def df_sub(x, y):
    return df_add(x, (-y[0], -y[1]))


def df_div(x, y):
    first = x[0] / y[0]
    rest = df_sub(x, df_mul(y, (first, jnp.zeros_like(first))))
    second = rest[0] / y[0]
    return quick(first, second)


def stencil(load, emit, count):
    value = load(0)
    rows, width = value.shape
    lane = iota(value.shape, 1)
    first, last = lane == 0, lane == width - 1
    before = jnp.zeros_like(value)
    up = pltpu.roll(value, width - 1, 1)
    for c in range(count):
        if c + 1 < count:
            following = load(c + 1)
            up_next = pltpu.roll(following, width - 1, 1)
        else:
            following, up_next = None, up
        down = pltpu.roll(value, 1, 1)
        beside = jnp.where(first, before, down) + jnp.where(last, up_next, up)
        emit(c, value, (beside + pltpu.roll(value, 1, 0)) + pltpu.roll(value, rows - 1, 0))
        value, before, up = following, down, up_next


def kernel(
    nlon, nlat,
    weight_in, land_in, theta, kappa, diag,
    out_theta, out_psi,
    weight, land, th, kp, skt, ext, edge, flat, dgx, dg, ocs, quarter, basis, rows_out, north, south, cols_out, east, west,
    tiles, fold, fold_edge, parts,
    in_sem, main_send, main_recv, edge_send, edge_recv, fold_send, fold_low_send, fold_far_send, fold_recv,
    diag_send, diag_recv, halo_send, halo_recv, red_send, red_recv, ready,
):
    levels, cy, cx = th.shape
    ny, nx = cy * nlat, cx * nlon
    strip = cx // nlat
    wide = strip + 2 * HALO
    by, bx = land.shape
    total = nlon * nlat
    i = lax.axis_index("lon")
    j = lax.axis_index("lat")
    t = i * nlat + j
    top = j == nlat - 1
    ends = jnp.logical_or(j == 0, top)

    def remote(src, dst, send, recv, lon, lat):
        return pltpu.make_async_remote_copy(
            src_ref=src, dst_ref=dst, send_sem=send, recv_sem=recv,
            device_id=(lon, lat), device_id_type=MESH,
        )

    def lon_of(value):
        return lax.rem(value + 2 * nlon, nlon)

    def lat_of(value):
        return lax.rem(value + 2 * nlat, nlat)

    def whole(ref, sem):
        return pltpu.make_async_copy(ref, ref, sem)

    def greet(lon, lat):
        pl.semaphore_signal(barrier, inc=1, device_id=(lon, lat), device_id_type=MESH)

    chunk = levels // 4
    loads = [
        pltpu.make_async_copy(theta.at[pl.ds(q * chunk, chunk)], th.at[pl.ds(q * chunk, chunk)], in_sem.at[q])
        for q in range(4)
    ]
    load_kappa = pltpu.make_async_copy(kappa, kp, in_sem.at[4])
    load_diag = pltpu.make_async_copy(diag, flat, in_sem.at[5])
    load_weight = pltpu.make_async_copy(weight_in, weight, in_sem.at[6])
    load_land = pltpu.make_async_copy(land_in, land, in_sem.at[7])
    load_kappa.start()
    load_weight.start()
    for copy in loads:
        copy.start()
    load_diag.start()
    load_land.start()
    ext[:, :, 0:HALO, :] = jnp.zeros((nlat + 1, 2, HALO, cy), F32)
    ext[:, :, HALO + strip:, :] = jnp.zeros((nlat + 1, 2, HALO, cy), F32)
    edge[...] = jnp.zeros_like(edge)
    dgx[:, 0:HALO, :] = jnp.zeros((nlat + 1, HALO, cy), F32)
    dgx[:, HALO + strip:, :] = jnp.zeros((nlat + 1, HALO, cy), F32)

    barrier = pltpu.get_barrier_semaphore()
    for d in range(1, nlat):
        greet(i, lax.rem(j + d, nlat))
    for d in range(1, nlon):
        greet(lax.rem(i + d, nlon), j)
    greet(nlon - 1 - i, nlat - 1)
    for shift in (1, 0, -1):
        other = lax.rem(total - 1 - t + shift + total, total)

        @pl.when(other != t)
        def _():
            greet(other // nlat, lax.rem(other, nlat))

    @pl.when(j == 0)
    def _():
        for lat in range(nlat):
            greet(lon_of(i - 1), lat)
        greet(lon_of(nlon - i), nlat - 1)

    @pl.when(top)
    def _():
        for lat in range(nlat):
            greet(lon_of(i + 1), lat)

    skt[:, 0:HALO, :] = jnp.zeros((2, HALO, cy), F32)
    skt[:, HALO + cx:, :] = jnp.zeros((2, HALO, cy), F32)
    load_kappa.wait()
    skt[1, HALO:HALO + cx, :] = kp[...].T
    load_weight.wait()
    column = jnp.zeros((cy, cx), F32)
    for q in range(4):
        loads[q].wait()
        for k in range(q * chunk, (q + 1) * chunk):
            column = column + weight[k] * th[k]
    skt[0, HALO:HALO + cx, :] = column.T

    @pl.when(top)
    def _():
        last_sums = column[cy - 8:, :]
        last_kappa = kp[cy - 8:, :]
        lanes8 = iota((8, LANES), 1)
        for m in range(nlat):
            start = strip * (nlat - 1 - m) - HALO
            tiles[m] = jnp.where(
                lanes8 < wide,
                pltpu.roll(last_sums, (-start) % cx, 1)[:, 0:LANES],
                pltpu.roll(last_kappa, (wide - start) % cx, 1)[:, 0:LANES],
            )

    load_diag.wait()
    for c in range(nlat):
        dgx[c, HALO:HALO + strip, :] = flat[:, c * cy:(c + 1) * cy]

    own_folds = [lax.rem(total - 1 - t + shift + total, total) == t for shift in (1, -1)]
    awaited = nlat + nlon + 3 + jnp.where(top, nlat + 1, 0)
    for own in own_folds:
        awaited = awaited - jnp.where(own, 1, 0)
    pl.semaphore_wait(barrier, awaited)
    for d in range(1, nlon):
        pl.semaphore_signal(
            ready, inc=1, device_id=(lax.rem(i + d, nlon), j), device_id_type=MESH
        )

    low_row = HALO - REACH
    span = strip + 2 * REACH

    def block_rows(m):
        return skt.at[:, pl.ds(m * strip + low_row, span), :]

    own_slot = ext.at[j, :, low_row:low_row + span, :]

    def main_copy(d):
        m = lax.rem(j + d, nlat)
        return remote(block_rows(m), own_slot, main_send, main_recv, i, m)

    for d in range(1, nlat):
        main_copy(d).start()
    pltpu.make_async_copy(block_rows(j), own_slot, main_recv).start()
    first_rows = skt.at[:, HALO:HALO + REACH, :]
    last_rows = skt.at[:, HALO + cx - REACH:HALO + cx, :]
    left_edge = remote(
        first_rows, edge.at[j, :, 0:REACH, :], edge_send.at[0], edge_recv, lon_of(i - 1), nlat - 1
    )
    right_edge = remote(
        last_rows, edge.at[j, :, low_row:HALO, :], edge_send.at[1], edge_recv, lon_of(i + 1), 0
    )
    left_edge.start()
    right_edge.start()

    def fold_copy(m):
        return remote(tiles.at[m], fold, fold_send, fold_recv.at[0], nlon - 1 - i, m)

    far_lon = lon_of(nlon - 2 - i)
    far_self = far_lon == i
    fold_far = remote(
        tiles.at[nlat - 1], fold_edge, fold_far_send, fold_recv.at[1], far_lon, nlat - 1
    )
    fold_far_own = pltpu.make_async_copy(tiles.at[nlat - 1], fold_edge, fold_recv.at[1])
    fold_low = remote(tiles.at[0], fold_edge, fold_low_send, fold_recv.at[1], lon_of(nlon - i), 0)

    @pl.when(top)
    def _():
        for m in range(nlat):
            fold_copy(m).start()
        fold_low.start()

        @pl.when(far_self)
        def _():
            fold_far_own.start()

        @pl.when(jnp.logical_not(far_self))
        def _():
            fold_far.start()

    after, before = lax.rem(t + 1, total), lax.rem(t + total - 1, total)
    depth = BASIS - 2
    own_low = slice(HALO, HALO + depth)
    own_high = slice(HALO + strip - depth, HALO + strip)
    halo_low = slice(HALO - depth, HALO)
    halo_high = slice(HALO + strip, HALO + strip + depth)
    diag_up = remote(
        dgx.at[0:nlat, own_high, :], dgx.at[0:nlat, halo_low, :], diag_send.at[0], diag_recv.at[0],
        after // nlat, lax.rem(after, nlat),
    )
    diag_down = remote(
        dgx.at[0:nlat, own_low, :], dgx.at[0:nlat, halo_high, :], diag_send.at[1], diag_recv.at[1],
        before // nlat, lax.rem(before, nlat),
    )
    diag_up.start()
    diag_down.start()
    middle = slice(HALO, HALO + strip)
    diag_fold = remote(
        dgx.at[nlat - 1, middle, :], dgx.at[nlat, middle, :], diag_send.at[2], diag_recv.at[2],
        nlon - 1 - i, nlat - 1 - j,
    )
    diag_fold.start()
    sides = []
    for n, (shift, src, dst) in enumerate(((1, own_low, halo_high), (-1, own_high, halo_low))):
        other = lax.rem(total - 1 - t + shift + total, total)
        src_ref, dst_ref = dgx.at[nlat - 1, src, :], dgx.at[nlat, dst, :]
        sides.append((
            remote(
                src_ref, dst_ref, diag_send.at[3 + n], diag_recv.at[3 + n], other // nlat, lax.rem(other, nlat)
            ),
            pltpu.make_async_copy(src_ref, dst_ref, diag_recv.at[3 + n]),
            own_folds[n],
        ))
    for far, near, own in sides:
        @pl.when(own)
        def _():
            near.start()

        @pl.when(jnp.logical_not(own))
        def _():
            far.start()

    rows_out[0] = th[:, 0, :]
    rows_out[1] = th[:, cy - 1, :]
    to_south = remote(rows_out.at[0], north, halo_send.at[0], halo_recv.at[0], i, lat_of(j - 1))
    to_north = remote(rows_out.at[1], south, halo_send.at[1], halo_recv.at[1], i, lat_of(j + 1))
    to_fold = remote(rows_out.at[1], north, halo_send.at[1], halo_recv.at[0], nlon - 1 - i, j)

    @pl.when(j > 0)
    def _():
        to_south.start()

    @pl.when(jnp.logical_not(top))
    def _():
        to_north.start()

    @pl.when(top)
    def _():
        to_fold.start()

    lane = iota((cy, LANES), 1)
    packed = jnp.zeros((cy, LANES), F32)
    for k in range(levels):
        packed = jnp.where(lane == k, pltpu.roll(th[k, :, 0:LANES], k, 1), packed)
        packed = jnp.where(
            lane == levels + k, pltpu.roll(th[k, :, cx - LANES:cx], levels + k + 1, 1), packed
        )
    cols_out[...] = packed
    to_west = remote(cols_out, east, halo_send.at[2], halo_recv.at[2], lon_of(i - 1), j)
    to_east = remote(cols_out, west, halo_send.at[3], halo_recv.at[3], lon_of(i + 1), j)
    to_west.start()
    to_east.start()

    load_land.wait()
    table = land[...].astype(F32).astype(BF16)
    row_block = (j * cy + iota((cy, by), 0)) >> 5
    on_rows = bdot(hot(row_block == iota((cy, by), 1)), table).astype(BF16)
    col_block = (i * cx + iota((bx, cx), 1)) >> 5
    cols_hot = hot(col_block == iota((bx, cx), 0))
    ocean = bdot(on_rows, cols_hot)
    west_block = lax.rem(i * (cx // BS) + bx - 1, bx)
    east_block = lax.rem((i + 1) * (cx // BS), bx)
    ocean_west = bdot(on_rows, hot(iota((bx, LANES), 0) == west_block))
    ocean_east = bdot(on_rows, hot(iota((bx, LANES), 0) == east_block))
    edge_row = iota((8, by), 0)
    edge_col = iota((8, by), 1)
    south_hot = hot(jnp.logical_and(edge_row == 0, edge_col == j * (cy // BS) - 1))
    north_block = jnp.where(top, by - 1, (j + 1) * (cy // BS))
    north_hot = hot(jnp.logical_and(edge_row == 0, edge_col == north_block))
    north_cols = jnp.where(top, bx - 1 - col_block, col_block)
    ocean_south = bdot(bdot(south_hot, table).astype(BF16), cols_hot)[0:1]
    ocean_north = bdot(
        bdot(north_hot, table).astype(BF16), hot(north_cols == iota((bx, cx), 0))
    )[0:1]

    strip_x = (strip * t - HALO + nx + iota((wide, bx), 0)) % nx >> 5
    strip_hot = hot(strip_x == iota((wide, bx), 1))
    on_cols = ndot(strip_hot, table).astype(BF16)
    ocs[:, 0:ny] = bdot(on_cols, hot((iota((by, ny), 1) >> 5) == iota((by, ny), 0)))
    mirror_hot = hot((bx - 1 - strip_x) == iota((wide, bx), 1))
    on_mirror = ndot(mirror_hot, table).astype(BF16)
    keep = jnp.logical_and(iota((by, LANES), 0) == by - 1, iota((by, LANES), 1) < 8)
    ocs[:, ny:ny + LANES] = bdot(on_mirror, hot(keep))

    diag_up.wait_recv()
    diag_down.wait_recv()
    diag_fold.wait_recv()
    for far, near, own in sides:
        far.wait_recv()
    for c in range(nlat):
        dg[:, c * cy:(c + 1) * cy] = dgx[c]
    dg[:, ny:] = flip_rows(flip_lanes(dgx[nlat]), (wide,))
    dg[...] = ocs[...] * ((dg[...] - 1.0) * 0.25)
    quarter[...] = ocs[...] * 0.25

    whole(ext.at[0:nlat, :, low_row:low_row + span, :], main_recv).wait()
    whole(fold, fold_recv.at[0]).wait()

    @pl.when(ends)
    def _():
        whole(edge.at[:, :, 0:REACH, :], edge_recv).wait()
        whole(fold_edge, fold_recv.at[1]).wait()
        spot = iota((8, LANES), 1) % wide
        outer = jnp.logical_or(
            jnp.logical_and(top, spot < HALO), jnp.logical_and(j == 0, spot >= wide - HALO)
        )
        fold[...] = jnp.where(outer, fold_edge[...], fold[...])

    row = iota((2 * wide, LANES), 0)
    source = jnp.where(row < wide, wide - 1 - row, 3 * wide - 1 - row)
    pick = hot(source == iota((2 * wide, LANES), 1))
    turn = hot(iota((LANES, 8), 0) == 7 - iota((LANES, 8), 1))
    folded = [ndot(pick, bdot(turn, piece).astype(BF16)) for piece in pieces(fold[...])]
    folded = (folded[0] + folded[1]) + folded[2]
    ext[nlat, 0] = folded[0:wide]
    ext[nlat, 1] = folded[wide:]

    @pl.when(j == 0)
    def _():
        ext[0:nlat, :, 0:HALO, :] = edge[...]

    @pl.when(top)
    def _():
        ext[0:nlat, :, HALO + strip:, :] = edge[...]

    def lanes_of(c):
        return slice(c * LANES, (c + 1) * LANES)

    def store_forcing(c, value, beside):
        rate = ocs[:, lanes_of(c)] * ext[c, 1]
        basis[0, :, lanes_of(c)] = value + rate * (beside - 4.0 * value)

    stencil(lambda c: ocs[:, lanes_of(c)] * ext[c, 0], store_forcing, nlat + 1)
    for step in range(BASIS - 1):
        def store_next(c, value, beside):
            lanes = lanes_of(c)
            basis[step + 1, :, lanes] = dg[:, lanes] * value - quarter[:, lanes] * beside

        stencil(lambda c: basis[step, :, lanes_of(c)], store_next, nlat + 1)

    zero = jnp.zeros((8, LANES), F32)

    def accumulate(c, carry):
        sums = list(carry)
        lanes = pl.ds(pl.multiple_of(c * LANES, LANES), LANES)
        for h in range(strip // 8):
            values = [basis[b, HALO + 8 * h:HALO + 8 * h + 8, lanes] for b in range(BASIS)]
            split = [halves(value) for value in values]
            for n, (a, b) in enumerate(PAIRS):
                (ah, al), (bh, bl) = split[a], split[b]
                e = ah * bl + al * values[b]
                s, f = two_sum(sums[2 * n], ah * bh)
                sums[2 * n], sums[2 * n + 1] = s, sums[2 * n + 1] + (e + f)
        return tuple(sums)

    sums = lax.fori_loop(0, ny // LANES, accumulate, (zero,) * (2 * len(PAIRS)))
    place = iota((SLOTS, LANES), 0)
    high = jnp.zeros((SLOTS, LANES), F32)
    low = jnp.zeros((SLOTS, LANES), F32)
    for n in range(len(PAIRS)):
        h, l = sums[2 * n], sums[2 * n + 1]
        for shift in (4, 2, 1):
            h, e = two_sum(h, pltpu.roll(h, shift, 0))
            l = l + pltpu.roll(l, shift, 0) + e
        high = jnp.where(place == n, h[0:1], high)
        low = jnp.where(place == n, l[0:1], low)
    shift = LANES // 2
    while shift:
        high, e = two_sum(high, pltpu.roll(high, shift, 1))
        low = low + pltpu.roll(low, shift, 1) + e
        shift //= 2
    spot = iota((SLOTS, LANES), 1)
    packed = jnp.where(spot == place, high, jnp.where(spot == place + SLOTS, low, 0.0))
    message = jnp.sum(packed, axis=0, keepdims=True)

    parts[pl.ds(t, 1), :] = message
    own_part = parts.at[pl.ds(t, 1), :]
    sizes = (nlon // 2, 2, nlat // 4, 4)
    offsets = [
        (a, b, c, d)
        for a in range(sizes[0]) for b in range(sizes[1]) for c in range(sizes[2]) for d in range(sizes[3])
    ]

    def hops(offset):
        return sum(min(o, n - o) for o, n in zip(offset, sizes) if n > 2 or o) - 0.5 * offset[1]

    offsets = sorted(offsets[1:], key=hops, reverse=True)
    place_of = (i // 2, lax.rem(i, 2), j // 4, lax.rem(j, 4))
    moved = [
        [lax.rem(place_of[n] + o, sizes[n]) * scale for o in range(sizes[n])]
        for n, scale in enumerate((2, 1, 4, 1))
    ]
    pl.semaphore_wait(ready, nlon - 1)
    for a, b, c, d in offsets:
        remote(own_part, own_part, red_send, red_recv, moved[0][a] + moved[1][b], moved[2][c] + moved[3][d]).start()

    to_south.wait_recv()
    to_west.wait_recv()
    to_east.wait_recv()

    @pl.when(j > 0)
    def _():
        to_north.wait_recv()

    @pl.when(j == 0)
    def _():
        south[...] = jnp.zeros_like(south)

    @pl.when(top)
    def _():
        north[...] = flip_lanes(north[...])

    west[...] = west[...] * ocean_west
    east[...] = east[...] * ocean_east
    scale = ocean * kp[...]
    first_row = iota((cy, cx), 0) == 0
    last_row = iota((cy, cx), 0) == cy - 1
    first_lane = iota((cy, cx), 1) == 0
    last_lane = iota((cy, cx), 1) == cx - 1

    def update(k, _):
        level = th[k]
        held = ocean * level
        from_west = pltpu.roll(west[...], LANES - levels - k, 1)
        from_east = pltpu.roll(east[...], LANES - 1 - k, 1)
        if cx > LANES:
            pad = jnp.zeros((cy, cx - LANES), F32)
            from_west = jnp.concatenate([from_west, pad], axis=1)
            from_east = jnp.concatenate([pad, from_east], axis=1)
        beside = jnp.where(first_lane, from_west, pltpu.roll(held, 1, 1))
        beside = beside + jnp.where(last_lane, from_east, pltpu.roll(held, cx - 1, 1))
        beside = beside + jnp.where(first_row, ocean_south * south[pl.ds(k, 1), :], pltpu.roll(held, 1, 0))
        beside = beside + jnp.where(last_row, ocean_north * north[pl.ds(k, 1), :], pltpu.roll(held, cy - 1, 0))
        out_theta[k] = level + scale * (beside - 4.0 * held)
        return 0

    lax.fori_loop(0, levels, update, 0)
    whole(parts.at[pl.ds(0, total - 1), :], red_recv).wait()
    value = parts[...]
    error = jnp.zeros_like(value)
    half = total // 2
    while half >= 8:
        value, e = two_sum(value[:half], value[half:])
        error = error[:half] + error[half:] + e
        half //= 2
    for shift in (4, 2, 1):
        value, e = two_sum(value, pltpu.roll(value, shift, 0))
        error = error + pltpu.roll(error, shift, 0) + e
    lane = iota((1, LANES), 1)
    error = jnp.where(
        jnp.logical_and(lane >= SLOTS, lane < 2 * SLOTS), pltpu.roll(error[0:1], SLOTS, 1), 0.0
    )
    message = value[0:1] + error
    high, low = quick(message, pltpu.roll(message, LANES - SLOTS, 1))

    gram = {}
    for n, (a, b) in enumerate(PAIRS):
        gram[a, b] = gram[b, a] = tuple(
            jnp.broadcast_to(x[:, n:n + 1], (1, LANES)) for x in (high, low)
        )
    size = BASIS - 1

    def scaled(x, factor):
        return x[0] * factor, x[1] * factor

    matrix = [
        [
            df_add(
                scaled(gram[a, b + 1], 4.0),
                df_add(scaled(gram[a, b], 4.0), gram[a, b]),
            )
            for b in range(size)
        ]
        for a in range(size)
    ]
    right = [gram[0, a] for a in range(size)]
    for p in range(size):
        for a in range(p + 1, size):
            factor = df_div(matrix[a][p], matrix[p][p])
            for b in range(p + 1, size):
                matrix[a][b] = df_sub(matrix[a][b], df_mul(factor, matrix[p][b]))
            right[a] = df_sub(right[a], df_mul(factor, right[p]))
    answer = [None] * size
    for p in reversed(range(size)):
        value = right[p]
        for b in range(p + 1, size):
            value = df_sub(value, df_mul(matrix[p][b], answer[b]))
        answer[p] = df_div(value, matrix[p][p])
    spread = [jnp.broadcast_to(x[0], (strip, LANES)) for x in answer]

    def combine(c, _):
        lanes = pl.ds(pl.multiple_of(c * LANES, LANES), LANES)
        value = spread[size - 1] * basis[size - 1, HALO:HALO + strip, lanes]
        for b in reversed(range(size - 1)):
            value = value + spread[b] * basis[b, HALO:HALO + strip, lanes]
        out_psi[:, lanes] = value
        return 0

    lax.fori_loop(0, ny // LANES, combine, 0)

    whole(ext.at[0:nlat - 1, :, low_row:low_row + span, :], main_send).wait()
    left_edge.wait_send()
    right_edge.wait_send()
    diag_up.wait_send()
    diag_down.wait_send()
    diag_fold.wait_send()
    for far, near, own in sides:
        @pl.when(jnp.logical_not(own))
        def _():
            far.wait_send()

    @pl.when(top)
    def _():
        whole(tiles, fold_send).wait()
        fold_low.wait_send()

        @pl.when(jnp.logical_not(far_self))
        def _():
            fold_far.wait_send()

    @pl.when(j > 0)
    def _():
        to_south.wait_send()

    to_north.wait_send()
    to_west.wait_send()
    to_east.wait_send()
    whole(parts.at[pl.ds(0, total - 1), :], red_send).wait()


def per_device(nlon, nlat, theta, kappa, layer_weight, diag, land_blocks):
    levels, cy, cx = theta.shape
    strip, ny = diag.shape
    wide = strip + 2 * HALO
    vmem = pl.BlockSpec(memory_space=pltpu.VMEM)
    hbm = pl.BlockSpec(memory_space=pltpu.HBM)
    dma = pltpu.SemaphoreType.DMA
    operands = (layer_weight, land_blocks, theta, kappa, diag)
    return pl.pallas_call(
        functools.partial(kernel, nlon, nlat),
        out_shape=(
            jax.ShapeDtypeStruct(theta.shape, F32),
            jax.ShapeDtypeStruct(diag.shape, F32),
        ),
        in_specs=[hbm] * 5,
        out_specs=(vmem, vmem),
        scratch_shapes=[
            pltpu.SMEM(layer_weight.shape, F32),
            pltpu.VMEM(land_blocks.shape, jnp.int32),
            pltpu.VMEM((levels, cy, cx), F32),
            pltpu.VMEM((cy, cx), F32),
            pltpu.VMEM((2, cx + 2 * HALO, cy), F32),
            pltpu.VMEM((nlat + 1, 2, wide, cy), F32),
            pltpu.VMEM((nlat, 2, HALO, cy), F32),
            pltpu.VMEM((strip, ny), F32),
            pltpu.VMEM((nlat + 1, wide, cy), F32),
            pltpu.VMEM((wide, ny + LANES), F32),
            pltpu.VMEM((wide, ny + LANES), F32),
            pltpu.VMEM((wide, ny + LANES), F32),
            pltpu.VMEM((BASIS, wide, ny + LANES), F32),
            pltpu.VMEM((2, levels, cx), F32),
            pltpu.VMEM((levels, cx), F32),
            pltpu.VMEM((levels, cx), F32),
            pltpu.VMEM((cy, LANES), F32),
            pltpu.VMEM((cy, LANES), F32),
            pltpu.VMEM((cy, LANES), F32),
            pltpu.VMEM((nlat, 8, LANES), F32),
            pltpu.VMEM((8, LANES), F32),
            pltpu.VMEM((8, LANES), F32),
            pltpu.VMEM((nlon * nlat, LANES), F32),
            dma((8,)),
            dma,
            dma,
            dma((2,)),
            dma,
            dma,
            dma,
            dma,
            dma((2,)),
            dma((5,)),
            dma((5,)),
            dma((4,)),
            dma((4,)),
            dma,
            dma,
            pltpu.SemaphoreType.REGULAR,
        ],
        compiler_params=pltpu.CompilerParams(
            collective_id=0, has_side_effects=True, vmem_limit_bytes=32 << 20
        ),
        name="ocean_step",
    )(*[pltpu.with_memory_space_constraint(x, pltpu.HBM) for x in operands])


def solution(mesh):
    placed = (P(None, "lat", "lon"), P("lat", "lon"), P(), P(("lon", "lat"), None), P())
    return jax.shard_map(
        functools.partial(per_device, mesh.shape["lon"], mesh.shape["lat"]),
        mesh=mesh,
        in_specs=placed,
        out_specs=(P(None, "lat", "lon"), P(("lon", "lat"), None)),
        check_vma=False,
    )
```

```python
import functools

import jax
import jax.numpy as jnp
from jax import lax
from jax.experimental import pallas as pl
from jax.experimental.pallas import tpu as pltpu
from jax.sharding import PartitionSpec as P

MESH = pl.DeviceIdType.MESH
BS = 32
HALO = 8
REACH = 5
PAD = 8
INNER = 4
LANES = 128
F32 = jnp.float32
BF16 = jnp.bfloat16
BASIS = 5
PAIRS = [(a, b) for a in range(BASIS) for b in range(a, BASIS) if a < BASIS - 1]
SLOTS = 16


def iota(shape, axis):
    return lax.broadcasted_iota(jnp.int32, shape, axis)


def hot(condition):
    return jnp.where(condition, 1.0, 0.0).astype(BF16)


def bdot(left, right):
    return jnp.dot(left, right, preferred_element_type=F32)


def ndot(left, right):
    return lax.dot_general(left, right, (((1,), (1,)), ((), ())), preferred_element_type=F32)


def pieces(value):
    first = value.astype(BF16)
    rest = value - first.astype(F32)
    second = rest.astype(BF16)
    third = (rest - second.astype(F32)).astype(BF16)
    return [first, second, third]


def flip_lanes(value):
    width = value.shape[1]
    turn = hot(iota((width, width), 0) + iota((width, width), 1) == width - 1)
    parts = [bdot(piece, turn) for piece in pieces(value)]
    return (parts[0] + parts[1]) + parts[2]


def flip_rows(value, groups):
    count = value.shape[0]
    row = iota((count, count), 0)
    ends, start = jnp.zeros((count, count), jnp.int32), 0
    for size in groups:
        ends = jnp.where(row >= start, 2 * start + size - 1, ends)
        start += size
    turn = hot(row + iota((count, count), 1) == ends)
    parts = [bdot(turn, piece) for piece in pieces(value)]
    return (parts[0] + parts[1]) + parts[2]


def two_sum(a, b):
    s = a + b
    t = s - a
    return s, (a - (s - t)) + (b - t)


def halves(a):
    t = a * 4097.0
    high = t - (t - a)
    return high, a - high


def two_prod(a, b):
    p = a * b
    ah, al = halves(a)
    bh, bl = halves(b)
    return p, ((ah * bh - p) + ah * bl + al * bh) + al * bl


def quick(a, b):
    s = a + b
    return s, b - (s - a)


def df_mul(x, y):
    p, e = two_prod(x[0], y[0])
    return quick(p, e + (x[0] * y[1] + x[1] * y[0]))


def df_add(x, y):
    s, e = two_sum(x[0], y[0])
    return quick(s, e + (x[1] + y[1]))


def df_sub(x, y):
    return df_add(x, (-y[0], -y[1]))


def df_div(x, y):
    first = x[0] / y[0]
    rest = df_sub(x, df_mul(y, (first, jnp.zeros_like(first))))
    second = rest[0] / y[0]
    return quick(first, second)


def stencil(ref, emit, low, high):
    count, _, width = ref.shape
    lane = iota((high - low, width), 1)
    first, last = lane == 0, lane == width - 1

    def load(c, shift=0):
        return ref[c, low + shift:high + shift, :]

    value = load(0)
    before = jnp.zeros_like(value)
    up = pltpu.roll(value, width - 1, 1)
    for c in range(count):
        if c + 1 < count:
            following = load(c + 1)
            up_next = pltpu.roll(following, width - 1, 1)
        else:
            following, up_next = None, up
        down = pltpu.roll(value, 1, 1)
        beside = jnp.where(first, before, down) + jnp.where(last, up_next, up)
        emit(c, value, (beside + load(c, -1)) + load(c, 1))
        value, before, up = following, down, up_next


def kernel(
    nlon, nlat,
    weight_in, land_in, theta, kappa, diag,
    out_theta, out_psi,
    weight, land, th, kp, sea, skt, ext, edge, flat, dgx, dg, ocs, quarter, basis, rows_out, north, south, cols_out, east, west,
    tiles, fold, fold_edge, parts,
    in_sem, main_send, main_recv, edge_send, edge_recv, fold_send, fold_low_send, fold_far_send, fold_recv,
    diag_send, diag_recv, halo_send, halo_recv, red_send, red_recv, ready,
):
    levels, cy, cx = th.shape
    ny, nx = cy * nlat, cx * nlon
    strip = cx // nlat
    wide = strip + 2 * HALO
    by, bx = land.shape
    total = nlon * nlat
    i = lax.axis_index("lon")
    j = lax.axis_index("lat")
    t = i * nlat + j
    top = j == nlat - 1
    ends = jnp.logical_or(j == 0, top)

    def remote(src, dst, send, recv, lon, lat):
        return pltpu.make_async_remote_copy(
            src_ref=src, dst_ref=dst, send_sem=send, recv_sem=recv,
            device_id=(lon, lat), device_id_type=MESH,
        )

    def lon_of(value):
        return lax.rem(value + 2 * nlon, nlon)

    def lat_of(value):
        return lax.rem(value + 2 * nlat, nlat)

    def whole(ref, sem):
        return pltpu.make_async_copy(ref, ref, sem)

    def greet(lon, lat):
        pl.semaphore_signal(barrier, inc=1, device_id=(lon, lat), device_id_type=MESH)

    chunk = levels // 4
    loads = [
        pltpu.make_async_copy(theta.at[pl.ds(q * chunk, chunk)], th.at[pl.ds(q * chunk, chunk)], in_sem.at[q])
        for q in range(4)
    ]
    load_kappa = pltpu.make_async_copy(kappa, kp, in_sem.at[4])
    load_diag = pltpu.make_async_copy(diag, flat, in_sem.at[5])
    load_weight = pltpu.make_async_copy(weight_in, weight, in_sem.at[6])
    load_land = pltpu.make_async_copy(land_in, land, in_sem.at[7])
    load_kappa.start()
    load_weight.start()
    for copy in loads:
        copy.start()
    load_diag.start()
    load_land.start()
    ext[:, :, 0:HALO, :] = jnp.zeros((nlat + 1, 2, HALO, cy), F32)
    ext[:, :, HALO + strip:, :] = jnp.zeros((nlat + 1, 2, HALO, cy), F32)
    edge[...] = jnp.zeros_like(edge)
    dgx[:, 0:HALO, :] = jnp.zeros((nlat + 1, HALO, cy), F32)
    dgx[:, HALO + strip:, :] = jnp.zeros((nlat + 1, HALO, cy), F32)


    barrier = pltpu.get_barrier_semaphore()
    for d in range(1, nlat):
        greet(i, lax.rem(j + d, nlat))
    for d in range(1, nlon):
        greet(lax.rem(i + d, nlon), j)
    greet(nlon - 1 - i, nlat - 1)
    for shift in (1, 0, -1):
        other = lax.rem(total - 1 - t + shift + total, total)

        @pl.when(other != t)
        def _():
            greet(other // nlat, lax.rem(other, nlat))

    @pl.when(j == 0)
    def _():
        for lat in range(nlat):
            greet(lon_of(i - 1), lat)
        greet(lon_of(nlon - i), nlat - 1)

    @pl.when(top)
    def _():
        for lat in range(nlat):
            greet(lon_of(i + 1), lat)

    skt[:, 0:HALO, :] = jnp.zeros((2, HALO, cy), F32)
    skt[:, HALO + cx:, :] = jnp.zeros((2, HALO, cy), F32)
    load_kappa.wait()
    skt[1, HALO:HALO + cx, :] = kp[...].T
    load_weight.wait()
    column = jnp.zeros((cy, cx), F32)
    for q in range(4):
        loads[q].wait()
        for k in range(q * chunk, (q + 1) * chunk):
            column = column + weight[k] * th[k]
    skt[0, HALO:HALO + cx, :] = column.T

    @pl.when(top)
    def _():
        last_sums = column[cy - 8:, :]
        last_kappa = kp[cy - 8:, :]
        lanes8 = iota((8, LANES), 1)
        for m in range(nlat):
            start = strip * (nlat - 1 - m) - HALO
            tiles[m] = jnp.where(
                lanes8 < wide,
                pltpu.roll(last_sums, (-start) % cx, 1)[:, 0:LANES],
                pltpu.roll(last_kappa, (wide - start) % cx, 1)[:, 0:LANES],
            )

    rows_out[0] = th[:, 0, :]
    rows_out[1] = th[:, cy - 1, :]
    load_diag.wait()
    for c in range(nlat):
        dgx[c, HALO:HALO + strip, :] = flat[:, c * cy:(c + 1) * cy]

    own_folds = [lax.rem(total - 1 - t + shift + total, total) == t for shift in (1, -1)]
    awaited = nlat + nlon + 3 + jnp.where(top, nlat + 1, 0)
    for own in own_folds:
        awaited = awaited - jnp.where(own, 1, 0)
    pl.semaphore_wait(barrier, awaited)
    for d in range(1, nlon):
        pl.semaphore_signal(
            ready, inc=1, device_id=(lax.rem(i + d, nlon), j), device_id_type=MESH
        )

    to_south = remote(rows_out.at[0], north, halo_send.at[0], halo_recv.at[0], i, lat_of(j - 1))
    to_north = remote(rows_out.at[1], south, halo_send.at[1], halo_recv.at[1], i, lat_of(j + 1))
    to_fold = remote(rows_out.at[1], north, halo_send.at[1], halo_recv.at[0], nlon - 1 - i, j)

    @pl.when(j > 0)
    def _():
        to_south.start()

    @pl.when(jnp.logical_not(top))
    def _():
        to_north.start()

    @pl.when(top)
    def _():
        to_fold.start()

    low_row = HALO - REACH
    span = strip + 2 * REACH

    def block_rows(m):
        return skt.at[:, pl.ds(m * strip + low_row, span), :]

    own_slot = ext.at[j, :, low_row:low_row + span, :]

    def main_copy(d):
        m = lax.rem(j + d, nlat)
        return remote(block_rows(m), own_slot, main_send, main_recv, i, m)

    for d in range(1, nlat):
        main_copy(d).start()
    pltpu.make_async_copy(block_rows(j), own_slot, main_recv).start()
    first_rows = skt.at[:, HALO:HALO + REACH, :]
    last_rows = skt.at[:, HALO + cx - REACH:HALO + cx, :]
    left_edge = remote(
        first_rows, edge.at[j, :, 0:REACH, :], edge_send.at[0], edge_recv, lon_of(i - 1), nlat - 1
    )
    right_edge = remote(
        last_rows, edge.at[j, :, low_row:HALO, :], edge_send.at[1], edge_recv, lon_of(i + 1), 0
    )
    left_edge.start()
    right_edge.start()

    def fold_copy(m):
        return remote(tiles.at[m], fold, fold_send, fold_recv.at[0], nlon - 1 - i, m)

    far_lon = lon_of(nlon - 2 - i)
    far_self = far_lon == i
    fold_far = remote(
        tiles.at[nlat - 1], fold_edge, fold_far_send, fold_recv.at[1], far_lon, nlat - 1
    )
    fold_far_own = pltpu.make_async_copy(tiles.at[nlat - 1], fold_edge, fold_recv.at[1])
    fold_low = remote(tiles.at[0], fold_edge, fold_low_send, fold_recv.at[1], lon_of(nlon - i), 0)

    @pl.when(top)
    def _():
        for m in range(nlat):
            fold_copy(m).start()
        fold_low.start()

        @pl.when(far_self)
        def _():
            fold_far_own.start()

        @pl.when(jnp.logical_not(far_self))
        def _():
            fold_far.start()

    after, before = lax.rem(t + 1, total), lax.rem(t + total - 1, total)
    depth = BASIS - 2
    own_low = slice(HALO, HALO + depth)
    own_high = slice(HALO + strip - depth, HALO + strip)
    halo_low = slice(HALO - depth, HALO)
    halo_high = slice(HALO + strip, HALO + strip + depth)
    diag_up = remote(
        dgx.at[0:nlat, own_high, :], dgx.at[0:nlat, halo_low, :], diag_send.at[0], diag_recv.at[0],
        after // nlat, lax.rem(after, nlat),
    )
    diag_down = remote(
        dgx.at[0:nlat, own_low, :], dgx.at[0:nlat, halo_high, :], diag_send.at[1], diag_recv.at[1],
        before // nlat, lax.rem(before, nlat),
    )
    diag_up.start()
    diag_down.start()
    middle = slice(HALO, HALO + strip)
    diag_fold = remote(
        dgx.at[nlat - 1, middle, :], dgx.at[nlat, middle, :], diag_send.at[2], diag_recv.at[2],
        nlon - 1 - i, nlat - 1 - j,
    )
    diag_fold.start()
    sides = []
    for n, (shift, src, dst) in enumerate(((1, own_low, halo_high), (-1, own_high, halo_low))):
        other = lax.rem(total - 1 - t + shift + total, total)
        src_ref, dst_ref = dgx.at[nlat - 1, src, :], dgx.at[nlat, dst, :]
        sides.append((
            remote(
                src_ref, dst_ref, diag_send.at[3 + n], diag_recv.at[3 + n], other // nlat, lax.rem(other, nlat)
            ),
            pltpu.make_async_copy(src_ref, dst_ref, diag_recv.at[3 + n]),
            own_folds[n],
        ))
    for far, near, own in sides:
        @pl.when(own)
        def _():
            near.start()

        @pl.when(jnp.logical_not(own))
        def _():
            far.start()

    lane = iota((cy, LANES), 1)
    packed = jnp.zeros((cy, LANES), F32)
    for k in range(levels):
        packed = jnp.where(lane == k, pltpu.roll(th[k, :, 0:LANES], k, 1), packed)
        packed = jnp.where(
            lane == levels + k, pltpu.roll(th[k, :, cx - LANES:cx], levels + k + 1, 1), packed
        )
    cols_out[...] = packed
    to_west = remote(cols_out, east, halo_send.at[2], halo_recv.at[2], lon_of(i - 1), j)
    to_east = remote(cols_out, west, halo_send.at[3], halo_recv.at[3], lon_of(i + 1), j)
    to_west.start()
    to_east.start()

    basis[:, :, 0:PAD, :] = jnp.zeros((BASIS, nlat + 1, PAD, cy), F32)
    tail = PAD + strip + 2 * INNER
    basis[:, :, tail:, :] = jnp.zeros((BASIS, nlat + 1, PAD, cy), F32)

    load_land.wait()
    table = land[...].astype(F32).astype(BF16)
    row_block = (j * cy + iota((cy, by), 0)) >> 5
    on_rows = bdot(hot(row_block == iota((cy, by), 1)), table).astype(BF16)
    col_block = (i * cx + iota((bx, cx), 1)) >> 5
    cols_hot = hot(col_block == iota((bx, cx), 0))
    ocean = bdot(on_rows, cols_hot)
    west_block = lax.rem(i * (cx // BS) + bx - 1, bx)
    east_block = lax.rem((i + 1) * (cx // BS), bx)
    ocean_west = bdot(on_rows, hot(iota((bx, LANES), 0) == west_block))
    ocean_east = bdot(on_rows, hot(iota((bx, LANES), 0) == east_block))
    edge_row = iota((8, by), 0)
    edge_col = iota((8, by), 1)
    south_hot = hot(jnp.logical_and(edge_row == 0, edge_col == j * (cy // BS) - 1))
    north_block = jnp.where(top, by - 1, (j + 1) * (cy // BS))
    north_hot = hot(jnp.logical_and(edge_row == 0, edge_col == north_block))
    north_cols = jnp.where(top, bx - 1 - col_block, col_block)
    ocean_south = bdot(bdot(south_hot, table).astype(BF16), cols_hot)[0:1]
    ocean_north = bdot(
        bdot(north_hot, table).astype(BF16), hot(north_cols == iota((bx, cx), 0))
    )[0:1]

    strip_x = (strip * t - HALO + nx + iota((wide, bx), 0)) % nx >> 5
    strip_hot = hot(strip_x == iota((wide, bx), 1))
    on_cols = ndot(strip_hot, table).astype(BF16)
    ocs[:, 0:ny] = bdot(on_cols, hot((iota((by, ny), 1) >> 5) == iota((by, ny), 0)))
    mirror_hot = hot((bx - 1 - strip_x) == iota((wide, bx), 1))
    on_mirror = ndot(mirror_hot, table).astype(BF16)
    keep = jnp.logical_and(iota((by, LANES), 0) == by - 1, iota((by, LANES), 1) < 8)
    ocs[:, ny:ny + LANES] = bdot(on_mirror, hot(keep))

    diag_up.wait_recv()
    diag_down.wait_recv()
    diag_fold.wait_recv()
    for far, near, own in sides:
        far.wait_recv()
    for c in range(nlat):
        dg[:, c * cy:(c + 1) * cy] = dgx[c]
    dg[:, ny:] = flip_rows(flip_lanes(dgx[nlat]), (wide,))
    dg[...] = ocs[...] * ((dg[...] - 1.0) * 0.25)
    quarter[...] = ocs[...] * 0.25

    whole(ext.at[0:nlat, :, low_row:low_row + span, :], main_recv).wait()
    whole(fold, fold_recv.at[0]).wait()

    @pl.when(ends)
    def _():
        whole(edge.at[:, :, 0:REACH, :], edge_recv).wait()
        whole(fold_edge, fold_recv.at[1]).wait()
        spot = iota((8, LANES), 1) % wide
        outer = jnp.logical_or(
            jnp.logical_and(top, spot < HALO), jnp.logical_and(j == 0, spot >= wide - HALO)
        )
        fold[...] = jnp.where(outer, fold_edge[...], fold[...])

    row = iota((2 * wide, LANES), 0)
    source = jnp.where(row < wide, wide - 1 - row, 3 * wide - 1 - row)
    pick = hot(source == iota((2 * wide, LANES), 1))
    turn = hot(iota((LANES, 8), 0) == 7 - iota((LANES, 8), 1))
    folded = [ndot(pick, bdot(turn, piece).astype(BF16)) for piece in pieces(fold[...])]
    folded = (folded[0] + folded[1]) + folded[2]
    ext[nlat, 0] = folded[0:wide]
    ext[nlat, 1] = folded[wide:]

    @pl.when(j == 0)
    def _():
        ext[0:nlat, :, 0:HALO, :] = edge[...]

    @pl.when(top)
    def _():
        ext[0:nlat, :, HALO + strip:, :] = edge[...]

    def lanes_of(c):
        return slice(c * LANES, (c + 1) * LANES)

    held = basis.at[BASIS - 1]
    shift = HALO - INNER
    own_start = PAD + INNER
    bottom, ceiling = PAD, PAD + strip + 2 * INNER
    for c in range(nlat + 1):
        rows = slice(shift - 1, wide - shift + 1)
        held[c, bottom - 1:ceiling + 1, :] = ocs[rows, lanes_of(c)] * ext[c, 0, rows, :]

    def store_forcing(c, value, beside):
        rows = slice(shift, wide - shift)
        rate = ocs[rows, lanes_of(c)] * ext[c, 1, rows, :]
        basis[0, c, bottom:ceiling, :] = value + rate * (beside - 4.0 * value)

    stencil(held, store_forcing, bottom, ceiling)
    for step in range(BASIS - 1):
        low, high = (bottom, ceiling) if step < BASIS - 2 else (own_start, own_start + strip)

        def store_next(c, value, beside):
            lanes, rows = lanes_of(c), slice(low - PAD + shift, high - PAD + shift)
            basis[step + 1, c, low:high, :] = dg[rows, lanes] * value - quarter[rows, lanes] * beside

        stencil(basis.at[step], store_next, low, high)

    zero = jnp.zeros((8, LANES), F32)

    def accumulate(c, carry):
        sums = list(carry)
        for h in range(strip // 8):
            start = own_start + 8 * h
            values = [basis[b, c, start:start + 8, :] for b in range(BASIS)]
            split = [halves(value) for value in values]
            for n, (a, b) in enumerate(PAIRS):
                (ah, al), (bh, bl) = split[a], split[b]
                e = ah * bl + al * values[b]
                s, f = quick(sums[2 * n], ah * bh)
                sums[2 * n], sums[2 * n + 1] = s, sums[2 * n + 1] + (e + f)
        return tuple(sums)

    sums = lax.fori_loop(0, ny // LANES, accumulate, (zero,) * (2 * len(PAIRS)))
    place = iota((SLOTS, LANES), 0)
    high = jnp.zeros((SLOTS, LANES), F32)
    low = jnp.zeros((SLOTS, LANES), F32)
    for n in range(len(PAIRS)):
        h, l = sums[2 * n], sums[2 * n + 1]
        for shift in (4, 2, 1):
            h, e = two_sum(h, pltpu.roll(h, shift, 0))
            l = l + pltpu.roll(l, shift, 0) + e
        high = jnp.where(place == n, h[0:1], high)
        low = jnp.where(place == n, l[0:1], low)
    shift = LANES // 2
    while shift:
        high, e = two_sum(high, pltpu.roll(high, shift, 1))
        low = low + pltpu.roll(low, shift, 1) + e
        shift //= 2
    spot = iota((SLOTS, LANES), 1)
    packed = jnp.where(spot == place, high, jnp.where(spot == place + SLOTS, low, 0.0))
    message = jnp.sum(packed, axis=0, keepdims=True)

    parts[pl.ds(t, 1), :] = message
    own_part = parts.at[pl.ds(t, 1), :]
    sizes = (nlon // 2, 2, nlat // 4, 4)
    offsets = [
        (a, b, c, d)
        for a in range(sizes[0]) for b in range(sizes[1]) for c in range(sizes[2]) for d in range(sizes[3])
    ]

    def hops(offset):
        return sum(min(o, n - o) for o, n in zip(offset, sizes) if n > 2 or o) - 0.5 * offset[1]

    offsets = sorted(offsets[1:], key=hops, reverse=True)
    place_of = (i // 2, lax.rem(i, 2), j // 4, lax.rem(j, 4))
    moved = [
        [lax.rem(place_of[n] + o, sizes[n]) * scale for o in range(sizes[n])]
        for n, scale in enumerate((2, 1, 4, 1))
    ]
    pl.semaphore_wait(ready, nlon - 1)
    for a, b, c, d in offsets:
        remote(own_part, own_part, red_send, red_recv, moved[0][a] + moved[1][b], moved[2][c] + moved[3][d]).start()

    to_south.wait_recv()
    to_west.wait_recv()
    to_east.wait_recv()

    @pl.when(j > 0)
    def _():
        to_north.wait_recv()

    @pl.when(j == 0)
    def _():
        south[...] = jnp.zeros_like(south)

    @pl.when(top)
    def _():
        north[...] = flip_lanes(north[...])

    west[...] = west[...] * ocean_west
    east[...] = east[...] * ocean_east
    kp[...] = ocean * kp[...]
    sea[...] = ocean
    north[...] = ocean_north * north[...]
    south[...] = ocean_south * south[...]
    part = 32
    tile_row, tile_lane = iota((part, LANES), 0), iota((part, LANES), 1)
    first_row, last_row = tile_row == 0, tile_row == part - 1
    first_lane, last_lane = tile_lane == 0, tile_lane == LANES - 1
    count = cy // part
    columns = cx // LANES

    def update(k, _):
        from_south, from_north = south[pl.ds(k, 1), :], north[pl.ds(k, 1), :]

        def load(c, n):
            rows, lanes = slice(c * part, (c + 1) * part), slice(n * LANES, (n + 1) * LANES)
            return sea[rows, lanes] * th[k, rows, lanes]

        def across(n, vector):
            return jnp.broadcast_to(vector[:, n * LANES:(n + 1) * LANES], (part, LANES))

        value = [load(0, n) for n in range(columns)]
        before = [across(n, from_south) for n in range(columns)]
        up = [pltpu.roll(v, part - 1, 0) for v in value]
        for c in range(count):
            rows = slice(c * part, (c + 1) * part)
            if c + 1 < count:
                following = [load(c + 1, n) for n in range(columns)]
                up_next = [pltpu.roll(v, part - 1, 0) for v in following]
            else:
                following, up_next = None, [across(n, from_north) for n in range(columns)]
            down = [pltpu.roll(v, 1, 0) for v in value]
            right = [pltpu.roll(west[rows, :], LANES - levels - k, 1)] + [pltpu.roll(v, 1, 1) for v in value]
            left = [pltpu.roll(v, LANES - 1, 1) for v in value] + [pltpu.roll(east[rows, :], LANES - 1 - k, 1)]
            for n in range(columns):
                lanes = slice(n * LANES, (n + 1) * LANES)
                beside = jnp.where(first_row, before[n], down[n]) + jnp.where(last_row, up_next[n], up[n])
                beside = beside + jnp.where(first_lane, right[n], right[n + 1])
                beside = beside + jnp.where(last_lane, left[n + 1], left[n])
                out_theta[k, rows, lanes] = th[k, rows, lanes] + kp[rows, lanes] * (beside - 4.0 * value[n])
            value, before, up = following, down, up_next
        return 0

    lax.fori_loop(0, levels, update, 0)
    whole(parts.at[pl.ds(0, total - 1), :], red_recv).wait()
    value = parts[...]
    error = jnp.zeros_like(value)
    half = total // 2
    while half >= 8:
        value, e = two_sum(value[:half], value[half:])
        error = error[:half] + error[half:] + e
        half //= 2
    for shift in (4, 2, 1):
        value, e = two_sum(value, pltpu.roll(value, shift, 0))
        error = error + pltpu.roll(error, shift, 0) + e
    lane = iota((1, LANES), 1)
    error = jnp.where(
        jnp.logical_and(lane >= SLOTS, lane < 2 * SLOTS), pltpu.roll(error[0:1], SLOTS, 1), 0.0
    )
    message = value[0:1] + error
    high, low = quick(message, pltpu.roll(message, LANES - SLOTS, 1))

    gram = {}
    for n, (a, b) in enumerate(PAIRS):
        gram[a, b] = gram[b, a] = tuple(
            jnp.broadcast_to(x[:, n:n + 1], (1, LANES)) for x in (high, low)
        )
    size = BASIS - 1

    def scaled(x, factor):
        return x[0] * factor, x[1] * factor

    matrix = [
        [
            df_add(
                scaled(gram[a, b + 1], 4.0),
                df_add(scaled(gram[a, b], 4.0), gram[a, b]),
            )
            for b in range(size)
        ]
        for a in range(size)
    ]
    right = [gram[0, a] for a in range(size)]
    for p in range(size):
        for a in range(p + 1, size):
            factor = df_div(matrix[a][p], matrix[p][p])
            for b in range(p + 1, size):
                matrix[a][b] = df_sub(matrix[a][b], df_mul(factor, matrix[p][b]))
            right[a] = df_sub(right[a], df_mul(factor, right[p]))
    answer = [None] * size
    for p in reversed(range(size)):
        value = right[p]
        for b in range(p + 1, size):
            value = df_sub(value, df_mul(matrix[p][b], answer[b]))
        answer[p] = df_div(value, matrix[p][p])
    spread = [jnp.broadcast_to(x[0], (strip, LANES)) for x in answer]

    own_rows = slice(own_start, own_start + strip)

    def combine(c, _):
        lanes = pl.ds(pl.multiple_of(c * LANES, LANES), LANES)
        value = spread[size - 1] * basis[size - 1, c, own_rows, :]
        for b in reversed(range(size - 1)):
            value = value + spread[b] * basis[b, c, own_rows, :]
        out_psi[:, lanes] = value
        return 0

    lax.fori_loop(0, ny // LANES, combine, 0)

    whole(ext.at[0:nlat - 1, :, low_row:low_row + span, :], main_send).wait()
    left_edge.wait_send()
    right_edge.wait_send()
    diag_up.wait_send()
    diag_down.wait_send()
    diag_fold.wait_send()
    for far, near, own in sides:
        @pl.when(jnp.logical_not(own))
        def _():
            far.wait_send()

    @pl.when(top)
    def _():
        whole(tiles, fold_send).wait()
        fold_low.wait_send()

        @pl.when(jnp.logical_not(far_self))
        def _():
            fold_far.wait_send()

    @pl.when(j > 0)
    def _():
        to_south.wait_send()

    to_north.wait_send()
    to_west.wait_send()
    to_east.wait_send()
    whole(parts.at[pl.ds(0, total - 1), :], red_send).wait()


def per_device(nlon, nlat, theta, kappa, layer_weight, diag, land_blocks):
    levels, cy, cx = theta.shape
    strip, ny = diag.shape
    wide = strip + 2 * HALO
    vmem = pl.BlockSpec(memory_space=pltpu.VMEM)
    hbm = pl.BlockSpec(memory_space=pltpu.HBM)
    dma = pltpu.SemaphoreType.DMA
    operands = (layer_weight, land_blocks, theta, kappa, diag)
    return pl.pallas_call(
        functools.partial(kernel, nlon, nlat),
        out_shape=(
            jax.ShapeDtypeStruct(theta.shape, F32),
            jax.ShapeDtypeStruct(diag.shape, F32),
        ),
        in_specs=[hbm] * 5,
        out_specs=(vmem, vmem),
        scratch_shapes=[
            pltpu.SMEM(layer_weight.shape, F32),
            pltpu.VMEM(land_blocks.shape, jnp.int32),
            pltpu.VMEM((levels, cy, cx), F32),
            pltpu.VMEM((cy, cx), F32),
            pltpu.VMEM((cy, cx), F32),
            pltpu.VMEM((2, cx + 2 * HALO, cy), F32),
            pltpu.VMEM((nlat + 1, 2, wide, cy), F32),
            pltpu.VMEM((nlat, 2, HALO, cy), F32),
            pltpu.VMEM((strip, ny), F32),
            pltpu.VMEM((nlat + 1, wide, cy), F32),
            pltpu.VMEM((wide, ny + LANES), F32),
            pltpu.VMEM((wide, ny + LANES), F32),
            pltpu.VMEM((wide, ny + LANES), F32),
            pltpu.VMEM((BASIS, nlat + 1, strip + 2 * INNER + 2 * PAD, cy), F32),
            pltpu.VMEM((2, levels, cx), F32),
            pltpu.VMEM((levels, cx), F32),
            pltpu.VMEM((levels, cx), F32),
            pltpu.VMEM((cy, LANES), F32),
            pltpu.VMEM((cy, LANES), F32),
            pltpu.VMEM((cy, LANES), F32),
            pltpu.VMEM((nlat, 8, LANES), F32),
            pltpu.VMEM((8, LANES), F32),
            pltpu.VMEM((8, LANES), F32),
            pltpu.VMEM((nlon * nlat, LANES), F32),
            dma((8,)),
            dma,
            dma,
            dma((2,)),
            dma,
            dma,
            dma,
            dma,
            dma((2,)),
            dma((5,)),
            dma((5,)),
            dma((4,)),
            dma((4,)),
            dma,
            dma,
            pltpu.SemaphoreType.REGULAR,
        ],
        compiler_params=pltpu.CompilerParams(
            collective_id=0, has_side_effects=True, vmem_limit_bytes=32 << 20
        ),
        name="ocean_step",
    )(*[pltpu.with_memory_space_constraint(x, pltpu.HBM) for x in operands])


def solution(mesh):
    placed = (P(None, "lat", "lon"), P("lat", "lon"), P(), P(("lon", "lat"), None), P())
    return jax.shard_map(
        functools.partial(per_device, mesh.shape["lon"], mesh.shape["lat"]),
        mesh=mesh,
        in_specs=placed,
        out_specs=(P(None, "lat", "lon"), P(("lon", "lat"), None)),
        check_vma=False,
    )
```

```python
import functools

import jax
import jax.numpy as jnp
from jax import lax
from jax.experimental import pallas as pl
from jax.experimental.pallas import tpu as pltpu
from jax.sharding import PartitionSpec as P

MESH = pl.DeviceIdType.MESH
BS = 32
HALO = 8
REACH = 5
PAD = 8
INNER = 4
LANES = 128
F32 = jnp.float32
BF16 = jnp.bfloat16
BASIS = 5
PAIRS = [(a, b) for a in range(BASIS) for b in range(a, BASIS) if a < BASIS - 1]
SLOTS = 16


def iota(shape, axis):
    return lax.broadcasted_iota(jnp.int32, shape, axis)


def hot(condition):
    return jnp.where(condition, 1.0, 0.0).astype(BF16)


def bdot(left, right):
    return jnp.dot(left, right, preferred_element_type=F32)


def ndot(left, right):
    return lax.dot_general(left, right, (((1,), (1,)), ((), ())), preferred_element_type=F32)


def pieces(value):
    first = value.astype(BF16)
    rest = value - first.astype(F32)
    second = rest.astype(BF16)
    third = (rest - second.astype(F32)).astype(BF16)
    return [first, second, third]


def flip_lanes(value):
    width = value.shape[1]
    turn = hot(iota((width, width), 0) + iota((width, width), 1) == width - 1)
    parts = [bdot(piece, turn) for piece in pieces(value)]
    return (parts[0] + parts[1]) + parts[2]


def flip_rows(value, groups):
    count = value.shape[0]
    row = iota((count, count), 0)
    ends, start = jnp.zeros((count, count), jnp.int32), 0
    for size in groups:
        ends = jnp.where(row >= start, 2 * start + size - 1, ends)
        start += size
    turn = hot(row + iota((count, count), 1) == ends)
    parts = [bdot(turn, piece) for piece in pieces(value)]
    return (parts[0] + parts[1]) + parts[2]


def two_sum(a, b):
    s = a + b
    t = s - a
    return s, (a - (s - t)) + (b - t)


def halves(a):
    t = a * 4097.0
    high = t - (t - a)
    return high, a - high


def two_prod(a, b):
    p = a * b
    ah, al = halves(a)
    bh, bl = halves(b)
    return p, ((ah * bh - p) + ah * bl + al * bh) + al * bl


def quick(a, b):
    s = a + b
    return s, b - (s - a)


def df_mul(x, y):
    p, e = two_prod(x[0], y[0])
    return quick(p, e + (x[0] * y[1] + x[1] * y[0]))


def df_add(x, y):
    s, e = two_sum(x[0], y[0])
    return quick(s, e + (x[1] + y[1]))


def df_sub(x, y):
    return df_add(x, (-y[0], -y[1]))


def df_div(x, y):
    first = x[0] / y[0]
    rest = df_sub(x, df_mul(y, (first, jnp.zeros_like(first))))
    second = rest[0] / y[0]
    return quick(first, second)


def stencil(ref, emit, low, high):
    count, _, width = ref.shape
    lane = iota((high - low, width), 1)
    first, last = lane == 0, lane == width - 1

    def load(c, shift=0):
        return ref[c, low + shift:high + shift, :]

    value = load(0)
    before = jnp.zeros_like(value)
    up = pltpu.roll(value, width - 1, 1)
    for c in range(count):
        if c + 1 < count:
            following = load(c + 1)
            up_next = pltpu.roll(following, width - 1, 1)
        else:
            following, up_next = None, up
        down = pltpu.roll(value, 1, 1)
        beside = jnp.where(first, before, down) + jnp.where(last, up_next, up)
        emit(c, value, (beside + load(c, -1)) + load(c, 1))
        value, before, up = following, down, up_next


def kernel(
    nlon, nlat,
    weight_in, land_in, theta, kappa, diag,
    out_theta, out_basis, out_parts,
    weight, land, th, kp, sea, skt, ext, edge, flat, dgx, dg, ocs, quarter, basis, rows_out, north, south, cols_out, east, west,
    tiles, fold, fold_edge, parts,
    in_sem, main_send, main_recv, edge_send, edge_recv, fold_send, fold_low_send, fold_far_send, fold_recv,
    diag_send, diag_recv, halo_send, halo_recv, red_send, red_recv, ready,
):
    levels, cy, cx = th.shape
    ny, nx = cy * nlat, cx * nlon
    strip = cx // nlat
    wide = strip + 2 * HALO
    by, bx = land.shape
    total = nlon * nlat
    i = lax.axis_index("lon")
    j = lax.axis_index("lat")
    t = i * nlat + j
    top = j == nlat - 1
    ends = jnp.logical_or(j == 0, top)

    def remote(src, dst, send, recv, lon, lat):
        return pltpu.make_async_remote_copy(
            src_ref=src, dst_ref=dst, send_sem=send, recv_sem=recv,
            device_id=(lon, lat), device_id_type=MESH,
        )

    def lon_of(value):
        return lax.rem(value + 2 * nlon, nlon)

    def lat_of(value):
        return lax.rem(value + 2 * nlat, nlat)

    def whole(ref, sem):
        return pltpu.make_async_copy(ref, ref, sem)

    def greet(lon, lat):
        pl.semaphore_signal(barrier, inc=1, device_id=(lon, lat), device_id_type=MESH)

    def ring(value, size):
        return min(value, size - value)

    lat_order = sorted(range(1, nlat), key=lambda d: -ring(d // 4, nlat // 4) - ring(d % 4, 4))
    lon_order = sorted(range(1, nlon), key=lambda d: -ring(d // 2, nlon // 2) - 0.5 * (d % 2))

    chunk = levels // 4
    loads = [
        pltpu.make_async_copy(theta.at[pl.ds(q * chunk, chunk)], th.at[pl.ds(q * chunk, chunk)], in_sem.at[q])
        for q in range(4)
    ]
    load_kappa = pltpu.make_async_copy(kappa, kp, in_sem.at[4])
    load_diag = pltpu.make_async_copy(diag, flat, in_sem.at[5])
    load_weight = pltpu.make_async_copy(weight_in, weight, in_sem.at[6])
    load_land = pltpu.make_async_copy(land_in, land, in_sem.at[7])
    load_kappa.start()
    load_weight.start()
    for copy in loads:
        copy.start()
    load_diag.start()
    load_land.start()
    ext[:, :, 0:HALO, :] = jnp.zeros((nlat + 1, 2, HALO, cy), F32)
    ext[:, :, HALO + strip:, :] = jnp.zeros((nlat + 1, 2, HALO, cy), F32)
    edge[...] = jnp.zeros_like(edge)
    dgx[:, 0:HALO, :] = jnp.zeros((nlat + 1, HALO, cy), F32)
    dgx[:, HALO + strip:, :] = jnp.zeros((nlat + 1, HALO, cy), F32)


    barrier = pltpu.get_barrier_semaphore()
    for d in lat_order:
        greet(i, lax.rem(j + d, nlat))
    for d in lon_order:
        greet(lax.rem(i + d, nlon), j)
    greet(nlon - 1 - i, nlat - 1)
    for shift in (1, 0, -1):
        other = lax.rem(total - 1 - t + shift + total, total)

        @pl.when(other != t)
        def _():
            greet(other // nlat, lax.rem(other, nlat))

    @pl.when(j == 0)
    def _():
        for lat in range(nlat):
            greet(lon_of(i - 1), lat)
        greet(lon_of(nlon - i), nlat - 1)

    @pl.when(top)
    def _():
        for lat in range(nlat):
            greet(lon_of(i + 1), lat)

    skt[:, 0:HALO, :] = jnp.zeros((2, HALO, cy), F32)
    skt[:, HALO + cx:, :] = jnp.zeros((2, HALO, cy), F32)
    load_kappa.wait()
    skt[1, HALO:HALO + cx, :] = kp[...].T
    load_weight.wait()
    column = jnp.zeros((cy, cx), F32)
    for q in range(4):
        loads[q].wait()
        for k in range(q * chunk, (q + 1) * chunk):
            column = column + weight[k] * th[k]
    skt[0, HALO:HALO + cx, :] = column.T

    @pl.when(top)
    def _():
        last_sums = column[cy - 8:, :]
        last_kappa = kp[cy - 8:, :]
        lanes8 = iota((8, LANES), 1)
        for m in range(nlat):
            start = strip * (nlat - 1 - m) - HALO
            tiles[m] = jnp.where(
                lanes8 < wide,
                pltpu.roll(last_sums, (-start) % cx, 1)[:, 0:LANES],
                pltpu.roll(last_kappa, (wide - start) % cx, 1)[:, 0:LANES],
            )

    load_diag.wait()
    for c in range(nlat):
        dgx[c, HALO:HALO + strip, :] = flat[:, c * cy:(c + 1) * cy]

    own_folds = [lax.rem(total - 1 - t + shift + total, total) == t for shift in (1, -1)]
    awaited = nlat + nlon + 3 + jnp.where(top, nlat + 1, 0)
    for own in own_folds:
        awaited = awaited - jnp.where(own, 1, 0)
    pl.semaphore_wait(barrier, awaited)
    for d in range(1, nlon):
        pl.semaphore_signal(
            ready, inc=1, device_id=(lax.rem(i + d, nlon), j), device_id_type=MESH
        )

    low_row = HALO - REACH
    span = strip + 2 * REACH

    def block_rows(m):
        return skt.at[:, pl.ds(m * strip + low_row, span), :]

    own_slot = ext.at[j, :, low_row:low_row + span, :]

    def main_copy(d):
        m = lax.rem(j + d, nlat)
        return remote(block_rows(m), own_slot, main_send, main_recv, i, m)

    for d in lat_order:
        main_copy(d).start()
    pltpu.make_async_copy(block_rows(j), own_slot, main_recv).start()
    first_rows = skt.at[:, HALO:HALO + REACH, :]
    last_rows = skt.at[:, HALO + cx - REACH:HALO + cx, :]
    left_edge = remote(
        first_rows, edge.at[j, :, 0:REACH, :], edge_send.at[0], edge_recv, lon_of(i - 1), nlat - 1
    )
    right_edge = remote(
        last_rows, edge.at[j, :, low_row:HALO, :], edge_send.at[1], edge_recv, lon_of(i + 1), 0
    )
    left_edge.start()
    right_edge.start()

    def fold_copy(m):
        return remote(tiles.at[m], fold, fold_send, fold_recv.at[0], nlon - 1 - i, m)

    far_lon = lon_of(nlon - 2 - i)
    far_self = far_lon == i
    fold_far = remote(
        tiles.at[nlat - 1], fold_edge, fold_far_send, fold_recv.at[1], far_lon, nlat - 1
    )
    fold_far_own = pltpu.make_async_copy(tiles.at[nlat - 1], fold_edge, fold_recv.at[1])
    fold_low = remote(tiles.at[0], fold_edge, fold_low_send, fold_recv.at[1], lon_of(nlon - i), 0)

    @pl.when(top)
    def _():
        for m in range(nlat):
            fold_copy(m).start()
        fold_low.start()

        @pl.when(far_self)
        def _():
            fold_far_own.start()

        @pl.when(jnp.logical_not(far_self))
        def _():
            fold_far.start()

    after, before = lax.rem(t + 1, total), lax.rem(t + total - 1, total)
    depth = BASIS - 2
    own_low = slice(HALO, HALO + depth)
    own_high = slice(HALO + strip - depth, HALO + strip)
    halo_low = slice(HALO - depth, HALO)
    halo_high = slice(HALO + strip, HALO + strip + depth)
    diag_up = remote(
        dgx.at[0:nlat, own_high, :], dgx.at[0:nlat, halo_low, :], diag_send.at[0], diag_recv.at[0],
        after // nlat, lax.rem(after, nlat),
    )
    diag_down = remote(
        dgx.at[0:nlat, own_low, :], dgx.at[0:nlat, halo_high, :], diag_send.at[1], diag_recv.at[1],
        before // nlat, lax.rem(before, nlat),
    )
    diag_up.start()
    diag_down.start()
    middle = slice(HALO, HALO + strip)
    diag_fold = remote(
        dgx.at[nlat - 1, middle, :], dgx.at[nlat, middle, :], diag_send.at[2], diag_recv.at[2],
        nlon - 1 - i, nlat - 1 - j,
    )
    diag_fold.start()
    sides = []
    for n, (shift, src, dst) in enumerate(((1, own_low, halo_high), (-1, own_high, halo_low))):
        other = lax.rem(total - 1 - t + shift + total, total)
        src_ref, dst_ref = dgx.at[nlat - 1, src, :], dgx.at[nlat, dst, :]
        sides.append((
            remote(
                src_ref, dst_ref, diag_send.at[3 + n], diag_recv.at[3 + n], other // nlat, lax.rem(other, nlat)
            ),
            pltpu.make_async_copy(src_ref, dst_ref, diag_recv.at[3 + n]),
            own_folds[n],
        ))
    for far, near, own in sides:
        @pl.when(own)
        def _():
            near.start()

        @pl.when(jnp.logical_not(own))
        def _():
            far.start()

    rows_out[0] = th[:, 0, :]
    rows_out[1] = th[:, cy - 1, :]
    to_south = remote(rows_out.at[0], north, halo_send.at[0], halo_recv.at[0], i, lat_of(j - 1))
    to_north = remote(rows_out.at[1], south, halo_send.at[1], halo_recv.at[1], i, lat_of(j + 1))
    to_fold = remote(rows_out.at[1], north, halo_send.at[1], halo_recv.at[0], nlon - 1 - i, j)

    @pl.when(j > 0)
    def _():
        to_south.start()

    @pl.when(jnp.logical_not(top))
    def _():
        to_north.start()

    @pl.when(top)
    def _():
        to_fold.start()

    lane = iota((cy, LANES), 1)
    packed = jnp.zeros((cy, LANES), F32)
    for k in range(levels):
        packed = jnp.where(lane == k, pltpu.roll(th[k, :, 0:LANES], k, 1), packed)
        packed = jnp.where(
            lane == levels + k, pltpu.roll(th[k, :, cx - LANES:cx], levels + k + 1, 1), packed
        )
    cols_out[...] = packed
    to_west = remote(cols_out, east, halo_send.at[2], halo_recv.at[2], lon_of(i - 1), j)
    to_east = remote(cols_out, west, halo_send.at[3], halo_recv.at[3], lon_of(i + 1), j)
    to_west.start()
    to_east.start()

    basis[:, :, 0:PAD, :] = jnp.zeros((BASIS, nlat + 1, PAD, cy), F32)
    tail = PAD + strip + 2 * INNER
    basis[:, :, tail:, :] = jnp.zeros((BASIS, nlat + 1, PAD, cy), F32)

    load_land.wait()
    table = land[...].astype(F32).astype(BF16)
    row_block = (j * cy + iota((cy, by), 0)) >> 5
    on_rows = bdot(hot(row_block == iota((cy, by), 1)), table).astype(BF16)
    col_block = (i * cx + iota((bx, cx), 1)) >> 5
    cols_hot = hot(col_block == iota((bx, cx), 0))
    ocean = bdot(on_rows, cols_hot)
    west_block = lax.rem(i * (cx // BS) + bx - 1, bx)
    east_block = lax.rem((i + 1) * (cx // BS), bx)
    ocean_west = bdot(on_rows, hot(iota((bx, LANES), 0) == west_block))
    ocean_east = bdot(on_rows, hot(iota((bx, LANES), 0) == east_block))
    edge_row = iota((8, by), 0)
    edge_col = iota((8, by), 1)
    south_hot = hot(jnp.logical_and(edge_row == 0, edge_col == j * (cy // BS) - 1))
    north_block = jnp.where(top, by - 1, (j + 1) * (cy // BS))
    north_hot = hot(jnp.logical_and(edge_row == 0, edge_col == north_block))
    north_cols = jnp.where(top, bx - 1 - col_block, col_block)
    ocean_south = bdot(bdot(south_hot, table).astype(BF16), cols_hot)[0:1]
    ocean_north = bdot(
        bdot(north_hot, table).astype(BF16), hot(north_cols == iota((bx, cx), 0))
    )[0:1]

    strip_x = (strip * t - HALO + nx + iota((wide, bx), 0)) % nx >> 5
    strip_hot = hot(strip_x == iota((wide, bx), 1))
    on_cols = ndot(strip_hot, table).astype(BF16)
    ocs[:, 0:ny] = bdot(on_cols, hot((iota((by, ny), 1) >> 5) == iota((by, ny), 0)))
    mirror_hot = hot((bx - 1 - strip_x) == iota((wide, bx), 1))
    on_mirror = ndot(mirror_hot, table).astype(BF16)
    keep = jnp.logical_and(iota((by, LANES), 0) == by - 1, iota((by, LANES), 1) < 8)
    ocs[:, ny:ny + LANES] = bdot(on_mirror, hot(keep))

    diag_up.wait_recv()
    diag_down.wait_recv()
    diag_fold.wait_recv()
    for far, near, own in sides:
        far.wait_recv()
    for c in range(nlat):
        dg[:, c * cy:(c + 1) * cy] = dgx[c]
    dg[:, ny:] = flip_rows(flip_lanes(dgx[nlat]), (wide,))
    dg[...] = ocs[...] * ((dg[...] - 1.0) * 0.25)
    quarter[...] = ocs[...] * 0.25

    whole(ext.at[0:nlat, :, low_row:low_row + span, :], main_recv).wait()
    whole(fold, fold_recv.at[0]).wait()

    @pl.when(ends)
    def _():
        whole(edge.at[:, :, 0:REACH, :], edge_recv).wait()
        whole(fold_edge, fold_recv.at[1]).wait()
        spot = iota((8, LANES), 1) % wide
        outer = jnp.logical_or(
            jnp.logical_and(top, spot < HALO), jnp.logical_and(j == 0, spot >= wide - HALO)
        )
        fold[...] = jnp.where(outer, fold_edge[...], fold[...])

    row = iota((2 * wide, LANES), 0)
    source = jnp.where(row < wide, wide - 1 - row, 3 * wide - 1 - row)
    pick = hot(source == iota((2 * wide, LANES), 1))
    turn = hot(iota((LANES, 8), 0) == 7 - iota((LANES, 8), 1))
    folded = [ndot(pick, bdot(turn, piece).astype(BF16)) for piece in pieces(fold[...])]
    folded = (folded[0] + folded[1]) + folded[2]
    ext[nlat, 0] = folded[0:wide]
    ext[nlat, 1] = folded[wide:]

    @pl.when(j == 0)
    def _():
        ext[0:nlat, :, 0:HALO, :] = edge[...]

    @pl.when(top)
    def _():
        ext[0:nlat, :, HALO + strip:, :] = edge[...]

    def lanes_of(c):
        return slice(c * LANES, (c + 1) * LANES)

    held = basis.at[BASIS - 1]
    shift = HALO - INNER
    own_start = PAD + INNER
    bottom, ceiling = PAD, PAD + strip + 2 * INNER
    for c in range(nlat + 1):
        rows = slice(shift - 1, wide - shift + 1)
        held[c, bottom - 1:ceiling + 1, :] = ocs[rows, lanes_of(c)] * ext[c, 0, rows, :]

    def store_forcing(c, value, beside):
        rows = slice(shift, wide - shift)
        rate = ocs[rows, lanes_of(c)] * ext[c, 1, rows, :]
        basis[0, c, bottom:ceiling, :] = value + rate * (beside - 4.0 * value)

    stencil(held, store_forcing, bottom, ceiling)
    for step in range(BASIS - 1):
        low, high = (bottom, ceiling) if step < BASIS - 2 else (own_start, own_start + strip)

        def store_next(c, value, beside):
            lanes, rows = lanes_of(c), slice(low - PAD + shift, high - PAD + shift)
            basis[step + 1, c, low:high, :] = dg[rows, lanes] * value - quarter[rows, lanes] * beside

        stencil(basis.at[step], store_next, low, high)

    zero = jnp.zeros((8, LANES), F32)

    def accumulate(c, carry):
        sums = list(carry)
        for h in range(strip // 8):
            start = own_start + 8 * h
            values = [basis[b, c, start:start + 8, :] for b in range(BASIS)]
            split = [halves(value) for value in values]
            for n, (a, b) in enumerate(PAIRS):
                (ah, al), (bh, bl) = split[a], split[b]
                e = ah * bl + al * values[b]
                s, f = quick(sums[2 * n], ah * bh)
                sums[2 * n], sums[2 * n + 1] = s, sums[2 * n + 1] + (e + f)
        return tuple(sums)

    sums = lax.fori_loop(0, ny // LANES, accumulate, (zero,) * (2 * len(PAIRS)))
    place = iota((SLOTS, LANES), 0)
    high = jnp.zeros((SLOTS, LANES), F32)
    low = jnp.zeros((SLOTS, LANES), F32)
    for n in range(len(PAIRS)):
        h, l = sums[2 * n], sums[2 * n + 1]
        for shift in (4, 2, 1):
            h, e = two_sum(h, pltpu.roll(h, shift, 0))
            l = l + pltpu.roll(l, shift, 0) + e
        high = jnp.where(place == n, h[0:1], high)
        low = jnp.where(place == n, l[0:1], low)
    shift = LANES // 2
    while shift:
        high, e = two_sum(high, pltpu.roll(high, shift, 1))
        low = low + pltpu.roll(low, shift, 1) + e
        shift //= 2
    spot = iota((SLOTS, LANES), 1)
    packed = jnp.where(spot == place, high, jnp.where(spot == place + SLOTS, low, 0.0))
    message = jnp.sum(packed, axis=0, keepdims=True)

    parts[pl.ds(t, 1), :] = message
    own_part = parts.at[pl.ds(t, 1), :]
    sizes = (nlon // 2, 2, nlat // 4, 4)
    offsets = [
        (a, b, c, d)
        for a in range(sizes[0]) for b in range(sizes[1]) for c in range(sizes[2]) for d in range(sizes[3])
    ]

    def hops(offset):
        return sum(min(o, n - o) for o, n in zip(offset, sizes) if n > 2 or o) - 0.5 * offset[1]

    offsets = sorted(offsets[1:], key=hops, reverse=True)
    place_of = (i // 2, lax.rem(i, 2), j // 4, lax.rem(j, 4))
    moved = [
        [lax.rem(place_of[n] + o, sizes[n]) * scale for o in range(sizes[n])]
        for n, scale in enumerate((2, 1, 4, 1))
    ]
    pl.semaphore_wait(ready, nlon - 1)
    for a, b, c, d in offsets:
        remote(own_part, own_part, red_send, red_recv, moved[0][a] + moved[1][b], moved[2][c] + moved[3][d]).start()

    to_south.wait_recv()
    to_west.wait_recv()
    to_east.wait_recv()

    @pl.when(j > 0)
    def _():
        to_north.wait_recv()

    @pl.when(j == 0)
    def _():
        south[...] = jnp.zeros_like(south)

    @pl.when(top)
    def _():
        north[...] = flip_lanes(north[...])

    west[...] = west[...] * ocean_west
    east[...] = east[...] * ocean_east
    kp[...] = ocean * kp[...]
    sea[...] = ocean
    north[...] = ocean_north * north[...]
    south[...] = ocean_south * south[...]
    part = 32
    tile_row, tile_lane = iota((part, LANES), 0), iota((part, LANES), 1)
    first_row, last_row = tile_row == 0, tile_row == part - 1
    first_lane, last_lane = tile_lane == 0, tile_lane == LANES - 1
    count = cy // part
    columns = cx // LANES

    def update(k, _):
        from_south, from_north = south[pl.ds(k, 1), :], north[pl.ds(k, 1), :]

        def load(c, n):
            rows, lanes = slice(c * part, (c + 1) * part), slice(n * LANES, (n + 1) * LANES)
            return sea[rows, lanes] * th[k, rows, lanes]

        def across(n, vector):
            return jnp.broadcast_to(vector[:, n * LANES:(n + 1) * LANES], (part, LANES))

        value = [load(0, n) for n in range(columns)]
        before = [across(n, from_south) for n in range(columns)]
        up = [pltpu.roll(v, part - 1, 0) for v in value]
        for c in range(count):
            rows = slice(c * part, (c + 1) * part)
            if c + 1 < count:
                following = [load(c + 1, n) for n in range(columns)]
                up_next = [pltpu.roll(v, part - 1, 0) for v in following]
            else:
                following, up_next = None, [across(n, from_north) for n in range(columns)]
            down = [pltpu.roll(v, 1, 0) for v in value]
            right = [pltpu.roll(west[rows, :], LANES - levels - k, 1)] + [pltpu.roll(v, 1, 1) for v in value]
            left = [pltpu.roll(v, LANES - 1, 1) for v in value] + [pltpu.roll(east[rows, :], LANES - 1 - k, 1)]
            for n in range(columns):
                lanes = slice(n * LANES, (n + 1) * LANES)
                beside = jnp.where(first_row, before[n], down[n]) + jnp.where(last_row, up_next[n], up[n])
                beside = beside + jnp.where(first_lane, right[n], right[n + 1])
                beside = beside + jnp.where(last_lane, left[n + 1], left[n])
                out_theta[k, rows, lanes] = th[k, rows, lanes] + kp[rows, lanes] * (beside - 4.0 * value[n])
            value, before, up = following, down, up_next
        return 0

    lax.fori_loop(0, levels, update, 0)
    whole(parts.at[pl.ds(0, total - 1), :], red_recv).wait()
    out_parts[...] = parts[...]
    out_basis[...] = basis[0:BASIS - 1, 0:nlat, own_start:own_start + strip, :]

    whole(ext.at[0:nlat - 1, :, low_row:low_row + span, :], main_send).wait()
    left_edge.wait_send()
    right_edge.wait_send()
    diag_up.wait_send()
    diag_down.wait_send()
    diag_fold.wait_send()
    for far, near, own in sides:
        @pl.when(jnp.logical_not(own))
        def _():
            far.wait_send()

    @pl.when(top)
    def _():
        whole(tiles, fold_send).wait()
        fold_low.wait_send()

        @pl.when(jnp.logical_not(far_self))
        def _():
            fold_far.wait_send()

    @pl.when(j > 0)
    def _():
        to_south.wait_send()

    to_north.wait_send()
    to_west.wait_send()
    to_east.wait_send()
    whole(parts.at[pl.ds(0, total - 1), :], red_send).wait()


def finish(fresh, vectors, parts, out_theta, out_psi, psi, out_sem):
    store_theta = pltpu.make_async_copy(fresh, out_theta, out_sem.at[0])
    store_theta.start()
    total = parts.shape[0]
    value = parts[...]
    error = jnp.zeros_like(value)
    half = total // 2
    while half >= 8:
        value, e = two_sum(value[:half], value[half:])
        error = error[:half] + error[half:] + e
        half //= 2
    for shift in (4, 2, 1):
        value, e = two_sum(value, pltpu.roll(value, shift, 0))
        error = error + pltpu.roll(error, shift, 0) + e
    lane = iota((1, LANES), 1)
    error = jnp.where(
        jnp.logical_and(lane >= SLOTS, lane < 2 * SLOTS), pltpu.roll(error[0:1], SLOTS, 1), 0.0
    )
    message = value[0:1] + error
    high, low = quick(message, pltpu.roll(message, LANES - SLOTS, 1))

    gram = {}
    for n, (a, b) in enumerate(PAIRS):
        gram[a, b] = gram[b, a] = tuple(
            jnp.broadcast_to(x[:, n:n + 1], (1, LANES)) for x in (high, low)
        )
    size = BASIS - 1

    def scaled(x, factor):
        return x[0] * factor, x[1] * factor

    matrix = [
        [
            df_add(
                scaled(gram[a, b + 1], 4.0),
                df_add(scaled(gram[a, b], 4.0), gram[a, b]),
            )
            for b in range(size)
        ]
        for a in range(size)
    ]
    right = [gram[0, a] for a in range(size)]
    for p in range(size):
        for a in range(p + 1, size):
            factor = df_div(matrix[a][p], matrix[p][p])
            for b in range(p + 1, size):
                matrix[a][b] = df_sub(matrix[a][b], df_mul(factor, matrix[p][b]))
            right[a] = df_sub(right[a], df_mul(factor, right[p]))
    answer = [None] * size
    for p in reversed(range(size)):
        value = right[p]
        for b in range(p + 1, size):
            value = df_sub(value, df_mul(matrix[p][b], answer[b]))
        answer[p] = df_div(value, matrix[p][p])
    strip = psi.shape[0]
    spread = [jnp.broadcast_to(x[0], (strip, LANES)) for x in answer]

    def combine(c, _):
        lanes = pl.ds(pl.multiple_of(c * LANES, LANES), LANES)
        value = spread[size - 1] * vectors[size - 1, c]
        for b in reversed(range(size - 1)):
            value = value + spread[b] * vectors[b, c]
        psi[:, lanes] = value
        return 0

    lax.fori_loop(0, vectors.shape[1], combine, 0)

    store_psi = pltpu.make_async_copy(psi, out_psi, out_sem.at[1])
    store_psi.start()
    store_psi.wait()
    store_theta.wait()


def per_device(nlon, nlat, theta, kappa, layer_weight, diag, land_blocks):
    levels, cy, cx = theta.shape
    strip, ny = diag.shape
    wide = strip + 2 * HALO
    vmem = pl.BlockSpec(memory_space=pltpu.VMEM)
    hbm = pl.BlockSpec(memory_space=pltpu.HBM)
    dma = pltpu.SemaphoreType.DMA
    operands = (layer_weight, land_blocks, theta, kappa, diag)
    fresh, vectors, parts = pl.pallas_call(
        functools.partial(kernel, nlon, nlat),
        out_shape=(
            jax.ShapeDtypeStruct(theta.shape, F32),
            jax.ShapeDtypeStruct((BASIS - 1, nlat, strip, cy), F32),
            jax.ShapeDtypeStruct((nlon * nlat, LANES), F32),
        ),
        in_specs=[hbm] * 5,
        out_specs=(vmem, vmem, vmem),
        scratch_shapes=[
            pltpu.SMEM(layer_weight.shape, F32),
            pltpu.VMEM(land_blocks.shape, jnp.int32),
            pltpu.VMEM((levels, cy, cx), F32),
            pltpu.VMEM((cy, cx), F32),
            pltpu.VMEM((cy, cx), F32),
            pltpu.VMEM((2, cx + 2 * HALO, cy), F32),
            pltpu.VMEM((nlat + 1, 2, wide, cy), F32),
            pltpu.VMEM((nlat, 2, HALO, cy), F32),
            pltpu.VMEM((strip, ny), F32),
            pltpu.VMEM((nlat + 1, wide, cy), F32),
            pltpu.VMEM((wide, ny + LANES), F32),
            pltpu.VMEM((wide, ny + LANES), F32),
            pltpu.VMEM((wide, ny + LANES), F32),
            pltpu.VMEM((BASIS, nlat + 1, strip + 2 * INNER + 2 * PAD, cy), F32),
            pltpu.VMEM((2, levels, cx), F32),
            pltpu.VMEM((levels, cx), F32),
            pltpu.VMEM((levels, cx), F32),
            pltpu.VMEM((cy, LANES), F32),
            pltpu.VMEM((cy, LANES), F32),
            pltpu.VMEM((cy, LANES), F32),
            pltpu.VMEM((nlat, 8, LANES), F32),
            pltpu.VMEM((8, LANES), F32),
            pltpu.VMEM((8, LANES), F32),
            pltpu.VMEM((nlon * nlat, LANES), F32),
            dma((8,)),
            dma,
            dma,
            dma((2,)),
            dma,
            dma,
            dma,
            dma,
            dma((2,)),
            dma((5,)),
            dma((5,)),
            dma((4,)),
            dma((4,)),
            dma,
            dma,
            pltpu.SemaphoreType.REGULAR,
        ],
        compiler_params=pltpu.CompilerParams(
            collective_id=0, has_side_effects=True, vmem_limit_bytes=32 << 20
        ),
        name="ocean_step",
    )(*[pltpu.with_memory_space_constraint(x, pltpu.HBM) for x in operands])
    return pl.pallas_call(
        finish,
        out_shape=(
            jax.ShapeDtypeStruct(theta.shape, F32),
            jax.ShapeDtypeStruct(diag.shape, F32),
        ),
        in_specs=[vmem, vmem, vmem],
        out_specs=(hbm, hbm),
        scratch_shapes=[pltpu.VMEM(diag.shape, F32), dma((2,))],
        compiler_params=pltpu.CompilerParams(vmem_limit_bytes=16 << 20),
        name="ocean_finish",
    )(fresh, vectors, parts)


def solution(mesh):
    placed = (P(None, "lat", "lon"), P("lat", "lon"), P(), P(("lon", "lat"), None), P())
    return jax.shard_map(
        functools.partial(per_device, mesh.shape["lon"], mesh.shape["lat"]),
        mesh=mesh,
        in_specs=placed,
        out_specs=(P(None, "lat", "lon"), P(("lon", "lat"), None)),
        check_vma=False,
    )
```

```python
import functools

import jax
import jax.numpy as jnp
from jax import lax
from jax.experimental import pallas as pl
from jax.experimental.pallas import tpu as pltpu
from jax.sharding import PartitionSpec as P

MESH = pl.DeviceIdType.MESH
BS = 32
HALO = 8
REACH = 5
PAD = 8
INNER = 4
LANES = 128
F32 = jnp.float32
BF16 = jnp.bfloat16
BASIS = 5
PAIRS = [(a, b) for a in range(BASIS) for b in range(a, BASIS) if a < BASIS - 1]
SLOTS = 16


def iota(shape, axis):
    return lax.broadcasted_iota(jnp.int32, shape, axis)


def hot(condition):
    return jnp.where(condition, 1.0, 0.0).astype(BF16)


def bdot(left, right):
    return jnp.dot(left, right, preferred_element_type=F32)


def ndot(left, right):
    return lax.dot_general(left, right, (((1,), (1,)), ((), ())), preferred_element_type=F32)


def pieces(value):
    first = value.astype(BF16)
    rest = value - first.astype(F32)
    second = rest.astype(BF16)
    third = (rest - second.astype(F32)).astype(BF16)
    return [first, second, third]


def flip_lanes(value):
    width = value.shape[1]
    turn = hot(iota((width, width), 0) + iota((width, width), 1) == width - 1)
    parts = [bdot(piece, turn) for piece in pieces(value)]
    return (parts[0] + parts[1]) + parts[2]


def flip_rows(value, groups):
    count = value.shape[0]
    row = iota((count, count), 0)
    ends, start = jnp.zeros((count, count), jnp.int32), 0
    for size in groups:
        ends = jnp.where(row >= start, 2 * start + size - 1, ends)
        start += size
    turn = hot(row + iota((count, count), 1) == ends)
    parts = [bdot(turn, piece) for piece in pieces(value)]
    return (parts[0] + parts[1]) + parts[2]


def two_sum(a, b):
    s = a + b
    t = s - a
    return s, (a - (s - t)) + (b - t)


def halves(a):
    t = a * 4097.0
    high = t - (t - a)
    return high, a - high


def two_prod(a, b):
    p = a * b
    ah, al = halves(a)
    bh, bl = halves(b)
    return p, ((ah * bh - p) + ah * bl + al * bh) + al * bl


def quick(a, b):
    s = a + b
    return s, b - (s - a)


def df_mul(x, y):
    p, e = two_prod(x[0], y[0])
    return quick(p, e + (x[0] * y[1] + x[1] * y[0]))


def df_add(x, y):
    s, e = two_sum(x[0], y[0])
    return quick(s, e + (x[1] + y[1]))


def df_sub(x, y):
    return df_add(x, (-y[0], -y[1]))


def df_div(x, y):
    first = x[0] / y[0]
    rest = df_sub(x, df_mul(y, (first, jnp.zeros_like(first))))
    second = rest[0] / y[0]
    return quick(first, second)


def stencil(ref, emit, low, high):
    count, _, width = ref.shape
    lane = iota((high - low, width), 1)
    first, last = lane == 0, lane == width - 1

    def load(c, shift=0):
        return ref[c, low + shift:high + shift, :]

    value = load(0)
    before = jnp.zeros_like(value)
    up = pltpu.roll(value, width - 1, 1)
    for c in range(count):
        if c + 1 < count:
            following = load(c + 1)
            up_next = pltpu.roll(following, width - 1, 1)
        else:
            following, up_next = None, up
        down = pltpu.roll(value, 1, 1)
        beside = jnp.where(first, before, down) + jnp.where(last, up_next, up)
        emit(c, value, (beside + load(c, -1)) + load(c, 1))
        value, before, up = following, down, up_next


def kernel(
    nlon, nlat,
    weight_in, land_in, theta, kappa, diag,
    out_theta, out_basis, out_parts,
    weight, land, th, kp, sea, skt, ext, edge, flat, dgx, dg, ocs, quarter, basis, rows_out, north, south, cols_out, east, west,
    tiles, fold, fold_edge, parts,
    in_sem, main_send, main_recv, edge_send, edge_recv, fold_send, fold_low_send, fold_far_send, fold_recv,
    diag_send, diag_recv, halo_send, halo_recv, red_send, red_recv, ready,
):
    levels, cy, cx = th.shape
    ny, nx = cy * nlat, cx * nlon
    strip = cx // nlat
    wide = strip + 2 * HALO
    by, bx = land.shape
    total = nlon * nlat
    i = lax.axis_index("lon")
    j = lax.axis_index("lat")
    t = i * nlat + j
    top = j == nlat - 1
    ends = jnp.logical_or(j == 0, top)

    def remote(src, dst, send, recv, lon, lat):
        return pltpu.make_async_remote_copy(
            src_ref=src, dst_ref=dst, send_sem=send, recv_sem=recv,
            device_id=(lon, lat), device_id_type=MESH,
        )

    def lon_of(value):
        return lax.rem(value + 2 * nlon, nlon)

    def lat_of(value):
        return lax.rem(value + 2 * nlat, nlat)

    def whole(ref, sem):
        return pltpu.make_async_copy(ref, ref, sem)

    def greet(lon, lat):
        pl.semaphore_signal(barrier, inc=1, device_id=(lon, lat), device_id_type=MESH)

    def ring(value, size):
        return min(value, size - value)

    lat_order = sorted(range(1, nlat), key=lambda d: -ring(d // 4, nlat // 4) - ring(d % 4, 4))
    lon_order = sorted(range(1, nlon), key=lambda d: -ring(d // 2, nlon // 2) - 0.5 * (d % 2))

    dgx[nlat, 0:HALO, :] = jnp.zeros((HALO, cy), F32)
    dgx[nlat, HALO + strip:, :] = jnp.zeros((HALO, cy), F32)

    barrier = pltpu.get_barrier_semaphore()
    for d in lat_order:
        greet(i, lax.rem(j + d, nlat))
    for d in lon_order:
        greet(lax.rem(i + d, nlon), j)
    greet(nlon - 1 - i, nlat - 1)
    for shift in (1, 0, -1):
        other = lax.rem(total - 1 - t + shift + total, total)

        @pl.when(other != t)
        def _():
            greet(other // nlat, lax.rem(other, nlat))

    @pl.when(j == 0)
    def _():
        for lat in range(nlat):
            greet(lon_of(i - 1), lat)
        greet(lon_of(nlon - i), nlat - 1)

    @pl.when(top)
    def _():
        for lat in range(nlat):
            greet(lon_of(i + 1), lat)

    chunk = levels // 4
    loads = [
        pltpu.make_async_copy(theta.at[pl.ds(q * chunk, chunk)], th.at[pl.ds(q * chunk, chunk)], in_sem.at[q])
        for q in range(4)
    ]
    load_kappa = pltpu.make_async_copy(kappa, kp, in_sem.at[4])
    load_diag = pltpu.make_async_copy(diag, flat, in_sem.at[5])
    load_weight = pltpu.make_async_copy(weight_in, weight, in_sem.at[6])
    load_land = pltpu.make_async_copy(land_in, land, in_sem.at[7])
    load_kappa.start()
    load_weight.start()
    for copy in loads:
        copy.start()
    load_diag.start()
    load_land.start()


    skt[:, 0:HALO, :] = jnp.zeros((2, HALO, cy), F32)
    skt[:, HALO + cx:, :] = jnp.zeros((2, HALO, cy), F32)
    load_kappa.wait()
    skt[1, HALO:HALO + cx, :] = kp[...].T
    load_weight.wait()
    column = jnp.zeros((cy, cx), F32)
    for q in range(4):
        loads[q].wait()
        for k in range(q * chunk, (q + 1) * chunk):
            column = column + weight[k] * th[k]
    skt[0, HALO:HALO + cx, :] = column.T

    @pl.when(top)
    def _():
        last_sums = column[cy - 8:, :]
        last_kappa = kp[cy - 8:, :]
        lanes8 = iota((8, LANES), 1)
        for m in range(nlat):
            start = strip * (nlat - 1 - m) - HALO
            tiles[m] = jnp.where(
                lanes8 < wide,
                pltpu.roll(last_sums, (-start) % cx, 1)[:, 0:LANES],
                pltpu.roll(last_kappa, (wide - start) % cx, 1)[:, 0:LANES],
            )

    load_diag.wait()
    for c in range(nlat):
        dgx[c, HALO:HALO + strip, :] = flat[:, c * cy:(c + 1) * cy]

    own_folds = [lax.rem(total - 1 - t + shift + total, total) == t for shift in (1, -1)]
    awaited = nlat + nlon + 3 + jnp.where(top, nlat + 1, 0)
    for own in own_folds:
        awaited = awaited - jnp.where(own, 1, 0)
    pl.semaphore_wait(barrier, awaited)
    for d in range(1, nlon):
        pl.semaphore_signal(
            ready, inc=1, device_id=(lax.rem(i + d, nlon), j), device_id_type=MESH
        )

    low_row = HALO - REACH
    span = strip + 2 * REACH

    def block_rows(m):
        return skt.at[:, pl.ds(m * strip + low_row, span), :]

    own_slot = ext.at[j, :, low_row:low_row + span, :]

    def main_copy(d):
        m = lax.rem(j + d, nlat)
        return remote(block_rows(m), own_slot, main_send, main_recv, i, m)

    for d in lat_order:
        main_copy(d).start()
    pltpu.make_async_copy(block_rows(j), own_slot, main_recv).start()
    first_rows = skt.at[:, HALO:HALO + REACH, :]
    last_rows = skt.at[:, HALO + cx - REACH:HALO + cx, :]
    left_edge = remote(
        first_rows, edge.at[j, :, 0:REACH, :], edge_send.at[0], edge_recv, lon_of(i - 1), nlat - 1
    )
    right_edge = remote(
        last_rows, edge.at[j, :, low_row:HALO, :], edge_send.at[1], edge_recv, lon_of(i + 1), 0
    )
    left_edge.start()
    right_edge.start()

    def fold_copy(m):
        return remote(tiles.at[m], fold, fold_send, fold_recv.at[0], nlon - 1 - i, m)

    far_lon = lon_of(nlon - 2 - i)
    far_self = far_lon == i
    fold_far = remote(
        tiles.at[nlat - 1], fold_edge, fold_far_send, fold_recv.at[1], far_lon, nlat - 1
    )
    fold_far_own = pltpu.make_async_copy(tiles.at[nlat - 1], fold_edge, fold_recv.at[1])
    fold_low = remote(tiles.at[0], fold_edge, fold_low_send, fold_recv.at[1], lon_of(nlon - i), 0)

    @pl.when(top)
    def _():
        for m in range(nlat):
            fold_copy(m).start()
        fold_low.start()

        @pl.when(far_self)
        def _():
            fold_far_own.start()

        @pl.when(jnp.logical_not(far_self))
        def _():
            fold_far.start()

    after, before = lax.rem(t + 1, total), lax.rem(t + total - 1, total)
    depth = BASIS - 2
    own_low = slice(HALO, HALO + depth)
    own_high = slice(HALO + strip - depth, HALO + strip)
    halo_low = slice(HALO - depth, HALO)
    halo_high = slice(HALO + strip, HALO + strip + depth)
    diag_up = remote(
        dgx.at[0:nlat, own_high, :], dgx.at[0:nlat, halo_low, :], diag_send.at[0], diag_recv.at[0],
        after // nlat, lax.rem(after, nlat),
    )
    diag_down = remote(
        dgx.at[0:nlat, own_low, :], dgx.at[0:nlat, halo_high, :], diag_send.at[1], diag_recv.at[1],
        before // nlat, lax.rem(before, nlat),
    )
    diag_up.start()
    diag_down.start()
    middle = slice(HALO, HALO + strip)
    diag_fold = remote(
        dgx.at[nlat - 1, middle, :], dgx.at[nlat, middle, :], diag_send.at[2], diag_recv.at[2],
        nlon - 1 - i, nlat - 1 - j,
    )
    diag_fold.start()
    sides = []
    for n, (shift, src, dst) in enumerate(((1, own_low, halo_high), (-1, own_high, halo_low))):
        other = lax.rem(total - 1 - t + shift + total, total)
        src_ref, dst_ref = dgx.at[nlat - 1, src, :], dgx.at[nlat, dst, :]
        sides.append((
            remote(
                src_ref, dst_ref, diag_send.at[3 + n], diag_recv.at[3 + n], other // nlat, lax.rem(other, nlat)
            ),
            pltpu.make_async_copy(src_ref, dst_ref, diag_recv.at[3 + n]),
            own_folds[n],
        ))
    for far, near, own in sides:
        @pl.when(own)
        def _():
            near.start()

        @pl.when(jnp.logical_not(own))
        def _():
            far.start()

    rows_out[0] = th[:, 0, :]
    rows_out[1] = th[:, cy - 1, :]
    to_south = remote(rows_out.at[0], north, halo_send.at[0], halo_recv.at[0], i, lat_of(j - 1))
    to_north = remote(rows_out.at[1], south, halo_send.at[1], halo_recv.at[1], i, lat_of(j + 1))
    to_fold = remote(rows_out.at[1], north, halo_send.at[1], halo_recv.at[0], nlon - 1 - i, j)

    @pl.when(j > 0)
    def _():
        to_south.start()

    @pl.when(jnp.logical_not(top))
    def _():
        to_north.start()

    @pl.when(top)
    def _():
        to_fold.start()

    lane = iota((cy, LANES), 1)
    packed = jnp.zeros((cy, LANES), F32)
    for k in range(levels):
        packed = jnp.where(lane == k, pltpu.roll(th[k, :, 0:LANES], k, 1), packed)
        packed = jnp.where(
            lane == levels + k, pltpu.roll(th[k, :, cx - LANES:cx], levels + k + 1, 1), packed
        )
    cols_out[...] = packed
    to_west = remote(cols_out, east, halo_send.at[2], halo_recv.at[2], lon_of(i - 1), j)
    to_east = remote(cols_out, west, halo_send.at[3], halo_recv.at[3], lon_of(i + 1), j)
    to_west.start()
    to_east.start()

    basis[:, :, 0:PAD, :] = jnp.zeros((BASIS, nlat + 1, PAD, cy), F32)
    tail = PAD + strip + 2 * INNER
    basis[:, :, tail:, :] = jnp.zeros((BASIS, nlat + 1, PAD, cy), F32)

    load_land.wait()
    table = land[...].astype(F32).astype(BF16)
    row_block = (j * cy + iota((cy, by), 0)) >> 5
    on_rows = bdot(hot(row_block == iota((cy, by), 1)), table).astype(BF16)
    col_block = (i * cx + iota((bx, cx), 1)) >> 5
    cols_hot = hot(col_block == iota((bx, cx), 0))
    ocean = bdot(on_rows, cols_hot)
    west_block = lax.rem(i * (cx // BS) + bx - 1, bx)
    east_block = lax.rem((i + 1) * (cx // BS), bx)
    ocean_west = bdot(on_rows, hot(iota((bx, LANES), 0) == west_block))
    ocean_east = bdot(on_rows, hot(iota((bx, LANES), 0) == east_block))
    edge_row = iota((8, by), 0)
    edge_col = iota((8, by), 1)
    south_hot = hot(jnp.logical_and(edge_row == 0, edge_col == j * (cy // BS) - 1))
    north_block = jnp.where(top, by - 1, (j + 1) * (cy // BS))
    north_hot = hot(jnp.logical_and(edge_row == 0, edge_col == north_block))
    north_cols = jnp.where(top, bx - 1 - col_block, col_block)
    ocean_south = bdot(bdot(south_hot, table).astype(BF16), cols_hot)[0:1]
    ocean_north = bdot(
        bdot(north_hot, table).astype(BF16), hot(north_cols == iota((bx, cx), 0))
    )[0:1]

    strip_x = (strip * t - HALO + nx + iota((wide, bx), 0)) % nx >> 5
    strip_hot = hot(strip_x == iota((wide, bx), 1))
    on_cols = ndot(strip_hot, table).astype(BF16)
    ocs[:, 0:ny] = bdot(on_cols, hot((iota((by, ny), 1) >> 5) == iota((by, ny), 0)))
    mirror_hot = hot((bx - 1 - strip_x) == iota((wide, bx), 1))
    on_mirror = ndot(mirror_hot, table).astype(BF16)
    keep = jnp.logical_and(iota((by, LANES), 0) == by - 1, iota((by, LANES), 1) < 8)
    ocs[:, ny:ny + LANES] = bdot(on_mirror, hot(keep))

    diag_up.wait_recv()
    diag_down.wait_recv()
    diag_fold.wait_recv()
    for far, near, own in sides:
        far.wait_recv()
    for c in range(nlat):
        dg[:, c * cy:(c + 1) * cy] = dgx[c]
    dg[:, ny:] = flip_rows(flip_lanes(dgx[nlat]), (wide,))
    dg[...] = ocs[...] * ((dg[...] - 1.0) * 0.25)
    quarter[...] = ocs[...] * 0.25

    whole(ext.at[0:nlat, :, low_row:low_row + span, :], main_recv).wait()
    whole(fold, fold_recv.at[0]).wait()

    @pl.when(ends)
    def _():
        whole(edge.at[:, :, 0:REACH, :], edge_recv).wait()
        whole(fold_edge, fold_recv.at[1]).wait()
        spot = iota((8, LANES), 1) % wide
        outer = jnp.logical_or(
            jnp.logical_and(top, spot < HALO), jnp.logical_and(j == 0, spot >= wide - HALO)
        )
        fold[...] = jnp.where(outer, fold_edge[...], fold[...])

    row = iota((2 * wide, LANES), 0)
    source = jnp.where(row < wide, wide - 1 - row, 3 * wide - 1 - row)
    pick = hot(source == iota((2 * wide, LANES), 1))
    turn = hot(iota((LANES, 8), 0) == 7 - iota((LANES, 8), 1))
    folded = [ndot(pick, bdot(turn, piece).astype(BF16)) for piece in pieces(fold[...])]
    folded = (folded[0] + folded[1]) + folded[2]
    ext[nlat, 0] = folded[0:wide]
    ext[nlat, 1] = folded[wide:]

    @pl.when(j == 0)
    def _():
        ext[0:nlat, :, low_row:HALO, :] = edge[:, :, low_row:, :]

    @pl.when(top)
    def _():
        ext[0:nlat, :, HALO + strip:HALO + strip + REACH, :] = edge[:, :, 0:REACH, :]

    def lanes_of(c):
        return slice(c * LANES, (c + 1) * LANES)

    held = basis.at[BASIS - 1]
    shift = HALO - INNER
    own_start = PAD + INNER
    bottom, ceiling = PAD, PAD + strip + 2 * INNER
    for c in range(nlat + 1):
        rows = slice(shift - 1, wide - shift + 1)
        held[c, bottom - 1:ceiling + 1, :] = ocs[rows, lanes_of(c)] * ext[c, 0, rows, :]

    def store_forcing(c, value, beside):
        rows = slice(shift, wide - shift)
        rate = ocs[rows, lanes_of(c)] * ext[c, 1, rows, :]
        basis[0, c, bottom:ceiling, :] = value + rate * (beside - 4.0 * value)

    stencil(held, store_forcing, bottom, ceiling)
    for step in range(BASIS - 1):
        low, high = (bottom, ceiling) if step < BASIS - 2 else (own_start, own_start + strip)

        def store_next(c, value, beside):
            lanes, rows = lanes_of(c), slice(low - PAD + shift, high - PAD + shift)
            basis[step + 1, c, low:high, :] = dg[rows, lanes] * value - quarter[rows, lanes] * beside

        stencil(basis.at[step], store_next, low, high)

    zero = jnp.zeros((8, LANES), F32)

    def accumulate(c, carry):
        sums = list(carry)
        for h in range(strip // 8):
            start = own_start + 8 * h
            values = [basis[b, c, start:start + 8, :] for b in range(BASIS)]
            split = [halves(value) for value in values]
            for n, (a, b) in enumerate(PAIRS):
                (ah, al), (bh, bl) = split[a], split[b]
                e = ah * bl + al * values[b]
                s, f = quick(sums[2 * n], ah * bh)
                sums[2 * n], sums[2 * n + 1] = s, sums[2 * n + 1] + (e + f)
        return tuple(sums)

    sums = lax.fori_loop(0, ny // LANES, accumulate, (zero,) * (2 * len(PAIRS)))
    place = iota((SLOTS, LANES), 0)
    high = jnp.zeros((SLOTS, LANES), F32)
    low = jnp.zeros((SLOTS, LANES), F32)
    for n in range(len(PAIRS)):
        h, l = sums[2 * n], sums[2 * n + 1]
        for shift in (4, 2, 1):
            h, e = two_sum(h, pltpu.roll(h, shift, 0))
            l = l + pltpu.roll(l, shift, 0) + e
        high = jnp.where(place == n, h[0:1], high)
        low = jnp.where(place == n, l[0:1], low)
    shift = LANES // 2
    while shift:
        high, e = two_sum(high, pltpu.roll(high, shift, 1))
        low = low + pltpu.roll(low, shift, 1) + e
        shift //= 2
    spot = iota((SLOTS, LANES), 1)
    packed = jnp.where(spot == place, high, jnp.where(spot == place + SLOTS, low, 0.0))
    message = jnp.sum(packed, axis=0, keepdims=True)

    parts[pl.ds(t, 1), :] = message
    own_part = parts.at[pl.ds(t, 1), :]
    sizes = (nlon // 2, 2, nlat // 4, 4)
    offsets = [
        (a, b, c, d)
        for a in range(sizes[0]) for b in range(sizes[1]) for c in range(sizes[2]) for d in range(sizes[3])
    ]

    def hops(offset):
        return sum(min(o, n - o) for o, n in zip(offset, sizes) if n > 2 or o) - 0.5 * offset[1]

    offsets = sorted(offsets[1:], key=hops, reverse=True)
    place_of = (i // 2, lax.rem(i, 2), j // 4, lax.rem(j, 4))
    moved = [
        [lax.rem(place_of[n] + o, sizes[n]) * scale for o in range(sizes[n])]
        for n, scale in enumerate((2, 1, 4, 1))
    ]
    pl.semaphore_wait(ready, nlon - 1)
    for a, b, c, d in offsets:
        remote(own_part, own_part, red_send, red_recv, moved[0][a] + moved[1][b], moved[2][c] + moved[3][d]).start()

    to_south.wait_recv()
    to_west.wait_recv()
    to_east.wait_recv()

    @pl.when(j > 0)
    def _():
        to_north.wait_recv()

    @pl.when(j == 0)
    def _():
        south[...] = jnp.zeros_like(south)

    @pl.when(top)
    def _():
        north[...] = flip_lanes(north[...])

    west[...] = west[...] * ocean_west
    east[...] = east[...] * ocean_east
    kp[...] = ocean * kp[...]
    sea[...] = ocean
    north[...] = ocean_north * north[...]
    south[...] = ocean_south * south[...]
    part = 32
    tile_row, tile_lane = iota((part, LANES), 0), iota((part, LANES), 1)
    first_row, last_row = tile_row == 0, tile_row == part - 1
    first_lane, last_lane = tile_lane == 0, tile_lane == LANES - 1
    count = cy // part
    columns = cx // LANES

    def update(k, _):
        from_south, from_north = south[pl.ds(k, 1), :], north[pl.ds(k, 1), :]

        def load(c, n):
            rows, lanes = slice(c * part, (c + 1) * part), slice(n * LANES, (n + 1) * LANES)
            return sea[rows, lanes] * th[k, rows, lanes]

        def across(n, vector):
            return jnp.broadcast_to(vector[:, n * LANES:(n + 1) * LANES], (part, LANES))

        value = [load(0, n) for n in range(columns)]
        before = [across(n, from_south) for n in range(columns)]
        up = [pltpu.roll(v, part - 1, 0) for v in value]
        for c in range(count):
            rows = slice(c * part, (c + 1) * part)
            if c + 1 < count:
                following = [load(c + 1, n) for n in range(columns)]
                up_next = [pltpu.roll(v, part - 1, 0) for v in following]
            else:
                following, up_next = None, [across(n, from_north) for n in range(columns)]
            down = [pltpu.roll(v, 1, 0) for v in value]
            right = [pltpu.roll(west[rows, :], LANES - levels - k, 1)] + [pltpu.roll(v, 1, 1) for v in value]
            left = [pltpu.roll(v, LANES - 1, 1) for v in value] + [pltpu.roll(east[rows, :], LANES - 1 - k, 1)]
            for n in range(columns):
                lanes = slice(n * LANES, (n + 1) * LANES)
                beside = jnp.where(first_row, before[n], down[n]) + jnp.where(last_row, up_next[n], up[n])
                beside = beside + jnp.where(first_lane, right[n], right[n + 1])
                beside = beside + jnp.where(last_lane, left[n + 1], left[n])
                out_theta[k, rows, lanes] = th[k, rows, lanes] + kp[rows, lanes] * (beside - 4.0 * value[n])
            value, before, up = following, down, up_next
        return 0

    lax.fori_loop(0, levels, update, 0)
    whole(parts.at[pl.ds(0, total - 1), :], red_recv).wait()
    out_parts[...] = parts[...]
    out_basis[...] = basis[0:BASIS - 1, 0:nlat, own_start:own_start + strip, :]

    whole(ext.at[0:nlat - 1, :, low_row:low_row + span, :], main_send).wait()
    left_edge.wait_send()
    right_edge.wait_send()
    diag_up.wait_send()
    diag_down.wait_send()
    diag_fold.wait_send()
    for far, near, own in sides:
        @pl.when(jnp.logical_not(own))
        def _():
            far.wait_send()

    @pl.when(top)
    def _():
        whole(tiles, fold_send).wait()
        fold_low.wait_send()

        @pl.when(jnp.logical_not(far_self))
        def _():
            fold_far.wait_send()

    @pl.when(j > 0)
    def _():
        to_south.wait_send()

    to_north.wait_send()
    to_west.wait_send()
    to_east.wait_send()
    whole(parts.at[pl.ds(0, total - 1), :], red_send).wait()


def finish(fresh, vectors, parts, out_theta, out_psi, psi, out_sem):
    pieces_of = fresh.shape[0] // 2
    stores = [
        pltpu.make_async_copy(fresh.at[pl.ds(2 * q, 2)], out_theta.at[pl.ds(2 * q, 2)], out_sem.at[0])
        for q in range(pieces_of)
    ]
    for copy in stores:
        copy.start()
    total = parts.shape[0]
    value = parts[...]
    error = jnp.zeros_like(value)
    half = total // 2
    while half >= 8:
        value, e = two_sum(value[:half], value[half:])
        error = error[:half] + error[half:] + e
        half //= 2
    for shift in (4, 2, 1):
        value, e = two_sum(value, pltpu.roll(value, shift, 0))
        error = error + pltpu.roll(error, shift, 0) + e
    lane = iota((1, LANES), 1)
    error = jnp.where(
        jnp.logical_and(lane >= SLOTS, lane < 2 * SLOTS), pltpu.roll(error[0:1], SLOTS, 1), 0.0
    )
    message = value[0:1] + error
    high, low = quick(message, pltpu.roll(message, LANES - SLOTS, 1))

    gram = {}
    for n, (a, b) in enumerate(PAIRS):
        gram[a, b] = gram[b, a] = tuple(
            jnp.broadcast_to(x[:, n:n + 1], (1, LANES)) for x in (high, low)
        )
    size = BASIS - 1

    def scaled(x, factor):
        return x[0] * factor, x[1] * factor

    matrix = [
        [
            df_add(
                scaled(gram[a, b + 1], 4.0),
                df_add(scaled(gram[a, b], 4.0), gram[a, b]),
            )
            for b in range(size)
        ]
        for a in range(size)
    ]
    right = [gram[0, a] for a in range(size)]
    for p in range(size):
        for a in range(p + 1, size):
            factor = df_div(matrix[a][p], matrix[p][p])
            for b in range(p + 1, size):
                matrix[a][b] = df_sub(matrix[a][b], df_mul(factor, matrix[p][b]))
            right[a] = df_sub(right[a], df_mul(factor, right[p]))
    answer = [None] * size
    for p in reversed(range(size)):
        value = right[p]
        for b in range(p + 1, size):
            value = df_sub(value, df_mul(matrix[p][b], answer[b]))
        answer[p] = df_div(value, matrix[p][p])
    strip = psi.shape[0]
    spread = [jnp.broadcast_to(x[0], (strip, LANES)) for x in answer]

    def combine(c, _):
        lanes = pl.ds(pl.multiple_of(c * LANES, LANES), LANES)
        value = spread[size - 1] * vectors[size - 1, c]
        for b in reversed(range(size - 1)):
            value = value + spread[b] * vectors[b, c]
        psi[:, lanes] = value
        return 0

    lax.fori_loop(0, vectors.shape[1], combine, 0)

    store_psi = pltpu.make_async_copy(psi, out_psi, out_sem.at[1])
    store_psi.start()
    store_psi.wait()
    pltpu.make_async_copy(fresh, out_theta, out_sem.at[0]).wait()


def per_device(nlon, nlat, theta, kappa, layer_weight, diag, land_blocks):
    levels, cy, cx = theta.shape
    strip, ny = diag.shape
    wide = strip + 2 * HALO
    vmem = pl.BlockSpec(memory_space=pltpu.VMEM)
    hbm = pl.BlockSpec(memory_space=pltpu.HBM)
    dma = pltpu.SemaphoreType.DMA
    operands = (layer_weight, land_blocks, theta, kappa, diag)
    fresh, vectors, parts = pl.pallas_call(
        functools.partial(kernel, nlon, nlat),
        out_shape=(
            jax.ShapeDtypeStruct(theta.shape, F32),
            jax.ShapeDtypeStruct((BASIS - 1, nlat, strip, cy), F32),
            jax.ShapeDtypeStruct((nlon * nlat, LANES), F32),
        ),
        in_specs=[hbm] * 5,
        out_specs=(vmem, vmem, vmem),
        scratch_shapes=[
            pltpu.SMEM(layer_weight.shape, F32),
            pltpu.VMEM(land_blocks.shape, jnp.int32),
            pltpu.VMEM((levels, cy, cx), F32),
            pltpu.VMEM((cy, cx), F32),
            pltpu.VMEM((cy, cx), F32),
            pltpu.VMEM((2, cx + 2 * HALO, cy), F32),
            pltpu.VMEM((nlat + 1, 2, wide, cy), F32),
            pltpu.VMEM((nlat, 2, HALO, cy), F32),
            pltpu.VMEM((strip, ny), F32),
            pltpu.VMEM((nlat + 1, wide, cy), F32),
            pltpu.VMEM((wide, ny + LANES), F32),
            pltpu.VMEM((wide, ny + LANES), F32),
            pltpu.VMEM((wide, ny + LANES), F32),
            pltpu.VMEM((BASIS, nlat + 1, strip + 2 * INNER + 2 * PAD, cy), F32),
            pltpu.VMEM((2, levels, cx), F32),
            pltpu.VMEM((levels, cx), F32),
            pltpu.VMEM((levels, cx), F32),
            pltpu.VMEM((cy, LANES), F32),
            pltpu.VMEM((cy, LANES), F32),
            pltpu.VMEM((cy, LANES), F32),
            pltpu.VMEM((nlat, 8, LANES), F32),
            pltpu.VMEM((8, LANES), F32),
            pltpu.VMEM((8, LANES), F32),
            pltpu.VMEM((nlon * nlat, LANES), F32),
            dma((8,)),
            dma,
            dma,
            dma((2,)),
            dma,
            dma,
            dma,
            dma,
            dma((2,)),
            dma((5,)),
            dma((5,)),
            dma((4,)),
            dma((4,)),
            dma,
            dma,
            pltpu.SemaphoreType.REGULAR,
        ],
        compiler_params=pltpu.CompilerParams(
            collective_id=0, has_side_effects=True, vmem_limit_bytes=32 << 20
        ),
        name="ocean_step",
    )(*[pltpu.with_memory_space_constraint(x, pltpu.HBM) for x in operands])
    return pl.pallas_call(
        finish,
        out_shape=(
            jax.ShapeDtypeStruct(theta.shape, F32),
            jax.ShapeDtypeStruct(diag.shape, F32),
        ),
        in_specs=[vmem, vmem, vmem],
        out_specs=(hbm, hbm),
        scratch_shapes=[pltpu.VMEM(diag.shape, F32), dma((2,))],
        compiler_params=pltpu.CompilerParams(vmem_limit_bytes=16 << 20),
        name="ocean_finish",
    )(fresh, vectors, parts)


def solution(mesh):
    placed = (P(None, "lat", "lon"), P("lat", "lon"), P(), P(("lon", "lat"), None), P())
    return jax.shard_map(
        functools.partial(per_device, mesh.shape["lon"], mesh.shape["lat"]),
        mesh=mesh,
        in_specs=placed,
        out_specs=(P(None, "lat", "lon"), P(("lon", "lat"), None)),
        check_vma=False,
    )
```

```python
import functools

import jax
import jax.numpy as jnp
from jax import lax
from jax.experimental import pallas as pl
from jax.experimental.pallas import tpu as pltpu
from jax.sharding import PartitionSpec as P

MESH = pl.DeviceIdType.MESH
BS = 32
HALO = 8
PAD = 8
INNER = 4
BODY = 24
SPAN = BODY + 3
LANES = 128
F32 = jnp.float32
BF16 = jnp.bfloat16
BASIS = 5
PAIRS = [(a, b) for a in range(BASIS) for b in range(a, BASIS) if a < BASIS - 1]
SLOTS = 16


def iota(shape, axis):
    return lax.broadcasted_iota(jnp.int32, shape, axis)


def hot(condition):
    return jnp.where(condition, 1.0, 0.0).astype(BF16)


def bdot(left, right):
    return jnp.dot(left, right, preferred_element_type=F32)


def ndot(left, right):
    return lax.dot_general(left, right, (((1,), (1,)), ((), ())), preferred_element_type=F32)


def pieces(value):
    first = value.astype(BF16)
    rest = value - first.astype(F32)
    second = rest.astype(BF16)
    third = (rest - second.astype(F32)).astype(BF16)
    return [first, second, third]


def flip_lanes(value):
    width = value.shape[1]
    turn = hot(iota((width, width), 0) + iota((width, width), 1) == width - 1)
    parts = [bdot(piece, turn) for piece in pieces(value)]
    return (parts[0] + parts[1]) + parts[2]


def flip_rows(value, groups):
    count = value.shape[0]
    row = iota((count, count), 0)
    ends, start = jnp.zeros((count, count), jnp.int32), 0
    for size in groups:
        ends = jnp.where(row >= start, 2 * start + size - 1, ends)
        start += size
    turn = hot(row + iota((count, count), 1) == ends)
    parts = [bdot(turn, piece) for piece in pieces(value)]
    return (parts[0] + parts[1]) + parts[2]


def two_sum(a, b):
    s = a + b
    t = s - a
    return s, (a - (s - t)) + (b - t)


def halves(a):
    t = a * 4097.0
    high = t - (t - a)
    return high, a - high


def two_prod(a, b):
    p = a * b
    ah, al = halves(a)
    bh, bl = halves(b)
    return p, ((ah * bh - p) + ah * bl + al * bh) + al * bl


def quick(a, b):
    s = a + b
    return s, b - (s - a)


def df_mul(x, y):
    p, e = two_prod(x[0], y[0])
    return quick(p, e + (x[0] * y[1] + x[1] * y[0]))


def df_add(x, y):
    s, e = two_sum(x[0], y[0])
    return quick(s, e + (x[1] + y[1]))


def df_sub(x, y):
    return df_add(x, (-y[0], -y[1]))


def df_div(x, y):
    first = x[0] / y[0]
    rest = df_sub(x, df_mul(y, (first, jnp.zeros_like(first))))
    second = rest[0] / y[0]
    return quick(first, second)


def stencil(ref, emit, low, high):
    count, _, width = ref.shape
    lane = iota((high - low, width), 1)
    first, last = lane == 0, lane == width - 1

    def load(c, shift=0):
        return ref[c, low + shift:high + shift, :]

    value = load(0)
    before = jnp.zeros_like(value)
    up = pltpu.roll(value, width - 1, 1)
    for c in range(count):
        if c + 1 < count:
            following = load(c + 1)
            up_next = pltpu.roll(following, width - 1, 1)
        else:
            following, up_next = None, up
        down = pltpu.roll(value, 1, 1)
        beside = jnp.where(first, before, down) + jnp.where(last, up_next, up)
        emit(c, value, (beside + load(c, -1)) + load(c, 1))
        value, before, up = following, down, up_next


def kernel(
    nlon, nlat,
    weight_in, land_in, theta, kappa, diag,
    out_theta, out_basis, out_parts,
    weight, land, th, kp, sea, turned, windows, packs, edge_packs, ext, edge, crossing, lined_here, flat, dgx, dg, ocs, quarter, basis, rows_out, north, south, cols_out, east, west,
    tiles, fold, fold_edge, parts,
    in_sem, main_send, main_recv, edge_send, edge_recv, fold_send, fold_low_send, fold_far_send, fold_recv,
    diag_send, diag_recv, halo_send, halo_recv, red_send, red_recv, ready,
):
    levels, cy, cx = th.shape
    ny, nx = cy * nlat, cx * nlon
    strip = cx // nlat
    wide = strip + 2 * HALO
    by, bx = land.shape
    total = nlon * nlat
    i = lax.axis_index("lon")
    j = lax.axis_index("lat")
    t = i * nlat + j
    top = j == nlat - 1
    ends = jnp.logical_or(j == 0, top)

    def remote(src, dst, send, recv, lon, lat):
        return pltpu.make_async_remote_copy(
            src_ref=src, dst_ref=dst, send_sem=send, recv_sem=recv,
            device_id=(lon, lat), device_id_type=MESH,
        )

    def lon_of(value):
        return lax.rem(value + 2 * nlon, nlon)

    def lat_of(value):
        return lax.rem(value + 2 * nlat, nlat)

    def whole(ref, sem):
        return pltpu.make_async_copy(ref, ref, sem)

    def greet(lon, lat):
        pl.semaphore_signal(barrier, inc=1, device_id=(lon, lat), device_id_type=MESH)

    def ring(value, size):
        return min(value, size - value)

    lat_order = sorted(range(1, nlat), key=lambda d: -ring(d // 4, nlat // 4) - ring(d % 4, 4))
    lon_order = sorted(range(1, nlon), key=lambda d: -ring(d // 2, nlon // 2) - 0.5 * (d % 2))

    dgx[nlat, 0:HALO, :] = jnp.zeros((HALO, cy), F32)
    dgx[nlat, HALO + strip:, :] = jnp.zeros((HALO, cy), F32)

    barrier = pltpu.get_barrier_semaphore()
    for d in lat_order:
        greet(i, lax.rem(j + d, nlat))
    for d in lon_order:
        greet(lax.rem(i + d, nlon), j)
    greet(nlon - 1 - i, nlat - 1)
    for shift in (1, 0, -1):
        other = lax.rem(total - 1 - t + shift + total, total)

        @pl.when(other != t)
        def _():
            greet(other // nlat, lax.rem(other, nlat))

    @pl.when(j == 0)
    def _():
        for lat in range(nlat):
            greet(lon_of(i - 1), lat)
        greet(lon_of(nlon - i), nlat - 1)

    @pl.when(top)
    def _():
        for lat in range(nlat):
            greet(lon_of(i + 1), lat)

    chunk = levels // 4
    loads = [
        pltpu.make_async_copy(theta.at[pl.ds(q * chunk, chunk)], th.at[pl.ds(q * chunk, chunk)], in_sem.at[q])
        for q in range(4)
    ]
    load_kappa = pltpu.make_async_copy(kappa, kp, in_sem.at[4])
    load_diag = pltpu.make_async_copy(diag, flat, in_sem.at[5])
    load_weight = pltpu.make_async_copy(weight_in, weight, in_sem.at[6])
    load_land = pltpu.make_async_copy(land_in, land, in_sem.at[7])
    load_kappa.start()
    load_weight.start()
    for copy in loads:
        copy.start()
    load_diag.start()
    load_land.start()


    load_land.wait()
    table = land[...].astype(F32).astype(BF16)
    row_block = (j * cy + iota((cy, by), 0)) >> 5
    on_rows = bdot(hot(row_block == iota((cy, by), 1)), table).astype(BF16)
    col_block = (i * cx + iota((bx, cx), 1)) >> 5
    cols_hot = hot(col_block == iota((bx, cx), 0))
    sea[...] = bdot(on_rows, cols_hot)
    load_kappa.wait()
    kp[...] = sea[...] * kp[...]
    load_weight.wait()
    column = jnp.zeros((cy, cx), F32)
    for q in range(4):
        loads[q].wait()
        for k in range(q * chunk, (q + 1) * chunk):
            column = column + weight[k] * th[k]
    held, rate = sea[...] * column, kp[...]
    block_row, block_lane = iota((cy, cx), 0), iota((cy, cx), 1)
    beside = jnp.where(block_row == 0, 0.0, pltpu.roll(held, 1, 0))
    beside = beside + jnp.where(block_row == cy - 1, 0.0, pltpu.roll(held, cy - 1, 0))
    beside = beside + jnp.where(block_lane == 0, 0.0, pltpu.roll(held, 1, 1))
    beside = beside + jnp.where(block_lane == cx - 1, 0.0, pltpu.roll(held, cx - 1, 1))
    force = held + rate * (beside - 4.0 * held)
    turned[0:HALO, :] = jnp.zeros((HALO, cy), F32)
    turned[HALO + cx:, :] = jnp.zeros((HALO, cy), F32)
    turned[HALO:HALO + cx, :] = force.T

    lane = iota((cy, LANES), 1)
    ring_columns = jnp.where(
        lane < 2,
        jnp.where(lane == 0, rate[:, 0:LANES], pltpu.roll(held[:, 0:LANES], 1, 1)),
        jnp.where(
            lane == 2, pltpu.roll(rate[:, cx - LANES:], 3, 1), pltpu.roll(held[:, cx - LANES:], 4, 1)
        ),
    )
    ring_rows = ring_columns.T[0:8]

    lines = jnp.concatenate([rate[0:1], rate[cy - 1:], held[0:1], held[cy - 1:]] * 2, axis=0)
    for m in range(nlat):
        windows[m] = pltpu.roll(lines, (HALO - strip * m) % cx, 1)[:, 0:LANES]
    lanes_here = iota((nlat, LANES), 1)
    lined = windows[:, 0, :]
    for g in range(1, 4):
        lined = jnp.where(lanes_here >= wide * g, pltpu.roll(windows[:, g, :], wide * g, 1), lined)
    for m in range(nlat):
        start = HALO - INNER + strip * m
        packs[m, 0:BODY, :] = turned[start:start + BODY, :]
        packs[m, BODY:BODY + 1, :] = lined[m:m + 1]
    packs[0, BODY + 1:SPAN, :] = ring_rows[0:2]
    packs[nlat - 1, BODY + 1:SPAN, :] = ring_rows[2:4]
    for n, (start, m) in enumerate(((HALO, nlat - 1), (HALO + cx - INNER, 0))):
        edge_packs[n, 0:INNER, :] = turned[start:start + INNER, :]
        edge_packs[n, INNER:INNER + 1, :] = lined[m:m + 1]
        edge_packs[n, INNER + 1:INNER + 3, :] = ring_rows[2 * n:2 * n + 2]

    @pl.when(top)
    def _():
        lanes8 = iota((8, LANES), 1)
        corner = pltpu.roll(ring_columns[cy - 8:], 3 * wide, 1)
        for m in range(nlat):
            start = strip * (nlat - 1 - m) - HALO
            tile = corner
            for g, field in ((2, held), (1, rate), (0, force)):
                shifted = pltpu.roll(field[cy - 8:], (g * wide - start) % cx, 1)[:, 0:LANES]
                tile = jnp.where(lanes8 < (g + 1) * wide, shifted, tile)
            tiles[m] = tile

    load_diag.wait()
    for c in range(nlat):
        dgx[c, HALO:HALO + strip, :] = flat[:, c * cy:(c + 1) * cy]

    own_folds = [lax.rem(total - 1 - t + shift + total, total) == t for shift in (1, -1)]
    awaited = nlat + nlon + 3 + jnp.where(top, nlat + 1, 0)
    for own in own_folds:
        awaited = awaited - jnp.where(own, 1, 0)
    pl.semaphore_wait(barrier, awaited)
    for d in range(1, nlon):
        pl.semaphore_signal(
            ready, inc=1, device_id=(lax.rem(i + d, nlon), j), device_id_type=MESH
        )

    own_slot = ext.at[j, 0:SPAN, :]

    def block_rows(m):
        return packs.at[m, 0:SPAN, :]

    def main_copy(d):
        m = lax.rem(j + d, nlat)
        return remote(block_rows(m), own_slot, main_send, main_recv, i, m)

    for d in lat_order:
        main_copy(d).start()
    pltpu.make_async_copy(block_rows(j), own_slot, main_recv).start()
    edge_slot = edge.at[j, 0:INNER + 3, :]
    left_edge = remote(
        edge_packs.at[0, 0:INNER + 3, :], edge_slot, edge_send.at[0], edge_recv, lon_of(i - 1), nlat - 1
    )
    right_edge = remote(
        edge_packs.at[1, 0:INNER + 3, :], edge_slot, edge_send.at[1], edge_recv, lon_of(i + 1), 0
    )
    left_edge.start()
    right_edge.start()

    def fold_copy(m):
        return remote(tiles.at[m], fold, fold_send, fold_recv.at[0], nlon - 1 - i, m)

    far_lon = lon_of(nlon - 2 - i)
    far_self = far_lon == i
    fold_far = remote(
        tiles.at[nlat - 1], fold_edge, fold_far_send, fold_recv.at[1], far_lon, nlat - 1
    )
    fold_far_own = pltpu.make_async_copy(tiles.at[nlat - 1], fold_edge, fold_recv.at[1])
    fold_low = remote(tiles.at[0], fold_edge, fold_low_send, fold_recv.at[1], lon_of(nlon - i), 0)

    @pl.when(top)
    def _():
        for m in range(nlat):
            fold_copy(m).start()
        fold_low.start()

        @pl.when(far_self)
        def _():
            fold_far_own.start()

        @pl.when(jnp.logical_not(far_self))
        def _():
            fold_far.start()

    after, before = lax.rem(t + 1, total), lax.rem(t + total - 1, total)
    depth = BASIS - 2
    own_low = slice(HALO, HALO + depth)
    own_high = slice(HALO + strip - depth, HALO + strip)
    halo_low = slice(HALO - depth, HALO)
    halo_high = slice(HALO + strip, HALO + strip + depth)
    diag_up = remote(
        dgx.at[0:nlat, own_high, :], dgx.at[0:nlat, halo_low, :], diag_send.at[0], diag_recv.at[0],
        after // nlat, lax.rem(after, nlat),
    )
    diag_down = remote(
        dgx.at[0:nlat, own_low, :], dgx.at[0:nlat, halo_high, :], diag_send.at[1], diag_recv.at[1],
        before // nlat, lax.rem(before, nlat),
    )
    diag_up.start()
    diag_down.start()
    middle = slice(HALO, HALO + strip)
    diag_fold = remote(
        dgx.at[nlat - 1, middle, :], dgx.at[nlat, middle, :], diag_send.at[2], diag_recv.at[2],
        nlon - 1 - i, nlat - 1 - j,
    )
    diag_fold.start()
    sides = []
    for n, (shift, src, dst) in enumerate(((1, own_low, halo_high), (-1, own_high, halo_low))):
        other = lax.rem(total - 1 - t + shift + total, total)
        src_ref, dst_ref = dgx.at[nlat - 1, src, :], dgx.at[nlat, dst, :]
        sides.append((
            remote(
                src_ref, dst_ref, diag_send.at[3 + n], diag_recv.at[3 + n], other // nlat, lax.rem(other, nlat)
            ),
            pltpu.make_async_copy(src_ref, dst_ref, diag_recv.at[3 + n]),
            own_folds[n],
        ))
    for far, near, own in sides:
        @pl.when(own)
        def _():
            near.start()

        @pl.when(jnp.logical_not(own))
        def _():
            far.start()

    rows_out[0] = th[:, 0, :]
    rows_out[1] = th[:, cy - 1, :]
    to_south = remote(rows_out.at[0], north, halo_send.at[0], halo_recv.at[0], i, lat_of(j - 1))
    to_north = remote(rows_out.at[1], south, halo_send.at[1], halo_recv.at[1], i, lat_of(j + 1))
    to_fold = remote(rows_out.at[1], north, halo_send.at[1], halo_recv.at[0], nlon - 1 - i, j)

    @pl.when(j > 0)
    def _():
        to_south.start()

    @pl.when(jnp.logical_not(top))
    def _():
        to_north.start()

    @pl.when(top)
    def _():
        to_fold.start()

    lane = iota((cy, LANES), 1)
    packed = jnp.zeros((cy, LANES), F32)
    for k in range(levels):
        packed = jnp.where(lane == k, pltpu.roll(th[k, :, 0:LANES], k, 1), packed)
        packed = jnp.where(
            lane == levels + k, pltpu.roll(th[k, :, cx - LANES:cx], levels + k + 1, 1), packed
        )
    cols_out[...] = packed
    to_west = remote(cols_out, east, halo_send.at[2], halo_recv.at[2], lon_of(i - 1), j)
    to_east = remote(cols_out, west, halo_send.at[3], halo_recv.at[3], lon_of(i + 1), j)
    to_west.start()
    to_east.start()

    basis[:, :, 0:PAD, :] = jnp.zeros((BASIS, nlat + 1, PAD, cy), F32)
    tail = PAD + strip + 2 * INNER
    basis[:, :, tail:, :] = jnp.zeros((BASIS, nlat + 1, PAD, cy), F32)

    west_block = lax.rem(i * (cx // BS) + bx - 1, bx)
    east_block = lax.rem((i + 1) * (cx // BS), bx)
    ocean_west = bdot(on_rows, hot(iota((bx, LANES), 0) == west_block))
    ocean_east = bdot(on_rows, hot(iota((bx, LANES), 0) == east_block))
    edge_row = iota((8, by), 0)
    edge_col = iota((8, by), 1)
    south_hot = hot(jnp.logical_and(edge_row == 0, edge_col == j * (cy // BS) - 1))
    north_block = jnp.where(top, by - 1, (j + 1) * (cy // BS))
    north_hot = hot(jnp.logical_and(edge_row == 0, edge_col == north_block))
    north_cols = jnp.where(top, bx - 1 - col_block, col_block)
    ocean_south = bdot(bdot(south_hot, table).astype(BF16), cols_hot)[0:1]
    ocean_north = bdot(
        bdot(north_hot, table).astype(BF16), hot(north_cols == iota((bx, cx), 0))
    )[0:1]

    strip_x = (strip * t - HALO + nx + iota((wide, bx), 0)) % nx >> 5
    strip_hot = hot(strip_x == iota((wide, bx), 1))
    on_cols = ndot(strip_hot, table).astype(BF16)
    ocs[:, 0:ny] = bdot(on_cols, hot((iota((by, ny), 1) >> 5) == iota((by, ny), 0)))
    mirror_hot = hot((bx - 1 - strip_x) == iota((wide, bx), 1))
    on_mirror = ndot(mirror_hot, table).astype(BF16)
    keep = jnp.logical_and(iota((by, LANES), 0) == by - 1, iota((by, LANES), 1) < 8)
    ocs[:, ny:ny + LANES] = bdot(on_mirror, hot(keep))

    diag_up.wait_recv()
    diag_down.wait_recv()
    diag_fold.wait_recv()
    for far, near, own in sides:
        far.wait_recv()
    for c in range(nlat):
        dg[:, c * cy:(c + 1) * cy] = dgx[c]
    dg[:, ny:] = flip_rows(flip_lanes(dgx[nlat]), (wide,))
    dg[...] = ocs[...] * ((dg[...] - 1.0) * 0.25)
    quarter[...] = ocs[...] * 0.25

    whole(ext.at[0:nlat, 0:SPAN, :], main_recv).wait()
    whole(fold, fold_recv.at[0]).wait()

    @pl.when(ends)
    def _():
        whole(edge.at[:, 0:INNER + 3, :], edge_recv).wait()
        whole(fold_edge, fold_recv.at[1]).wait()
        spot = iota((8, LANES), 1)
        outer = jnp.logical_or(
            jnp.logical_and(top, spot % wide < HALO), jnp.logical_and(j == 0, spot % wide >= wide - HALO)
        )
        outer = jnp.logical_and(outer, spot < 3 * wide)
        fold[...] = jnp.where(outer, fold_edge[...], fold[...])

    turn = hot(iota((LANES, 8), 0) == 7 - iota((LANES, 8), 1))

    def unfold(tile, pick):
        parts = [ndot(pick, bdot(turn, piece).astype(BF16)) for piece in pieces(tile)]
        return (parts[0] + parts[1]) + parts[2]

    row = iota((3 * wide + 8, LANES), 0)
    source = jnp.where(row < 3 * wide, (row // wide) * wide + wide - 1 - row % wide, row)
    folded = unfold(fold[...], hot(source == iota((3 * wide + 8, LANES), 1)))
    crossing[...] = folded[INNER:INNER + BODY]
    corner_main = folded[3 * wide:]
    lined_here[...] = ext[:, BODY, :]

    def fix_edge(into, inner_row, outer_row, first, mine, theirs):
        spot = iota((nlat, LANES), 1) % wide
        from_edge = spot < HALO if first else spot >= wide - HALO
        lined_here[...] = jnp.where(from_edge, edge[:, INNER, :], lined_here[...])
        ext[:, into:into + INNER, :] = edge[:, 0:INNER, :]
        ext[:, outer_row, :] = ext[:, outer_row, :] + edge[:, INNER + 1, :] * ext[:, BODY + 2, :]
        ext[:, inner_row, :] = ext[:, inner_row, :] + ext[:, BODY + 1, :] * edge[:, INNER + 2, :]
        pick = hot(3 * wide + iota((8, LANES), 0) == iota((8, LANES), 1))
        corner_edge = unfold(fold_edge[...], pick)
        line = iota((BODY, LANES), 0)
        across_out = corner_edge[theirs:theirs + 1] * corner_main[mine + 1:mine + 2]
        across_in = corner_main[mine:mine + 1] * corner_edge[theirs + 1:theirs + 2]
        crossing[...] = crossing[...] + jnp.where(
            line == outer_row, across_out, jnp.where(line == inner_row, across_in, 0.0)
        )

    @pl.when(j == 0)
    def _():
        fix_edge(0, INNER, INNER - 1, True, 2, 0)

    @pl.when(top)
    def _():
        fix_edge(INNER + strip, INNER + strip - 1, INNER + strip, False, 0, 2)

    columns_of = jnp.concatenate(
        [lined_here[...], jnp.zeros((LANES - nlat, LANES), F32)], axis=0
    ).T
    square = (wide, LANES)
    virtual = iota(square, 1) == nlat
    rate_low, rate_high, held_low, held_high = [columns_of[g * wide:(g + 1) * wide] for g in range(4)]
    rate_low = jnp.where(virtual, jnp.broadcast_to(folded[wide:2 * wide, 0:1], square), rate_low)
    held_low = jnp.where(virtual, jnp.broadcast_to(folded[2 * wide:3 * wide, 0:1], square), held_low)
    rows = slice(HALO - INNER, HALO - INNER + BODY)
    add_high = (rate_high * pltpu.roll(held_low, LANES - 1, 1))[rows]
    add_low = (rate_low * pltpu.roll(held_high, 1, 1))[rows]

    def lanes_of(c):
        return slice(c * LANES, (c + 1) * LANES)

    shift = HALO - INNER
    own_start = PAD + INNER
    bottom, ceiling = PAD, PAD + BODY
    body_lane = iota((BODY, LANES), 1)
    for c in range(nlat + 1):
        value = ext[c, 0:BODY, :] if c < nlat else crossing[...]
        value = jnp.where(body_lane == 0, value + add_low[:, c:c + 1], value)
        basis[0, c, bottom:ceiling, :] = jnp.where(
            body_lane == LANES - 1, value + add_high[:, c:c + 1], value
        )
    for step in range(BASIS - 1):
        low, high = (bottom, ceiling) if step < BASIS - 2 else (own_start, own_start + strip)

        def store_next(c, value, beside):
            lanes, rows = lanes_of(c), slice(low - PAD + shift, high - PAD + shift)
            basis[step + 1, c, low:high, :] = dg[rows, lanes] * value - quarter[rows, lanes] * beside

        stencil(basis.at[step], store_next, low, high)

    zero = jnp.zeros((8, LANES), F32)

    def accumulate(c, carry):
        sums = list(carry)
        for h in range(strip // 8):
            start = own_start + 8 * h
            values = [basis[b, c, start:start + 8, :] for b in range(BASIS)]
            split = [halves(value) for value in values]
            for n, (a, b) in enumerate(PAIRS):
                (ah, al), (bh, bl) = split[a], split[b]
                e = ah * bl + al * values[b]
                s, f = quick(sums[2 * n], ah * bh)
                sums[2 * n], sums[2 * n + 1] = s, sums[2 * n + 1] + (e + f)
        return tuple(sums)

    sums = lax.fori_loop(0, ny // LANES, accumulate, (zero,) * (2 * len(PAIRS)))
    place = iota((SLOTS, LANES), 0)
    high = jnp.zeros((SLOTS, LANES), F32)
    low = jnp.zeros((SLOTS, LANES), F32)
    for n in range(len(PAIRS)):
        h, l = sums[2 * n], sums[2 * n + 1]
        for shift in (4, 2, 1):
            h, e = two_sum(h, pltpu.roll(h, shift, 0))
            l = l + pltpu.roll(l, shift, 0) + e
        high = jnp.where(place == n, h[0:1], high)
        low = jnp.where(place == n, l[0:1], low)
    shift = LANES // 2
    while shift:
        high, e = two_sum(high, pltpu.roll(high, shift, 1))
        low = low + pltpu.roll(low, shift, 1) + e
        shift //= 2
    spot = iota((SLOTS, LANES), 1)
    packed = jnp.where(spot == place, high, jnp.where(spot == place + SLOTS, low, 0.0))
    message = jnp.sum(packed, axis=0, keepdims=True)

    parts[pl.ds(t, 1), :] = message
    own_part = parts.at[pl.ds(t, 1), :]
    sizes = (nlon // 2, 2, nlat // 4, 4)
    offsets = [
        (a, b, c, d)
        for a in range(sizes[0]) for b in range(sizes[1]) for c in range(sizes[2]) for d in range(sizes[3])
    ]

    def hops(offset):
        return sum(min(o, n - o) for o, n in zip(offset, sizes) if n > 2 or o) - 0.5 * offset[1]

    offsets = sorted(offsets[1:], key=hops, reverse=True)
    place_of = (i // 2, lax.rem(i, 2), j // 4, lax.rem(j, 4))
    moved = [
        [lax.rem(place_of[n] + o, sizes[n]) * scale for o in range(sizes[n])]
        for n, scale in enumerate((2, 1, 4, 1))
    ]
    pl.semaphore_wait(ready, nlon - 1)
    for a, b, c, d in offsets:
        remote(own_part, own_part, red_send, red_recv, moved[0][a] + moved[1][b], moved[2][c] + moved[3][d]).start()

    to_south.wait_recv()
    to_west.wait_recv()
    to_east.wait_recv()

    @pl.when(j > 0)
    def _():
        to_north.wait_recv()

    @pl.when(j == 0)
    def _():
        south[...] = jnp.zeros_like(south)

    @pl.when(top)
    def _():
        north[...] = flip_lanes(north[...])

    west[...] = west[...] * ocean_west
    east[...] = east[...] * ocean_east
    north[...] = ocean_north * north[...]
    south[...] = ocean_south * south[...]
    part = 32
    tile_row, tile_lane = iota((part, LANES), 0), iota((part, LANES), 1)
    first_row, last_row = tile_row == 0, tile_row == part - 1
    first_lane, last_lane = tile_lane == 0, tile_lane == LANES - 1
    count = cy // part
    columns = cx // LANES

    def update(k, _):
        from_south, from_north = south[pl.ds(k, 1), :], north[pl.ds(k, 1), :]

        def load(c, n):
            rows, lanes = slice(c * part, (c + 1) * part), slice(n * LANES, (n + 1) * LANES)
            return sea[rows, lanes] * th[k, rows, lanes]

        def across(n, vector):
            return jnp.broadcast_to(vector[:, n * LANES:(n + 1) * LANES], (part, LANES))

        value = [load(0, n) for n in range(columns)]
        before = [across(n, from_south) for n in range(columns)]
        up = [pltpu.roll(v, part - 1, 0) for v in value]
        for c in range(count):
            rows = slice(c * part, (c + 1) * part)
            if c + 1 < count:
                following = [load(c + 1, n) for n in range(columns)]
                up_next = [pltpu.roll(v, part - 1, 0) for v in following]
            else:
                following, up_next = None, [across(n, from_north) for n in range(columns)]
            down = [pltpu.roll(v, 1, 0) for v in value]
            right = [pltpu.roll(west[rows, :], LANES - levels - k, 1)] + [pltpu.roll(v, 1, 1) for v in value]
            left = [pltpu.roll(v, LANES - 1, 1) for v in value] + [pltpu.roll(east[rows, :], LANES - 1 - k, 1)]
            for n in range(columns):
                lanes = slice(n * LANES, (n + 1) * LANES)
                beside = jnp.where(first_row, before[n], down[n]) + jnp.where(last_row, up_next[n], up[n])
                beside = beside + jnp.where(first_lane, right[n], right[n + 1])
                beside = beside + jnp.where(last_lane, left[n + 1], left[n])
                out_theta[k, rows, lanes] = th[k, rows, lanes] + kp[rows, lanes] * (beside - 4.0 * value[n])
            value, before, up = following, down, up_next
        return 0

    lax.fori_loop(0, levels, update, 0)
    whole(parts.at[pl.ds(0, total - 1), :], red_recv).wait()
    out_parts[...] = parts[...]
    out_basis[...] = basis[0:BASIS - 1, 0:nlat, own_start:own_start + strip, :]

    whole(ext.at[0:nlat - 1, 0:SPAN, :], main_send).wait()
    left_edge.wait_send()
    right_edge.wait_send()
    diag_up.wait_send()
    diag_down.wait_send()
    diag_fold.wait_send()
    for far, near, own in sides:
        @pl.when(jnp.logical_not(own))
        def _():
            far.wait_send()

    @pl.when(top)
    def _():
        whole(tiles, fold_send).wait()
        fold_low.wait_send()

        @pl.when(jnp.logical_not(far_self))
        def _():
            fold_far.wait_send()

    @pl.when(j > 0)
    def _():
        to_south.wait_send()

    to_north.wait_send()
    to_west.wait_send()
    to_east.wait_send()
    whole(parts.at[pl.ds(0, total - 1), :], red_send).wait()


def finish(fresh, vectors, parts, out_theta, out_psi, psi, out_sem):
    pieces_of = fresh.shape[0] // 2
    stores = [
        pltpu.make_async_copy(fresh.at[pl.ds(2 * q, 2)], out_theta.at[pl.ds(2 * q, 2)], out_sem.at[0])
        for q in range(pieces_of)
    ]
    for copy in stores:
        copy.start()
    total = parts.shape[0]
    value = parts[...]
    error = jnp.zeros_like(value)
    half = total // 2
    while half >= 8:
        value, e = two_sum(value[:half], value[half:])
        error = error[:half] + error[half:] + e
        half //= 2
    for shift in (4, 2, 1):
        value, e = two_sum(value, pltpu.roll(value, shift, 0))
        error = error + pltpu.roll(error, shift, 0) + e
    lane = iota((1, LANES), 1)
    error = jnp.where(
        jnp.logical_and(lane >= SLOTS, lane < 2 * SLOTS), pltpu.roll(error[0:1], SLOTS, 1), 0.0
    )
    message = value[0:1] + error
    high, low = quick(message, pltpu.roll(message, LANES - SLOTS, 1))

    gram = {}
    for n, (a, b) in enumerate(PAIRS):
        gram[a, b] = gram[b, a] = tuple(
            jnp.broadcast_to(x[:, n:n + 1], (1, LANES)) for x in (high, low)
        )
    size = BASIS - 1

    def scaled(x, factor):
        return x[0] * factor, x[1] * factor

    matrix = [
        [
            df_add(
                scaled(gram[a, b + 1], 4.0),
                df_add(scaled(gram[a, b], 4.0), gram[a, b]),
            )
            for b in range(size)
        ]
        for a in range(size)
    ]
    right = [gram[0, a] for a in range(size)]
    for p in range(size):
        for a in range(p + 1, size):
            factor = df_div(matrix[a][p], matrix[p][p])
            for b in range(p + 1, size):
                matrix[a][b] = df_sub(matrix[a][b], df_mul(factor, matrix[p][b]))
            right[a] = df_sub(right[a], df_mul(factor, right[p]))
    answer = [None] * size
    for p in reversed(range(size)):
        value = right[p]
        for b in range(p + 1, size):
            value = df_sub(value, df_mul(matrix[p][b], answer[b]))
        answer[p] = df_div(value, matrix[p][p])
    strip = psi.shape[0]
    spread = [jnp.broadcast_to(x[0], (strip, LANES)) for x in answer]

    def combine(c, _):
        lanes = pl.ds(pl.multiple_of(c * LANES, LANES), LANES)
        value = spread[size - 1] * vectors[size - 1, c]
        for b in reversed(range(size - 1)):
            value = value + spread[b] * vectors[b, c]
        psi[:, lanes] = value
        return 0

    lax.fori_loop(0, vectors.shape[1], combine, 0)

    store_psi = pltpu.make_async_copy(psi, out_psi, out_sem.at[1])
    store_psi.start()
    store_psi.wait()
    pltpu.make_async_copy(fresh, out_theta, out_sem.at[0]).wait()


def per_device(nlon, nlat, theta, kappa, layer_weight, diag, land_blocks):
    levels, cy, cx = theta.shape
    strip, ny = diag.shape
    wide = strip + 2 * HALO
    vmem = pl.BlockSpec(memory_space=pltpu.VMEM)
    hbm = pl.BlockSpec(memory_space=pltpu.HBM)
    dma = pltpu.SemaphoreType.DMA
    operands = (layer_weight, land_blocks, theta, kappa, diag)
    fresh, vectors, parts = pl.pallas_call(
        functools.partial(kernel, nlon, nlat),
        out_shape=(
            jax.ShapeDtypeStruct(theta.shape, F32),
            jax.ShapeDtypeStruct((BASIS - 1, nlat, strip, cy), F32),
            jax.ShapeDtypeStruct((nlon * nlat, LANES), F32),
        ),
        in_specs=[hbm] * 5,
        out_specs=(vmem, vmem, vmem),
        scratch_shapes=[
            pltpu.SMEM(layer_weight.shape, F32),
            pltpu.VMEM(land_blocks.shape, jnp.int32),
            pltpu.VMEM((levels, cy, cx), F32),
            pltpu.VMEM((cy, cx), F32),
            pltpu.VMEM((cy, cx), F32),
            pltpu.VMEM((cx + 2 * HALO, cy), F32),
            pltpu.VMEM((nlat, 8, LANES), F32),
            pltpu.VMEM((nlat, wide, cy), F32),
            pltpu.VMEM((2, HALO, cy), F32),
            pltpu.VMEM((nlat, wide, cy), F32),
            pltpu.VMEM((nlat, HALO, cy), F32),
            pltpu.VMEM((BODY, LANES), F32),
            pltpu.VMEM((nlat, LANES), F32),
            pltpu.VMEM((strip, ny), F32),
            pltpu.VMEM((nlat + 1, wide, cy), F32),
            pltpu.VMEM((wide, ny + LANES), F32),
            pltpu.VMEM((wide, ny + LANES), F32),
            pltpu.VMEM((wide, ny + LANES), F32),
            pltpu.VMEM((BASIS, nlat + 1, strip + 2 * INNER + 2 * PAD, cy), F32),
            pltpu.VMEM((2, levels, cx), F32),
            pltpu.VMEM((levels, cx), F32),
            pltpu.VMEM((levels, cx), F32),
            pltpu.VMEM((cy, LANES), F32),
            pltpu.VMEM((cy, LANES), F32),
            pltpu.VMEM((cy, LANES), F32),
            pltpu.VMEM((nlat, 8, LANES), F32),
            pltpu.VMEM((8, LANES), F32),
            pltpu.VMEM((8, LANES), F32),
            pltpu.VMEM((nlon * nlat, LANES), F32),
            dma((8,)),
            dma,
            dma,
            dma((2,)),
            dma,
            dma,
            dma,
            dma,
            dma((2,)),
            dma((5,)),
            dma((5,)),
            dma((4,)),
            dma((4,)),
            dma,
            dma,
            pltpu.SemaphoreType.REGULAR,
        ],
        compiler_params=pltpu.CompilerParams(
            collective_id=0, has_side_effects=True, vmem_limit_bytes=32 << 20
        ),
        name="ocean_step",
    )(*[pltpu.with_memory_space_constraint(x, pltpu.HBM) for x in operands])
    return pl.pallas_call(
        finish,
        out_shape=(
            jax.ShapeDtypeStruct(theta.shape, F32),
            jax.ShapeDtypeStruct(diag.shape, F32),
        ),
        in_specs=[vmem, vmem, vmem],
        out_specs=(hbm, hbm),
        scratch_shapes=[pltpu.VMEM(diag.shape, F32), dma((2,))],
        compiler_params=pltpu.CompilerParams(vmem_limit_bytes=16 << 20),
        name="ocean_finish",
    )(fresh, vectors, parts)


def solution(mesh):
    placed = (P(None, "lat", "lon"), P("lat", "lon"), P(), P(("lon", "lat"), None), P())
    return jax.shard_map(
        functools.partial(per_device, mesh.shape["lon"], mesh.shape["lat"]),
        mesh=mesh,
        in_specs=placed,
        out_specs=(P(None, "lat", "lon"), P(("lon", "lat"), None)),
        check_vma=False,
    )
```

```python
import functools

import jax
import jax.numpy as jnp
from jax import lax
from jax.experimental import pallas as pl
from jax.experimental.pallas import tpu as pltpu
from jax.sharding import PartitionSpec as P

MESH = pl.DeviceIdType.MESH
BS = 32
HALO = 8
PAD = 8
INNER = 4
BODY = 24
SPAN = BODY + 3
LANES = 128
F32 = jnp.float32
BF16 = jnp.bfloat16
BASIS = 5
PAIRS = [(a, b) for a in range(BASIS) for b in range(a, BASIS) if a < BASIS - 1]
SLOTS = 16


def iota(shape, axis):
    return lax.broadcasted_iota(jnp.int32, shape, axis)


def hot(condition):
    return jnp.where(condition, 1.0, 0.0).astype(BF16)


def bdot(left, right):
    return jnp.dot(left, right, preferred_element_type=F32)


def ndot(left, right):
    return lax.dot_general(left, right, (((1,), (1,)), ((), ())), preferred_element_type=F32)


def pieces(value):
    first = value.astype(BF16)
    rest = value - first.astype(F32)
    second = rest.astype(BF16)
    third = (rest - second.astype(F32)).astype(BF16)
    return [first, second, third]


def flip_lanes(value):
    width = value.shape[1]
    turn = hot(iota((width, width), 0) + iota((width, width), 1) == width - 1)
    parts = [bdot(piece, turn) for piece in pieces(value)]
    return (parts[0] + parts[1]) + parts[2]


def flip_rows(value, groups):
    count = value.shape[0]
    row = iota((count, count), 0)
    ends, start = jnp.zeros((count, count), jnp.int32), 0
    for size in groups:
        ends = jnp.where(row >= start, 2 * start + size - 1, ends)
        start += size
    turn = hot(row + iota((count, count), 1) == ends)
    parts = [bdot(turn, piece) for piece in pieces(value)]
    return (parts[0] + parts[1]) + parts[2]


def two_sum(a, b):
    s = a + b
    t = s - a
    return s, (a - (s - t)) + (b - t)


def halves(a):
    t = a * 4097.0
    high = t - (t - a)
    return high, a - high


def two_prod(a, b):
    p = a * b
    ah, al = halves(a)
    bh, bl = halves(b)
    return p, ((ah * bh - p) + ah * bl + al * bh) + al * bl


def quick(a, b):
    s = a + b
    return s, b - (s - a)


def df_mul(x, y):
    p, e = two_prod(x[0], y[0])
    return quick(p, e + (x[0] * y[1] + x[1] * y[0]))


def df_add(x, y):
    s, e = two_sum(x[0], y[0])
    return quick(s, e + (x[1] + y[1]))


def df_sub(x, y):
    return df_add(x, (-y[0], -y[1]))


def df_div(x, y):
    first = x[0] / y[0]
    rest = df_sub(x, df_mul(y, (first, jnp.zeros_like(first))))
    second = rest[0] / y[0]
    return quick(first, second)


def stencil(ref, emit, low, high):
    count, _, width = ref.shape
    lane = iota((high - low, width), 1)
    first, last = lane == 0, lane == width - 1

    def load(c, shift=0):
        return ref[c, low + shift:high + shift, :]

    value = load(0)
    before = jnp.zeros_like(value)
    up = pltpu.roll(value, width - 1, 1)
    for c in range(count):
        if c + 1 < count:
            following = load(c + 1)
            up_next = pltpu.roll(following, width - 1, 1)
        else:
            following, up_next = None, up
        down = pltpu.roll(value, 1, 1)
        beside = jnp.where(first, before, down) + jnp.where(last, up_next, up)
        emit(c, value, (beside + load(c, -1)) + load(c, 1))
        value, before, up = following, down, up_next


def kernel(
    nlon, nlat,
    weight_in, land_in, theta, kappa, diag,
    out_theta, out_basis, out_parts,
    weight, land, th, kp, sea, turned, windows, packs, edge_packs, ext, edge, crossing, lined_here, flat, dgx, dg, ocs, quarter, basis, rows_out, north, south, cols_out, east, west,
    tiles, fold, fold_edge, parts,
    in_sem, main_send, main_recv, edge_send, edge_recv, fold_send, fold_low_send, fold_far_send, fold_recv,
    diag_send, diag_recv, halo_send, halo_recv, red_send, red_recv, ready,
):
    levels, cy, cx = th.shape
    ny, nx = cy * nlat, cx * nlon
    strip = cx // nlat
    wide = strip + 2 * HALO
    by, bx = land.shape
    total = nlon * nlat
    i = lax.axis_index("lon")
    j = lax.axis_index("lat")
    t = i * nlat + j
    top = j == nlat - 1
    ends = jnp.logical_or(j == 0, top)

    def remote(src, dst, send, recv, lon, lat):
        return pltpu.make_async_remote_copy(
            src_ref=src, dst_ref=dst, send_sem=send, recv_sem=recv,
            device_id=(lon, lat), device_id_type=MESH,
        )

    def lon_of(value):
        return lax.rem(value + 2 * nlon, nlon)

    def lat_of(value):
        return lax.rem(value + 2 * nlat, nlat)

    def whole(ref, sem):
        return pltpu.make_async_copy(ref, ref, sem)

    def greet(lon, lat):
        pl.semaphore_signal(barrier, inc=1, device_id=(lon, lat), device_id_type=MESH)

    def ring(value, size):
        return min(value, size - value)

    lat_order = sorted(range(1, nlat), key=lambda d: -ring(d // 4, nlat // 4) - ring(d % 4, 4))
    lon_order = sorted(range(1, nlon), key=lambda d: -ring(d // 2, nlon // 2) - 0.5 * (d % 2))

    dgx[nlat, 0:HALO, :] = jnp.zeros((HALO, cy), F32)
    dgx[nlat, HALO + strip:, :] = jnp.zeros((HALO, cy), F32)

    barrier = pltpu.get_barrier_semaphore()
    for d in lat_order:
        greet(i, lax.rem(j + d, nlat))
    for d in lon_order:
        greet(lax.rem(i + d, nlon), j)
    greet(nlon - 1 - i, nlat - 1)
    for shift in (1, 0, -1):
        other = lax.rem(total - 1 - t + shift + total, total)

        @pl.when(other != t)
        def _():
            greet(other // nlat, lax.rem(other, nlat))

    @pl.when(j == 0)
    def _():
        for lat in range(nlat):
            greet(lon_of(i - 1), lat)
        greet(lon_of(nlon - i), nlat - 1)

    @pl.when(top)
    def _():
        for lat in range(nlat):
            greet(lon_of(i + 1), lat)

    chunk = levels // 4
    loads = [
        pltpu.make_async_copy(theta.at[pl.ds(q * chunk, chunk)], th.at[pl.ds(q * chunk, chunk)], in_sem.at[q])
        for q in range(4)
    ]
    load_kappa = pltpu.make_async_copy(kappa, kp, in_sem.at[4])
    load_diag = pltpu.make_async_copy(diag, flat, in_sem.at[5])
    load_weight = pltpu.make_async_copy(weight_in, weight, in_sem.at[6])
    load_land = pltpu.make_async_copy(land_in, land, in_sem.at[7])
    load_kappa.start()
    load_weight.start()
    for copy in loads:
        copy.start()
    load_diag.start()
    load_land.start()


    load_land.wait()
    table = land[...].astype(F32).astype(BF16)
    row_block = (j * cy + iota((cy, by), 0)) >> 5
    on_rows = bdot(hot(row_block == iota((cy, by), 1)), table).astype(BF16)
    col_block = (i * cx + iota((bx, cx), 1)) >> 5
    cols_hot = hot(col_block == iota((bx, cx), 0))
    sea[...] = bdot(on_rows, cols_hot)
    load_kappa.wait()
    kp[...] = sea[...] * kp[...]
    load_weight.wait()
    column = jnp.zeros((cy, cx), F32)
    for q in range(4):
        loads[q].wait()
        for k in range(q * chunk, (q + 1) * chunk):
            column = column + weight[k] * th[k]
    held, rate = sea[...] * column, kp[...]
    block_row, block_lane = iota((cy, cx), 0), iota((cy, cx), 1)
    beside = jnp.where(block_row == 0, 0.0, pltpu.roll(held, 1, 0))
    beside = beside + jnp.where(block_row == cy - 1, 0.0, pltpu.roll(held, cy - 1, 0))
    beside = beside + jnp.where(block_lane == 0, 0.0, pltpu.roll(held, 1, 1))
    beside = beside + jnp.where(block_lane == cx - 1, 0.0, pltpu.roll(held, cx - 1, 1))
    force = held + rate * (beside - 4.0 * held)
    turned[0:HALO, :] = jnp.zeros((HALO, cy), F32)
    turned[HALO + cx:, :] = jnp.zeros((HALO, cy), F32)
    turned[HALO:HALO + cx, :] = force.T

    lane = iota((cy, LANES), 1)
    ring_columns = jnp.where(
        lane < 2,
        jnp.where(lane == 0, rate[:, 0:LANES], pltpu.roll(held[:, 0:LANES], 1, 1)),
        jnp.where(
            lane == 2, pltpu.roll(rate[:, cx - LANES:], 3, 1), pltpu.roll(held[:, cx - LANES:], 4, 1)
        ),
    )
    ring_rows = ring_columns.T[0:8]

    lines = jnp.concatenate([rate[0:1], rate[cy - 1:], held[0:1], held[cy - 1:]] * 2, axis=0)
    for m in range(nlat):
        windows[m] = pltpu.roll(lines, (HALO - strip * m) % cx, 1)[:, 0:LANES]
    lanes_here = iota((nlat, LANES), 1)
    lined = windows[:, 0, :]
    for g in range(1, 4):
        lined = jnp.where(lanes_here >= wide * g, pltpu.roll(windows[:, g, :], wide * g, 1), lined)
    for m in range(nlat):
        start = HALO - INNER + strip * m
        packs[m, 0:BODY, :] = turned[start:start + BODY, :]
        packs[m, BODY:BODY + 1, :] = lined[m:m + 1]
    packs[0, BODY + 1:SPAN, :] = ring_rows[0:2]
    packs[nlat - 1, BODY + 1:SPAN, :] = ring_rows[2:4]
    for n, (start, m) in enumerate(((HALO, nlat - 1), (HALO + cx - INNER, 0))):
        edge_packs[n, 0:INNER, :] = turned[start:start + INNER, :]
        edge_packs[n, INNER:INNER + 1, :] = lined[m:m + 1]
        edge_packs[n, INNER + 1:INNER + 3, :] = ring_rows[2 * n:2 * n + 2]

    @pl.when(top)
    def _():
        lanes8 = iota((8, LANES), 1)
        corner = pltpu.roll(ring_columns[cy - 8:], 3 * wide, 1)
        for m in range(nlat):
            start = strip * (nlat - 1 - m) - HALO
            tile = corner
            for g, field in ((2, held), (1, rate), (0, force)):
                shifted = pltpu.roll(field[cy - 8:], (g * wide - start) % cx, 1)[:, 0:LANES]
                tile = jnp.where(lanes8 < (g + 1) * wide, shifted, tile)
            tiles[m] = tile

    load_diag.wait()
    for c in range(nlat):
        dgx[c, HALO:HALO + strip, :] = flat[:, c * cy:(c + 1) * cy]

    own_folds = [lax.rem(total - 1 - t + shift + total, total) == t for shift in (1, -1)]
    awaited = nlat + nlon + 3 + jnp.where(top, nlat + 1, 0)
    for own in own_folds:
        awaited = awaited - jnp.where(own, 1, 0)
    pl.semaphore_wait(barrier, awaited)
    for d in range(1, nlon):
        pl.semaphore_signal(
            ready, inc=1, device_id=(lax.rem(i + d, nlon), j), device_id_type=MESH
        )

    own_slot = ext.at[j, 0:SPAN, :]

    def block_rows(m):
        return packs.at[m, 0:SPAN, :]

    def main_copy(d):
        m = lax.rem(j + d, nlat)
        return remote(block_rows(m), own_slot, main_send, main_recv, i, m)

    for d in lat_order:
        main_copy(d).start()
    pltpu.make_async_copy(block_rows(j), own_slot, main_recv).start()
    edge_slot = edge.at[j, 0:INNER + 3, :]
    left_edge = remote(
        edge_packs.at[0, 0:INNER + 3, :], edge_slot, edge_send.at[0], edge_recv, lon_of(i - 1), nlat - 1
    )
    right_edge = remote(
        edge_packs.at[1, 0:INNER + 3, :], edge_slot, edge_send.at[1], edge_recv, lon_of(i + 1), 0
    )
    left_edge.start()
    right_edge.start()

    def fold_copy(m):
        return remote(tiles.at[m], fold, fold_send, fold_recv.at[0], nlon - 1 - i, m)

    far_lon = lon_of(nlon - 2 - i)
    far_self = far_lon == i
    fold_far = remote(
        tiles.at[nlat - 1], fold_edge, fold_far_send, fold_recv.at[1], far_lon, nlat - 1
    )
    fold_far_own = pltpu.make_async_copy(tiles.at[nlat - 1], fold_edge, fold_recv.at[1])
    fold_low = remote(tiles.at[0], fold_edge, fold_low_send, fold_recv.at[1], lon_of(nlon - i), 0)

    @pl.when(top)
    def _():
        for m in range(nlat):
            fold_copy(m).start()
        fold_low.start()

        @pl.when(far_self)
        def _():
            fold_far_own.start()

        @pl.when(jnp.logical_not(far_self))
        def _():
            fold_far.start()

    after, before = lax.rem(t + 1, total), lax.rem(t + total - 1, total)
    depth = BASIS - 2
    own_low = slice(HALO, HALO + depth)
    own_high = slice(HALO + strip - depth, HALO + strip)
    halo_low = slice(HALO - depth, HALO)
    halo_high = slice(HALO + strip, HALO + strip + depth)
    diag_up = remote(
        dgx.at[0:nlat, own_high, :], dgx.at[0:nlat, halo_low, :], diag_send.at[0], diag_recv.at[0],
        after // nlat, lax.rem(after, nlat),
    )
    diag_down = remote(
        dgx.at[0:nlat, own_low, :], dgx.at[0:nlat, halo_high, :], diag_send.at[1], diag_recv.at[1],
        before // nlat, lax.rem(before, nlat),
    )
    diag_up.start()
    diag_down.start()
    middle = slice(HALO, HALO + strip)
    diag_fold = remote(
        dgx.at[nlat - 1, middle, :], dgx.at[nlat, middle, :], diag_send.at[2], diag_recv.at[2],
        nlon - 1 - i, nlat - 1 - j,
    )
    diag_fold.start()
    sides = []
    for n, (shift, src, dst) in enumerate(((1, own_low, halo_high), (-1, own_high, halo_low))):
        other = lax.rem(total - 1 - t + shift + total, total)
        src_ref, dst_ref = dgx.at[nlat - 1, src, :], dgx.at[nlat, dst, :]
        sides.append((
            remote(
                src_ref, dst_ref, diag_send.at[3 + n], diag_recv.at[3 + n], other // nlat, lax.rem(other, nlat)
            ),
            pltpu.make_async_copy(src_ref, dst_ref, diag_recv.at[3 + n]),
            own_folds[n],
        ))
    for far, near, own in sides:
        @pl.when(own)
        def _():
            near.start()

        @pl.when(jnp.logical_not(own))
        def _():
            far.start()

    rows_out[0] = th[:, 0, :]
    rows_out[1] = th[:, cy - 1, :]
    to_south = remote(rows_out.at[0], north, halo_send.at[0], halo_recv.at[0], i, lat_of(j - 1))
    to_north = remote(rows_out.at[1], south, halo_send.at[1], halo_recv.at[1], i, lat_of(j + 1))
    to_fold = remote(rows_out.at[1], north, halo_send.at[1], halo_recv.at[0], nlon - 1 - i, j)

    @pl.when(j > 0)
    def _():
        to_south.start()

    @pl.when(jnp.logical_not(top))
    def _():
        to_north.start()

    @pl.when(top)
    def _():
        to_fold.start()

    lane = iota((cy, LANES), 1)
    packed = jnp.zeros((cy, LANES), F32)
    for k in range(levels):
        packed = jnp.where(lane == k, pltpu.roll(th[k, :, 0:LANES], k, 1), packed)
        packed = jnp.where(
            lane == levels + k, pltpu.roll(th[k, :, cx - LANES:cx], levels + k + 1, 1), packed
        )
    cols_out[...] = packed
    to_west = remote(cols_out, east, halo_send.at[2], halo_recv.at[2], lon_of(i - 1), j)
    to_east = remote(cols_out, west, halo_send.at[3], halo_recv.at[3], lon_of(i + 1), j)
    to_west.start()
    to_east.start()

    basis[:, :, 0:PAD, :] = jnp.zeros((BASIS, nlat + 1, PAD, cy), F32)
    tail = PAD + strip + 2 * INNER
    basis[:, :, tail:, :] = jnp.zeros((BASIS, nlat + 1, PAD, cy), F32)

    west_block = lax.rem(i * (cx // BS) + bx - 1, bx)
    east_block = lax.rem((i + 1) * (cx // BS), bx)
    ocean_west = bdot(on_rows, hot(iota((bx, LANES), 0) == west_block))
    ocean_east = bdot(on_rows, hot(iota((bx, LANES), 0) == east_block))
    edge_row = iota((8, by), 0)
    edge_col = iota((8, by), 1)
    south_hot = hot(jnp.logical_and(edge_row == 0, edge_col == j * (cy // BS) - 1))
    north_block = jnp.where(top, by - 1, (j + 1) * (cy // BS))
    north_hot = hot(jnp.logical_and(edge_row == 0, edge_col == north_block))
    north_cols = jnp.where(top, bx - 1 - col_block, col_block)
    ocean_south = bdot(bdot(south_hot, table).astype(BF16), cols_hot)[0:1]
    ocean_north = bdot(
        bdot(north_hot, table).astype(BF16), hot(north_cols == iota((bx, cx), 0))
    )[0:1]

    strip_x = (strip * t - HALO + nx + iota((wide, bx), 0)) % nx >> 5
    strip_hot = hot(strip_x == iota((wide, bx), 1))
    on_cols = ndot(strip_hot, table).astype(BF16)
    ocs[:, 0:ny] = bdot(on_cols, hot((iota((by, ny), 1) >> 5) == iota((by, ny), 0)))
    mirror_hot = hot((bx - 1 - strip_x) == iota((wide, bx), 1))
    on_mirror = ndot(mirror_hot, table).astype(BF16)
    keep = jnp.logical_and(iota((by, LANES), 0) == by - 1, iota((by, LANES), 1) < 8)
    ocs[:, ny:ny + LANES] = bdot(on_mirror, hot(keep))

    diag_up.wait_recv()
    diag_down.wait_recv()
    diag_fold.wait_recv()
    for far, near, own in sides:
        far.wait_recv()
    for c in range(nlat):
        dg[:, c * cy:(c + 1) * cy] = dgx[c]
    dg[:, ny:] = flip_rows(flip_lanes(dgx[nlat]), (wide,))
    dg[...] = ocs[...] * ((dg[...] - 1.0) * 0.25)
    quarter[...] = ocs[...] * 0.25

    whole(ext.at[0:nlat, 0:SPAN, :], main_recv).wait()
    whole(fold, fold_recv.at[0]).wait()

    @pl.when(ends)
    def _():
        whole(edge.at[:, 0:INNER + 3, :], edge_recv).wait()
        whole(fold_edge, fold_recv.at[1]).wait()
        spot = iota((8, LANES), 1)
        outer = jnp.logical_or(
            jnp.logical_and(top, spot % wide < HALO), jnp.logical_and(j == 0, spot % wide >= wide - HALO)
        )
        outer = jnp.logical_and(outer, spot < 3 * wide)
        merged = jnp.where(outer, fold_edge[...], fold[...])
        fold[...] = jnp.where(spot >= 3 * wide + 4, pltpu.roll(fold_edge[...], 4, 1), merged)

    row = iota((3 * wide + 8, LANES), 0)
    source = jnp.where(row < 3 * wide, (row // wide) * wide + wide - 1 - row % wide, row)
    pick = hot(source == iota((3 * wide + 8, LANES), 1))
    reversed_rows = jnp.concatenate(
        [fold[q:q + 1, :] for q in reversed(range(8))] + [jnp.zeros((LANES - 8, LANES), F32)], axis=0
    )
    folded = [ndot(pick, piece) for piece in pieces(reversed_rows)]
    folded = (folded[0] + folded[1]) + folded[2]
    crossing[...] = folded[INNER:INNER + BODY]
    corner_main, corner_edge = folded[3 * wide:3 * wide + 4], folded[3 * wide + 4:]
    lined_here[...] = ext[:, BODY, :]

    def fix_edge(into, inner_row, outer_row, first, mine, theirs):
        spot = iota((nlat, LANES), 1) % wide
        from_edge = spot < HALO if first else spot >= wide - HALO
        lined_here[...] = jnp.where(from_edge, edge[:, INNER, :], lined_here[...])
        ext[:, into:into + INNER, :] = edge[:, 0:INNER, :]
        ext[:, outer_row, :] = ext[:, outer_row, :] + edge[:, INNER + 1, :] * ext[:, BODY + 2, :]
        ext[:, inner_row, :] = ext[:, inner_row, :] + ext[:, BODY + 1, :] * edge[:, INNER + 2, :]
        line = iota((BODY, LANES), 0)
        across_out = corner_edge[theirs:theirs + 1] * corner_main[mine + 1:mine + 2]
        across_in = corner_main[mine:mine + 1] * corner_edge[theirs + 1:theirs + 2]
        crossing[...] = crossing[...] + jnp.where(
            line == outer_row, across_out, jnp.where(line == inner_row, across_in, 0.0)
        )

    @pl.when(j == 0)
    def _():
        fix_edge(0, INNER, INNER - 1, True, 2, 0)

    @pl.when(top)
    def _():
        fix_edge(INNER + strip, INNER + strip - 1, INNER + strip, False, 0, 2)

    columns_of = jnp.concatenate(
        [lined_here[...], jnp.zeros((LANES - nlat, LANES), F32)], axis=0
    ).T
    square = (wide, LANES)
    virtual = iota(square, 1) == nlat
    rate_low, rate_high, held_low, held_high = [columns_of[g * wide:(g + 1) * wide] for g in range(4)]
    rate_low = jnp.where(virtual, jnp.broadcast_to(folded[wide:2 * wide, 0:1], square), rate_low)
    held_low = jnp.where(virtual, jnp.broadcast_to(folded[2 * wide:3 * wide, 0:1], square), held_low)
    rows = slice(HALO - INNER, HALO - INNER + BODY)
    add_high = (rate_high * pltpu.roll(held_low, LANES - 1, 1))[rows]
    add_low = (rate_low * pltpu.roll(held_high, 1, 1))[rows]

    def lanes_of(c):
        return slice(c * LANES, (c + 1) * LANES)

    shift = HALO - INNER
    own_start = PAD + INNER
    bottom, ceiling = PAD, PAD + BODY
    body_lane = iota((BODY, LANES), 1)
    for c in range(nlat + 1):
        value = ext[c, 0:BODY, :] if c < nlat else crossing[...]
        value = jnp.where(body_lane == 0, value + add_low[:, c:c + 1], value)
        basis[0, c, bottom:ceiling, :] = jnp.where(
            body_lane == LANES - 1, value + add_high[:, c:c + 1], value
        )
    for step in range(BASIS - 1):
        low, high = (bottom, ceiling) if step < BASIS - 2 else (own_start, own_start + strip)

        def store_next(c, value, beside):
            lanes, rows = lanes_of(c), slice(low - PAD + shift, high - PAD + shift)
            basis[step + 1, c, low:high, :] = dg[rows, lanes] * value - quarter[rows, lanes] * beside

        stencil(basis.at[step], store_next, low, high)

    zero = jnp.zeros((8, LANES), F32)

    def accumulate(c, carry):
        sums = list(carry)
        for h in range(strip // 8):
            start = own_start + 8 * h
            values = [basis[b, c, start:start + 8, :] for b in range(BASIS)]
            split = [halves(value) for value in values]
            for n, (a, b) in enumerate(PAIRS):
                (ah, al), (bh, bl) = split[a], split[b]
                e = ah * bl + al * values[b]
                s, f = quick(sums[2 * n], ah * bh)
                sums[2 * n], sums[2 * n + 1] = s, sums[2 * n + 1] + (e + f)
        return tuple(sums)

    sums = lax.fori_loop(0, ny // LANES, accumulate, (zero,) * (2 * len(PAIRS)))
    packed_sums = [(sums[2 * n], sums[2 * n + 1]) for n in range(len(PAIRS))]
    packed_sums += [(zero, zero)] * (SLOTS - len(PAIRS))
    eight = iota((8, LANES), 0)
    for shift in (4, 2, 1):
        keep_row = (eight & shift) == 0
        merged = []
        for n in range(0, len(packed_sums), 2):
            (ah, al), (bh, bl) = packed_sums[n:n + 2]
            h, e = two_sum(
                jnp.where(keep_row, ah, pltpu.roll(bh, shift, 0)),
                jnp.where(keep_row, pltpu.roll(ah, 8 - shift, 0), bh),
            )
            l = jnp.where(keep_row, al, pltpu.roll(bl, shift, 0))
            l = l + jnp.where(keep_row, pltpu.roll(al, 8 - shift, 0), bl)
            merged.append((h, l + e))
        packed_sums = merged
    high, low = [jnp.concatenate([packed_sums[0][n], packed_sums[1][n]], axis=0) for n in range(2)]
    place = iota((SLOTS, LANES), 0)
    within = place & 7
    place = (place & 8) + ((within & 4) >> 2) + (within & 2) + ((within & 1) << 2)
    shift = LANES // 2
    while shift:
        high, e = two_sum(high, pltpu.roll(high, shift, 1))
        low = low + pltpu.roll(low, shift, 1) + e
        shift //= 2
    spot = iota((SLOTS, LANES), 1)
    packed = jnp.where(spot == place, high, jnp.where(spot == place + SLOTS, low, 0.0))
    message = jnp.sum(packed, axis=0, keepdims=True)

    parts[pl.ds(t, 1), :] = message
    own_part = parts.at[pl.ds(t, 1), :]
    sizes = (nlon // 2, 2, nlat // 4, 4)
    offsets = [
        (a, b, c, d)
        for a in range(sizes[0]) for b in range(sizes[1]) for c in range(sizes[2]) for d in range(sizes[3])
    ]

    def hops(offset):
        return sum(min(o, n - o) for o, n in zip(offset, sizes) if n > 2 or o) - 0.5 * offset[1]

    offsets = sorted(offsets[1:], key=hops, reverse=True)
    place_of = (i // 2, lax.rem(i, 2), j // 4, lax.rem(j, 4))
    moved = [
        [lax.rem(place_of[n] + o, sizes[n]) * scale for o in range(sizes[n])]
        for n, scale in enumerate((2, 1, 4, 1))
    ]
    pl.semaphore_wait(ready, nlon - 1)
    for a, b, c, d in offsets:
        remote(own_part, own_part, red_send, red_recv, moved[0][a] + moved[1][b], moved[2][c] + moved[3][d]).start()

    to_south.wait_recv()
    to_west.wait_recv()
    to_east.wait_recv()

    @pl.when(j > 0)
    def _():
        to_north.wait_recv()

    @pl.when(j == 0)
    def _():
        south[...] = jnp.zeros_like(south)

    @pl.when(top)
    def _():
        north[...] = flip_lanes(north[...])

    west[...] = west[...] * ocean_west
    east[...] = east[...] * ocean_east
    north[...] = ocean_north * north[...]
    south[...] = ocean_south * south[...]
    part = 32
    tile_row, tile_lane = iota((part, LANES), 0), iota((part, LANES), 1)
    first_row, last_row = tile_row == 0, tile_row == part - 1
    first_lane, last_lane = tile_lane == 0, tile_lane == LANES - 1
    count = cy // part
    columns = cx // LANES

    def update(k, _):
        from_south, from_north = south[pl.ds(k, 1), :], north[pl.ds(k, 1), :]

        def load(c, n):
            rows, lanes = slice(c * part, (c + 1) * part), slice(n * LANES, (n + 1) * LANES)
            return sea[rows, lanes] * th[k, rows, lanes]

        def across(n, vector):
            return jnp.broadcast_to(vector[:, n * LANES:(n + 1) * LANES], (part, LANES))

        value = [load(0, n) for n in range(columns)]
        before = [across(n, from_south) for n in range(columns)]
        up = [pltpu.roll(v, part - 1, 0) for v in value]
        for c in range(count):
            rows = slice(c * part, (c + 1) * part)
            if c + 1 < count:
                following = [load(c + 1, n) for n in range(columns)]
                up_next = [pltpu.roll(v, part - 1, 0) for v in following]
            else:
                following, up_next = None, [across(n, from_north) for n in range(columns)]
            down = [pltpu.roll(v, 1, 0) for v in value]
            right = [pltpu.roll(west[rows, :], LANES - levels - k, 1)] + [pltpu.roll(v, 1, 1) for v in value]
            left = [pltpu.roll(v, LANES - 1, 1) for v in value] + [pltpu.roll(east[rows, :], LANES - 1 - k, 1)]
            for n in range(columns):
                lanes = slice(n * LANES, (n + 1) * LANES)
                beside = jnp.where(first_row, before[n], down[n]) + jnp.where(last_row, up_next[n], up[n])
                beside = beside + jnp.where(first_lane, right[n], right[n + 1])
                beside = beside + jnp.where(last_lane, left[n + 1], left[n])
                out_theta[k, rows, lanes] = th[k, rows, lanes] + kp[rows, lanes] * (beside - 4.0 * value[n])
            value, before, up = following, down, up_next
        return 0

    lax.fori_loop(0, levels, update, 0)
    whole(parts.at[pl.ds(0, total - 1), :], red_recv).wait()
    out_parts[...] = parts[...]
    out_basis[...] = basis[0:BASIS - 1, 0:nlat, own_start:own_start + strip, :]

    whole(ext.at[0:nlat - 1, 0:SPAN, :], main_send).wait()
    left_edge.wait_send()
    right_edge.wait_send()
    diag_up.wait_send()
    diag_down.wait_send()
    diag_fold.wait_send()
    for far, near, own in sides:
        @pl.when(jnp.logical_not(own))
        def _():
            far.wait_send()

    @pl.when(top)
    def _():
        whole(tiles, fold_send).wait()
        fold_low.wait_send()

        @pl.when(jnp.logical_not(far_self))
        def _():
            fold_far.wait_send()

    @pl.when(j > 0)
    def _():
        to_south.wait_send()

    to_north.wait_send()
    to_west.wait_send()
    to_east.wait_send()
    whole(parts.at[pl.ds(0, total - 1), :], red_send).wait()


def finish(fresh, vectors, parts, out_theta, out_psi, psi, out_sem):
    pieces_of = fresh.shape[0] // 2
    stores = [
        pltpu.make_async_copy(fresh.at[pl.ds(2 * q, 2)], out_theta.at[pl.ds(2 * q, 2)], out_sem.at[0])
        for q in range(pieces_of)
    ]
    for copy in stores:
        copy.start()
    total = parts.shape[0]
    value = parts[...]
    error = jnp.zeros_like(value)
    half = total // 2
    while half >= 8:
        value, e = two_sum(value[:half], value[half:])
        error = error[:half] + error[half:] + e
        half //= 2
    for shift in (4, 2, 1):
        value, e = two_sum(value, pltpu.roll(value, shift, 0))
        error = error + pltpu.roll(error, shift, 0) + e
    lane = iota((1, LANES), 1)
    error = jnp.where(
        jnp.logical_and(lane >= SLOTS, lane < 2 * SLOTS), pltpu.roll(error[0:1], SLOTS, 1), 0.0
    )
    message = value[0:1] + error
    high, low = quick(message, pltpu.roll(message, LANES - SLOTS, 1))

    gram = {}
    for n, (a, b) in enumerate(PAIRS):
        gram[a, b] = gram[b, a] = tuple(
            jnp.broadcast_to(x[:, n:n + 1], (1, LANES)) for x in (high, low)
        )
    size = BASIS - 1

    def scaled(x, factor):
        return x[0] * factor, x[1] * factor

    row = iota((8, LANES), 0)

    def stacked(entries):
        return tuple(
            jnp.where(row == 0, e[0], jnp.where(row == 1, e[1], jnp.where(row == 2, e[2], e[3])))
            for e in zip(*entries)
        )

    columns = [stacked([gram[a, b] for a in range(size)]) for b in range(size + 1)]
    right = columns[0]
    columns = [
        df_add(scaled(columns[b + 1], 4.0), df_add(scaled(columns[b], 4.0), columns[b]))
        for b in range(size)
    ]

    def pivot_row(x, p):
        return tuple(jnp.broadcast_to(v[p:p + 1], (8, LANES)) for v in x)

    for p in range(size):
        pivot = pivot_row(columns[p], p)
        factor = df_div(columns[p], pivot)
        factor = tuple(jnp.where(row == p, 0.0, f) for f in factor)
        for b in range(p + 1, size):
            columns[b] = df_sub(columns[b], df_mul(factor, pivot_row(columns[b], p)))
        right = df_sub(right, df_mul(factor, pivot_row(right, p)))
    diagonal = stacked([tuple(v[p:p + 1] for v in columns[p]) for p in range(size)])
    answer = df_div(right, diagonal)
    answer = [(answer[0][p:p + 1],) for p in range(size)]
    strip = psi.shape[0]
    spread = [jnp.broadcast_to(x[0], (strip, LANES)) for x in answer]

    def combine(c, _):
        lanes = pl.ds(pl.multiple_of(c * LANES, LANES), LANES)
        value = spread[size - 1] * vectors[size - 1, c]
        for b in reversed(range(size - 1)):
            value = value + spread[b] * vectors[b, c]
        psi[:, lanes] = value
        return 0

    lax.fori_loop(0, vectors.shape[1], combine, 0)

    store_psi = pltpu.make_async_copy(psi, out_psi, out_sem.at[1])
    store_psi.start()
    store_psi.wait()
    pltpu.make_async_copy(fresh, out_theta, out_sem.at[0]).wait()


def per_device(nlon, nlat, theta, kappa, layer_weight, diag, land_blocks):
    levels, cy, cx = theta.shape
    strip, ny = diag.shape
    wide = strip + 2 * HALO
    vmem = pl.BlockSpec(memory_space=pltpu.VMEM)
    hbm = pl.BlockSpec(memory_space=pltpu.HBM)
    dma = pltpu.SemaphoreType.DMA
    operands = (layer_weight, land_blocks, theta, kappa, diag)
    fresh, vectors, parts = pl.pallas_call(
        functools.partial(kernel, nlon, nlat),
        out_shape=(
            jax.ShapeDtypeStruct(theta.shape, F32),
            jax.ShapeDtypeStruct((BASIS - 1, nlat, strip, cy), F32),
            jax.ShapeDtypeStruct((nlon * nlat, LANES), F32),
        ),
        in_specs=[hbm] * 5,
        out_specs=(vmem, vmem, vmem),
        scratch_shapes=[
            pltpu.SMEM(layer_weight.shape, F32),
            pltpu.VMEM(land_blocks.shape, jnp.int32),
            pltpu.VMEM((levels, cy, cx), F32),
            pltpu.VMEM((cy, cx), F32),
            pltpu.VMEM((cy, cx), F32),
            pltpu.VMEM((cx + 2 * HALO, cy), F32),
            pltpu.VMEM((nlat, 8, LANES), F32),
            pltpu.VMEM((nlat, wide, cy), F32),
            pltpu.VMEM((2, HALO, cy), F32),
            pltpu.VMEM((nlat, wide, cy), F32),
            pltpu.VMEM((nlat, HALO, cy), F32),
            pltpu.VMEM((BODY, LANES), F32),
            pltpu.VMEM((nlat, LANES), F32),
            pltpu.VMEM((strip, ny), F32),
            pltpu.VMEM((nlat + 1, wide, cy), F32),
            pltpu.VMEM((wide, ny + LANES), F32),
            pltpu.VMEM((wide, ny + LANES), F32),
            pltpu.VMEM((wide, ny + LANES), F32),
            pltpu.VMEM((BASIS, nlat + 1, strip + 2 * INNER + 2 * PAD, cy), F32),
            pltpu.VMEM((2, levels, cx), F32),
            pltpu.VMEM((levels, cx), F32),
            pltpu.VMEM((levels, cx), F32),
            pltpu.VMEM((cy, LANES), F32),
            pltpu.VMEM((cy, LANES), F32),
            pltpu.VMEM((cy, LANES), F32),
            pltpu.VMEM((nlat, 8, LANES), F32),
            pltpu.VMEM((8, LANES), F32),
            pltpu.VMEM((8, LANES), F32),
            pltpu.VMEM((nlon * nlat, LANES), F32),
            dma((8,)),
            dma,
            dma,
            dma((2,)),
            dma,
            dma,
            dma,
            dma,
            dma((2,)),
            dma((5,)),
            dma((5,)),
            dma((4,)),
            dma((4,)),
            dma,
            dma,
            pltpu.SemaphoreType.REGULAR,
        ],
        compiler_params=pltpu.CompilerParams(
            collective_id=0, has_side_effects=True, vmem_limit_bytes=32 << 20
        ),
        name="ocean_step",
    )(*[pltpu.with_memory_space_constraint(x, pltpu.HBM) for x in operands])
    return pl.pallas_call(
        finish,
        out_shape=(
            jax.ShapeDtypeStruct(theta.shape, F32),
            jax.ShapeDtypeStruct(diag.shape, F32),
        ),
        in_specs=[vmem, vmem, vmem],
        out_specs=(hbm, hbm),
        scratch_shapes=[pltpu.VMEM(diag.shape, F32), dma((2,))],
        compiler_params=pltpu.CompilerParams(vmem_limit_bytes=16 << 20),
        name="ocean_finish",
    )(fresh, vectors, parts)


def solution(mesh):
    placed = (P(None, "lat", "lon"), P("lat", "lon"), P(), P(("lon", "lat"), None), P())
    return jax.shard_map(
        functools.partial(per_device, mesh.shape["lon"], mesh.shape["lat"]),
        mesh=mesh,
        in_specs=placed,
        out_specs=(P(None, "lat", "lon"), P(("lon", "lat"), None)),
        check_vma=False,
    )
```

```python
import functools

import jax
import jax.numpy as jnp
from jax import lax
from jax.experimental import pallas as pl
from jax.experimental.pallas import tpu as pltpu
from jax.sharding import PartitionSpec as P

MESH = pl.DeviceIdType.MESH
BS = 32
HALO = 8
PAD = 8
INNER = 4
BODY = 24
SPAN = BODY + 3
LANES = 128
F32 = jnp.float32
BF16 = jnp.bfloat16
BASIS = 5
PAIRS = [(a, b) for a in range(BASIS) for b in range(a, BASIS) if a < BASIS - 1]
SLOTS = 16


def iota(shape, axis):
    return lax.broadcasted_iota(jnp.int32, shape, axis)


def hot(condition):
    return jnp.where(condition, 1.0, 0.0).astype(BF16)


def bdot(left, right):
    return jnp.dot(left, right, preferred_element_type=F32)


def ndot(left, right):
    return lax.dot_general(left, right, (((1,), (1,)), ((), ())), preferred_element_type=F32)


def pieces(value):
    first = value.astype(BF16)
    rest = value - first.astype(F32)
    second = rest.astype(BF16)
    third = (rest - second.astype(F32)).astype(BF16)
    return [first, second, third]


def flip_lanes(value):
    width = value.shape[1]
    turn = hot(iota((width, width), 0) + iota((width, width), 1) == width - 1)
    parts = [bdot(piece, turn) for piece in pieces(value)]
    return (parts[0] + parts[1]) + parts[2]


def flip_rows(value, groups):
    count = value.shape[0]
    row = iota((count, count), 0)
    ends, start = jnp.zeros((count, count), jnp.int32), 0
    for size in groups:
        ends = jnp.where(row >= start, 2 * start + size - 1, ends)
        start += size
    turn = hot(row + iota((count, count), 1) == ends)
    parts = [bdot(turn, piece) for piece in pieces(value)]
    return (parts[0] + parts[1]) + parts[2]


def two_sum(a, b):
    s = a + b
    t = s - a
    return s, (a - (s - t)) + (b - t)


def halves(a):
    t = a * 4097.0
    high = t - (t - a)
    return high, a - high


def two_prod(a, b):
    p = a * b
    ah, al = halves(a)
    bh, bl = halves(b)
    return p, ((ah * bh - p) + ah * bl + al * bh) + al * bl


def quick(a, b):
    s = a + b
    return s, b - (s - a)


def df_mul(x, y):
    p, e = two_prod(x[0], y[0])
    return quick(p, e + (x[0] * y[1] + x[1] * y[0]))


def df_add(x, y):
    s, e = two_sum(x[0], y[0])
    return quick(s, e + (x[1] + y[1]))


def df_sub(x, y):
    return df_add(x, (-y[0], -y[1]))


def df_div(x, y):
    first = x[0] / y[0]
    rest = df_sub(x, df_mul(y, (first, jnp.zeros_like(first))))
    second = rest[0] / y[0]
    return quick(first, second)


def stencil(ref, emit, low, high):
    count, _, width = ref.shape
    lane = iota((high - low, width), 1)
    first, last = lane == 0, lane == width - 1

    def load(c, shift=0):
        return ref[c, low + shift:high + shift, :]

    value = load(0)
    before = jnp.zeros_like(value)
    up = pltpu.roll(value, width - 1, 1)
    for c in range(count):
        if c + 1 < count:
            following = load(c + 1)
            up_next = pltpu.roll(following, width - 1, 1)
        else:
            following, up_next = None, up
        down = pltpu.roll(value, 1, 1)
        beside = jnp.where(first, before, down) + jnp.where(last, up_next, up)
        emit(c, value, (beside + load(c, -1)) + load(c, 1))
        value, before, up = following, down, up_next


def kernel(
    nlon, nlat,
    weight_in, land_in, theta, kappa, diag,
    out_theta, out_basis, out_parts,
    weight, land, th, kp, sea, turned, windows, packs, edge_packs, ext, edge, crossing, lined_here, flat, dgx, dg, ocs, quarter, basis, rows_out, north, south, cols_out, east, west,
    tiles, fold, fold_edge, parts,
    in_sem, main_send, main_recv, edge_send, edge_recv, fold_send, fold_low_send, fold_far_send, fold_recv,
    diag_send, diag_recv, halo_send, halo_recv, red_send, red_recv, ready,
):
    levels, cy, cx = th.shape
    ny, nx = cy * nlat, cx * nlon
    strip = cx // nlat
    wide = strip + 2 * HALO
    by, bx = land.shape
    total = nlon * nlat
    i = lax.axis_index("lon")
    j = lax.axis_index("lat")
    t = i * nlat + j
    top = j == nlat - 1
    ends = jnp.logical_or(j == 0, top)

    def remote(src, dst, send, recv, lon, lat):
        return pltpu.make_async_remote_copy(
            src_ref=src, dst_ref=dst, send_sem=send, recv_sem=recv,
            device_id=(lon, lat), device_id_type=MESH,
        )

    def lon_of(value):
        return lax.rem(value + 2 * nlon, nlon)

    def lat_of(value):
        return lax.rem(value + 2 * nlat, nlat)

    def whole(ref, sem):
        return pltpu.make_async_copy(ref, ref, sem)

    def greet(lon, lat):
        pl.semaphore_signal(barrier, inc=1, device_id=(lon, lat), device_id_type=MESH)

    def ring(value, size):
        return min(value, size - value)

    lat_order = sorted(range(1, nlat), key=lambda d: -ring(d // 4, nlat // 4) - ring(d % 4, 4))
    lon_order = sorted(range(1, nlon), key=lambda d: -ring(d // 2, nlon // 2) - 0.5 * (d % 2))

    dgx[nlat, 0:HALO, :] = jnp.zeros((HALO, cy), F32)
    dgx[nlat, HALO + strip:, :] = jnp.zeros((HALO, cy), F32)

    barrier = pltpu.get_barrier_semaphore()
    for d in lat_order:
        greet(i, lax.rem(j + d, nlat))
    for d in lon_order:
        greet(lax.rem(i + d, nlon), j)
    greet(nlon - 1 - i, nlat - 1)
    for shift in (1, 0, -1):
        other = lax.rem(total - 1 - t + shift + total, total)

        @pl.when(other != t)
        def _():
            greet(other // nlat, lax.rem(other, nlat))

    @pl.when(j == 0)
    def _():
        for lat in range(nlat):
            greet(lon_of(i - 1), lat)
        greet(lon_of(nlon - i), nlat - 1)

    @pl.when(top)
    def _():
        for lat in range(nlat):
            greet(lon_of(i + 1), lat)

    chunk = levels // 4
    loads = [
        pltpu.make_async_copy(theta.at[pl.ds(q * chunk, chunk)], th.at[pl.ds(q * chunk, chunk)], in_sem.at[q])
        for q in range(4)
    ]
    load_kappa = pltpu.make_async_copy(kappa, kp, in_sem.at[4])
    load_diag = pltpu.make_async_copy(diag, flat, in_sem.at[5])
    load_weight = pltpu.make_async_copy(weight_in, weight, in_sem.at[6])
    load_land = pltpu.make_async_copy(land_in, land, in_sem.at[7])
    load_kappa.start()
    load_weight.start()
    for copy in loads:
        copy.start()
    load_diag.start()
    load_land.start()


    load_land.wait()
    table = land[...].astype(F32).astype(BF16)
    row_block = (j * cy + iota((cy, by), 0)) >> 5
    on_rows = bdot(hot(row_block == iota((cy, by), 1)), table).astype(BF16)
    col_block = (i * cx + iota((bx, cx), 1)) >> 5
    cols_hot = hot(col_block == iota((bx, cx), 0))
    sea[...] = bdot(on_rows, cols_hot)
    load_kappa.wait()
    kp[...] = sea[...] * kp[...]
    load_weight.wait()
    column = jnp.zeros((cy, cx), F32)
    for q in range(4):
        loads[q].wait()
        for k in range(q * chunk, (q + 1) * chunk):
            column = column + weight[k] * th[k]
    held, rate = sea[...] * column, kp[...]
    block_row, block_lane = iota((cy, cx), 0), iota((cy, cx), 1)
    beside = jnp.where(block_row == 0, 0.0, pltpu.roll(held, 1, 0))
    beside = beside + jnp.where(block_row == cy - 1, 0.0, pltpu.roll(held, cy - 1, 0))
    beside = beside + jnp.where(block_lane == 0, 0.0, pltpu.roll(held, 1, 1))
    beside = beside + jnp.where(block_lane == cx - 1, 0.0, pltpu.roll(held, cx - 1, 1))
    force = held + rate * (beside - 4.0 * held)
    turned[0:HALO, :] = jnp.zeros((HALO, cy), F32)
    turned[HALO + cx:, :] = jnp.zeros((HALO, cy), F32)
    turned[HALO:HALO + cx, :] = force.T

    lane = iota((cy, LANES), 1)
    ring_columns = jnp.where(
        lane < 2,
        jnp.where(lane == 0, rate[:, 0:LANES], pltpu.roll(held[:, 0:LANES], 1, 1)),
        jnp.where(
            lane == 2, pltpu.roll(rate[:, cx - LANES:], 3, 1), pltpu.roll(held[:, cx - LANES:], 4, 1)
        ),
    )
    ring_rows = ring_columns.T[0:8]

    lines = jnp.concatenate([rate[0:1], rate[cy - 1:], held[0:1], held[cy - 1:]] * 2, axis=0)
    for m in range(nlat):
        windows[m] = pltpu.roll(lines, (HALO - strip * m) % cx, 1)[:, 0:LANES]
    lanes_here = iota((nlat, LANES), 1)
    lined = windows[:, 0, :]
    for g in range(1, 4):
        lined = jnp.where(lanes_here >= wide * g, pltpu.roll(windows[:, g, :], wide * g, 1), lined)
    for m in range(nlat):
        start = HALO - INNER + strip * m
        packs[m, 0:BODY, :] = turned[start:start + BODY, :]
        packs[m, BODY:BODY + 1, :] = lined[m:m + 1]
    packs[0, BODY + 1:SPAN, :] = ring_rows[0:2]
    packs[nlat - 1, BODY + 1:SPAN, :] = ring_rows[2:4]
    for n, (start, m) in enumerate(((HALO, nlat - 1), (HALO + cx - INNER, 0))):
        edge_packs[n, 0:INNER, :] = turned[start:start + INNER, :]
        edge_packs[n, INNER:INNER + 1, :] = lined[m:m + 1]
        edge_packs[n, INNER + 1:INNER + 3, :] = ring_rows[2 * n:2 * n + 2]

    @pl.when(top)
    def _():
        lanes8 = iota((8, LANES), 1)
        corner = pltpu.roll(ring_columns[cy - 8:], 3 * wide, 1)
        for m in range(nlat):
            start = strip * (nlat - 1 - m) - HALO
            tile = corner
            for g, field in ((2, held), (1, rate), (0, force)):
                shifted = pltpu.roll(field[cy - 8:], (g * wide - start) % cx, 1)[:, 0:LANES]
                tile = jnp.where(lanes8 < (g + 1) * wide, shifted, tile)
            tiles[m] = tile

    load_diag.wait()
    for c in range(nlat):
        dgx[c, HALO:HALO + strip, :] = flat[:, c * cy:(c + 1) * cy]

    own_folds = [lax.rem(total - 1 - t + shift + total, total) == t for shift in (1, -1)]
    awaited = nlat + nlon + 3 + jnp.where(top, nlat + 1, 0)
    for own in own_folds:
        awaited = awaited - jnp.where(own, 1, 0)
    pl.semaphore_wait(barrier, awaited)

    own_slot = ext.at[j, 0:SPAN, :]

    def block_rows(m):
        return packs.at[m, 0:SPAN, :]

    def main_copy(d):
        m = lax.rem(j + d, nlat)
        return remote(block_rows(m), own_slot, main_send, main_recv, i, m)

    for d in lat_order:
        main_copy(d).start()
    pltpu.make_async_copy(block_rows(j), own_slot, main_recv).start()
    edge_slot = edge.at[j, 0:INNER + 3, :]
    left_edge = remote(
        edge_packs.at[0, 0:INNER + 3, :], edge_slot, edge_send.at[0], edge_recv, lon_of(i - 1), nlat - 1
    )
    right_edge = remote(
        edge_packs.at[1, 0:INNER + 3, :], edge_slot, edge_send.at[1], edge_recv, lon_of(i + 1), 0
    )
    left_edge.start()
    right_edge.start()

    def fold_copy(m):
        return remote(tiles.at[m], fold, fold_send, fold_recv.at[0], nlon - 1 - i, m)

    far_lon = lon_of(nlon - 2 - i)
    far_self = far_lon == i
    fold_far = remote(
        tiles.at[nlat - 1], fold_edge, fold_far_send, fold_recv.at[1], far_lon, nlat - 1
    )
    fold_far_own = pltpu.make_async_copy(tiles.at[nlat - 1], fold_edge, fold_recv.at[1])
    fold_low = remote(tiles.at[0], fold_edge, fold_low_send, fold_recv.at[1], lon_of(nlon - i), 0)

    @pl.when(top)
    def _():
        for m in range(nlat):
            fold_copy(m).start()
        fold_low.start()

        @pl.when(far_self)
        def _():
            fold_far_own.start()

        @pl.when(jnp.logical_not(far_self))
        def _():
            fold_far.start()

    for d in range(1, nlon):
        pl.semaphore_signal(
            ready, inc=1, device_id=(lax.rem(i + d, nlon), j), device_id_type=MESH
        )

    after, before = lax.rem(t + 1, total), lax.rem(t + total - 1, total)
    depth = BASIS - 2
    own_low = slice(HALO, HALO + depth)
    own_high = slice(HALO + strip - depth, HALO + strip)
    halo_low = slice(HALO - depth, HALO)
    halo_high = slice(HALO + strip, HALO + strip + depth)
    diag_up = remote(
        dgx.at[0:nlat, own_high, :], dgx.at[0:nlat, halo_low, :], diag_send.at[0], diag_recv.at[0],
        after // nlat, lax.rem(after, nlat),
    )
    diag_down = remote(
        dgx.at[0:nlat, own_low, :], dgx.at[0:nlat, halo_high, :], diag_send.at[1], diag_recv.at[1],
        before // nlat, lax.rem(before, nlat),
    )
    diag_up.start()
    diag_down.start()
    middle = slice(HALO, HALO + strip)
    diag_fold = remote(
        dgx.at[nlat - 1, middle, :], dgx.at[nlat, middle, :], diag_send.at[2], diag_recv.at[2],
        nlon - 1 - i, nlat - 1 - j,
    )
    diag_fold.start()
    sides = []
    for n, (shift, src, dst) in enumerate(((1, own_low, halo_high), (-1, own_high, halo_low))):
        other = lax.rem(total - 1 - t + shift + total, total)
        src_ref, dst_ref = dgx.at[nlat - 1, src, :], dgx.at[nlat, dst, :]
        sides.append((
            remote(
                src_ref, dst_ref, diag_send.at[3 + n], diag_recv.at[3 + n], other // nlat, lax.rem(other, nlat)
            ),
            pltpu.make_async_copy(src_ref, dst_ref, diag_recv.at[3 + n]),
            own_folds[n],
        ))
    for far, near, own in sides:
        @pl.when(own)
        def _():
            near.start()

        @pl.when(jnp.logical_not(own))
        def _():
            far.start()

    rows_out[0] = th[:, 0, :]
    rows_out[1] = th[:, cy - 1, :]
    to_south = remote(rows_out.at[0], north, halo_send.at[0], halo_recv.at[0], i, lat_of(j - 1))
    to_north = remote(rows_out.at[1], south, halo_send.at[1], halo_recv.at[1], i, lat_of(j + 1))
    to_fold = remote(rows_out.at[1], north, halo_send.at[1], halo_recv.at[0], nlon - 1 - i, j)

    @pl.when(j > 0)
    def _():
        to_south.start()

    @pl.when(jnp.logical_not(top))
    def _():
        to_north.start()

    @pl.when(top)
    def _():
        to_fold.start()

    lane = iota((cy, LANES), 1)
    packed = jnp.zeros((cy, LANES), F32)
    for k in range(levels):
        packed = jnp.where(lane == k, pltpu.roll(th[k, :, 0:LANES], k, 1), packed)
        packed = jnp.where(
            lane == levels + k, pltpu.roll(th[k, :, cx - LANES:cx], levels + k + 1, 1), packed
        )
    cols_out[...] = packed
    to_west = remote(cols_out, east, halo_send.at[2], halo_recv.at[2], lon_of(i - 1), j)
    to_east = remote(cols_out, west, halo_send.at[3], halo_recv.at[3], lon_of(i + 1), j)
    to_west.start()
    to_east.start()

    basis[:, :, 0:PAD, :] = jnp.zeros((BASIS, nlat + 1, PAD, cy), F32)
    tail = PAD + strip + 2 * INNER
    basis[:, :, tail:, :] = jnp.zeros((BASIS, nlat + 1, PAD, cy), F32)

    west_block = lax.rem(i * (cx // BS) + bx - 1, bx)
    east_block = lax.rem((i + 1) * (cx // BS), bx)
    ocean_west = bdot(on_rows, hot(iota((bx, LANES), 0) == west_block))
    ocean_east = bdot(on_rows, hot(iota((bx, LANES), 0) == east_block))
    edge_row = iota((8, by), 0)
    edge_col = iota((8, by), 1)
    south_hot = hot(jnp.logical_and(edge_row == 0, edge_col == j * (cy // BS) - 1))
    north_block = jnp.where(top, by - 1, (j + 1) * (cy // BS))
    north_hot = hot(jnp.logical_and(edge_row == 0, edge_col == north_block))
    north_cols = jnp.where(top, bx - 1 - col_block, col_block)
    ocean_south = bdot(bdot(south_hot, table).astype(BF16), cols_hot)[0:1]
    ocean_north = bdot(
        bdot(north_hot, table).astype(BF16), hot(north_cols == iota((bx, cx), 0))
    )[0:1]

    strip_x = (strip * t - HALO + nx + iota((wide, bx), 0)) % nx >> 5
    strip_hot = hot(strip_x == iota((wide, bx), 1))
    on_cols = ndot(strip_hot, table).astype(BF16)
    ocs[:, 0:ny] = bdot(on_cols, hot((iota((by, ny), 1) >> 5) == iota((by, ny), 0)))
    mirror_hot = hot((bx - 1 - strip_x) == iota((wide, bx), 1))
    on_mirror = ndot(mirror_hot, table).astype(BF16)
    keep = jnp.logical_and(iota((by, LANES), 0) == by - 1, iota((by, LANES), 1) < 8)
    ocs[:, ny:ny + LANES] = bdot(on_mirror, hot(keep))

    diag_up.wait_recv()
    diag_down.wait_recv()
    diag_fold.wait_recv()
    for far, near, own in sides:
        far.wait_recv()
    for c in range(nlat):
        dg[:, c * cy:(c + 1) * cy] = dgx[c]
    dg[:, ny:] = flip_rows(flip_lanes(dgx[nlat]), (wide,))
    dg[...] = ocs[...] * ((dg[...] - 1.0) * 0.25)
    quarter[...] = ocs[...] * 0.25

    whole(ext.at[0:nlat, 0:SPAN, :], main_recv).wait()
    whole(fold, fold_recv.at[0]).wait()

    @pl.when(ends)
    def _():
        whole(edge.at[:, 0:INNER + 3, :], edge_recv).wait()
        whole(fold_edge, fold_recv.at[1]).wait()
        spot = iota((8, LANES), 1)
        outer = jnp.logical_or(
            jnp.logical_and(top, spot % wide < HALO), jnp.logical_and(j == 0, spot % wide >= wide - HALO)
        )
        outer = jnp.logical_and(outer, spot < 3 * wide)
        merged = jnp.where(outer, fold_edge[...], fold[...])
        fold[...] = jnp.where(spot >= 3 * wide + 4, pltpu.roll(fold_edge[...], 4, 1), merged)

    row = iota((3 * wide + 8, LANES), 0)
    source = jnp.where(row < 3 * wide, (row // wide) * wide + wide - 1 - row % wide, row)
    pick = hot(source == iota((3 * wide + 8, LANES), 1))
    reversed_rows = jnp.concatenate(
        [fold[q:q + 1, :] for q in reversed(range(8))] + [jnp.zeros((LANES - 8, LANES), F32)], axis=0
    )
    folded = [ndot(pick, piece) for piece in pieces(reversed_rows)]
    folded = (folded[0] + folded[1]) + folded[2]
    crossing[...] = folded[INNER:INNER + BODY]
    corner_main, corner_edge = folded[3 * wide:3 * wide + 4], folded[3 * wide + 4:]
    lined_here[...] = ext[:, BODY, :]

    def fix_edge(into, inner_row, outer_row, first, mine, theirs):
        spot = iota((nlat, LANES), 1) % wide
        from_edge = spot < HALO if first else spot >= wide - HALO
        lined_here[...] = jnp.where(from_edge, edge[:, INNER, :], lined_here[...])
        ext[:, into:into + INNER, :] = edge[:, 0:INNER, :]
        ext[:, outer_row, :] = ext[:, outer_row, :] + edge[:, INNER + 1, :] * ext[:, BODY + 2, :]
        ext[:, inner_row, :] = ext[:, inner_row, :] + ext[:, BODY + 1, :] * edge[:, INNER + 2, :]
        line = iota((BODY, LANES), 0)
        across_out = corner_edge[theirs:theirs + 1] * corner_main[mine + 1:mine + 2]
        across_in = corner_main[mine:mine + 1] * corner_edge[theirs + 1:theirs + 2]
        crossing[...] = crossing[...] + jnp.where(
            line == outer_row, across_out, jnp.where(line == inner_row, across_in, 0.0)
        )

    @pl.when(j == 0)
    def _():
        fix_edge(0, INNER, INNER - 1, True, 2, 0)

    @pl.when(top)
    def _():
        fix_edge(INNER + strip, INNER + strip - 1, INNER + strip, False, 0, 2)

    columns_of = jnp.concatenate(
        [lined_here[...], jnp.zeros((LANES - nlat, LANES), F32)], axis=0
    ).T
    square = (wide, LANES)
    virtual = iota(square, 1) == nlat
    rate_low, rate_high, held_low, held_high = [columns_of[g * wide:(g + 1) * wide] for g in range(4)]
    rate_low = jnp.where(virtual, jnp.broadcast_to(folded[wide:2 * wide, 0:1], square), rate_low)
    held_low = jnp.where(virtual, jnp.broadcast_to(folded[2 * wide:3 * wide, 0:1], square), held_low)
    rows = slice(HALO - INNER, HALO - INNER + BODY)
    add_high = (rate_high * pltpu.roll(held_low, LANES - 1, 1))[rows]
    add_low = (rate_low * pltpu.roll(held_high, 1, 1))[rows]

    def lanes_of(c):
        return slice(c * LANES, (c + 1) * LANES)

    shift = HALO - INNER
    own_start = PAD + INNER
    bottom, ceiling = PAD, PAD + BODY
    body_lane = iota((BODY, LANES), 1)
    for c in range(nlat + 1):
        value = ext[c, 0:BODY, :] if c < nlat else crossing[...]
        value = jnp.where(body_lane == 0, value + add_low[:, c:c + 1], value)
        basis[0, c, bottom:ceiling, :] = jnp.where(
            body_lane == LANES - 1, value + add_high[:, c:c + 1], value
        )
    for step in range(BASIS - 1):
        low, high = (bottom, ceiling) if step < BASIS - 2 else (own_start, own_start + strip)

        def store_next(c, value, beside):
            lanes, rows = lanes_of(c), slice(low - PAD + shift, high - PAD + shift)
            basis[step + 1, c, low:high, :] = dg[rows, lanes] * value - quarter[rows, lanes] * beside

        stencil(basis.at[step], store_next, low, high)

    zero = jnp.zeros((8, LANES), F32)

    def accumulate(c, carry):
        sums = list(carry)
        for h in range(strip // 8):
            start = own_start + 8 * h
            values = [basis[b, c, start:start + 8, :] for b in range(BASIS)]
            split = [halves(value) for value in values]
            for n, (a, b) in enumerate(PAIRS):
                (ah, al), (bh, bl) = split[a], split[b]
                e = ah * bl + al * values[b]
                s, f = quick(sums[2 * n], ah * bh)
                sums[2 * n], sums[2 * n + 1] = s, sums[2 * n + 1] + (e + f)
        return tuple(sums)

    sums = lax.fori_loop(0, ny // LANES, accumulate, (zero,) * (2 * len(PAIRS)))
    packed_sums = [(sums[2 * n], sums[2 * n + 1]) for n in range(len(PAIRS))]
    packed_sums += [(zero, zero)] * (SLOTS - len(PAIRS))
    eight = iota((8, LANES), 0)
    for shift in (4, 2, 1):
        keep_row = (eight & shift) == 0
        merged = []
        for n in range(0, len(packed_sums), 2):
            (ah, al), (bh, bl) = packed_sums[n:n + 2]
            h, e = two_sum(
                jnp.where(keep_row, ah, pltpu.roll(bh, shift, 0)),
                jnp.where(keep_row, pltpu.roll(ah, 8 - shift, 0), bh),
            )
            l = jnp.where(keep_row, al, pltpu.roll(bl, shift, 0))
            l = l + jnp.where(keep_row, pltpu.roll(al, 8 - shift, 0), bl)
            merged.append((h, l + e))
        packed_sums = merged
    high, low = [jnp.concatenate([packed_sums[0][n], packed_sums[1][n]], axis=0) for n in range(2)]
    place = iota((SLOTS, LANES), 0)
    within = place & 7
    place = (place & 8) + ((within & 4) >> 2) + (within & 2) + ((within & 1) << 2)
    shift = LANES // 2
    while shift:
        high, e = two_sum(high, pltpu.roll(high, shift, 1))
        low = low + pltpu.roll(low, shift, 1) + e
        shift //= 2
    spot = iota((SLOTS, LANES), 1)
    packed = jnp.where(spot == place, high, jnp.where(spot == place + SLOTS, low, 0.0))
    message = jnp.sum(packed, axis=0, keepdims=True)

    parts[pl.ds(t, 1), :] = message
    own_part = parts.at[pl.ds(t, 1), :]
    sizes = (nlon // 2, 2, nlat // 4, 4)
    offsets = [
        (a, b, c, d)
        for a in range(sizes[0]) for b in range(sizes[1]) for c in range(sizes[2]) for d in range(sizes[3])
    ]

    def hops(offset):
        return sum(min(o, n - o) for o, n in zip(offset, sizes) if n > 2 or o) - 0.5 * offset[1]

    offsets = sorted(offsets[1:], key=hops, reverse=True)
    place_of = (i // 2, lax.rem(i, 2), j // 4, lax.rem(j, 4))
    moved = [
        [lax.rem(place_of[n] + o, sizes[n]) * scale for o in range(sizes[n])]
        for n, scale in enumerate((2, 1, 4, 1))
    ]
    pl.semaphore_wait(ready, nlon - 1)
    for a, b, c, d in offsets:
        remote(own_part, own_part, red_send, red_recv, moved[0][a] + moved[1][b], moved[2][c] + moved[3][d]).start()

    to_south.wait_recv()
    to_west.wait_recv()
    to_east.wait_recv()

    @pl.when(j > 0)
    def _():
        to_north.wait_recv()

    @pl.when(j == 0)
    def _():
        south[...] = jnp.zeros_like(south)

    @pl.when(top)
    def _():
        north[...] = flip_lanes(north[...])

    west[...] = west[...] * ocean_west
    east[...] = east[...] * ocean_east
    north[...] = ocean_north * north[...]
    south[...] = ocean_south * south[...]
    part = 32
    tile_row, tile_lane = iota((part, LANES), 0), iota((part, LANES), 1)
    first_row, last_row = tile_row == 0, tile_row == part - 1
    first_lane, last_lane = tile_lane == 0, tile_lane == LANES - 1
    count = cy // part
    columns = cx // LANES

    def update(k, _):
        from_south, from_north = south[pl.ds(k, 1), :], north[pl.ds(k, 1), :]

        def load(c, n):
            rows, lanes = slice(c * part, (c + 1) * part), slice(n * LANES, (n + 1) * LANES)
            return sea[rows, lanes] * th[k, rows, lanes]

        def across(n, vector):
            return jnp.broadcast_to(vector[:, n * LANES:(n + 1) * LANES], (part, LANES))

        value = [load(0, n) for n in range(columns)]
        before = [across(n, from_south) for n in range(columns)]
        up = [pltpu.roll(v, part - 1, 0) for v in value]
        for c in range(count):
            rows = slice(c * part, (c + 1) * part)
            if c + 1 < count:
                following = [load(c + 1, n) for n in range(columns)]
                up_next = [pltpu.roll(v, part - 1, 0) for v in following]
            else:
                following, up_next = None, [across(n, from_north) for n in range(columns)]
            down = [pltpu.roll(v, 1, 0) for v in value]
            right = [pltpu.roll(west[rows, :], LANES - levels - k, 1)] + [pltpu.roll(v, 1, 1) for v in value]
            left = [pltpu.roll(v, LANES - 1, 1) for v in value] + [pltpu.roll(east[rows, :], LANES - 1 - k, 1)]
            for n in range(columns):
                lanes = slice(n * LANES, (n + 1) * LANES)
                beside = jnp.where(first_row, before[n], down[n]) + jnp.where(last_row, up_next[n], up[n])
                beside = beside + jnp.where(first_lane, right[n], right[n + 1])
                beside = beside + jnp.where(last_lane, left[n + 1], left[n])
                out_theta[k, rows, lanes] = th[k, rows, lanes] + kp[rows, lanes] * (beside - 4.0 * value[n])
            value, before, up = following, down, up_next
        return 0

    lax.fori_loop(0, levels, update, 0)
    out_basis[...] = basis[0:BASIS - 1, 0:nlat, own_start:own_start + strip, :]
    whole(parts.at[pl.ds(0, total - 1), :], red_recv).wait()
    out_parts[...] = parts[...]

    whole(ext.at[0:nlat - 1, 0:SPAN, :], main_send).wait()
    left_edge.wait_send()
    right_edge.wait_send()
    diag_up.wait_send()
    diag_down.wait_send()
    diag_fold.wait_send()
    for far, near, own in sides:
        @pl.when(jnp.logical_not(own))
        def _():
            far.wait_send()

    @pl.when(top)
    def _():
        whole(tiles, fold_send).wait()
        fold_low.wait_send()

        @pl.when(jnp.logical_not(far_self))
        def _():
            fold_far.wait_send()

    @pl.when(j > 0)
    def _():
        to_south.wait_send()

    to_north.wait_send()
    to_west.wait_send()
    to_east.wait_send()
    whole(parts.at[pl.ds(0, total - 1), :], red_send).wait()


def finish(fresh, vectors, parts, out_theta, out_psi, psi, out_sem):
    pieces_of = fresh.shape[0] // 2
    stores = [
        pltpu.make_async_copy(fresh.at[pl.ds(2 * q, 2)], out_theta.at[pl.ds(2 * q, 2)], out_sem.at[0])
        for q in range(pieces_of)
    ]
    for copy in stores:
        copy.start()
    total = parts.shape[0]
    value = parts[...]
    error = jnp.zeros_like(value)
    half = total // 2
    while half >= 8:
        value, e = two_sum(value[:half], value[half:])
        error = error[:half] + error[half:] + e
        half //= 2
    for shift in (4, 2, 1):
        value, e = two_sum(value, pltpu.roll(value, shift, 0))
        error = error + pltpu.roll(error, shift, 0) + e
    lane = iota((1, LANES), 1)
    error = jnp.where(
        jnp.logical_and(lane >= SLOTS, lane < 2 * SLOTS), pltpu.roll(error[0:1], SLOTS, 1), 0.0
    )
    message = value[0:1] + error
    high, low = quick(message, pltpu.roll(message, LANES - SLOTS, 1))

    gram = {}
    for n, (a, b) in enumerate(PAIRS):
        gram[a, b] = gram[b, a] = tuple(
            jnp.broadcast_to(x[:, n:n + 1], (1, LANES)) for x in (high, low)
        )
    size = BASIS - 1

    def scaled(x, factor):
        return x[0] * factor, x[1] * factor

    matrix = [
        [
            df_add(
                scaled(gram[a, b + 1], 4.0),
                df_add(scaled(gram[a, b], 4.0), gram[a, b]),
            )
            for b in range(size)
        ]
        for a in range(size)
    ]
    right = [gram[0, a] for a in range(size)]
    for p in range(size):
        for a in range(p + 1, size):
            factor = df_div(matrix[a][p], matrix[p][p])
            for b in range(p + 1, size):
                matrix[a][b] = df_sub(matrix[a][b], df_mul(factor, matrix[p][b]))
            right[a] = df_sub(right[a], df_mul(factor, right[p]))
    answer = [None] * size
    for p in reversed(range(size)):
        value = right[p][0]
        for b in range(p + 1, size):
            value = value - matrix[p][b][0] * answer[b][0]
        answer[p] = (value / matrix[p][p][0],)
    strip = psi.shape[0]
    spread = [jnp.broadcast_to(x[0], (strip, LANES)) for x in answer]

    def combine(c, _):
        lanes = pl.ds(pl.multiple_of(c * LANES, LANES), LANES)
        value = spread[size - 1] * vectors[size - 1, c]
        for b in reversed(range(size - 1)):
            value = value + spread[b] * vectors[b, c]
        psi[:, lanes] = value
        return 0

    lax.fori_loop(0, vectors.shape[1], combine, 0)

    store_psi = pltpu.make_async_copy(psi, out_psi, out_sem.at[1])
    store_psi.start()
    store_psi.wait()
    pltpu.make_async_copy(fresh, out_theta, out_sem.at[0]).wait()


def per_device(nlon, nlat, theta, kappa, layer_weight, diag, land_blocks):
    levels, cy, cx = theta.shape
    strip, ny = diag.shape
    wide = strip + 2 * HALO
    vmem = pl.BlockSpec(memory_space=pltpu.VMEM)
    hbm = pl.BlockSpec(memory_space=pltpu.HBM)
    dma = pltpu.SemaphoreType.DMA
    operands = (layer_weight, land_blocks, theta, kappa, diag)
    fresh, vectors, parts = pl.pallas_call(
        functools.partial(kernel, nlon, nlat),
        out_shape=(
            jax.ShapeDtypeStruct(theta.shape, F32),
            jax.ShapeDtypeStruct((BASIS - 1, nlat, strip, cy), F32),
            jax.ShapeDtypeStruct((nlon * nlat, LANES), F32),
        ),
        in_specs=[hbm] * 5,
        out_specs=(vmem, vmem, vmem),
        scratch_shapes=[
            pltpu.SMEM(layer_weight.shape, F32),
            pltpu.VMEM(land_blocks.shape, jnp.int32),
            pltpu.VMEM((levels, cy, cx), F32),
            pltpu.VMEM((cy, cx), F32),
            pltpu.VMEM((cy, cx), F32),
            pltpu.VMEM((cx + 2 * HALO, cy), F32),
            pltpu.VMEM((nlat, 8, LANES), F32),
            pltpu.VMEM((nlat, wide, cy), F32),
            pltpu.VMEM((2, HALO, cy), F32),
            pltpu.VMEM((nlat, wide, cy), F32),
            pltpu.VMEM((nlat, HALO, cy), F32),
            pltpu.VMEM((BODY, LANES), F32),
            pltpu.VMEM((nlat, LANES), F32),
            pltpu.VMEM((strip, ny), F32),
            pltpu.VMEM((nlat + 1, wide, cy), F32),
            pltpu.VMEM((wide, ny + LANES), F32),
            pltpu.VMEM((wide, ny + LANES), F32),
            pltpu.VMEM((wide, ny + LANES), F32),
            pltpu.VMEM((BASIS, nlat + 1, strip + 2 * INNER + 2 * PAD, cy), F32),
            pltpu.VMEM((2, levels, cx), F32),
            pltpu.VMEM((levels, cx), F32),
            pltpu.VMEM((levels, cx), F32),
            pltpu.VMEM((cy, LANES), F32),
            pltpu.VMEM((cy, LANES), F32),
            pltpu.VMEM((cy, LANES), F32),
            pltpu.VMEM((nlat, 8, LANES), F32),
            pltpu.VMEM((8, LANES), F32),
            pltpu.VMEM((8, LANES), F32),
            pltpu.VMEM((nlon * nlat, LANES), F32),
            dma((8,)),
            dma,
            dma,
            dma((2,)),
            dma,
            dma,
            dma,
            dma,
            dma((2,)),
            dma((5,)),
            dma((5,)),
            dma((4,)),
            dma((4,)),
            dma,
            dma,
            pltpu.SemaphoreType.REGULAR,
        ],
        compiler_params=pltpu.CompilerParams(
            collective_id=0, has_side_effects=True, vmem_limit_bytes=32 << 20
        ),
        name="ocean_step",
    )(*[pltpu.with_memory_space_constraint(x, pltpu.HBM) for x in operands])
    return pl.pallas_call(
        finish,
        out_shape=(
            jax.ShapeDtypeStruct(theta.shape, F32),
            jax.ShapeDtypeStruct(diag.shape, F32),
        ),
        in_specs=[vmem, vmem, vmem],
        out_specs=(hbm, hbm),
        scratch_shapes=[pltpu.VMEM(diag.shape, F32), dma((2,))],
        compiler_params=pltpu.CompilerParams(vmem_limit_bytes=16 << 20),
        name="ocean_finish",
    )(fresh, vectors, parts)


def solution(mesh):
    placed = (P(None, "lat", "lon"), P("lat", "lon"), P(), P(("lon", "lat"), None), P())
    return jax.shard_map(
        functools.partial(per_device, mesh.shape["lon"], mesh.shape["lat"]),
        mesh=mesh,
        in_specs=placed,
        out_specs=(P(None, "lat", "lon"), P(("lon", "lat"), None)),
        check_vma=False,
    )
```

```python
import functools

import jax
import jax.numpy as jnp
from jax import lax
from jax.experimental import pallas as pl
from jax.experimental.pallas import tpu as pltpu
from jax.sharding import PartitionSpec as P

MESH = pl.DeviceIdType.MESH
BS = 32
HALO = 8
PAD = 8
INNER = 4
BODY = 24
SPAN = BODY + 3
LANES = 128
F32 = jnp.float32
BF16 = jnp.bfloat16
BASIS = 5
PAIRS = [(a, b) for a in range(BASIS) for b in range(a, BASIS) if a < BASIS - 1]
SLOTS = 16


def iota(shape, axis):
    return lax.broadcasted_iota(jnp.int32, shape, axis)


def hot(condition):
    return jnp.where(condition, 1.0, 0.0).astype(BF16)


def bdot(left, right):
    return jnp.dot(left, right, preferred_element_type=F32)


def ndot(left, right):
    return lax.dot_general(left, right, (((1,), (1,)), ((), ())), preferred_element_type=F32)


def pieces(value):
    first = value.astype(BF16)
    rest = value - first.astype(F32)
    second = rest.astype(BF16)
    third = (rest - second.astype(F32)).astype(BF16)
    return [first, second, third]


def flip_lanes(value):
    width = value.shape[1]
    turn = hot(iota((width, width), 0) + iota((width, width), 1) == width - 1)
    parts = [bdot(piece, turn) for piece in pieces(value)]
    return (parts[0] + parts[1]) + parts[2]


def flip_rows(value, groups):
    count = value.shape[0]
    row = iota((count, count), 0)
    ends, start = jnp.zeros((count, count), jnp.int32), 0
    for size in groups:
        ends = jnp.where(row >= start, 2 * start + size - 1, ends)
        start += size
    turn = hot(row + iota((count, count), 1) == ends)
    parts = [bdot(turn, piece) for piece in pieces(value)]
    return (parts[0] + parts[1]) + parts[2]


def two_sum(a, b):
    s = a + b
    t = s - a
    return s, (a - (s - t)) + (b - t)


def halves(a):
    t = a * 4097.0
    high = t - (t - a)
    return high, a - high


def two_prod(a, b):
    p = a * b
    ah, al = halves(a)
    bh, bl = halves(b)
    return p, ((ah * bh - p) + ah * bl + al * bh) + al * bl


def quick(a, b):
    s = a + b
    return s, b - (s - a)


def df_mul(x, y):
    p, e = two_prod(x[0], y[0])
    return quick(p, e + (x[0] * y[1] + x[1] * y[0]))


def df_add(x, y):
    s, e = two_sum(x[0], y[0])
    return quick(s, e + (x[1] + y[1]))


def df_sub(x, y):
    return df_add(x, (-y[0], -y[1]))


def df_div(x, y):
    first = x[0] / y[0]
    rest = df_sub(x, df_mul(y, (first, jnp.zeros_like(first))))
    second = rest[0] / y[0]
    return quick(first, second)


def stencil(ref, emit, low, high):
    count, _, width = ref.shape
    lane = iota((high - low, width), 1)
    first, last = lane == 0, lane == width - 1

    def load(c, shift=0):
        return ref[c, low + shift:high + shift, :]

    value = load(0)
    before = jnp.zeros_like(value)
    up = pltpu.roll(value, width - 1, 1)
    for c in range(count):
        if c + 1 < count:
            following = load(c + 1)
            up_next = pltpu.roll(following, width - 1, 1)
        else:
            following, up_next = None, up
        down = pltpu.roll(value, 1, 1)
        beside = jnp.where(first, before, down) + jnp.where(last, up_next, up)
        emit(c, value, (beside + load(c, -1)) + load(c, 1))
        value, before, up = following, down, up_next


def kernel(
    nlon, nlat,
    weight_in, land_in, theta, kappa, diag,
    out_theta, out_basis, out_parts,
    weight, land, th, kp, sea, turned, windows, packs, edge_packs, ext, edge, crossing, lined_here, flat, dgx, dg, ocs, quarter, basis, rows_out, north, south, cols_out, east, west,
    tiles, fold, fold_edge, parts,
    in_sem, main_send, main_recv, edge_send, edge_recv, fold_send, fold_low_send, fold_far_send, fold_recv,
    diag_send, diag_recv, halo_send, halo_recv, red_send, red_recv, ready,
):
    levels, cy, cx = th.shape
    ny, nx = cy * nlat, cx * nlon
    strip = cx // nlat
    wide = strip + 2 * HALO
    by, bx = land.shape
    total = nlon * nlat
    i = lax.axis_index("lon")
    j = lax.axis_index("lat")
    t = i * nlat + j
    top = j == nlat - 1
    ends = jnp.logical_or(j == 0, top)

    def remote(src, dst, send, recv, lon, lat):
        return pltpu.make_async_remote_copy(
            src_ref=src, dst_ref=dst, send_sem=send, recv_sem=recv,
            device_id=(lon, lat), device_id_type=MESH,
        )

    def lon_of(value):
        return lax.rem(value + 2 * nlon, nlon)

    def lat_of(value):
        return lax.rem(value + 2 * nlat, nlat)

    def whole(ref, sem):
        return pltpu.make_async_copy(ref, ref, sem)

    def greet(lon, lat):
        pl.semaphore_signal(barrier, inc=1, device_id=(lon, lat), device_id_type=MESH)

    def ring(value, size):
        return min(value, size - value)

    lat_order = sorted(range(1, nlat), key=lambda d: -ring(d // 4, nlat // 4) - ring(d % 4, 4))
    lon_order = sorted(range(1, nlon), key=lambda d: -ring(d // 2, nlon // 2) - 0.5 * (d % 2))

    dgx[nlat, 0:HALO, :] = jnp.zeros((HALO, cy), F32)
    dgx[nlat, HALO + strip:, :] = jnp.zeros((HALO, cy), F32)

    barrier = pltpu.get_barrier_semaphore()
    for d in lat_order:
        greet(i, lax.rem(j + d, nlat))
    for d in lon_order:
        greet(lax.rem(i + d, nlon), j)
    greet(nlon - 1 - i, nlat - 1)
    for shift in (1, 0, -1):
        other = lax.rem(total - 1 - t + shift + total, total)

        @pl.when(other != t)
        def _():
            greet(other // nlat, lax.rem(other, nlat))

    @pl.when(j == 0)
    def _():
        for lat in range(nlat):
            greet(lon_of(i - 1), lat)
        greet(lon_of(nlon - i), nlat - 1)

    @pl.when(top)
    def _():
        for lat in range(nlat):
            greet(lon_of(i + 1), lat)

    chunk = levels // 4
    loads = [
        pltpu.make_async_copy(theta.at[pl.ds(q * chunk, chunk)], th.at[pl.ds(q * chunk, chunk)], in_sem.at[q])
        for q in range(4)
    ]
    load_kappa = pltpu.make_async_copy(kappa, kp, in_sem.at[4])
    load_diag = pltpu.make_async_copy(diag, flat, in_sem.at[5])
    load_weight = pltpu.make_async_copy(weight_in, weight, in_sem.at[6])
    load_land = pltpu.make_async_copy(land_in, land, in_sem.at[7])
    load_kappa.start()
    load_weight.start()
    for copy in loads:
        copy.start()
    load_diag.start()
    load_land.start()


    load_land.wait()
    table = land[...].astype(F32).astype(BF16)
    row_block = (j * cy + iota((cy, by), 0)) >> 5
    on_rows = bdot(hot(row_block == iota((cy, by), 1)), table).astype(BF16)
    col_block = (i * cx + iota((bx, cx), 1)) >> 5
    cols_hot = hot(col_block == iota((bx, cx), 0))
    sea[...] = bdot(on_rows, cols_hot)
    load_kappa.wait()
    kp[...] = sea[...] * kp[...]
    load_weight.wait()
    column = jnp.zeros((cy, cx), F32)
    for q in range(4):
        loads[q].wait()
        for k in range(q * chunk, (q + 1) * chunk):
            column = column + weight[k] * th[k]
    held, rate = sea[...] * column, kp[...]
    block_row, block_lane = iota((cy, cx), 0), iota((cy, cx), 1)
    beside = jnp.where(block_row == 0, 0.0, pltpu.roll(held, 1, 0))
    beside = beside + jnp.where(block_row == cy - 1, 0.0, pltpu.roll(held, cy - 1, 0))
    beside = beside + jnp.where(block_lane == 0, 0.0, pltpu.roll(held, 1, 1))
    beside = beside + jnp.where(block_lane == cx - 1, 0.0, pltpu.roll(held, cx - 1, 1))
    force = held + rate * (beside - 4.0 * held)
    turned[0:HALO, :] = jnp.zeros((HALO, cy), F32)
    turned[HALO + cx:, :] = jnp.zeros((HALO, cy), F32)
    turned[HALO:HALO + cx, :] = force.T

    lane = iota((cy, LANES), 1)
    ring_columns = jnp.where(
        lane < 2,
        jnp.where(lane == 0, rate[:, 0:LANES], pltpu.roll(held[:, 0:LANES], 1, 1)),
        jnp.where(
            lane == 2, pltpu.roll(rate[:, cx - LANES:], 3, 1), pltpu.roll(held[:, cx - LANES:], 4, 1)
        ),
    )
    ring_rows = ring_columns.T[0:8]

    lines = jnp.concatenate([rate[0:1], rate[cy - 1:], held[0:1], held[cy - 1:]] * 2, axis=0)
    for m in range(nlat):
        windows[m] = pltpu.roll(lines, (HALO - strip * m) % cx, 1)[:, 0:LANES]
    lanes_here = iota((nlat, LANES), 1)
    lined = windows[:, 0, :]
    for g in range(1, 4):
        lined = jnp.where(lanes_here >= wide * g, pltpu.roll(windows[:, g, :], wide * g, 1), lined)
    for m in range(nlat):
        start = HALO - INNER + strip * m
        packs[m, 0:BODY, :] = turned[start:start + BODY, :]
        packs[m, BODY:BODY + 1, :] = lined[m:m + 1]
    packs[0, BODY + 1:SPAN, :] = ring_rows[0:2]
    packs[nlat - 1, BODY + 1:SPAN, :] = ring_rows[2:4]
    for n, (start, m) in enumerate(((HALO, nlat - 1), (HALO + cx - INNER, 0))):
        edge_packs[n, 0:INNER, :] = turned[start:start + INNER, :]
        edge_packs[n, INNER:INNER + 1, :] = lined[m:m + 1]
        edge_packs[n, INNER + 1:INNER + 3, :] = ring_rows[2 * n:2 * n + 2]

    @pl.when(top)
    def _():
        lanes8 = iota((8, LANES), 1)
        corner = pltpu.roll(ring_columns[cy - 8:], 3 * wide, 1)
        for m in range(nlat):
            start = strip * (nlat - 1 - m) - HALO
            tile = corner
            for g, field in ((2, held), (1, rate), (0, force)):
                shifted = pltpu.roll(field[cy - 8:], (g * wide - start) % cx, 1)[:, 0:LANES]
                tile = jnp.where(lanes8 < (g + 1) * wide, shifted, tile)
            tiles[m] = tile

    load_diag.wait()
    for c in range(nlat):
        dgx[c, HALO:HALO + strip, :] = flat[:, c * cy:(c + 1) * cy]

    own_folds = [lax.rem(total - 1 - t + shift + total, total) == t for shift in (1, -1)]
    awaited = nlat + nlon + 3 + jnp.where(top, nlat + 1, 0)
    for own in own_folds:
        awaited = awaited - jnp.where(own, 1, 0)
    pl.semaphore_wait(barrier, awaited)

    own_slot = ext.at[j, 0:SPAN, :]

    def block_rows(m):
        return packs.at[m, 0:SPAN, :]

    def main_copy(d):
        m = lax.rem(j + d, nlat)
        return remote(block_rows(m), own_slot, main_send, main_recv, i, m)

    for d in lat_order:
        main_copy(d).start()
    pltpu.make_async_copy(block_rows(j), own_slot, main_recv).start()
    edge_slot = edge.at[j, 0:INNER + 3, :]
    left_edge = remote(
        edge_packs.at[0, 0:INNER + 3, :], edge_slot, edge_send.at[0], edge_recv, lon_of(i - 1), nlat - 1
    )
    right_edge = remote(
        edge_packs.at[1, 0:INNER + 3, :], edge_slot, edge_send.at[1], edge_recv, lon_of(i + 1), 0
    )
    left_edge.start()
    right_edge.start()

    def fold_copy(m):
        return remote(tiles.at[m], fold, fold_send, fold_recv.at[0], nlon - 1 - i, m)

    far_lon = lon_of(nlon - 2 - i)
    far_self = far_lon == i
    fold_far = remote(
        tiles.at[nlat - 1], fold_edge, fold_far_send, fold_recv.at[1], far_lon, nlat - 1
    )
    fold_far_own = pltpu.make_async_copy(tiles.at[nlat - 1], fold_edge, fold_recv.at[1])
    fold_low = remote(tiles.at[0], fold_edge, fold_low_send, fold_recv.at[1], lon_of(nlon - i), 0)

    @pl.when(top)
    def _():
        for m in range(nlat):
            fold_copy(m).start()
        fold_low.start()

        @pl.when(far_self)
        def _():
            fold_far_own.start()

        @pl.when(jnp.logical_not(far_self))
        def _():
            fold_far.start()

    for d in range(1, nlon):
        pl.semaphore_signal(
            ready, inc=1, device_id=(lax.rem(i + d, nlon), j), device_id_type=MESH
        )

    after, before = lax.rem(t + 1, total), lax.rem(t + total - 1, total)
    depth = BASIS - 2
    own_low = slice(HALO, HALO + depth)
    own_high = slice(HALO + strip - depth, HALO + strip)
    halo_low = slice(HALO - depth, HALO)
    halo_high = slice(HALO + strip, HALO + strip + depth)
    diag_up = remote(
        dgx.at[0:nlat, own_high, :], dgx.at[0:nlat, halo_low, :], diag_send.at[0], diag_recv.at[0],
        after // nlat, lax.rem(after, nlat),
    )
    diag_down = remote(
        dgx.at[0:nlat, own_low, :], dgx.at[0:nlat, halo_high, :], diag_send.at[1], diag_recv.at[1],
        before // nlat, lax.rem(before, nlat),
    )
    diag_up.start()
    diag_down.start()
    middle = slice(HALO, HALO + strip)
    diag_fold = remote(
        dgx.at[nlat - 1, middle, :], dgx.at[nlat, middle, :], diag_send.at[2], diag_recv.at[2],
        nlon - 1 - i, nlat - 1 - j,
    )
    diag_fold.start()
    sides = []
    for n, (shift, src, dst) in enumerate(((1, own_low, halo_high), (-1, own_high, halo_low))):
        other = lax.rem(total - 1 - t + shift + total, total)
        src_ref, dst_ref = dgx.at[nlat - 1, src, :], dgx.at[nlat, dst, :]
        sides.append((
            remote(
                src_ref, dst_ref, diag_send.at[3 + n], diag_recv.at[3 + n], other // nlat, lax.rem(other, nlat)
            ),
            pltpu.make_async_copy(src_ref, dst_ref, diag_recv.at[3 + n]),
            own_folds[n],
        ))
    for far, near, own in sides:
        @pl.when(own)
        def _():
            near.start()

        @pl.when(jnp.logical_not(own))
        def _():
            far.start()

    rows_out[0] = th[:, 0, :]
    rows_out[1] = th[:, cy - 1, :]
    to_south = remote(rows_out.at[0], north, halo_send.at[0], halo_recv.at[0], i, lat_of(j - 1))
    to_north = remote(rows_out.at[1], south, halo_send.at[1], halo_recv.at[1], i, lat_of(j + 1))
    to_fold = remote(rows_out.at[1], north, halo_send.at[1], halo_recv.at[0], nlon - 1 - i, j)


    lane = iota((cy, LANES), 1)
    packed = jnp.zeros((cy, LANES), F32)
    for k in range(levels):
        packed = jnp.where(lane == k, pltpu.roll(th[k, :, 0:LANES], k, 1), packed)
        packed = jnp.where(
            lane == levels + k, pltpu.roll(th[k, :, cx - LANES:cx], levels + k + 1, 1), packed
        )
    cols_out[...] = packed
    to_west = remote(cols_out, east, halo_send.at[2], halo_recv.at[2], lon_of(i - 1), j)
    to_east = remote(cols_out, west, halo_send.at[3], halo_recv.at[3], lon_of(i + 1), j)

    basis[:, :, 0:PAD, :] = jnp.zeros((BASIS, nlat + 1, PAD, cy), F32)
    tail = PAD + strip + 2 * INNER
    basis[:, :, tail:, :] = jnp.zeros((BASIS, nlat + 1, PAD, cy), F32)

    west_block = lax.rem(i * (cx // BS) + bx - 1, bx)
    east_block = lax.rem((i + 1) * (cx // BS), bx)
    ocean_west = bdot(on_rows, hot(iota((bx, LANES), 0) == west_block))
    ocean_east = bdot(on_rows, hot(iota((bx, LANES), 0) == east_block))
    edge_row = iota((8, by), 0)
    edge_col = iota((8, by), 1)
    south_hot = hot(jnp.logical_and(edge_row == 0, edge_col == j * (cy // BS) - 1))
    north_block = jnp.where(top, by - 1, (j + 1) * (cy // BS))
    north_hot = hot(jnp.logical_and(edge_row == 0, edge_col == north_block))
    north_cols = jnp.where(top, bx - 1 - col_block, col_block)
    ocean_south = bdot(bdot(south_hot, table).astype(BF16), cols_hot)[0:1]
    ocean_north = bdot(
        bdot(north_hot, table).astype(BF16), hot(north_cols == iota((bx, cx), 0))
    )[0:1]

    strip_x = (strip * t - HALO + nx + iota((wide, bx), 0)) % nx >> 5
    strip_hot = hot(strip_x == iota((wide, bx), 1))
    on_cols = ndot(strip_hot, table).astype(BF16)
    ocs[:, 0:ny] = bdot(on_cols, hot((iota((by, ny), 1) >> 5) == iota((by, ny), 0)))
    mirror_hot = hot((bx - 1 - strip_x) == iota((wide, bx), 1))
    on_mirror = ndot(mirror_hot, table).astype(BF16)
    keep = jnp.logical_and(iota((by, LANES), 0) == by - 1, iota((by, LANES), 1) < 8)
    ocs[:, ny:ny + LANES] = bdot(on_mirror, hot(keep))

    diag_up.wait_recv()
    diag_down.wait_recv()
    diag_fold.wait_recv()
    for far, near, own in sides:
        far.wait_recv()
    for c in range(nlat):
        dg[:, c * cy:(c + 1) * cy] = dgx[c]
    dg[:, ny:] = flip_rows(flip_lanes(dgx[nlat]), (wide,))
    dg[...] = ocs[...] * ((dg[...] - 1.0) * 0.25)
    quarter[...] = ocs[...] * 0.25

    whole(ext.at[0:nlat, 0:SPAN, :], main_recv).wait()
    @pl.when(j > 0)
    def _():
        to_south.start()

    @pl.when(jnp.logical_not(top))
    def _():
        to_north.start()

    @pl.when(top)
    def _():
        to_fold.start()

    to_west.start()
    to_east.start()
    whole(fold, fold_recv.at[0]).wait()

    @pl.when(ends)
    def _():
        whole(edge.at[:, 0:INNER + 3, :], edge_recv).wait()
        whole(fold_edge, fold_recv.at[1]).wait()
        spot = iota((8, LANES), 1)
        outer = jnp.logical_or(
            jnp.logical_and(top, spot % wide < HALO), jnp.logical_and(j == 0, spot % wide >= wide - HALO)
        )
        outer = jnp.logical_and(outer, spot < 3 * wide)
        merged = jnp.where(outer, fold_edge[...], fold[...])
        fold[...] = jnp.where(spot >= 3 * wide + 4, pltpu.roll(fold_edge[...], 4, 1), merged)

    row = iota((3 * wide + 8, LANES), 0)
    source = jnp.where(row < 3 * wide, (row // wide) * wide + wide - 1 - row % wide, row)
    pick = hot(source == iota((3 * wide + 8, LANES), 1))
    reversed_rows = jnp.concatenate(
        [fold[q:q + 1, :] for q in reversed(range(8))] + [jnp.zeros((LANES - 8, LANES), F32)], axis=0
    )
    folded = [ndot(pick, piece) for piece in pieces(reversed_rows)]
    folded = (folded[0] + folded[1]) + folded[2]
    crossing[...] = folded[INNER:INNER + BODY]
    corner_main, corner_edge = folded[3 * wide:3 * wide + 4], folded[3 * wide + 4:]
    lined_here[...] = ext[:, BODY, :]

    def fix_edge(into, inner_row, outer_row, first, mine, theirs):
        spot = iota((nlat, LANES), 1) % wide
        from_edge = spot < HALO if first else spot >= wide - HALO
        lined_here[...] = jnp.where(from_edge, edge[:, INNER, :], lined_here[...])
        ext[:, into:into + INNER, :] = edge[:, 0:INNER, :]
        ext[:, outer_row, :] = ext[:, outer_row, :] + edge[:, INNER + 1, :] * ext[:, BODY + 2, :]
        ext[:, inner_row, :] = ext[:, inner_row, :] + ext[:, BODY + 1, :] * edge[:, INNER + 2, :]
        line = iota((BODY, LANES), 0)
        across_out = corner_edge[theirs:theirs + 1] * corner_main[mine + 1:mine + 2]
        across_in = corner_main[mine:mine + 1] * corner_edge[theirs + 1:theirs + 2]
        crossing[...] = crossing[...] + jnp.where(
            line == outer_row, across_out, jnp.where(line == inner_row, across_in, 0.0)
        )

    @pl.when(j == 0)
    def _():
        fix_edge(0, INNER, INNER - 1, True, 2, 0)

    @pl.when(top)
    def _():
        fix_edge(INNER + strip, INNER + strip - 1, INNER + strip, False, 0, 2)

    columns_of = jnp.concatenate(
        [lined_here[...], jnp.zeros((LANES - nlat, LANES), F32)], axis=0
    ).T
    square = (wide, LANES)
    virtual = iota(square, 1) == nlat
    rate_low, rate_high, held_low, held_high = [columns_of[g * wide:(g + 1) * wide] for g in range(4)]
    rate_low = jnp.where(virtual, jnp.broadcast_to(folded[wide:2 * wide, 0:1], square), rate_low)
    held_low = jnp.where(virtual, jnp.broadcast_to(folded[2 * wide:3 * wide, 0:1], square), held_low)
    rows = slice(HALO - INNER, HALO - INNER + BODY)
    add_high = (rate_high * pltpu.roll(held_low, LANES - 1, 1))[rows]
    add_low = (rate_low * pltpu.roll(held_high, 1, 1))[rows]

    def lanes_of(c):
        return slice(c * LANES, (c + 1) * LANES)

    shift = HALO - INNER
    own_start = PAD + INNER
    bottom, ceiling = PAD, PAD + BODY
    body_lane = iota((BODY, LANES), 1)
    for c in range(nlat + 1):
        value = ext[c, 0:BODY, :] if c < nlat else crossing[...]
        value = jnp.where(body_lane == 0, value + add_low[:, c:c + 1], value)
        basis[0, c, bottom:ceiling, :] = jnp.where(
            body_lane == LANES - 1, value + add_high[:, c:c + 1], value
        )
    for step in range(BASIS - 1):
        low, high = (bottom, ceiling) if step < BASIS - 2 else (own_start, own_start + strip)

        def store_next(c, value, beside):
            lanes, rows = lanes_of(c), slice(low - PAD + shift, high - PAD + shift)
            basis[step + 1, c, low:high, :] = dg[rows, lanes] * value - quarter[rows, lanes] * beside

        stencil(basis.at[step], store_next, low, high)

    zero = jnp.zeros((8, LANES), F32)

    def accumulate(c, carry):
        sums = list(carry)
        for h in range(strip // 8):
            start = own_start + 8 * h
            values = [basis[b, c, start:start + 8, :] for b in range(BASIS)]
            split = [halves(value) for value in values]
            for n, (a, b) in enumerate(PAIRS):
                (ah, al), (bh, bl) = split[a], split[b]
                e = ah * bl + al * values[b]
                s, f = quick(sums[2 * n], ah * bh)
                sums[2 * n], sums[2 * n + 1] = s, sums[2 * n + 1] + (e + f)
        return tuple(sums)

    sums = lax.fori_loop(0, ny // LANES, accumulate, (zero,) * (2 * len(PAIRS)), unroll=2)
    packed_sums = [(sums[2 * n], sums[2 * n + 1]) for n in range(len(PAIRS))]
    packed_sums += [(zero, zero)] * (SLOTS - len(PAIRS))
    eight = iota((8, LANES), 0)
    for shift in (4, 2, 1):
        keep_row = (eight & shift) == 0
        merged = []
        for n in range(0, len(packed_sums), 2):
            (ah, al), (bh, bl) = packed_sums[n:n + 2]
            h, e = two_sum(
                jnp.where(keep_row, ah, pltpu.roll(bh, shift, 0)),
                jnp.where(keep_row, pltpu.roll(ah, 8 - shift, 0), bh),
            )
            l = jnp.where(keep_row, al, pltpu.roll(bl, shift, 0))
            l = l + jnp.where(keep_row, pltpu.roll(al, 8 - shift, 0), bl)
            merged.append((h, l + e))
        packed_sums = merged
    high, low = [jnp.concatenate([packed_sums[0][n], packed_sums[1][n]], axis=0) for n in range(2)]
    place = iota((SLOTS, LANES), 0)
    within = place & 7
    place = (place & 8) + ((within & 4) >> 2) + (within & 2) + ((within & 1) << 2)
    shift = LANES // 2
    while shift:
        high, e = two_sum(high, pltpu.roll(high, shift, 1))
        low = low + pltpu.roll(low, shift, 1) + e
        shift //= 2
    spot = iota((SLOTS, LANES), 1)
    packed = jnp.where(spot == place, high, jnp.where(spot == place + SLOTS, low, 0.0))
    message = jnp.sum(packed, axis=0, keepdims=True)

    parts[pl.ds(t, 1), :] = message
    own_part = parts.at[pl.ds(t, 1), :]
    sizes = (nlon // 2, 2, nlat // 4, 4)
    offsets = [
        (a, b, c, d)
        for a in range(sizes[0]) for b in range(sizes[1]) for c in range(sizes[2]) for d in range(sizes[3])
    ]

    def hops(offset):
        return sum(min(o, n - o) for o, n in zip(offset, sizes) if n > 2 or o) - 0.5 * offset[1]

    offsets = sorted(offsets[1:], key=hops, reverse=True)
    place_of = (i // 2, lax.rem(i, 2), j // 4, lax.rem(j, 4))
    moved = [
        [lax.rem(place_of[n] + o, sizes[n]) * scale for o in range(sizes[n])]
        for n, scale in enumerate((2, 1, 4, 1))
    ]
    pl.semaphore_wait(ready, nlon - 1)
    for a, b, c, d in offsets:
        remote(own_part, own_part, red_send, red_recv, moved[0][a] + moved[1][b], moved[2][c] + moved[3][d]).start()

    to_south.wait_recv()
    to_west.wait_recv()
    to_east.wait_recv()

    @pl.when(j > 0)
    def _():
        to_north.wait_recv()

    @pl.when(j == 0)
    def _():
        south[...] = jnp.zeros_like(south)

    @pl.when(top)
    def _():
        north[...] = flip_lanes(north[...])

    west[...] = west[...] * ocean_west
    east[...] = east[...] * ocean_east
    north[...] = ocean_north * north[...]
    south[...] = ocean_south * south[...]
    part = 32
    tile_row, tile_lane = iota((part, LANES), 0), iota((part, LANES), 1)
    first_row, last_row = tile_row == 0, tile_row == part - 1
    first_lane, last_lane = tile_lane == 0, tile_lane == LANES - 1
    count = cy // part
    columns = cx // LANES

    def update(k, _):
        from_south, from_north = south[pl.ds(k, 1), :], north[pl.ds(k, 1), :]

        def load(c, n):
            rows, lanes = slice(c * part, (c + 1) * part), slice(n * LANES, (n + 1) * LANES)
            return sea[rows, lanes] * th[k, rows, lanes]

        def across(n, vector):
            return jnp.broadcast_to(vector[:, n * LANES:(n + 1) * LANES], (part, LANES))

        value = [load(0, n) for n in range(columns)]
        before = [across(n, from_south) for n in range(columns)]
        up = [pltpu.roll(v, part - 1, 0) for v in value]
        for c in range(count):
            rows = slice(c * part, (c + 1) * part)
            if c + 1 < count:
                following = [load(c + 1, n) for n in range(columns)]
                up_next = [pltpu.roll(v, part - 1, 0) for v in following]
            else:
                following, up_next = None, [across(n, from_north) for n in range(columns)]
            down = [pltpu.roll(v, 1, 0) for v in value]
            right = [pltpu.roll(west[rows, :], LANES - levels - k, 1)] + [pltpu.roll(v, 1, 1) for v in value]
            left = [pltpu.roll(v, LANES - 1, 1) for v in value] + [pltpu.roll(east[rows, :], LANES - 1 - k, 1)]
            for n in range(columns):
                lanes = slice(n * LANES, (n + 1) * LANES)
                beside = jnp.where(first_row, before[n], down[n]) + jnp.where(last_row, up_next[n], up[n])
                beside = beside + jnp.where(first_lane, right[n], right[n + 1])
                beside = beside + jnp.where(last_lane, left[n + 1], left[n])
                out_theta[k, rows, lanes] = th[k, rows, lanes] + kp[rows, lanes] * (beside - 4.0 * value[n])
            value, before, up = following, down, up_next
        return 0

    lax.fori_loop(0, levels, update, 0)
    out_basis[...] = basis[0:BASIS - 1, 0:nlat, own_start:own_start + strip, :]
    whole(parts.at[pl.ds(0, total - 1), :], red_recv).wait()
    out_parts[...] = parts[...]

    whole(ext.at[0:nlat - 1, 0:SPAN, :], main_send).wait()
    left_edge.wait_send()
    right_edge.wait_send()
    diag_up.wait_send()
    diag_down.wait_send()
    diag_fold.wait_send()
    for far, near, own in sides:
        @pl.when(jnp.logical_not(own))
        def _():
            far.wait_send()

    @pl.when(top)
    def _():
        whole(tiles, fold_send).wait()
        fold_low.wait_send()

        @pl.when(jnp.logical_not(far_self))
        def _():
            fold_far.wait_send()

    @pl.when(j > 0)
    def _():
        to_south.wait_send()

    to_north.wait_send()
    to_west.wait_send()
    to_east.wait_send()
    whole(parts.at[pl.ds(0, total - 1), :], red_send).wait()


def finish(fresh, vectors, parts, out_theta, out_psi, psi, out_sem):
    pieces_of = fresh.shape[0] // 2
    stores = [
        pltpu.make_async_copy(fresh.at[pl.ds(2 * q, 2)], out_theta.at[pl.ds(2 * q, 2)], out_sem.at[0])
        for q in range(pieces_of)
    ]
    for copy in stores:
        copy.start()
    total = parts.shape[0]
    value = parts[...]
    error = jnp.zeros_like(value)
    half = total // 2
    while half >= 8:
        value, e = two_sum(value[:half], value[half:])
        error = error[:half] + error[half:] + e
        half //= 2
    for shift in (4, 2, 1):
        value, e = two_sum(value, pltpu.roll(value, shift, 0))
        error = error + pltpu.roll(error, shift, 0) + e
    lane = iota((1, LANES), 1)
    error = jnp.where(
        jnp.logical_and(lane >= SLOTS, lane < 2 * SLOTS), pltpu.roll(error[0:1], SLOTS, 1), 0.0
    )
    message = value[0:1] + error
    high, low = quick(message, pltpu.roll(message, LANES - SLOTS, 1))

    gram = {}
    for n, (a, b) in enumerate(PAIRS):
        gram[a, b] = gram[b, a] = tuple(
            jnp.broadcast_to(x[:, n:n + 1], (1, LANES)) for x in (high, low)
        )
    size = BASIS - 1

    def scaled(x, factor):
        return x[0] * factor, x[1] * factor

    matrix = [
        [
            df_add(
                scaled(gram[a, b + 1], 4.0),
                df_add(scaled(gram[a, b], 4.0), gram[a, b]),
            )
            for b in range(size)
        ]
        for a in range(size)
    ]
    right = [gram[0, a] for a in range(size)]
    for p in range(size):
        for a in range(p + 1, size):
            factor = df_div(matrix[a][p], matrix[p][p])
            for b in range(p + 1, size):
                matrix[a][b] = df_sub(matrix[a][b], df_mul(factor, matrix[p][b]))
            right[a] = df_sub(right[a], df_mul(factor, right[p]))
    answer = [None] * size
    for p in reversed(range(size)):
        value = right[p][0]
        for b in range(p + 1, size):
            value = value - matrix[p][b][0] * answer[b][0]
        answer[p] = (value / matrix[p][p][0],)
    strip = psi.shape[0]
    spread = [jnp.broadcast_to(x[0], (strip, LANES)) for x in answer]

    def combine(c, _):
        lanes = pl.ds(pl.multiple_of(c * LANES, LANES), LANES)
        value = spread[size - 1] * vectors[size - 1, c]
        for b in reversed(range(size - 1)):
            value = value + spread[b] * vectors[b, c]
        psi[:, lanes] = value
        return 0

    lax.fori_loop(0, vectors.shape[1], combine, 0)

    store_psi = pltpu.make_async_copy(psi, out_psi, out_sem.at[1])
    store_psi.start()
    store_psi.wait()
    pltpu.make_async_copy(fresh, out_theta, out_sem.at[0]).wait()


def per_device(nlon, nlat, theta, kappa, layer_weight, diag, land_blocks):
    levels, cy, cx = theta.shape
    strip, ny = diag.shape
    wide = strip + 2 * HALO
    vmem = pl.BlockSpec(memory_space=pltpu.VMEM)
    hbm = pl.BlockSpec(memory_space=pltpu.HBM)
    dma = pltpu.SemaphoreType.DMA
    operands = (layer_weight, land_blocks, theta, kappa, diag)
    fresh, vectors, parts = pl.pallas_call(
        functools.partial(kernel, nlon, nlat),
        out_shape=(
            jax.ShapeDtypeStruct(theta.shape, F32),
            jax.ShapeDtypeStruct((BASIS - 1, nlat, strip, cy), F32),
            jax.ShapeDtypeStruct((nlon * nlat, LANES), F32),
        ),
        in_specs=[hbm] * 5,
        out_specs=(vmem, vmem, vmem),
        scratch_shapes=[
            pltpu.SMEM(layer_weight.shape, F32),
            pltpu.VMEM(land_blocks.shape, jnp.int32),
            pltpu.VMEM((levels, cy, cx), F32),
            pltpu.VMEM((cy, cx), F32),
            pltpu.VMEM((cy, cx), F32),
            pltpu.VMEM((cx + 2 * HALO, cy), F32),
            pltpu.VMEM((nlat, 8, LANES), F32),
            pltpu.VMEM((nlat, wide, cy), F32),
            pltpu.VMEM((2, HALO, cy), F32),
            pltpu.VMEM((nlat, wide, cy), F32),
            pltpu.VMEM((nlat, HALO, cy), F32),
            pltpu.VMEM((BODY, LANES), F32),
            pltpu.VMEM((nlat, LANES), F32),
            pltpu.VMEM((strip, ny), F32),
            pltpu.VMEM((nlat + 1, wide, cy), F32),
            pltpu.VMEM((wide, ny + LANES), F32),
            pltpu.VMEM((wide, ny + LANES), F32),
            pltpu.VMEM((wide, ny + LANES), F32),
            pltpu.VMEM((BASIS, nlat + 1, strip + 2 * INNER + 2 * PAD, cy), F32),
            pltpu.VMEM((2, levels, cx), F32),
            pltpu.VMEM((levels, cx), F32),
            pltpu.VMEM((levels, cx), F32),
            pltpu.VMEM((cy, LANES), F32),
            pltpu.VMEM((cy, LANES), F32),
            pltpu.VMEM((cy, LANES), F32),
            pltpu.VMEM((nlat, 8, LANES), F32),
            pltpu.VMEM((8, LANES), F32),
            pltpu.VMEM((8, LANES), F32),
            pltpu.VMEM((nlon * nlat, LANES), F32),
            dma((8,)),
            dma,
            dma,
            dma((2,)),
            dma,
            dma,
            dma,
            dma,
            dma((2,)),
            dma((5,)),
            dma((5,)),
            dma((4,)),
            dma((4,)),
            dma,
            dma,
            pltpu.SemaphoreType.REGULAR,
        ],
        compiler_params=pltpu.CompilerParams(
            collective_id=0, has_side_effects=True, vmem_limit_bytes=32 << 20
        ),
        name="ocean_step",
    )(*[pltpu.with_memory_space_constraint(x, pltpu.HBM) for x in operands])
    return pl.pallas_call(
        finish,
        out_shape=(
            jax.ShapeDtypeStruct(theta.shape, F32),
            jax.ShapeDtypeStruct(diag.shape, F32),
        ),
        in_specs=[vmem, vmem, vmem],
        out_specs=(hbm, hbm),
        scratch_shapes=[pltpu.VMEM(diag.shape, F32), dma((2,))],
        compiler_params=pltpu.CompilerParams(vmem_limit_bytes=16 << 20),
        name="ocean_finish",
    )(fresh, vectors, parts)


def solution(mesh):
    placed = (P(None, "lat", "lon"), P("lat", "lon"), P(), P(("lon", "lat"), None), P())
    return jax.shard_map(
        functools.partial(per_device, mesh.shape["lon"], mesh.shape["lat"]),
        mesh=mesh,
        in_specs=placed,
        out_specs=(P(None, "lat", "lon"), P(("lon", "lat"), None)),
        check_vma=False,
    )
```

```python
import functools

import jax
import jax.numpy as jnp
from jax import lax
from jax.experimental import pallas as pl
from jax.experimental.pallas import tpu as pltpu
from jax.sharding import PartitionSpec as P

MESH = pl.DeviceIdType.MESH
BS = 32
HALO = 8
PAD = 8
INNER = 4
BODY = 24
SPAN = BODY + 3
LANES = 128
F32 = jnp.float32
BF16 = jnp.bfloat16
BASIS = 5
PAIRS = [(a, b) for a in range(BASIS) for b in range(a, BASIS) if a < BASIS - 1]
SLOTS = 16


def iota(shape, axis):
    return lax.broadcasted_iota(jnp.int32, shape, axis)


def hot(condition):
    return jnp.where(condition, 1.0, 0.0).astype(BF16)


def bdot(left, right):
    return jnp.dot(left, right, preferred_element_type=F32)


def ndot(left, right):
    return lax.dot_general(left, right, (((1,), (1,)), ((), ())), preferred_element_type=F32)


def pieces(value):
    first = value.astype(BF16)
    rest = value - first.astype(F32)
    second = rest.astype(BF16)
    third = (rest - second.astype(F32)).astype(BF16)
    return [first, second, third]


def flip_lanes(value):
    width = value.shape[1]
    turn = hot(iota((width, width), 0) + iota((width, width), 1) == width - 1)
    parts = [bdot(piece, turn) for piece in pieces(value)]
    return (parts[0] + parts[1]) + parts[2]


def flip_rows(value, groups):
    count = value.shape[0]
    row = iota((count, count), 0)
    ends, start = jnp.zeros((count, count), jnp.int32), 0
    for size in groups:
        ends = jnp.where(row >= start, 2 * start + size - 1, ends)
        start += size
    turn = hot(row + iota((count, count), 1) == ends)
    parts = [bdot(turn, piece) for piece in pieces(value)]
    return (parts[0] + parts[1]) + parts[2]


def two_sum(a, b):
    s = a + b
    t = s - a
    return s, (a - (s - t)) + (b - t)


def halves(a):
    t = a * 4097.0
    high = t - (t - a)
    return high, a - high


def two_prod(a, b):
    p = a * b
    ah, al = halves(a)
    bh, bl = halves(b)
    return p, ((ah * bh - p) + ah * bl + al * bh) + al * bl


def quick(a, b):
    s = a + b
    return s, b - (s - a)


def df_mul(x, y):
    p, e = two_prod(x[0], y[0])
    return quick(p, e + (x[0] * y[1] + x[1] * y[0]))


def df_add(x, y):
    s, e = two_sum(x[0], y[0])
    return quick(s, e + (x[1] + y[1]))


def df_sub(x, y):
    return df_add(x, (-y[0], -y[1]))


def df_div(x, y):
    first = x[0] / y[0]
    rest = df_sub(x, df_mul(y, (first, jnp.zeros_like(first))))
    second = rest[0] / y[0]
    return quick(first, second)


def stencil(ref, emit, low, high):
    count, _, width = ref.shape
    lane = iota((high - low, width), 1)
    first, last = lane == 0, lane == width - 1

    def load(c, shift=0):
        return ref[c, low + shift:high + shift, :]

    value = load(0)
    before = jnp.zeros_like(value)
    up = pltpu.roll(value, width - 1, 1)
    for c in range(count):
        if c + 1 < count:
            following = load(c + 1)
            up_next = pltpu.roll(following, width - 1, 1)
        else:
            following, up_next = None, up
        down = pltpu.roll(value, 1, 1)
        beside = jnp.where(first, before, down) + jnp.where(last, up_next, up)
        emit(c, value, (beside + load(c, -1)) + load(c, 1))
        value, before, up = following, down, up_next


def kernel(
    nlon, nlat,
    weight_in, land_in, theta, kappa, diag,
    out_theta, out_basis, out_parts,
    weight, land, th, kp, sea, turned, windows, packs, edge_packs, ext, edge, crossing, lined_here, flat, dgx, dg, ocs, quarter, basis, rows_out, north, south, cols_out, east, west,
    tiles, fold, fold_edge, parts,
    in_sem, main_send, main_recv, edge_send, edge_recv, fold_send, fold_low_send, fold_far_send, fold_recv,
    diag_send, diag_recv, halo_send, halo_recv, red_send, red_recv, ready,
):
    levels, cy, cx = th.shape
    ny, nx = cy * nlat, cx * nlon
    strip = cx // nlat
    wide = strip + 2 * HALO
    by, bx = land.shape
    total = nlon * nlat
    i = lax.axis_index("lon")
    j = lax.axis_index("lat")
    t = i * nlat + j
    top = j == nlat - 1
    ends = jnp.logical_or(j == 0, top)

    def remote(src, dst, send, recv, lon, lat):
        return pltpu.make_async_remote_copy(
            src_ref=src, dst_ref=dst, send_sem=send, recv_sem=recv,
            device_id=(lon, lat), device_id_type=MESH,
        )

    def lon_of(value):
        return lax.rem(value + 2 * nlon, nlon)

    def lat_of(value):
        return lax.rem(value + 2 * nlat, nlat)

    def whole(ref, sem):
        return pltpu.make_async_copy(ref, ref, sem)

    def greet(lon, lat):
        pl.semaphore_signal(barrier, inc=1, device_id=(lon, lat), device_id_type=MESH)

    def ring(value, size):
        return min(value, size - value)

    lat_order = sorted(range(1, nlat), key=lambda d: -ring(d // 4, nlat // 4) - ring(d % 4, 4))
    lon_order = sorted(range(1, nlon), key=lambda d: -ring(d // 2, nlon // 2) - 0.5 * (d % 2))

    dgx[nlat, 0:HALO, :] = jnp.zeros((HALO, cy), F32)
    dgx[nlat, HALO + strip:, :] = jnp.zeros((HALO, cy), F32)

    barrier = pltpu.get_barrier_semaphore()
    for d in lat_order:
        greet(i, lax.rem(j + d, nlat))
    for d in lon_order:
        greet(lax.rem(i + d, nlon), j)
    greet(nlon - 1 - i, nlat - 1)
    for shift in (1, 0, -1):
        other = lax.rem(total - 1 - t + shift + total, total)

        @pl.when(other != t)
        def _():
            greet(other // nlat, lax.rem(other, nlat))

    @pl.when(j == 0)
    def _():
        for lat in range(nlat):
            greet(lon_of(i - 1), lat)
        greet(lon_of(nlon - i), nlat - 1)

    @pl.when(top)
    def _():
        for lat in range(nlat):
            greet(lon_of(i + 1), lat)

    chunk = levels // 4
    loads = [
        pltpu.make_async_copy(theta.at[pl.ds(q * chunk, chunk)], th.at[pl.ds(q * chunk, chunk)], in_sem.at[q])
        for q in range(4)
    ]
    load_kappa = pltpu.make_async_copy(kappa, kp, in_sem.at[4])
    load_diag = pltpu.make_async_copy(diag, flat, in_sem.at[5])
    load_weight = pltpu.make_async_copy(weight_in, weight, in_sem.at[6])
    load_land = pltpu.make_async_copy(land_in, land, in_sem.at[7])
    load_kappa.start()
    load_weight.start()
    for copy in loads:
        copy.start()
    load_diag.start()
    load_land.start()


    load_land.wait()
    table = land[...].astype(F32).astype(BF16)
    row_block = (j * cy + iota((cy, by), 0)) >> 5
    on_rows = bdot(hot(row_block == iota((cy, by), 1)), table).astype(BF16)
    col_block = (i * cx + iota((bx, cx), 1)) >> 5
    cols_hot = hot(col_block == iota((bx, cx), 0))
    sea[...] = bdot(on_rows, cols_hot)
    load_kappa.wait()
    kp[...] = sea[...] * kp[...]
    load_weight.wait()
    column = jnp.zeros((cy, cx), F32)
    for q in range(4):
        loads[q].wait()
        for k in range(q * chunk, (q + 1) * chunk):
            column = column + weight[k] * th[k]
    held, rate = sea[...] * column, kp[...]
    block_row, block_lane = iota((cy, cx), 0), iota((cy, cx), 1)
    beside = jnp.where(block_row == 0, 0.0, pltpu.roll(held, 1, 0))
    beside = beside + jnp.where(block_row == cy - 1, 0.0, pltpu.roll(held, cy - 1, 0))
    beside = beside + jnp.where(block_lane == 0, 0.0, pltpu.roll(held, 1, 1))
    beside = beside + jnp.where(block_lane == cx - 1, 0.0, pltpu.roll(held, cx - 1, 1))
    force = held + rate * (beside - 4.0 * held)
    turned[0:HALO, :] = jnp.zeros((HALO, cy), F32)
    turned[HALO + cx:, :] = jnp.zeros((HALO, cy), F32)
    turned[HALO:HALO + cx, :] = force.T

    lane = iota((cy, LANES), 1)
    ring_columns = jnp.where(
        lane < 2,
        jnp.where(lane == 0, rate[:, 0:LANES], pltpu.roll(held[:, 0:LANES], 1, 1)),
        jnp.where(
            lane == 2, pltpu.roll(rate[:, cx - LANES:], 3, 1), pltpu.roll(held[:, cx - LANES:], 4, 1)
        ),
    )
    ring_rows = ring_columns.T[0:8]

    lines = jnp.concatenate([rate[0:1], rate[cy - 1:], held[0:1], held[cy - 1:]] * 2, axis=0)
    for m in range(nlat):
        windows[m] = pltpu.roll(lines, (HALO - strip * m) % cx, 1)[:, 0:LANES]
    lanes_here = iota((nlat, LANES), 1)
    lined = windows[:, 0, :]
    for g in range(1, 4):
        lined = jnp.where(lanes_here >= wide * g, pltpu.roll(windows[:, g, :], wide * g, 1), lined)
    for m in range(nlat):
        start = HALO - INNER + strip * m
        packs[m, 0:BODY, :] = turned[start:start + BODY, :]
        packs[m, BODY:BODY + 1, :] = lined[m:m + 1]
    packs[0, BODY + 1:SPAN, :] = ring_rows[0:2]
    packs[nlat - 1, BODY + 1:SPAN, :] = ring_rows[2:4]
    for n, (start, m) in enumerate(((HALO, nlat - 1), (HALO + cx - INNER, 0))):
        edge_packs[n, 0:INNER, :] = turned[start:start + INNER, :]
        edge_packs[n, INNER:INNER + 1, :] = lined[m:m + 1]
        edge_packs[n, INNER + 1:INNER + 3, :] = ring_rows[2 * n:2 * n + 2]

    @pl.when(top)
    def _():
        lanes8 = iota((8, LANES), 1)
        corner = pltpu.roll(ring_columns[cy - 8:], 3 * wide, 1)
        for m in range(nlat):
            start = strip * (nlat - 1 - m) - HALO
            tile = corner
            for g, field in ((2, held), (1, rate), (0, force)):
                shifted = pltpu.roll(field[cy - 8:], (g * wide - start) % cx, 1)[:, 0:LANES]
                tile = jnp.where(lanes8 < (g + 1) * wide, shifted, tile)
            tiles[m] = tile

    load_diag.wait()
    for c in range(nlat):
        dgx[c, HALO:HALO + strip, :] = flat[:, c * cy:(c + 1) * cy]

    own_folds = [lax.rem(total - 1 - t + shift + total, total) == t for shift in (1, -1)]
    awaited = nlat + nlon + 3 + jnp.where(top, nlat + 1, 0)
    for own in own_folds:
        awaited = awaited - jnp.where(own, 1, 0)
    pl.semaphore_wait(barrier, awaited)

    own_slot = ext.at[j, 0:SPAN, :]

    def block_rows(m):
        return packs.at[m, 0:SPAN, :]

    def main_copy(d):
        m = lax.rem(j + d, nlat)
        return remote(block_rows(m), own_slot, main_send, main_recv, i, m)

    for d in lat_order:
        main_copy(d).start()
    pltpu.make_async_copy(block_rows(j), own_slot, main_recv).start()
    edge_slot = edge.at[j, 0:INNER + 3, :]
    left_edge = remote(
        edge_packs.at[0, 0:INNER + 3, :], edge_slot, edge_send.at[0], edge_recv, lon_of(i - 1), nlat - 1
    )
    right_edge = remote(
        edge_packs.at[1, 0:INNER + 3, :], edge_slot, edge_send.at[1], edge_recv, lon_of(i + 1), 0
    )
    left_edge.start()
    right_edge.start()

    def fold_copy(m):
        return remote(tiles.at[m], fold, fold_send, fold_recv.at[0], nlon - 1 - i, m)

    far_lon = lon_of(nlon - 2 - i)
    far_self = far_lon == i
    fold_far = remote(
        tiles.at[nlat - 1], fold_edge, fold_far_send, fold_recv.at[1], far_lon, nlat - 1
    )
    fold_far_own = pltpu.make_async_copy(tiles.at[nlat - 1], fold_edge, fold_recv.at[1])
    fold_low = remote(tiles.at[0], fold_edge, fold_low_send, fold_recv.at[1], lon_of(nlon - i), 0)

    @pl.when(top)
    def _():
        for m in range(nlat):
            fold_copy(m).start()
        fold_low.start()

        @pl.when(far_self)
        def _():
            fold_far_own.start()

        @pl.when(jnp.logical_not(far_self))
        def _():
            fold_far.start()

    for d in range(1, nlon):
        pl.semaphore_signal(
            ready, inc=1, device_id=(lax.rem(i + d, nlon), j), device_id_type=MESH
        )

    after, before = lax.rem(t + 1, total), lax.rem(t + total - 1, total)
    depth = BASIS - 2
    own_low = slice(HALO, HALO + depth)
    own_high = slice(HALO + strip - depth, HALO + strip)
    halo_low = slice(HALO - depth, HALO)
    halo_high = slice(HALO + strip, HALO + strip + depth)
    diag_up = remote(
        dgx.at[0:nlat, own_high, :], dgx.at[0:nlat, halo_low, :], diag_send.at[0], diag_recv.at[0],
        after // nlat, lax.rem(after, nlat),
    )
    diag_down = remote(
        dgx.at[0:nlat, own_low, :], dgx.at[0:nlat, halo_high, :], diag_send.at[1], diag_recv.at[1],
        before // nlat, lax.rem(before, nlat),
    )
    diag_up.start()
    diag_down.start()
    middle = slice(HALO, HALO + strip)
    diag_fold = remote(
        dgx.at[nlat - 1, middle, :], dgx.at[nlat, middle, :], diag_send.at[2], diag_recv.at[2],
        nlon - 1 - i, nlat - 1 - j,
    )
    diag_fold.start()
    sides = []
    for n, (shift, src, dst) in enumerate(((1, own_low, halo_high), (-1, own_high, halo_low))):
        other = lax.rem(total - 1 - t + shift + total, total)
        src_ref, dst_ref = dgx.at[nlat - 1, src, :], dgx.at[nlat, dst, :]
        sides.append((
            remote(
                src_ref, dst_ref, diag_send.at[3 + n], diag_recv.at[3 + n], other // nlat, lax.rem(other, nlat)
            ),
            pltpu.make_async_copy(src_ref, dst_ref, diag_recv.at[3 + n]),
            own_folds[n],
        ))
    for far, near, own in sides:
        @pl.when(own)
        def _():
            near.start()

        @pl.when(jnp.logical_not(own))
        def _():
            far.start()

    rows_out[0] = th[:, 0, :]
    rows_out[1] = th[:, cy - 1, :]
    to_south = remote(rows_out.at[0], north, halo_send.at[0], halo_recv.at[0], i, lat_of(j - 1))
    to_north = remote(rows_out.at[1], south, halo_send.at[1], halo_recv.at[1], i, lat_of(j + 1))
    to_fold = remote(rows_out.at[1], north, halo_send.at[1], halo_recv.at[0], nlon - 1 - i, j)


    lane = iota((cy, LANES), 1)
    packed = jnp.zeros((cy, LANES), F32)
    for k in range(levels):
        packed = jnp.where(lane == k, pltpu.roll(th[k, :, 0:LANES], k, 1), packed)
        packed = jnp.where(
            lane == levels + k, pltpu.roll(th[k, :, cx - LANES:cx], levels + k + 1, 1), packed
        )
    cols_out[...] = packed
    to_west = remote(cols_out, east, halo_send.at[2], halo_recv.at[2], lon_of(i - 1), j)
    to_east = remote(cols_out, west, halo_send.at[3], halo_recv.at[3], lon_of(i + 1), j)

    basis[:, :, 0:PAD, :] = jnp.zeros((BASIS, nlat + 1, PAD, cy), F32)
    tail = PAD + strip + 2 * INNER
    basis[:, :, tail:, :] = jnp.zeros((BASIS, nlat + 1, PAD, cy), F32)

    west_block = lax.rem(i * (cx // BS) + bx - 1, bx)
    east_block = lax.rem((i + 1) * (cx // BS), bx)
    ocean_west = bdot(on_rows, hot(iota((bx, LANES), 0) == west_block))
    ocean_east = bdot(on_rows, hot(iota((bx, LANES), 0) == east_block))
    edge_row = iota((8, by), 0)
    edge_col = iota((8, by), 1)
    south_hot = hot(jnp.logical_and(edge_row == 0, edge_col == j * (cy // BS) - 1))
    north_block = jnp.where(top, by - 1, (j + 1) * (cy // BS))
    north_hot = hot(jnp.logical_and(edge_row == 0, edge_col == north_block))
    north_cols = jnp.where(top, bx - 1 - col_block, col_block)
    ocean_south = bdot(bdot(south_hot, table).astype(BF16), cols_hot)[0:1]
    ocean_north = bdot(
        bdot(north_hot, table).astype(BF16), hot(north_cols == iota((bx, cx), 0))
    )[0:1]

    strip_x = (strip * t - HALO + nx + iota((wide, bx), 0)) % nx >> 5
    strip_hot = hot(strip_x == iota((wide, bx), 1))
    on_cols = ndot(strip_hot, table).astype(BF16)
    ocs[:, 0:ny] = bdot(on_cols, hot((iota((by, ny), 1) >> 5) == iota((by, ny), 0)))
    mirror_hot = hot((bx - 1 - strip_x) == iota((wide, bx), 1))
    on_mirror = ndot(mirror_hot, table).astype(BF16)
    keep = jnp.logical_and(iota((by, LANES), 0) == by - 1, iota((by, LANES), 1) < 8)
    ocs[:, ny:ny + LANES] = bdot(on_mirror, hot(keep))

    diag_up.wait_recv()
    diag_down.wait_recv()
    diag_fold.wait_recv()
    for far, near, own in sides:
        far.wait_recv()
    for c in range(nlat):
        dg[:, c * cy:(c + 1) * cy] = dgx[c]
    dg[:, ny:] = flip_rows(flip_lanes(dgx[nlat]), (wide,))
    dg[...] = ocs[...] * ((dg[...] - 1.0) * 0.25)
    quarter[...] = ocs[...] * 0.25

    whole(ext.at[0:nlat, 0:SPAN, :], main_recv).wait()
    @pl.when(j > 0)
    def _():
        to_south.start()

    @pl.when(jnp.logical_not(top))
    def _():
        to_north.start()

    @pl.when(top)
    def _():
        to_fold.start()

    to_west.start()
    to_east.start()
    whole(fold, fold_recv.at[0]).wait()

    @pl.when(ends)
    def _():
        whole(edge.at[:, 0:INNER + 3, :], edge_recv).wait()
        whole(fold_edge, fold_recv.at[1]).wait()
        spot = iota((8, LANES), 1)
        outer = jnp.logical_or(
            jnp.logical_and(top, spot % wide < HALO), jnp.logical_and(j == 0, spot % wide >= wide - HALO)
        )
        outer = jnp.logical_and(outer, spot < 3 * wide)
        merged = jnp.where(outer, fold_edge[...], fold[...])
        fold[...] = jnp.where(spot >= 3 * wide + 4, pltpu.roll(fold_edge[...], 4, 1), merged)

    row = iota((3 * wide + 8, LANES), 0)
    source = jnp.where(row < 3 * wide, (row // wide) * wide + wide - 1 - row % wide, row)
    pick = hot(source == iota((3 * wide + 8, LANES), 1))
    reversed_rows = jnp.concatenate(
        [fold[q:q + 1, :] for q in reversed(range(8))] + [jnp.zeros((LANES - 8, LANES), F32)], axis=0
    )
    folded = [ndot(pick, piece) for piece in pieces(reversed_rows)]
    folded = (folded[0] + folded[1]) + folded[2]
    crossing[...] = folded[INNER:INNER + BODY]
    corner_main, corner_edge = folded[3 * wide:3 * wide + 4], folded[3 * wide + 4:]
    lined_here[...] = ext[:, BODY, :]

    def fix_edge(into, inner_row, outer_row, first, mine, theirs):
        spot = iota((nlat, LANES), 1) % wide
        from_edge = spot < HALO if first else spot >= wide - HALO
        lined_here[...] = jnp.where(from_edge, edge[:, INNER, :], lined_here[...])
        ext[:, into:into + INNER, :] = edge[:, 0:INNER, :]
        ext[:, outer_row, :] = ext[:, outer_row, :] + edge[:, INNER + 1, :] * ext[:, BODY + 2, :]
        ext[:, inner_row, :] = ext[:, inner_row, :] + ext[:, BODY + 1, :] * edge[:, INNER + 2, :]
        line = iota((BODY, LANES), 0)
        across_out = corner_edge[theirs:theirs + 1] * corner_main[mine + 1:mine + 2]
        across_in = corner_main[mine:mine + 1] * corner_edge[theirs + 1:theirs + 2]
        crossing[...] = crossing[...] + jnp.where(
            line == outer_row, across_out, jnp.where(line == inner_row, across_in, 0.0)
        )

    @pl.when(j == 0)
    def _():
        fix_edge(0, INNER, INNER - 1, True, 2, 0)

    @pl.when(top)
    def _():
        fix_edge(INNER + strip, INNER + strip - 1, INNER + strip, False, 0, 2)

    columns_of = jnp.concatenate(
        [lined_here[...], jnp.zeros((LANES - nlat, LANES), F32)], axis=0
    ).T
    square = (wide, LANES)
    virtual = iota(square, 1) == nlat
    rate_low, rate_high, held_low, held_high = [columns_of[g * wide:(g + 1) * wide] for g in range(4)]
    rate_low = jnp.where(virtual, jnp.broadcast_to(folded[wide:2 * wide, 0:1], square), rate_low)
    held_low = jnp.where(virtual, jnp.broadcast_to(folded[2 * wide:3 * wide, 0:1], square), held_low)
    rows = slice(HALO - INNER, HALO - INNER + BODY)
    add_high = (rate_high * pltpu.roll(held_low, LANES - 1, 1))[rows]
    add_low = (rate_low * pltpu.roll(held_high, 1, 1))[rows]

    def lanes_of(c):
        return slice(c * LANES, (c + 1) * LANES)

    shift = HALO - INNER
    own_start = PAD + INNER
    bottom, ceiling = PAD, PAD + BODY
    body_lane = iota((BODY, LANES), 1)
    for c in range(nlat + 1):
        value = ext[c, 0:BODY, :] if c < nlat else crossing[...]
        value = jnp.where(body_lane == 0, value + add_low[:, c:c + 1], value)
        basis[0, c, bottom:ceiling, :] = jnp.where(
            body_lane == LANES - 1, value + add_high[:, c:c + 1], value
        )
    for step in range(BASIS - 1):
        low, high = (bottom, ceiling) if step < BASIS - 2 else (own_start, own_start + strip)

        def store_next(c, value, beside):
            lanes, rows = lanes_of(c), slice(low - PAD + shift, high - PAD + shift)
            basis[step + 1, c, low:high, :] = dg[rows, lanes] * value - quarter[rows, lanes] * beside

        stencil(basis.at[step], store_next, low, high)

    zero = jnp.zeros((8, LANES), F32)

    def accumulate(c, carry):
        sums = list(carry)
        for h in range(strip // 8):
            start = own_start + 8 * h
            values = [basis[b, c, start:start + 8, :] for b in range(BASIS)]
            split = [halves(value) for value in values]
            for n, (a, b) in enumerate(PAIRS):
                (ah, al), (bh, bl) = split[a], split[b]
                e = ah * bl + al * values[b]
                s, f = quick(sums[2 * n], ah * bh)
                sums[2 * n], sums[2 * n + 1] = s, sums[2 * n + 1] + (e + f)
        return tuple(sums)

    sums = lax.fori_loop(0, ny // LANES, accumulate, (zero,) * (2 * len(PAIRS)))
    packed_sums = [(sums[2 * n], sums[2 * n + 1]) for n in range(len(PAIRS))]
    packed_sums += [(zero, zero)] * (SLOTS - len(PAIRS))
    eight = iota((8, LANES), 0)
    for shift in (4, 2, 1):
        keep_row = (eight & shift) == 0
        merged = []
        for n in range(0, len(packed_sums), 2):
            (ah, al), (bh, bl) = packed_sums[n:n + 2]
            h, e = two_sum(
                jnp.where(keep_row, ah, pltpu.roll(bh, shift, 0)),
                jnp.where(keep_row, pltpu.roll(ah, 8 - shift, 0), bh),
            )
            l = jnp.where(keep_row, al, pltpu.roll(bl, shift, 0))
            l = l + jnp.where(keep_row, pltpu.roll(al, 8 - shift, 0), bl)
            merged.append((h, l + e))
        packed_sums = merged
    high, low = [jnp.concatenate([packed_sums[0][n], packed_sums[1][n]], axis=0) for n in range(2)]
    place = iota((SLOTS, LANES), 0)
    within = place & 7
    place = (place & 8) + ((within & 4) >> 2) + (within & 2) + ((within & 1) << 2)
    shift = LANES // 2
    while shift:
        high, e = two_sum(high, pltpu.roll(high, shift, 1))
        low = low + pltpu.roll(low, shift, 1) + e
        shift //= 2
    spot = iota((SLOTS, LANES), 1)
    packed = jnp.where(spot == place, high, jnp.where(spot == place + SLOTS, low, 0.0))
    message = jnp.sum(packed, axis=0, keepdims=True)

    parts[pl.ds(t, 1), :] = message
    own_part = parts.at[pl.ds(t, 1), :]
    sizes = (nlon // 2, 2, nlat // 4, 4)
    offsets = [
        (a, b, c, d)
        for a in range(sizes[0]) for b in range(sizes[1]) for c in range(sizes[2]) for d in range(sizes[3])
    ]

    def hops(offset):
        return sum(min(o, n - o) for o, n in zip(offset, sizes) if n > 2 or o) - 0.5 * offset[1]

    offsets = sorted(offsets[1:], key=hops, reverse=True)
    place_of = (i // 2, lax.rem(i, 2), j // 4, lax.rem(j, 4))
    moved = [
        [lax.rem(place_of[n] + o, sizes[n]) * scale for o in range(sizes[n])]
        for n, scale in enumerate((2, 1, 4, 1))
    ]
    pl.semaphore_wait(ready, nlon - 1)
    for a, b, c, d in offsets:
        remote(own_part, own_part, red_send, red_recv, moved[0][a] + moved[1][b], moved[2][c] + moved[3][d]).start()

    to_south.wait_recv()
    to_west.wait_recv()
    to_east.wait_recv()

    @pl.when(j > 0)
    def _():
        to_north.wait_recv()

    @pl.when(j == 0)
    def _():
        south[...] = jnp.zeros_like(south)

    @pl.when(top)
    def _():
        north[...] = flip_lanes(north[...])

    west[...] = west[...] * ocean_west
    east[...] = east[...] * ocean_east
    north[...] = ocean_north * north[...]
    south[...] = ocean_south * south[...]
    part = 32
    tile_row, tile_lane = iota((part, LANES), 0), iota((part, LANES), 1)
    first_row, last_row = tile_row == 0, tile_row == part - 1
    first_lane, last_lane = tile_lane == 0, tile_lane == LANES - 1
    count = cy // part
    columns = cx // LANES

    def update(k, _):
        from_south, from_north = south[pl.ds(k, 1), :], north[pl.ds(k, 1), :]

        def load(c, n):
            rows, lanes = slice(c * part, (c + 1) * part), slice(n * LANES, (n + 1) * LANES)
            return sea[rows, lanes] * th[k, rows, lanes]

        def across(n, vector):
            return jnp.broadcast_to(vector[:, n * LANES:(n + 1) * LANES], (part, LANES))

        value = [load(0, n) for n in range(columns)]
        before = [across(n, from_south) for n in range(columns)]
        up = [pltpu.roll(v, part - 1, 0) for v in value]
        for c in range(count):
            rows = slice(c * part, (c + 1) * part)
            if c + 1 < count:
                following = [load(c + 1, n) for n in range(columns)]
                up_next = [pltpu.roll(v, part - 1, 0) for v in following]
            else:
                following, up_next = None, [across(n, from_north) for n in range(columns)]
            down = [pltpu.roll(v, 1, 0) for v in value]
            right = [pltpu.roll(west[rows, :], LANES - levels - k, 1)] + [pltpu.roll(v, 1, 1) for v in value]
            left = [pltpu.roll(v, LANES - 1, 1) for v in value] + [pltpu.roll(east[rows, :], LANES - 1 - k, 1)]
            for n in range(columns):
                lanes = slice(n * LANES, (n + 1) * LANES)
                beside = jnp.where(first_row, before[n], down[n]) + jnp.where(last_row, up_next[n], up[n])
                beside = beside + jnp.where(first_lane, right[n], right[n + 1])
                beside = beside + jnp.where(last_lane, left[n + 1], left[n])
                out_theta[k, rows, lanes] = th[k, rows, lanes] + kp[rows, lanes] * (beside - 4.0 * value[n])
            value, before, up = following, down, up_next
        return 0

    lax.fori_loop(0, levels, update, 0)
    out_basis[...] = basis[0:BASIS - 1, 0:nlat, own_start:own_start + strip, :]
    whole(parts.at[pl.ds(0, total - 1), :], red_recv).wait()
    out_parts[...] = parts[...]

    whole(ext.at[0:nlat - 1, 0:SPAN, :], main_send).wait()
    left_edge.wait_send()
    right_edge.wait_send()
    diag_up.wait_send()
    diag_down.wait_send()
    diag_fold.wait_send()
    for far, near, own in sides:
        @pl.when(jnp.logical_not(own))
        def _():
            far.wait_send()

    @pl.when(top)
    def _():
        whole(tiles, fold_send).wait()
        fold_low.wait_send()

        @pl.when(jnp.logical_not(far_self))
        def _():
            fold_far.wait_send()

    @pl.when(j > 0)
    def _():
        to_south.wait_send()

    to_north.wait_send()
    to_west.wait_send()
    to_east.wait_send()
    whole(parts.at[pl.ds(0, total - 1), :], red_send).wait()


def finish(fresh, vectors, parts, out_theta, out_psi, psi, out_sem):
    pieces_of = fresh.shape[0] // 2
    stores = [
        pltpu.make_async_copy(fresh.at[pl.ds(2 * q, 2)], out_theta.at[pl.ds(2 * q, 2)], out_sem.at[0])
        for q in range(pieces_of)
    ]
    for copy in stores:
        copy.start()
    total = parts.shape[0]
    value = parts[...]
    error = jnp.zeros_like(value)
    half = total // 2
    while half >= 8:
        value, e = two_sum(value[:half], value[half:])
        error = error[:half] + error[half:] + e
        half //= 2
    for shift in (4, 2, 1):
        value, e = two_sum(value, pltpu.roll(value, shift, 0))
        error = error + pltpu.roll(error, shift, 0) + e
    lane = iota((1, LANES), 1)
    error = jnp.where(
        jnp.logical_and(lane >= SLOTS, lane < 2 * SLOTS), pltpu.roll(error[0:1], SLOTS, 1), 0.0
    )
    message = value[0:1] + error
    high, low = quick(message, pltpu.roll(message, LANES - SLOTS, 1))

    gram = {}
    for n, (a, b) in enumerate(PAIRS):
        gram[a, b] = gram[b, a] = tuple(
            jnp.broadcast_to(x[:, n:n + 1], (1, LANES)) for x in (high, low)
        )
    size = BASIS - 1

    def scaled(x, factor):
        return x[0] * factor, x[1] * factor

    matrix = [
        [
            df_add(
                scaled(gram[a, b + 1], 4.0),
                df_add(scaled(gram[a, b], 4.0), gram[a, b]),
            )
            for b in range(size)
        ]
        for a in range(size)
    ]
    right = [gram[0, a] for a in range(size)]
    for p in range(size):
        for a in range(p + 1, size):
            factor = df_div(matrix[a][p], matrix[p][p])
            for b in range(p + 1, size):
                matrix[a][b] = df_sub(matrix[a][b], df_mul(factor, matrix[p][b]))
            right[a] = df_sub(right[a], df_mul(factor, right[p]))
    answer = [None] * size
    for p in reversed(range(size)):
        value = right[p][0]
        for b in range(p + 1, size):
            value = value - matrix[p][b][0] * answer[b][0]
        answer[p] = (value / matrix[p][p][0],)
    strip = psi.shape[0]
    spread = [jnp.broadcast_to(x[0], (strip, LANES)) for x in answer]

    def combine(c, _):
        lanes = pl.ds(pl.multiple_of(c * LANES, LANES), LANES)
        value = spread[size - 1] * vectors[size - 1, c]
        for b in reversed(range(size - 1)):
            value = value + spread[b] * vectors[b, c]
        psi[:, lanes] = value
        return 0

    lax.fori_loop(0, vectors.shape[1], combine, 0)

    store_psi = pltpu.make_async_copy(psi, out_psi, out_sem.at[1])
    store_psi.start()
    store_psi.wait()
    pltpu.make_async_copy(fresh, out_theta, out_sem.at[0]).wait()


def per_device(nlon, nlat, theta, kappa, layer_weight, diag, land_blocks):
    levels, cy, cx = theta.shape
    strip, ny = diag.shape
    wide = strip + 2 * HALO
    vmem = pl.BlockSpec(memory_space=pltpu.VMEM)
    hbm = pl.BlockSpec(memory_space=pltpu.HBM)
    dma = pltpu.SemaphoreType.DMA
    operands = (layer_weight, land_blocks, theta, kappa, diag)
    fresh, vectors, parts = pl.pallas_call(
        functools.partial(kernel, nlon, nlat),
        out_shape=(
            jax.ShapeDtypeStruct(theta.shape, F32),
            jax.ShapeDtypeStruct((BASIS - 1, nlat, strip, cy), F32),
            jax.ShapeDtypeStruct((nlon * nlat, LANES), F32),
        ),
        in_specs=[hbm] * 5,
        out_specs=(vmem, vmem, vmem),
        scratch_shapes=[
            pltpu.SMEM(layer_weight.shape, F32),
            pltpu.VMEM(land_blocks.shape, jnp.int32),
            pltpu.VMEM((levels, cy, cx), F32),
            pltpu.VMEM((cy, cx), F32),
            pltpu.VMEM((cy, cx), F32),
            pltpu.VMEM((cx + 2 * HALO, cy), F32),
            pltpu.VMEM((nlat, 8, LANES), F32),
            pltpu.VMEM((nlat, wide, cy), F32),
            pltpu.VMEM((2, HALO, cy), F32),
            pltpu.VMEM((nlat, wide, cy), F32),
            pltpu.VMEM((nlat, HALO, cy), F32),
            pltpu.VMEM((BODY, LANES), F32),
            pltpu.VMEM((nlat, LANES), F32),
            pltpu.VMEM((strip, ny), F32),
            pltpu.VMEM((nlat + 1, wide, cy), F32),
            pltpu.VMEM((wide, ny + LANES), F32),
            pltpu.VMEM((wide, ny + LANES), F32),
            pltpu.VMEM((wide, ny + LANES), F32),
            pltpu.VMEM((BASIS, nlat + 1, strip + 2 * INNER + 2 * PAD, cy), F32),
            pltpu.VMEM((2, levels, cx), F32),
            pltpu.VMEM((levels, cx), F32),
            pltpu.VMEM((levels, cx), F32),
            pltpu.VMEM((cy, LANES), F32),
            pltpu.VMEM((cy, LANES), F32),
            pltpu.VMEM((cy, LANES), F32),
            pltpu.VMEM((nlat, 8, LANES), F32),
            pltpu.VMEM((8, LANES), F32),
            pltpu.VMEM((8, LANES), F32),
            pltpu.VMEM((nlon * nlat, LANES), F32),
            dma((8,)),
            dma,
            dma,
            dma((2,)),
            dma,
            dma,
            dma,
            dma,
            dma((2,)),
            dma((5,)),
            dma((5,)),
            dma((4,)),
            dma((4,)),
            dma,
            dma,
            pltpu.SemaphoreType.REGULAR,
        ],
        compiler_params=pltpu.CompilerParams(
            collective_id=0, has_side_effects=True, vmem_limit_bytes=32 << 20,
        ),
        name="ocean_step",
    )(*[pltpu.with_memory_space_constraint(x, pltpu.HBM) for x in operands])
    return pl.pallas_call(
        finish,
        out_shape=(
            jax.ShapeDtypeStruct(theta.shape, F32),
            jax.ShapeDtypeStruct(diag.shape, F32),
        ),
        in_specs=[vmem, vmem, vmem],
        out_specs=(hbm, hbm),
        scratch_shapes=[pltpu.VMEM(diag.shape, F32), dma((2,))],
        compiler_params=pltpu.CompilerParams(vmem_limit_bytes=16 << 20),
        name="ocean_finish",
    )(fresh, vectors, parts)


def solution(mesh):
    placed = (P(None, "lat", "lon"), P("lat", "lon"), P(), P(("lon", "lat"), None), P())
    return jax.shard_map(
        functools.partial(per_device, mesh.shape["lon"], mesh.shape["lat"]),
        mesh=mesh,
        in_specs=placed,
        out_specs=(P(None, "lat", "lon"), P(("lon", "lat"), None)),
        check_vma=False,
    )
```
